32 devices in a mesh: grp: 2 (over x), ctx: 4 (over z), wsh: 4 (over y, core).
Axes of the slice: x: 2, y: 2, z: 4, core: 2. Of those that a mesh axis runs over, the one named last changes fastest.
Arguments:
- inputs: bfloat16 [2, 4, 2048, 1024], P('grp', 'wsh', 'ctx'), may hold values from -6 to 6
- w_qkv: bfloat16 [1024, 3072], P('wsh'), may hold values from -0.1875 to 0.1875
- w_out: bfloat16 [1024, 1024], P('wsh'), may hold values from -0.1875 to 0.1875
- w_up: bfloat16 [1024, 4096], P('wsh'), may hold values from -0.1875 to 0.1875
- w_down: bfloat16 [4096, 1024], P('wsh'), may hold values from -0.09375 to 0.09375
- norm_gains: float32 [4, 1024], replicated, may hold values from 0.5 to 1.5
- norm_biases: float32 [4, 1024], replicated, may hold values from -2 to 2
- block_map: int32 [2, 4, 4, 2], P('grp', 'wsh', 'ctx'), may hold values from 0 to 1024, as said below
- out_grad: bfloat16 [2, 4, 2048, 1024], P('grp', 'wsh', 'ctx'), may hold values from -6 to 6
Outputs:
- output: bfloat16 [2, 4, 2048, 1024], P('grp', 'wsh', 'ctx')
- input_grad: float32 [2, 4, 2048, 1024], P('grp', 'wsh', 'ctx')
- grad_qkv: float32 [1024, 3072], P('wsh')
- grad_attn_out: float32 [1024, 1024], P('wsh')
- grad_up: float32 [1024, 4096], P('wsh')
- grad_down: float32 [4096, 1024], P('wsh')
- grad_gains: float32 [4, 1024], replicated
- grad_biases: float32 [4, 1024], replicated
The draws below stay inside these ranges and needn't reach their ends.
Inputs may be any that keep to these rules, and one draw needn't show every extreme that they name: `block_map`: for each grp and wsh index the 4 context blocks are the 2 prompt blocks (sequence 0, first positions 0, 512, 1024 and so on) and one block of each continuation 1 to 4 // 2 (first position 1024), in an order drawn for each family.
All inputs are finite; a program needn't handle non-finite values.
Results may differ from the reference program's by a relative error of at most 0.017.
Values may be sent and summed in bfloat16 or wider, within the bound.
A program may use at most 384 MiB of HBM per device.

```python
import math
import jax
import jax.numpy as jnp
from jax import lax

D = 1024
HEADS = 16
DH = 64
FF = 4096
BLK = 512
FAM = 2048
N_GRP = 2
N_CTX = 4
N_WSH = 4


def draw_block_map(key, part):
    half_count = N_CTX // 2
    block_kind = jnp.arange(N_CTX, dtype=jnp.int32)
    seq_of = jnp.where(block_kind < half_count, 0, block_kind - half_count + 1).astype(jnp.int32)
    offset_of = jnp.where(block_kind < half_count, block_kind * BLK, half_count * BLK).astype(jnp.int32)
    family_keys = jax.random.split(key, N_GRP * N_WSH)
    orders = jax.vmap(lambda family_key: jax.random.permutation(family_key, N_CTX))(family_keys)
    block_table = jnp.stack([seq_of[orders], offset_of[orders]], axis=-1)
    return block_table.reshape(N_GRP, N_WSH, N_CTX, 2).astype(jnp.int32)


def block_levels(rng, dims, shards, least, largest):
    loudness, own = 1.0, jax.random.fold_in(rng, 6)
    for dim, parts in shards:
        steps = jnp.exp(jax.random.uniform(jax.random.fold_in(own, dim), (parts,), jnp.float32, least / len(shards), largest / len(shards)))
        loudness = loudness * jnp.repeat(steps, dims[dim] // parts).reshape([-1 if axis == dim else 1 for axis in range(len(dims))])
    return loudness


def scatter_about(own_key, dims, scale, reach, pieces=(), kind=jnp.bfloat16):
    values = jax.random.normal(own_key, dims, jnp.float32) * scale
    if len(pieces) > 0:
        values = block_levels(own_key, dims, pieces, -0.22, 0.18) * values
    return jnp.clip(values, min=-reach, max=reach).astype(kind)


def setup_inputs(seed: int = 0) -> dict:
    streams_of = jax.random.split(jax.random.key(seed), 10)
    return {
        "inputs": scatter_about(streams_of[0], (N_GRP, N_WSH, FAM, D), 1.0, 6.0, ((0, 2), (1, 4), (2, 4))),
        "w_qkv": scatter_about(streams_of[1], (D, 3 * D), D ** -0.5, 0.1875, ((0, 4),)),
        "w_out": scatter_about(streams_of[2], (D, D), D ** -0.5, 0.1875, ((0, 4),)),
        "w_up": scatter_about(streams_of[3], (D, FF), D ** -0.5, 0.1875, ((0, 4),)),
        "w_down": scatter_about(streams_of[4], (FF, D), FF ** -0.5, 0.09375, ((0, 4),)),
        "norm_gains": jnp.clip(1.0 + 0.1 * jax.random.normal(streams_of[5], (4, D), jnp.float32), 0.5, 1.5),
        "norm_biases": scatter_about(streams_of[6], (4, D), 0.3, 2.0, (), jnp.float32),
        "block_map": draw_block_map(jax.random.fold_in(streams_of[9], 71), 0),
        "out_grad": scatter_about(streams_of[8], (N_GRP, N_WSH, FAM, D), 1.0, 6.0, ((0, 2), (1, 4), (2, 4))),
    }


EPS = 1e-05
ALPHA = 32.0
NEG = -1e+30

@jax.custom_vjp
def low(v):
    return lax.optimization_barrier(v.astype(jnp.bfloat16)).astype(jnp.float32)

@jax.custom_vjp
def low_back(v):
    return v

def low_keep(v):
    return (low(v), None)

def low_pass(kept, grad):
    return (grad,)

def back_keep(v):
    return (v, None)

def back_low(kept, grad):
    return (low(grad),)
low.defvjp(low_keep, low_pass)
low_back.defvjp(back_keep, back_low)

def matmul(left_side, right_side):
    return jnp.dot(left_side, right_side, precision=lax.Precision.HIGHEST, preferred_element_type=jnp.float32)

def layer_norm(values, gain_row, bias_row):
    centre = values - lax.optimization_barrier(jnp.mean(values, axis=-1, keepdims=True))
    spread = lax.optimization_barrier(jnp.mean(centre * centre, axis=-1, keepdims=True))
    return centre * lax.rsqrt(spread + EPS) * gain_row + bias_row

def family_attention(queries, key_heads, value_heads, seq_ids, positions):
    total_rows = queries.shape[0]
    step_rows = min(total_rows, 512)
    block_count = total_rows // step_rows

    def one_block(block_args):
        query_block, seq_block, position_block = block_args
        raw_scores = low_back(jnp.einsum('qhd,khd->hqk', query_block, key_heads, precision=lax.Precision.HIGHEST))
        permit = ((seq_ids[None, :] == seq_block[:, None]) | (seq_ids[None, :] == 0)) & (positions[None, :] <= position_block[:, None])
        logits = jnp.where(permit[None], raw_scores * ALPHA, NEG)
        top_score = lax.optimization_barrier(jnp.max(logits, axis=-1, keepdims=True))
        exponent = jnp.exp(logits - top_score)
        probability = exponent / lax.optimization_barrier(jnp.sum(exponent, axis=-1, keepdims=True))
        return jnp.einsum('hqk,khd->qhd', low(probability), value_heads, precision=lax.Precision.HIGHEST)
    blocks_out = lax.map(jax.checkpoint(one_block), (queries.reshape(block_count, step_rows, HEADS, DH), seq_ids.reshape(block_count, step_rows), positions.reshape(block_count, step_rows)))
    return blocks_out.reshape(total_rows, HEADS, DH)

def reference(inputs, w_qkv, w_out, w_up, w_down, norm_gains, norm_biases, block_map, out_grad):
    families = N_GRP * N_WSH
    seq_ids = jnp.broadcast_to(block_map[:, :, :, 0:1], (N_GRP, N_WSH, N_CTX, BLK)).reshape(families, FAM).astype(jnp.int32)
    positions = (block_map[:, :, :, 1:2] + jnp.arange(BLK, dtype=jnp.int32)).reshape(families, FAM).astype(jnp.int32)
    query_scale = 1.0 / (ALPHA * math.sqrt(DH))

    def forward(tokens, qkv_weight, out_weight, up_weight, down_weight, gain_rows, bias_rows):
        normed = low(layer_norm(tokens, gain_rows[0], bias_rows[0]))
        projected = matmul(normed, qkv_weight)
        queries = low(low_back(projected[:, :D] * query_scale))
        key_heads = low(low_back(projected[:, D:2 * D]))
        value_heads = low(low_back(projected[:, 2 * D:]))

        def one_family(family_args):
            return family_attention(family_args[0], family_args[1], family_args[2], family_args[3], family_args[4])
        attended = lax.map(one_family, (queries.reshape(families, FAM, HEADS, DH), key_heads.reshape(families, FAM, HEADS, DH), value_heads.reshape(families, FAM, HEADS, DH), seq_ids, positions))
        attended = low(low_back(attended.reshape(-1, D)))
        branch = low_back(matmul(attended, out_weight))
        hidden = tokens + layer_norm(branch, gain_rows[1], bias_rows[1])
        pre_ffn = low(layer_norm(hidden, gain_rows[2], bias_rows[2]))
        upward = low_back(matmul(pre_ffn, up_weight))
        activated = low(jax.nn.gelu(upward, approximate=True))
        downward = low_back(matmul(activated, down_weight))
        return hidden + layer_norm(downward, gain_rows[3], bias_rows[3])
    primal_out, pullback = jax.vjp(forward, inputs.astype(jnp.float32).reshape(-1, D), w_qkv.astype(jnp.float32), w_out.astype(jnp.float32), w_up.astype(jnp.float32), w_down.astype(jnp.float32), norm_gains, norm_biases)
    gradients = pullback(out_grad.astype(jnp.float32).reshape(-1, D))
    full_shape = inputs.shape
    return (primal_out.astype(jnp.bfloat16).reshape(full_shape), gradients[0].reshape(full_shape), gradients[1], gradients[2], gradients[3], gradients[4], gradients[5], gradients[6])
```

```python
import functools
import math

import jax
import jax.numpy as jnp
from jax import lax
from jax.experimental import pallas as pl
from jax.experimental.pallas import tpu as pltpu
from jax.sharding import PartitionSpec as P

D = 1024
HEADS = 16
DH = 64
BLK = 512
PAIRS = HEADS // 2
QT = 256

EPS = 1e-05
ALPHA = 32.0
NEG = -1e30
LOG2E = 1.4426950408889634
C2 = ALPHA * LOG2E
QSCALE = 1.0 / (ALPHA * math.sqrt(DH))


def layer_norm(values, gain_row, bias_row):
    centre = values - jnp.mean(values, axis=-1, keepdims=True)
    spread = jnp.mean(centre * centre, axis=-1, keepdims=True)
    return centre * lax.rsqrt(spread + EPS) * gain_row + bias_row


def gelu_tanh(values):
    return jax.nn.gelu(values, approximate=True)


def dot_dims(left_side, right_side, left_dim, right_dim):
    return lax.dot_general(
        left_side,
        right_side,
        (((left_dim,), (right_dim,)), ((), ())),
        preferred_element_type=jnp.float32,
    )


def contract_last(left_side, right_side):
    return dot_dims(left_side, right_side, 1, 1)


def contract_rows(left_side, right_side):
    return dot_dims(left_side, right_side, 0, 0)


def head_lanes(head, rows):
    lane = lax.broadcasted_iota(jnp.int32, (rows, 128), 1)
    return (lane >= DH) if head else (lane < DH)


def causal_tile():
    row = lax.broadcasted_iota(jnp.int32, (QT, QT), 0)
    col = lax.broadcasted_iota(jnp.int32, (QT, QT), 1)
    return col <= row


def attn_fwd_kernel(slots, slot_ref, q_ref, k_ref, v_ref, o_ref, lse_ref):
    own_slot = slot_ref[0]
    causal = causal_tile()
    for tile in range(BLK // QT):
        rows = pl.ds(tile * QT, QT)
        own_keys = (tile + 1) * QT
        q_pair = q_ref[rows, :]
        outs, lses = [], []
        for head in range(2):
            q_head = jnp.where(head_lanes(head, QT), q_pair, jnp.zeros_like(q_pair))
            diag = contract_last(q_head, k_ref[pl.ds(tile * QT, QT), :])
            diag = jnp.where(causal, diag, NEG)
            parts = [(diag, tile * QT, QT, None)]
            top = jnp.max(diag, axis=-1, keepdims=True)
            if tile:
                low_part = contract_last(q_head, k_ref[pl.ds(0, tile * QT), :])
                parts.append((low_part, 0, tile * QT, None))
                top = jnp.maximum(top, jnp.max(low_part, axis=-1, keepdims=True))
            for slot in range(slots):
                visible = slot < own_slot
                part = contract_last(q_head, k_ref[pl.ds((slot + 1) * BLK, BLK), :])
                parts.append((part, (slot + 1) * BLK, BLK, visible))
                slot_top = jnp.max(part, axis=-1, keepdims=True)
                top = jnp.maximum(top, jnp.where(visible, slot_top, NEG))
            shift = top * C2
            total = jnp.zeros((QT, 1), jnp.float32)
            acc = jnp.zeros((QT, 128), jnp.float32)
            for part, start, size, visible in parts:
                row_shift = shift if visible is None else shift + jnp.where(visible, 0.0, 1e30)
                expo = jnp.exp2(part * C2 - row_shift)
                total = total + jnp.sum(expo, axis=-1, keepdims=True)
                acc = acc + dot_dims(expo.astype(jnp.bfloat16), v_ref[pl.ds(start, size), :], 1, 0)
            outs.append(acc / total)
            lses.append(jnp.broadcast_to(shift + jnp.log2(total), (QT, 128)))
        first = head_lanes(0, QT)
        o_ref[rows, :] = jnp.where(first, outs[0], outs[1]).astype(jnp.bfloat16)
        lse_ref[0, rows, :] = jnp.where(first, lses[0], lses[1])


def attention_forward(own_slot, queries, keys_values, slots):
    keys = (slots + 1) * BLK
    return pl.pallas_call(
        functools.partial(attn_fwd_kernel, slots),
        out_shape=(
            jax.ShapeDtypeStruct((BLK, D), jnp.bfloat16),
            jax.ShapeDtypeStruct((PAIRS, BLK, 128), jnp.float32),
        ),
        grid_spec=pltpu.PrefetchScalarGridSpec(
            num_scalar_prefetch=1,
            grid=(PAIRS,),
            in_specs=[
                pl.BlockSpec((BLK, 128), lambda i, s: (0, i)),
                pl.BlockSpec((keys, 128), lambda i, s: (0, i)),
                pl.BlockSpec((keys, 128), lambda i, s: (0, i + PAIRS)),
            ],
            out_specs=(
                pl.BlockSpec((BLK, 128), lambda i, s: (0, i)),
                pl.BlockSpec((1, BLK, 128), lambda i, s: (i, 0, 0)),
            ),
        ),
        compiler_params=pltpu.CompilerParams(vmem_limit_bytes=48 << 20),
        cost_estimate=pl.CostEstimate(
            flops=4 * BLK * keys * D, bytes_accessed=16 << 20, transcendentals=BLK * keys * HEADS
        ),
        name="attn_fwd",
    )(own_slot, queries, keys_values, keys_values)


def attn_bwd_kernel(
    slots, slot_ref, q_ref, k_ref, v_ref, o_ref, do_ref, lse_ref, dq_ref, dk_ref, dv_ref, dk_acc, dv_acc
):
    own_slot = slot_ref[0]
    causal = causal_tile()
    dk_acc[...] = jnp.zeros_like(dk_acc)
    dv_acc[...] = jnp.zeros_like(dv_acc)
    for tile in range(BLK // QT):
        rows = pl.ds(tile * QT, QT)
        q_pair = q_ref[rows, :]
        do_pair = do_ref[rows, :]
        q_turned = q_pair.T
        do_turned = do_pair.T
        prod = do_pair.astype(jnp.float32) * o_ref[rows, :].astype(jnp.float32)
        lse_pair = lse_ref[0, rows, :]
        dqs = []
        for head in range(2):
            lanes = head_lanes(head, QT)
            turned = slice(head * DH, (head + 1) * DH)
            q_head = jnp.where(lanes, q_pair, jnp.zeros_like(q_pair))
            do_head = jnp.where(lanes, do_pair, jnp.zeros_like(do_pair))
            delta = jnp.sum(jnp.where(lanes, prod, 0.0), axis=-1, keepdims=True)
            lse = lse_pair[:, head * DH : head * DH + 1]
            spans = [(tile * QT, QT, None, True)]
            if tile:
                spans.append((0, tile * QT, None, False))
            spans += [((s + 1) * BLK, BLK, s < own_slot, False) for s in range(slots)]
            dq = jnp.zeros((QT, 128), jnp.float32)
            for start, size, visible, diagonal in spans:
                keys = pl.ds(start, size)
                k_part = k_ref[keys, :]
                row_shift = lse if visible is None else lse + jnp.where(visible, 0.0, 1e30)
                prob = jnp.exp2(contract_last(q_head, k_part) * C2 - row_shift)
                if diagonal:
                    prob = jnp.where(causal, prob, 0.0)
                dprob = contract_last(do_head, v_ref[keys, :])
                dlogit = (prob * (dprob - delta)).astype(jnp.bfloat16)
                dq = dq + dot_dims(dlogit, k_part, 1, 0)
                dk_acc[turned, keys] += dot_dims(q_turned[turned, :], dlogit, 1, 0)
                dv_acc[turned, keys] += dot_dims(
                    do_turned[turned, :], prob.astype(jnp.bfloat16), 1, 0
                )
            dqs.append(dq)
        dq_ref[rows, :] = (
            jnp.where(head_lanes(0, QT), dqs[0], dqs[1]) * ALPHA
        ).astype(jnp.bfloat16) * jnp.bfloat16(QSCALE)
    dk_ref[...] = (dk_acc[...] * ALPHA).astype(jnp.bfloat16)
    dv_ref[...] = dv_acc[...].astype(jnp.bfloat16)


def attention_backward(own_slot, queries, keys_values, attended, grad_out, lse, slots):
    keys = (slots + 1) * BLK
    pair = pl.BlockSpec((BLK, 128), lambda i, s: (0, i))
    turned = pl.BlockSpec((128, keys), lambda i, s: (i, 0))
    return pl.pallas_call(
        functools.partial(attn_bwd_kernel, slots),
        out_shape=(
            jax.ShapeDtypeStruct((BLK, D), jnp.bfloat16),
            jax.ShapeDtypeStruct((D, keys), jnp.bfloat16),
            jax.ShapeDtypeStruct((D, keys), jnp.bfloat16),
        ),
        grid_spec=pltpu.PrefetchScalarGridSpec(
            num_scalar_prefetch=1,
            grid=(PAIRS,),
            in_specs=[
                pair,
                pl.BlockSpec((keys, 128), lambda i, s: (0, i)),
                pl.BlockSpec((keys, 128), lambda i, s: (0, i + PAIRS)),
                pair,
                pair,
                pl.BlockSpec((1, BLK, 128), lambda i, s: (i, 0, 0)),
            ],
            out_specs=(pair, turned, turned),
            scratch_shapes=[pltpu.VMEM((128, keys), jnp.float32)] * 2,
        ),
        compiler_params=pltpu.CompilerParams(vmem_limit_bytes=48 << 20),
        cost_estimate=pl.CostEstimate(
            flops=10 * BLK * keys * D, bytes_accessed=24 << 20, transcendentals=BLK * keys * HEADS
        ),
        name="attn_bwd",
    )(own_slot, queries, keys_values, keys_values, attended, grad_out, lse)


def per_device(n_ctx, inputs, w_qkv, w_out, w_up, w_down, norm_gains, norm_biases, block_map, out_grad):
    slots = n_ctx // 2
    raw = inputs.reshape(BLK, D)
    tokens = raw.astype(jnp.float32)
    block_entry = block_map.reshape(2)
    own_slot = block_entry[1] // BLK
    own_tag = jnp.where(block_entry[0] == 0, own_slot, n_ctx)
    tag_rows = jnp.full((16, D), own_tag.astype(jnp.bfloat16))
    full_qkv = lax.all_gather(w_qkv, "wsh", axis=0, tiled=True)
    shared = lax.all_gather(jnp.concatenate([raw, tag_rows], axis=0), "ctx", axis=0)
    full_out, full_up, full_down = (
        lax.all_gather(w_out, "wsh", axis=0, tiled=True),
        lax.all_gather(w_up, "wsh", axis=0, tiled=True),
        lax.all_gather(w_down, "wsh", axis=0, tiled=True),
    )
    tags = shared[:, BLK, 0].astype(jnp.int32)
    prompt = [
        lax.dynamic_index_in_dim(shared, jnp.argmax(tags == slot), 0, keepdims=False)[:BLK]
        for slot in range(slots)
    ]
    slot_vec = own_slot.reshape(1)

    first_norm, first_back = jax.vjp(layer_norm, tokens, norm_gains[0], norm_biases[0])
    normed_low = first_norm.astype(jnp.bfloat16)
    prompt_low = layer_norm(
        jnp.concatenate(prompt, axis=0).astype(jnp.float32), norm_gains[0], norm_biases[0]
    ).astype(jnp.bfloat16)
    every_low = jnp.concatenate([normed_low, prompt_low], axis=0)
    queries = (
        jnp.dot(normed_low, full_qkv[:, :D], preferred_element_type=jnp.float32) * QSCALE
    ).astype(jnp.bfloat16)
    keys_values = jnp.dot(
        every_low, full_qkv[:, D:], preferred_element_type=jnp.float32
    ).astype(jnp.bfloat16)
    attn_low, lse = attention_forward(slot_vec, queries, keys_values, slots)

    branch = jnp.dot(attn_low, full_out, preferred_element_type=jnp.float32)
    post_attn, attn_back = jax.vjp(layer_norm, branch, norm_gains[1], norm_biases[1])
    hidden = tokens + post_attn
    pre_ffn, ffn_back = jax.vjp(layer_norm, hidden, norm_gains[2], norm_biases[2])
    ffn_low = pre_ffn.astype(jnp.bfloat16)
    upward = jnp.dot(ffn_low, full_up, preferred_element_type=jnp.float32)
    activated, gelu_back = jax.vjp(gelu_tanh, upward)
    active_low = activated.astype(jnp.bfloat16)
    downward = jnp.dot(active_low, full_down, preferred_element_type=jnp.float32)
    post_ffn, post_back = jax.vjp(layer_norm, downward, norm_gains[3], norm_biases[3])
    result = (hidden + post_ffn).astype(jnp.bfloat16).reshape(1, 1, BLK, D)
    seed_grad = out_grad.reshape(BLK, D).astype(jnp.float32)
    grad_down_in, gain_grad3, bias_grad3 = post_back(seed_grad)
    down_low = grad_down_in.astype(jnp.bfloat16)
    term_down = contract_rows(active_low, down_low).astype(jnp.bfloat16)
    grad_active = contract_last(down_low, full_down)
    up_low = gelu_back(grad_active)[0].astype(jnp.bfloat16)
    term_up = contract_rows(ffn_low, up_low).astype(jnp.bfloat16)
    grad_pre_ffn, gain_grad2, bias_grad2 = ffn_back(contract_last(up_low, full_up))
    grad_hidden = seed_grad + grad_pre_ffn
    grad_branch, gain_grad1, bias_grad1 = attn_back(grad_hidden)
    branch_low = grad_branch.astype(jnp.bfloat16)
    term_out = contract_rows(attn_low, branch_low).astype(jnp.bfloat16)
    grad_out_low = contract_last(branch_low, full_out).astype(jnp.bfloat16)

    grad_q, grad_k, grad_v = attention_backward(
        slot_vec, queries, keys_values, attn_low, grad_out_low, lse, slots
    )
    grad_kv = jnp.concatenate([grad_k, grad_v], axis=0)
    grad_normed_kv = dot_dims(grad_kv, full_qkv[:, D:], 0, 1)
    partial = grad_normed_kv[BLK:].astype(jnp.bfloat16)
    totals = lax.psum(partial, "ctx").reshape(slots, BLK, D)
    from_others = lax.dynamic_index_in_dim(
        totals, jnp.minimum(own_slot, slots - 1), 0, keepdims=False
    ).astype(jnp.float32)
    from_others = jnp.where(own_slot < slots, from_others, 0.0)
    grad_normed = contract_last(grad_q, full_qkv[:, :D]) + grad_normed_kv[:BLK] + from_others
    term_qkv = jnp.concatenate(
        [
            contract_rows(normed_low, grad_q).astype(jnp.bfloat16),
            dot_dims(every_low, grad_kv, 0, 1).astype(jnp.bfloat16),
        ],
        axis=1,
    )
    grad_tokens, gain_grad0, bias_grad0 = first_back(grad_normed)
    grad_input = (grad_hidden + grad_tokens).reshape(1, 1, BLK, D)

    def reduced(term):
        shard = lax.psum_scatter(term, "wsh", scatter_dimension=0, tiled=True)
        return lax.psum(shard, ("grp", "ctx")).astype(jnp.float32)

    summed_down, summed_up, summed_out, summed_qkv = (
        reduced(term_down),
        reduced(term_up),
        reduced(term_out),
        reduced(term_qkv),
    )
    gain_stack = jnp.stack([gain_grad0, gain_grad1, gain_grad2, gain_grad3])
    bias_stack = jnp.stack([bias_grad0, bias_grad1, bias_grad2, bias_grad3])
    gain_total, bias_total = lax.psum((gain_stack, bias_stack), ("grp", "ctx", "wsh"))
    return (
        result,
        grad_input,
        summed_qkv,
        summed_out,
        summed_up,
        summed_down,
        gain_total,
        bias_total,
    )


def solution(mesh):
    rows = P("wsh", None)
    blocks = P("grp", "wsh", "ctx", None)
    return jax.shard_map(
        functools.partial(per_device, mesh.shape["ctx"]),
        mesh=mesh,
        in_specs=(blocks, rows, rows, rows, rows, P(), P(), blocks, blocks),
        out_specs=(blocks, blocks, rows, rows, rows, rows, P(), P()),
        check_vma=False,
    )
```

```python
import functools
import math

import jax
import jax.numpy as jnp
from jax import lax
from jax.experimental import pallas as pl
from jax.experimental.pallas import tpu as pltpu
from jax.sharding import PartitionSpec as P

D = 1024
HEADS = 16
DH = 64
BLK = 512
PAIRS = HEADS // 2
QT = 256

EPS = 1e-05
ALPHA = 32.0
NEG = -1e30
LOG2E = 1.4426950408889634
C2 = ALPHA * LOG2E
MESH = pl.DeviceIdType.MESH
QSCALE = 1.0 / (ALPHA * math.sqrt(DH))


def layer_norm(values, gain_row, bias_row):
    centre = values - jnp.mean(values, axis=-1, keepdims=True)
    spread = jnp.mean(centre * centre, axis=-1, keepdims=True)
    return centre * lax.rsqrt(spread + EPS) * gain_row + bias_row


def gelu_tanh(values):
    return jax.nn.gelu(values, approximate=True)


def dot_dims(left_side, right_side, left_dim, right_dim):
    return lax.dot_general(
        left_side,
        right_side,
        (((left_dim,), (right_dim,)), ((), ())),
        preferred_element_type=jnp.float32,
    )


def contract_last(left_side, right_side):
    return dot_dims(left_side, right_side, 1, 1)


def contract_rows(left_side, right_side):
    return dot_dims(left_side, right_side, 0, 0)


def head_lanes(head, rows):
    lane = lax.broadcasted_iota(jnp.int32, (rows, 128), 1)
    return (lane >= DH) if head else (lane < DH)


def causal_tile():
    row = lax.broadcasted_iota(jnp.int32, (QT, QT), 0)
    col = lax.broadcasted_iota(jnp.int32, (QT, QT), 1)
    return col <= row


def attn_fwd_kernel(slots, slot_ref, q_ref, k_ref, v_ref, o_ref, lse_ref):
    own_slot = slot_ref[0]
    causal = causal_tile()
    for tile in range(BLK // QT):
        rows = pl.ds(tile * QT, QT)
        own_keys = (tile + 1) * QT
        q_pair = q_ref[rows, :]
        outs, lses = [], []
        for head in range(2):
            q_head = jnp.where(head_lanes(head, QT), q_pair, jnp.zeros_like(q_pair))
            diag = contract_last(q_head, k_ref[pl.ds(tile * QT, QT), :])
            diag = jnp.where(causal, diag, NEG)
            parts = [(diag, tile * QT, QT, None)]
            top = jnp.max(diag, axis=-1, keepdims=True)
            if tile:
                low_part = contract_last(q_head, k_ref[pl.ds(0, tile * QT), :])
                parts.append((low_part, 0, tile * QT, None))
                top = jnp.maximum(top, jnp.max(low_part, axis=-1, keepdims=True))
            for slot in range(slots):
                visible = slot < own_slot
                part = contract_last(q_head, k_ref[pl.ds((slot + 1) * BLK, BLK), :])
                parts.append((part, (slot + 1) * BLK, BLK, visible))
                slot_top = jnp.max(part, axis=-1, keepdims=True)
                top = jnp.maximum(top, jnp.where(visible, slot_top, NEG))
            shift = top * C2
            total = jnp.zeros((QT, 1), jnp.float32)
            acc = jnp.zeros((QT, 128), jnp.float32)
            for part, start, size, visible in parts:
                row_shift = shift if visible is None else shift + jnp.where(visible, 0.0, 1e30)
                expo = jnp.exp2(part * C2 - row_shift)
                total = total + jnp.sum(expo, axis=-1, keepdims=True)
                acc = acc + dot_dims(expo.astype(jnp.bfloat16), v_ref[pl.ds(start, size), :], 1, 0)
            outs.append(acc / total)
            lses.append(jnp.broadcast_to(shift + jnp.log2(total), (QT, 128)))
        first = head_lanes(0, QT)
        o_ref[rows, :] = jnp.where(first, outs[0], outs[1]).astype(jnp.bfloat16)
        lse_ref[0, rows, :] = jnp.where(first, lses[0], lses[1])


def attention_forward(own_slot, queries, keys_values, slots):
    keys = (slots + 1) * BLK
    return pl.pallas_call(
        functools.partial(attn_fwd_kernel, slots),
        out_shape=(
            jax.ShapeDtypeStruct((BLK, D), jnp.bfloat16),
            jax.ShapeDtypeStruct((PAIRS, BLK, 128), jnp.float32),
        ),
        grid_spec=pltpu.PrefetchScalarGridSpec(
            num_scalar_prefetch=1,
            grid=(PAIRS,),
            in_specs=[
                pl.BlockSpec((BLK, 128), lambda i, s: (0, i)),
                pl.BlockSpec((keys, 128), lambda i, s: (0, i)),
                pl.BlockSpec((keys, 128), lambda i, s: (0, i + PAIRS)),
            ],
            out_specs=(
                pl.BlockSpec((BLK, 128), lambda i, s: (0, i)),
                pl.BlockSpec((1, BLK, 128), lambda i, s: (i, 0, 0)),
            ),
        ),
        compiler_params=pltpu.CompilerParams(vmem_limit_bytes=48 << 20),
        cost_estimate=pl.CostEstimate(
            flops=4 * BLK * keys * D, bytes_accessed=16 << 20, transcendentals=BLK * keys * HEADS
        ),
        name="attn_fwd",
    )(own_slot, queries, keys_values, keys_values)


def attn_bwd_kernel(
    slots, slot_ref, q_ref, k_ref, v_ref, o_ref, do_ref, lse_ref, dq_ref, dk_ref, dv_ref, dk_acc, dv_acc
):
    own_slot = slot_ref[0]
    causal = causal_tile()
    dk_acc[...] = jnp.zeros_like(dk_acc)
    dv_acc[...] = jnp.zeros_like(dv_acc)
    for tile in range(BLK // QT):
        rows = pl.ds(tile * QT, QT)
        q_pair = q_ref[rows, :]
        do_pair = do_ref[rows, :]
        q_turned = q_pair.T
        do_turned = do_pair.T
        prod = do_pair.astype(jnp.float32) * o_ref[rows, :].astype(jnp.float32)
        lse_pair = lse_ref[0, rows, :]
        dqs = []
        for head in range(2):
            lanes = head_lanes(head, QT)
            turned = slice(head * DH, (head + 1) * DH)
            q_head = jnp.where(lanes, q_pair, jnp.zeros_like(q_pair))
            do_head = jnp.where(lanes, do_pair, jnp.zeros_like(do_pair))
            delta = jnp.sum(jnp.where(lanes, prod, 0.0), axis=-1, keepdims=True)
            lse = lse_pair[:, head * DH : head * DH + 1]
            spans = [(tile * QT, QT, None, True)]
            if tile:
                spans.append((0, tile * QT, None, False))
            spans += [((s + 1) * BLK, BLK, s < own_slot, False) for s in range(slots)]
            dq = jnp.zeros((QT, 128), jnp.float32)
            for start, size, visible, diagonal in spans:
                keys = pl.ds(start, size)
                k_part = k_ref[keys, :]
                row_shift = lse if visible is None else lse + jnp.where(visible, 0.0, 1e30)
                prob = jnp.exp2(contract_last(q_head, k_part) * C2 - row_shift)
                if diagonal:
                    prob = jnp.where(causal, prob, 0.0)
                dprob = contract_last(do_head, v_ref[keys, :])
                dlogit = (prob * (dprob - delta)).astype(jnp.bfloat16)
                dq = dq + dot_dims(dlogit, k_part, 1, 0)
                dk_acc[turned, keys] += dot_dims(q_turned[turned, :], dlogit, 1, 0)
                dv_acc[turned, keys] += dot_dims(
                    do_turned[turned, :], prob.astype(jnp.bfloat16), 1, 0
                )
            dqs.append(dq)
        dq_ref[rows, :] = (
            jnp.where(head_lanes(0, QT), dqs[0], dqs[1]) * ALPHA
        ).astype(jnp.bfloat16) * jnp.bfloat16(QSCALE)
    dk_ref[...] = (dk_acc[...] * ALPHA).astype(jnp.bfloat16)
    dv_ref[...] = dv_acc[...].astype(jnp.bfloat16)


def attention_backward(own_slot, queries, keys_values, attended, grad_out, lse, slots):
    keys = (slots + 1) * BLK
    pair = pl.BlockSpec((BLK, 128), lambda i, s: (0, i))
    turned = pl.BlockSpec((128, keys), lambda i, s: (i, 0))
    return pl.pallas_call(
        functools.partial(attn_bwd_kernel, slots),
        out_shape=(
            jax.ShapeDtypeStruct((BLK, D), jnp.bfloat16),
            jax.ShapeDtypeStruct((D, keys), jnp.bfloat16),
            jax.ShapeDtypeStruct((D, keys), jnp.bfloat16),
        ),
        grid_spec=pltpu.PrefetchScalarGridSpec(
            num_scalar_prefetch=1,
            grid=(PAIRS,),
            in_specs=[
                pair,
                pl.BlockSpec((keys, 128), lambda i, s: (0, i)),
                pl.BlockSpec((keys, 128), lambda i, s: (0, i + PAIRS)),
                pair,
                pair,
                pl.BlockSpec((1, BLK, 128), lambda i, s: (i, 0, 0)),
            ],
            out_specs=(pair, turned, turned),
            scratch_shapes=[pltpu.VMEM((128, keys), jnp.float32)] * 2,
        ),
        compiler_params=pltpu.CompilerParams(vmem_limit_bytes=48 << 20),
        cost_estimate=pl.CostEstimate(
            flops=10 * BLK * keys * D, bytes_accessed=24 << 20, transcendentals=BLK * keys * HEADS
        ),
        name="attn_bwd",
    )(own_slot, queries, keys_values, keys_values, attended, grad_out, lse)


TILE = 256


def piece_parts(n_ctx):
    row_parts = min(n_ctx, 8)
    return row_parts, n_ctx // row_parts


def reduce_kernel(n_ctx, widths, *refs):
    count = len(widths)
    terms, outs = refs[:count], refs[count : 2 * count]
    (r1, r2, r3, r4, fin, local, stage) = refs[2 * count : 2 * count + 7]
    (sem_local, sem_out, send1, recv1, send2, recv2, send3, recv3, send4, recv4, send5, recv5, send6, recv6) = refs[
        2 * count + 7 :
    ]
    grp, ctx, wsh = lax.axis_index("grp"), lax.axis_index("ctx"), lax.axis_index("wsh")
    side, core = wsh // 2, wsh % 2
    core_peer = (grp, ctx, side * 2 + 1 - core)
    side_peer = (grp, ctx, (1 - side) * 2 + core)
    grp_peer = (1 - grp, ctx, wsh)
    ctx_peers = [(grp, lax.rem(ctx + step, n_ctx), wsh) for step in range(1, n_ctx)]

    barrier = pltpu.get_barrier_semaphore()
    for peer in [core_peer, side_peer, grp_peer] + ctx_peers:
        pl.semaphore_signal(barrier, inc=1, device_id=peer, device_id_type=MESH)
    pl.semaphore_wait(barrier, n_ctx + 2)

    row_parts, col_parts = piece_parts(n_ctx)
    half = TILE // 2
    part_rows, part_cols = half // row_parts, TILE // col_parts
    ranges, first = [], 0
    for rows, cols in widths:
        across = cols // TILE
        ranges.append((first, first + (rows // TILE) * across, across))
        first = ranges[-1][1]
    chunks = first

    def block(index, across):
        return (
            pl.ds(pl.multiple_of((index // across) * TILE, TILE), TILE),
            pl.ds(pl.multiple_of((index % across) * TILE, TILE), TILE),
        )

    def by_range(index, act):
        for place, (low, high, across) in enumerate(ranges):

            @pl.when((index >= low) & (index < high))
            def _(place=place, low=low, across=across):
                act(place, block(index - low, across))

    def part_of(position, offset):
        return (
            pl.ds(pl.multiple_of(offset + (position // col_parts) * part_rows, part_rows), part_rows),
            pl.ds(pl.multiple_of((position % col_parts) * part_cols, part_cols), part_cols),
        )

    def remote(src, dst, send, recv, peer):
        return pltpu.make_async_remote_copy(
            src_ref=src, dst_ref=dst, send_sem=send, recv_sem=recv, device_id=peer, device_id_type=MESH
        )

    def step_load(index):
        slot = lax.rem(index, 4)

        def act(place, span):
            term = terms[place]
            pltpu.make_async_copy(term.at[:, core, span[0], span[1]], local.at[slot], sem_local.at[slot]).start()
            remote(
                term.at[:, 1 - core, span[0], span[1]], r1.at[index], send1.at[slot], recv1.at[index], core_peer
            ).start()

        by_range(index, act)

    def step_core(index):
        slot = lax.rem(index, 4)
        pltpu.make_async_copy(local.at[slot], local.at[slot], sem_local.at[slot]).wait()
        whole = remote(r1.at[index], r1.at[index], send1.at[slot], recv1.at[index], core_peer)
        whole.wait_send()
        whole.wait_recv()
        r1[index] = r1[index] + local[slot]
        remote(r1.at[index, 1 - side], r2.at[index], send2.at[slot], recv2.at[index], side_peer).start()

    half_keep = pl.ds(pl.multiple_of(grp * half, half), half)
    half_give = pl.ds(pl.multiple_of((1 - grp) * half, half), half)

    def step_side(index):
        slot = lax.rem(index, 4)
        move = remote(r1.at[index, 1 - side], r2.at[index], send2.at[slot], recv2.at[index], side_peer)
        move.wait_send()
        move.wait_recv()
        r2[index] = r2[index] + r1[index, side]
        remote(r2.at[index, half_give], r3.at[index], send3.at[slot], recv3.at[index], grp_peer).start()

    def step_grp(index):
        slot = lax.rem(index, 4)
        move = remote(r2.at[index, half_give], r3.at[index], send3.at[slot], recv3.at[index], grp_peer)
        move.wait_send()
        move.wait_recv()
        r3[index] = r3[index] + r2[index, half_keep]
        for place, peer in enumerate(ctx_peers):
            rows, cols = part_of(peer[1], 0)
            remote(r3.at[index, rows, cols], r4.at[index, place], send4.at[slot], recv4.at[index], peer).start()

    def step_ctx(index):
        slot = lax.rem(index, 4)
        move = remote(r4.at[index], r4.at[index], send4.at[slot], recv4.at[index], ctx_peers[0])
        move.wait_send()
        move.wait_recv()
        rows, cols = part_of(ctx, 0)
        total = r3[index, rows, cols].astype(jnp.float32)
        for place in range(n_ctx - 1):
            total = total + r4[index, place].astype(jnp.float32)
        rows, cols = part_of(ctx, grp * half)
        fin[index, rows, cols] = total.astype(jnp.bfloat16)
        for peer in ctx_peers:
            here = fin.at[index, rows, cols]
            remote(here, here, send5.at[slot], recv5.at[index], peer).start()

    def step_back(index):
        slot = lax.rem(index, 4)
        move = remote(r4.at[index], r4.at[index], send5.at[slot], recv5.at[index], ctx_peers[0])
        move.wait_send()
        move.wait_recv()
        here = fin.at[index, half_keep]
        remote(here, here, send6.at[slot], recv6.at[index], grp_peer).start()

    def step_out(index):
        slot = lax.rem(index, 4)
        here = fin.at[index, half_give]
        move = remote(here, here, send6.at[slot], recv6.at[index], grp_peer)
        move.wait_send()
        move.wait_recv()

        @pl.when(index >= 4)
        def _():
            pltpu.make_async_copy(stage.at[slot], stage.at[slot], sem_out.at[slot]).wait()

        stage[slot] = fin[index].astype(jnp.float32)

        def act(place, span):
            pltpu.make_async_copy(stage.at[slot], outs[place].at[span[0], span[1]], sem_out.at[slot]).start()

        by_range(index, act)

    stages = (step_core, step_side, step_grp, step_ctx, step_back, step_out)

    step_load(0)
    step_load(1)

    def body(step, carry):
        @pl.when(step + 2 < chunks)
        def _():
            step_load(step + 2)

        for lag, act in enumerate(stages):
            index = step - lag

            @pl.when((index >= 0) & (index < chunks))
            def _(act=act, index=index):
                act(index)

        return carry

    lax.fori_loop(0, chunks + len(stages) - 1, body, 0)
    for slot in range(4):
        pltpu.make_async_copy(stage.at[slot], stage.at[slot], sem_out.at[slot]).wait()


def reduce_terms(n_ctx, terms):
    widths = [(term.shape[0] // 4, term.shape[1]) for term in terms]
    chunks = sum((rows // TILE) * (cols // TILE) for rows, cols in widths)
    row_parts, col_parts = piece_parts(n_ctx)
    part = (TILE // 2 // row_parts, TILE // col_parts)
    low = jnp.bfloat16
    dma = pltpu.SemaphoreType.DMA
    hbm = pl.BlockSpec(memory_space=pl.ANY)
    return pl.pallas_call(
        functools.partial(reduce_kernel, n_ctx, widths),
        out_shape=[jax.ShapeDtypeStruct(width, jnp.float32) for width in widths],
        in_specs=[hbm] * len(terms),
        out_specs=[hbm] * len(terms),
        scratch_shapes=[
            pltpu.VMEM((chunks, 2, TILE, TILE), low),
            pltpu.VMEM((chunks, TILE, TILE), low),
            pltpu.VMEM((chunks, TILE // 2, TILE), low),
            pltpu.VMEM((chunks, n_ctx - 1) + part, low),
            pltpu.VMEM((chunks, TILE, TILE), low),
            pltpu.VMEM((4, 2, TILE, TILE), low),
            pltpu.VMEM((4, TILE, TILE), jnp.float32),
            dma((4,)),
            dma((4,)),
        ]
        + [dma((4,)), dma((chunks,))] * 6,
        compiler_params=pltpu.CompilerParams(
            collective_id=0, has_side_effects=True, vmem_limit_bytes=60 << 20
        ),
        cost_estimate=pl.CostEstimate(flops=1 << 20, bytes_accessed=256 << 20, transcendentals=0),
        name="reduce_grads",
    )(*[term.reshape(2, 2, width[0], width[1]) for term, width in zip(terms, widths)])


def per_device(n_ctx, inputs, w_qkv, w_out, w_up, w_down, norm_gains, norm_biases, block_map, out_grad):
    slots = n_ctx // 2
    raw = inputs.reshape(BLK, D)
    tokens = raw.astype(jnp.float32)
    block_entry = block_map.reshape(2)
    own_slot = block_entry[1] // BLK
    own_tag = jnp.where(block_entry[0] == 0, own_slot, n_ctx)
    tag_rows = jnp.full((16, D), own_tag.astype(jnp.bfloat16))
    full_qkv = lax.all_gather(w_qkv, "wsh", axis=0, tiled=True)
    shared = lax.all_gather(jnp.concatenate([raw, tag_rows], axis=0), "ctx", axis=0)
    full_out, full_up, full_down = (
        lax.all_gather(w_out, "wsh", axis=0, tiled=True),
        lax.all_gather(w_up, "wsh", axis=0, tiled=True),
        lax.all_gather(w_down, "wsh", axis=0, tiled=True),
    )
    tags = shared[:, BLK, 0].astype(jnp.int32)
    prompt = [
        lax.dynamic_index_in_dim(shared, jnp.argmax(tags == slot), 0, keepdims=False)[:BLK]
        for slot in range(slots)
    ]
    slot_vec = own_slot.reshape(1)

    first_norm, first_back = jax.vjp(layer_norm, tokens, norm_gains[0], norm_biases[0])
    normed_low = first_norm.astype(jnp.bfloat16)
    prompt_low = layer_norm(
        jnp.concatenate(prompt, axis=0).astype(jnp.float32), norm_gains[0], norm_biases[0]
    ).astype(jnp.bfloat16)
    every_low = jnp.concatenate([normed_low, prompt_low], axis=0)
    queries = (
        jnp.dot(normed_low, full_qkv[:, :D], preferred_element_type=jnp.float32) * QSCALE
    ).astype(jnp.bfloat16)
    keys_values = jnp.dot(
        every_low, full_qkv[:, D:], preferred_element_type=jnp.float32
    ).astype(jnp.bfloat16)
    attn_low, lse = attention_forward(slot_vec, queries, keys_values, slots)

    branch = jnp.dot(attn_low, full_out, preferred_element_type=jnp.float32)
    post_attn, attn_back = jax.vjp(layer_norm, branch, norm_gains[1], norm_biases[1])
    hidden = tokens + post_attn
    pre_ffn, ffn_back = jax.vjp(layer_norm, hidden, norm_gains[2], norm_biases[2])
    ffn_low = pre_ffn.astype(jnp.bfloat16)
    upward = jnp.dot(ffn_low, full_up, preferred_element_type=jnp.float32)
    activated, gelu_back = jax.vjp(gelu_tanh, upward)
    active_low = activated.astype(jnp.bfloat16)
    downward = jnp.dot(active_low, full_down, preferred_element_type=jnp.float32)
    post_ffn, post_back = jax.vjp(layer_norm, downward, norm_gains[3], norm_biases[3])
    result = (hidden + post_ffn).astype(jnp.bfloat16).reshape(1, 1, BLK, D)
    seed_grad = out_grad.reshape(BLK, D).astype(jnp.float32)
    grad_down_in, gain_grad3, bias_grad3 = post_back(seed_grad)
    down_low = grad_down_in.astype(jnp.bfloat16)
    term_down = contract_rows(active_low, down_low).astype(jnp.bfloat16)
    grad_active = contract_last(down_low, full_down)
    up_low = gelu_back(grad_active)[0].astype(jnp.bfloat16)
    term_up = contract_rows(ffn_low, up_low).astype(jnp.bfloat16)
    grad_pre_ffn, gain_grad2, bias_grad2 = ffn_back(contract_last(up_low, full_up))
    grad_hidden = seed_grad + grad_pre_ffn
    grad_branch, gain_grad1, bias_grad1 = attn_back(grad_hidden)
    branch_low = grad_branch.astype(jnp.bfloat16)
    term_out = contract_rows(attn_low, branch_low).astype(jnp.bfloat16)
    grad_out_low = contract_last(branch_low, full_out).astype(jnp.bfloat16)

    grad_q, grad_k, grad_v = attention_backward(
        slot_vec, queries, keys_values, attn_low, grad_out_low, lse, slots
    )
    grad_kv = jnp.concatenate([grad_k, grad_v], axis=0)
    grad_normed_kv = dot_dims(grad_kv, full_qkv[:, D:], 0, 1)
    partial = grad_normed_kv[BLK:].astype(jnp.bfloat16)
    totals = lax.psum(partial, "ctx").reshape(slots, BLK, D)
    from_others = lax.dynamic_index_in_dim(
        totals, jnp.minimum(own_slot, slots - 1), 0, keepdims=False
    ).astype(jnp.float32)
    from_others = jnp.where(own_slot < slots, from_others, 0.0)
    grad_normed = contract_last(grad_q, full_qkv[:, :D]) + grad_normed_kv[:BLK] + from_others
    term_qkv = jnp.concatenate(
        [
            contract_rows(normed_low, grad_q).astype(jnp.bfloat16),
            dot_dims(every_low, grad_kv, 0, 1).astype(jnp.bfloat16),
        ],
        axis=1,
    )
    grad_tokens, gain_grad0, bias_grad0 = first_back(grad_normed)
    grad_input = (grad_hidden + grad_tokens).reshape(1, 1, BLK, D)

    summed_down, summed_up, summed_out, summed_qkv = reduce_terms(
        n_ctx, [term_down, term_up, term_out, term_qkv]
    )
    gain_stack = jnp.stack([gain_grad0, gain_grad1, gain_grad2, gain_grad3])
    bias_stack = jnp.stack([bias_grad0, bias_grad1, bias_grad2, bias_grad3])
    gain_total, bias_total = lax.psum((gain_stack, bias_stack), ("grp", "ctx", "wsh"))
    return (
        result,
        grad_input,
        summed_qkv,
        summed_out,
        summed_up,
        summed_down,
        gain_total,
        bias_total,
    )


def solution(mesh):
    rows = P("wsh", None)
    blocks = P("grp", "wsh", "ctx", None)
    return jax.shard_map(
        functools.partial(per_device, mesh.shape["ctx"]),
        mesh=mesh,
        in_specs=(blocks, rows, rows, rows, rows, P(), P(), blocks, blocks),
        out_specs=(blocks, blocks, rows, rows, rows, rows, P(), P()),
        check_vma=False,
    )
```

```python
import functools
import math

import jax
import jax.numpy as jnp
from jax import lax
from jax.experimental import pallas as pl
from jax.experimental.pallas import tpu as pltpu
from jax.sharding import PartitionSpec as P

D = 1024
HEADS = 16
DH = 64
BLK = 512
PAIRS = HEADS // 2
QT = 256

EPS = 1e-05
ALPHA = 32.0
NEG = -1e30
LOG2E = 1.4426950408889634
C2 = ALPHA * LOG2E
MESH = pl.DeviceIdType.MESH
QSCALE = 1.0 / (ALPHA * math.sqrt(DH))


def layer_norm(values, gain_row, bias_row):
    centre = values - jnp.mean(values, axis=-1, keepdims=True)
    spread = jnp.mean(centre * centre, axis=-1, keepdims=True)
    return centre * lax.rsqrt(spread + EPS) * gain_row + bias_row


def gelu_tanh(values):
    return jax.nn.gelu(values, approximate=True)


def dot_dims(left_side, right_side, left_dim, right_dim):
    return lax.dot_general(
        left_side,
        right_side,
        (((left_dim,), (right_dim,)), ((), ())),
        preferred_element_type=jnp.float32,
    )


def contract_last(left_side, right_side):
    return dot_dims(left_side, right_side, 1, 1)


def contract_rows(left_side, right_side):
    return dot_dims(left_side, right_side, 0, 0)


def head_lanes(head, rows):
    lane = lax.broadcasted_iota(jnp.int32, (rows, 128), 1)
    return (lane >= DH) if head else (lane < DH)


def causal_tile():
    row = lax.broadcasted_iota(jnp.int32, (QT, QT), 0)
    col = lax.broadcasted_iota(jnp.int32, (QT, QT), 1)
    return col <= row


PIECE = 128
SPAN = 512
CHAIN = 64


def remote(src, dst, send, recv, peer):
    return pltpu.make_async_remote_copy(
        src_ref=src, dst_ref=dst, send_sem=send, recv_sem=recv, device_id=peer, device_id_type=MESH
    )


def local_wait(ref, sem):
    pltpu.make_async_copy(ref, ref, sem).wait()


def aligned(start, size):
    return pl.ds(pl.multiple_of(start, size), size)


def softmax_block(q_ref, kv_ref, acc, top_ref, sum_ref, pair, base, own, visible):
    lanes = aligned(pair * 128, 128)
    value_lanes = aligned(D + pair * 128, 128)
    causal = causal_tile()
    first = head_lanes(0, QT)
    for tile in range(BLK // QT):
        rows = pl.ds(tile * QT, QT)
        q_pair = q_ref[rows, lanes]
        if own:
            spans = [(tile * QT, QT, True)] + ([(0, tile * QT, False)] if tile else [])
        else:
            spans = [(0, BLK, False)]
            old_top, old_sum = top_ref[pair, rows, :], sum_ref[pair, rows, :]
        tops, sums, outs = [], [], []
        for head in range(2):
            q_head = jnp.where(head_lanes(head, QT), q_pair, jnp.zeros_like(q_pair))
            parts = []
            for start, size, diagonal in spans:
                part = contract_last(q_head, kv_ref[pl.ds(base + start, size), lanes])
                parts.append(jnp.where(causal, part, NEG) if diagonal else part)
            top = functools.reduce(
                jnp.maximum, [jnp.max(part, axis=-1, keepdims=True) for part in parts]
            )
            top = top * C2
            if not own:
                top = jnp.maximum(
                    jnp.where(visible, top, NEG), old_top[:, head * DH : head * DH + 1]
                )
            shift = top if own else top + jnp.where(visible, 0.0, 1e30)
            total = jnp.zeros((QT, 1), jnp.float32)
            out = jnp.zeros((QT, 128), jnp.float32)
            for part, (start, size, _) in zip(parts, spans):
                expo = jnp.exp2(part * C2 - shift)
                total = total + jnp.sum(expo, axis=-1, keepdims=True)
                out = out + dot_dims(
                    expo.astype(jnp.bfloat16), kv_ref[pl.ds(base + start, size), value_lanes], 1, 0
                )
            tops.append(jnp.broadcast_to(top, (QT, 128)))
            sums.append(jnp.broadcast_to(total, (QT, 128)))
            outs.append(out)
        new_top = jnp.where(first, tops[0], tops[1])
        new_sum = jnp.where(first, sums[0], sums[1])
        new_out = jnp.where(first, outs[0], outs[1])
        if not own:
            keep = jnp.exp2(old_top - new_top)
            new_sum = new_sum + old_sum * keep
            new_out = new_out + acc[rows, lanes] * keep
        top_ref[pair, rows, :] = new_top
        sum_ref[pair, rows, :] = new_sum
        acc[rows, lanes] = new_out


def forward_kernel(n_ctx, *refs):
    slots = n_ctx // 2
    (slot_ref, gain_ref, bias_ref, x_hbm, w_qkv, w_out, w_up, w_down) = refs[:8]
    (a_out, q_out, kv_out, o_out, lse_out, full_qkv, full_out, full_up, full_down) = refs[8:17]
    (x_own, left, right, a_all, q_all, kv_all, weight, acc, low_out, tops, sums) = refs[17:28]
    (sem_in, sem_out, side_s, side_r, grp_s, grp_r, cs_s, cs_r, cg_s, cg_r, own_s, own_r, left_s, left_r, right_s, right_r) = refs[28:]
    grp, ctx, wsh = lax.axis_index("grp"), lax.axis_index("ctx"), lax.axis_index("wsh")
    side, core = wsh // 2, wsh % 2
    core_peer = (grp, ctx, side * 2 + 1 - core)
    side_peer = (grp, ctx, (1 - side) * 2 + core)
    grp_peer = (1 - grp, ctx, wsh)
    next_ctx = (grp, lax.rem(ctx + 1, n_ctx), wsh)
    last_ctx = (grp, lax.rem(ctx + n_ctx - 1, n_ctx), wsh)

    load = pltpu.make_async_copy(x_hbm, x_own, sem_in.at[0])
    load.start()
    barrier = pltpu.get_barrier_semaphore()
    for peer in (core_peer, side_peer, grp_peer, next_ctx, last_ctx):
        pl.semaphore_signal(barrier, inc=1, device_id=peer, device_id_type=MESH)
    pl.semaphore_wait(barrier, 5)

    shards = (w_qkv, w_out, w_up, w_down)
    fulls = (weight, full_out, full_up, full_down)
    ranges, start = [], 0
    for shard in shards:
        across = shard.shape[1] // SPAN
        ranges.append((start, start + across * (shard.shape[0] // (2 * PIECE)), across))
        start = ranges[-1][1]
    pieces = start

    def by_range(index, act):
        for place, (low, high, across) in enumerate(ranges):

            @pl.when((index >= low) & (index < high))
            def _(place=place, low=low, across=across):
                act(place, (index - low) // across, aligned(((index - low) % across) * SPAN, SPAN))

    def rows_of(place, owner, half, group):
        shard_rows = shards[place].shape[0]
        return aligned(owner * shard_rows + half * (shard_rows // 2) + group * PIECE, PIECE)

    sides_owner = (1 - side) * 2 + core

    def send_piece(index, carry):
        def act(place, group, cols):
            remote(
                shards[place].at[rows_of(place, 0, grp, group), cols],
                fulls[place].at[rows_of(place, wsh, grp, group), cols],
                side_s.at[index],
                side_r.at[index],
                side_peer,
            ).start()

        by_range(index, act)
        return carry

    def own_copies():
        copies = []
        across = shards[0].shape[1] // SPAN
        for place in range(4):
            shard_rows = shards[place].shape[0]
            mine = aligned(wsh * shard_rows, shard_rows)
            steps = range(across) if place == 0 else [None]
            for step in steps:
                cols = slice(None) if step is None else pl.ds(step * SPAN, SPAN)
                number = len(copies)
                copies.append(
                    remote(
                        shards[place].at[:, cols],
                        fulls[place].at[mine, cols],
                        own_s.at[number],
                        own_r.at[number],
                        core_peer,
                    )
                )
        return copies

    lax.fori_loop(0, pieces, send_piece, 0)
    for copy in own_copies():
        copy.start()
    for place in range(4):
        shard_rows = shards[place].shape[0]
        pltpu.make_async_copy(
            shards[place], fulls[place].at[aligned(wsh * shard_rows, shard_rows), :], sem_in.at[1 + place]
        ).start()
    load.wait()

    own_tag = slot_ref[1]
    chain_chunks = slots * (BLK // CHAIN)

    def chain_step(stream, send, recv, number, is_first, is_last, target):
        slot = number // (BLK // CHAIN)
        spot = aligned((number % (BLK // CHAIN)) * CHAIN, CHAIN)
        mine = jnp.where(own_tag == slot, x_own[spot, :], jnp.zeros((CHAIN, D), jnp.bfloat16))
        here = stream.at[slot, spot]

        @pl.when(is_first)
        def _():
            stream[slot, spot, :] = mine

        @pl.when(jnp.logical_not(is_first))
        def _():
            remote(here, here, send.at[number], recv.at[number], target).wait_recv()
            stream[slot, spot, :] = stream[slot, spot, :] + mine

        @pl.when(jnp.logical_not(is_last))
        def _():
            remote(here, here, send.at[number], recv.at[number], target).start()

    def tick(step):
        number = step - ctx

        @pl.when((number >= 0) & (number < chain_chunks))
        def _():
            chain_step(left, left_s, left_r, number, ctx == 0, ctx == n_ctx - 1, next_ctx)

        back = step - (n_ctx - 1 - ctx)

        @pl.when((back >= 0) & (back < chain_chunks))
        def _():
            chain_step(right, right_s, right_r, back, ctx == n_ctx - 1, ctx == 0, last_ctx)

        @pl.when(step < pieces)
        def _():
            def act(place, group, cols):
                here = fulls[place].at[rows_of(place, sides_owner, grp, group), cols]
                remote(here, here, side_s.at[step], side_r.at[step], side_peer).wait_recv()
                remote(here, here, grp_s.at[step], grp_r.at[step], grp_peer).start()
                remote(here, here, cs_s.at[step], cs_r.at[step], core_peer).start()

            by_range(step, act)

        @pl.when((step >= 1) & (step <= pieces))
        def _():
            def act(place, group, cols):
                here = fulls[place].at[rows_of(place, sides_owner, 1 - grp, group), cols]
                remote(here, here, grp_s.at[step - 1], grp_r.at[step - 1], grp_peer).wait_recv()
                remote(here, here, cg_s.at[step - 1], cg_r.at[step - 1], core_peer).start()

            by_range(step - 1, act)

    def normalise(source, dest):
        gain, bias = gain_ref[...], bias_ref[...]

        def body(index, carry):
            rows = aligned(index * 128, 128)
            values = source(rows).astype(jnp.float32)
            a_all[aligned(dest + index * 128, 128), :] = layer_norm(values, gain, bias).astype(
                jnp.bfloat16
            )
            return carry

        lax.fori_loop(0, BLK // 128, body, 0)

    def piece_ready(index):
        here = fulls[0].at[pl.ds(0, PIECE), pl.ds(0, SPAN)]
        remote(here, here, cs_s.at[index], cs_r.at[index], core_peer).wait_recv()
        remote(here, here, cg_s.at[index], cg_r.at[index], core_peer).wait_recv()
        whole = fulls[0].at[pl.ds(0, 2 * PIECE), pl.ds(0, SPAN)]
        remote(whole, whole, own_s.at[index], own_r.at[index], core_peer).wait_recv()

    tick(0)
    normalise(lambda rows: x_own[rows, :], 0)
    tick(1)
    shard_rows = w_qkv.shape[0]
    local_wait(weight.at[pl.ds(0, shard_rows), :], sem_in.at[1])

    def project_q(index, carry):
        tick(index + 2)
        piece_ready(index)
        cols = aligned(index * SPAN, SPAN)
        q_all[:, cols] = (
            jnp.dot(a_all[pl.ds(0, BLK), :], weight[:, cols], preferred_element_type=jnp.float32) * QSCALE
        ).astype(jnp.bfloat16)
        return carry

    lax.fori_loop(0, D // SPAN, project_q, 0)
    head_ticks = 2 + D // SPAN

    def project_kv(index, base):
        cols = aligned(index * SPAN, SPAN)
        rows = aligned(base, BLK)
        kv_all[rows, cols] = jnp.dot(
            a_all[rows, :], weight[:, aligned(D + index * SPAN, SPAN)], preferred_element_type=jnp.float32
        ).astype(jnp.bfloat16)

    def own_kv(index, carry):
        tick(index + head_ticks)
        piece_ready(index + D // SPAN)
        project_kv(index, 0)
        return carry

    lax.fori_loop(0, 2 * D // SPAN, own_kv, 0)
    own_ticks = head_ticks + 2 * D // SPAN
    outputs = [
        pltpu.make_async_copy(weight, full_qkv, sem_out.at[0]),
        pltpu.make_async_copy(q_all, q_out, sem_out.at[1]),
    ]
    for copy in outputs:
        copy.start()

    def own_attention(pair, carry):
        tick(pair + own_ticks)
        softmax_block(q_all, kv_all, acc, tops, sums, pair, 0, True, None)
        return carry

    lax.fori_loop(0, PAIRS, own_attention, 0)
    used = own_ticks + PAIRS
    per_slot = 2 * D // SPAN + PAIRS

    need = BLK // CHAIN + n_ctx - 1
    early = max(0, need - used)
    if early:
        lax.fori_loop(0, early, lambda index, carry: (tick(used + index), carry)[1], 0)

    def each_slot(slot, carry):
        base = pl.multiple_of((slot + 1) * BLK, BLK)
        visible = slot < slot_ref[0]
        begin = early + used + slot * per_slot

        def total(rows):
            joined = left[slot, rows, :] + right[slot, rows, :]
            return jnp.where(own_tag == slot, x_own[rows, :], joined)

        normalise(total, base)

        def slot_kv(index, inner):
            tick(begin + index)
            project_kv(index, base)
            return inner

        lax.fori_loop(0, 2 * D // SPAN, slot_kv, 0)

        def slot_attention(pair, inner):
            tick(begin + 2 * D // SPAN + pair)
            softmax_block(q_all, kv_all, acc, tops, sums, pair, base, False, visible)
            return inner

        lax.fori_loop(0, PAIRS, slot_attention, 0)
        return carry

    lax.fori_loop(0, slots, each_slot, 0)
    done_ticks = early + used + slots * per_slot

    def finish(pair, carry):
        lanes = aligned(pair * 128, 128)
        low_out[:, lanes] = (acc[:, lanes] / sums[pair]).astype(jnp.bfloat16)
        tops[pair] = tops[pair] + jnp.log2(sums[pair])
        return carry

    lax.fori_loop(0, PAIRS, finish, 0)
    outputs += [
        pltpu.make_async_copy(a_all, a_out, sem_out.at[2]),
        pltpu.make_async_copy(kv_all, kv_out, sem_out.at[3]),
        pltpu.make_async_copy(low_out, o_out, sem_out.at[4]),
        pltpu.make_async_copy(tops, lse_out, sem_out.at[5]),
    ]
    for copy in outputs[2:]:
        copy.start()
    all_ticks = max(pieces + 1, chain_chunks + n_ctx - 1)
    if all_ticks > done_ticks:
        lax.fori_loop(done_ticks, all_ticks, lambda index, carry: (tick(index), carry)[1], 0)

    def drain(index, carry):
        here = fulls[0].at[pl.ds(0, PIECE), pl.ds(0, SPAN)]

        @pl.when(index >= ranges[0][1])
        def _():
            remote(here, here, cs_s.at[index], cs_r.at[index], core_peer).wait_recv()
            remote(here, here, cg_s.at[index], cg_r.at[index], core_peer).wait_recv()

        remote(here, here, side_s.at[index], side_r.at[index], side_peer).wait_send()
        remote(here, here, grp_s.at[index], grp_r.at[index], grp_peer).wait_send()
        remote(here, here, cs_s.at[index], cs_r.at[index], core_peer).wait_send()
        remote(here, here, cg_s.at[index], cg_r.at[index], core_peer).wait_send()
        return carry

    lax.fori_loop(0, pieces, drain, 0)
    copies = own_copies()
    for number, copy in enumerate(copies):
        copy.wait_send()
        if number >= len(copies) - 3:
            copy.wait_recv()
    for place in range(1, 4):
        rows = shards[place].shape[0]
        pltpu.make_async_copy(
            shards[place], fulls[place].at[aligned(wsh * rows, rows), :], sem_in.at[1 + place]
        ).wait()

    def drain_chain(index, carry):
        here = left.at[0, pl.ds(0, CHAIN)]

        @pl.when(ctx < n_ctx - 1)
        def _():
            remote(here, here, left_s.at[index], left_r.at[index], next_ctx).wait_send()

        @pl.when(ctx > 0)
        def _():
            remote(here, here, right_s.at[index], right_r.at[index], last_ctx).wait_send()

        return carry

    lax.fori_loop(0, chain_chunks, drain_chain, 0)
    for copy in outputs:
        copy.wait()


def forward_part(n_ctx, tags, gain, bias, raw, w_qkv, w_out, w_up, w_down):
    slots = n_ctx // 2
    every = (slots + 1) * BLK
    low, full = jnp.bfloat16, jnp.float32
    dma = pltpu.SemaphoreType.DMA
    hbm = pl.BlockSpec(memory_space=pl.ANY)
    vmem = pl.BlockSpec(memory_space=pltpu.VMEM)
    shards = (w_qkv, w_out, w_up, w_down)
    pieces = sum(w.shape[0] * w.shape[1] // (2 * PIECE * SPAN) for w in shards)
    own = w_qkv.shape[1] // SPAN + 3
    chain = slots * (BLK // CHAIN)
    shape = jax.ShapeDtypeStruct
    return pl.pallas_call(
        functools.partial(forward_kernel, n_ctx),
        out_shape=[
            shape((every, D), low),
            shape((BLK, D), low),
            shape((every, 2 * D), low),
            shape((BLK, D), low),
            shape((PAIRS, BLK, 128), full),
        ]
        + [shape((4 * w.shape[0], w.shape[1]), low) for w in shards],
        in_specs=[pl.BlockSpec(memory_space=pltpu.SMEM), vmem, vmem] + [hbm] * 5,
        out_specs=[hbm] * 9,
        scratch_shapes=[
            pltpu.VMEM((BLK, D), low),
            pltpu.VMEM((slots, BLK, D), low),
            pltpu.VMEM((slots, BLK, D), low),
            pltpu.VMEM((every, D), low),
            pltpu.VMEM((BLK, D), low),
            pltpu.VMEM((every, 2 * D), low),
            pltpu.VMEM((D, 3 * D), low),
            pltpu.VMEM((BLK, D), full),
            pltpu.VMEM((BLK, D), low),
            pltpu.VMEM((PAIRS, BLK, 128), full),
            pltpu.VMEM((PAIRS, BLK, 128), full),
            dma((5,)),
            dma((6,)),
        ]
        + [dma((pieces,))] * 8
        + [dma((own,))] * 2
        + [dma((chain,))] * 4,
        compiler_params=pltpu.CompilerParams(
            collective_id=1, has_side_effects=True, vmem_limit_bytes=60 << 20
        ),
        cost_estimate=pl.CostEstimate(flops=20 << 30, bytes_accessed=64 << 20, transcendentals=1 << 24),
        name="gather_attend",
    )(tags, gain, bias, raw, *shards)


def attn_bwd_kernel(
    slots, slot_ref, q_ref, k_ref, v_ref, o_ref, do_ref, lse_ref, dq_ref, dk_ref, dv_ref, dk_acc, dv_acc
):
    own_slot = slot_ref[0]
    causal = causal_tile()
    dk_acc[...] = jnp.zeros_like(dk_acc)
    dv_acc[...] = jnp.zeros_like(dv_acc)
    for tile in range(BLK // QT):
        rows = pl.ds(tile * QT, QT)
        q_pair = q_ref[rows, :]
        do_pair = do_ref[rows, :]
        q_turned = q_pair.T
        do_turned = do_pair.T
        prod = do_pair.astype(jnp.float32) * o_ref[rows, :].astype(jnp.float32)
        lse_pair = lse_ref[0, rows, :]
        dqs = []
        for head in range(2):
            lanes = head_lanes(head, QT)
            turned = slice(head * DH, (head + 1) * DH)
            q_head = jnp.where(lanes, q_pair, jnp.zeros_like(q_pair))
            do_head = jnp.where(lanes, do_pair, jnp.zeros_like(do_pair))
            delta = jnp.sum(jnp.where(lanes, prod, 0.0), axis=-1, keepdims=True)
            lse = lse_pair[:, head * DH : head * DH + 1]
            spans = [(tile * QT, QT, None, True)]
            if tile:
                spans.append((0, tile * QT, None, False))
            spans += [((s + 1) * BLK, BLK, s < own_slot, False) for s in range(slots)]
            dq = jnp.zeros((QT, 128), jnp.float32)
            for start, size, visible, diagonal in spans:
                keys = pl.ds(start, size)
                k_part = k_ref[keys, :]
                row_shift = lse if visible is None else lse + jnp.where(visible, 0.0, 1e30)
                prob = jnp.exp2(contract_last(q_head, k_part) * C2 - row_shift)
                if diagonal:
                    prob = jnp.where(causal, prob, 0.0)
                dprob = contract_last(do_head, v_ref[keys, :])
                dlogit = (prob * (dprob - delta)).astype(jnp.bfloat16)
                dq = dq + dot_dims(dlogit, k_part, 1, 0)
                dk_acc[turned, keys] += dot_dims(q_turned[turned, :], dlogit, 1, 0)
                dv_acc[turned, keys] += dot_dims(
                    do_turned[turned, :], prob.astype(jnp.bfloat16), 1, 0
                )
            dqs.append(dq)
        dq_ref[rows, :] = (
            jnp.where(head_lanes(0, QT), dqs[0], dqs[1]) * ALPHA
        ).astype(jnp.bfloat16) * jnp.bfloat16(QSCALE)
    dk_ref[...] = (dk_acc[...] * ALPHA).astype(jnp.bfloat16)
    dv_ref[...] = dv_acc[...].astype(jnp.bfloat16)


def attention_backward(own_slot, queries, keys_values, attended, grad_out, lse, slots):
    keys = (slots + 1) * BLK
    pair = pl.BlockSpec((BLK, 128), lambda i, s: (0, i))
    turned = pl.BlockSpec((128, keys), lambda i, s: (i, 0))
    return pl.pallas_call(
        functools.partial(attn_bwd_kernel, slots),
        out_shape=(
            jax.ShapeDtypeStruct((BLK, D), jnp.bfloat16),
            jax.ShapeDtypeStruct((D, keys), jnp.bfloat16),
            jax.ShapeDtypeStruct((D, keys), jnp.bfloat16),
        ),
        grid_spec=pltpu.PrefetchScalarGridSpec(
            num_scalar_prefetch=1,
            grid=(PAIRS,),
            in_specs=[
                pair,
                pl.BlockSpec((keys, 128), lambda i, s: (0, i)),
                pl.BlockSpec((keys, 128), lambda i, s: (0, i + PAIRS)),
                pair,
                pair,
                pl.BlockSpec((1, BLK, 128), lambda i, s: (i, 0, 0)),
            ],
            out_specs=(pair, turned, turned),
            scratch_shapes=[pltpu.VMEM((128, keys), jnp.float32)] * 2,
        ),
        compiler_params=pltpu.CompilerParams(vmem_limit_bytes=48 << 20),
        cost_estimate=pl.CostEstimate(
            flops=10 * BLK * keys * D, bytes_accessed=24 << 20, transcendentals=BLK * keys * HEADS
        ),
        name="attn_bwd",
    )(own_slot, queries, keys_values, keys_values, attended, grad_out, lse)


TILE = 256


def piece_parts(n_ctx):
    row_parts = min(n_ctx, 8)
    return row_parts, n_ctx // row_parts


def reduce_kernel(n_ctx, widths, *refs):
    count = len(widths)
    terms, outs = refs[:count], refs[count : 2 * count]
    (r1, r2, r3, r4, fin, local, stage) = refs[2 * count : 2 * count + 7]
    (sem_local, sem_out, send1, recv1, send2, recv2, send3, recv3, send4, recv4, send5, recv5, send6, recv6) = refs[
        2 * count + 7 :
    ]
    grp, ctx, wsh = lax.axis_index("grp"), lax.axis_index("ctx"), lax.axis_index("wsh")
    side, core = wsh // 2, wsh % 2
    core_peer = (grp, ctx, side * 2 + 1 - core)
    side_peer = (grp, ctx, (1 - side) * 2 + core)
    grp_peer = (1 - grp, ctx, wsh)
    ctx_peers = [(grp, lax.rem(ctx + step, n_ctx), wsh) for step in range(1, n_ctx)]

    barrier = pltpu.get_barrier_semaphore()
    for peer in [core_peer, side_peer, grp_peer] + ctx_peers:
        pl.semaphore_signal(barrier, inc=1, device_id=peer, device_id_type=MESH)
    pl.semaphore_wait(barrier, n_ctx + 2)

    row_parts, col_parts = piece_parts(n_ctx)
    half = TILE // 2
    part_rows, part_cols = half // row_parts, TILE // col_parts
    ranges, first = [], 0
    for rows, cols in widths:
        across = cols // TILE
        ranges.append((first, first + (rows // TILE) * across, across))
        first = ranges[-1][1]
    chunks = first

    def block(index, across):
        return (
            pl.ds(pl.multiple_of((index // across) * TILE, TILE), TILE),
            pl.ds(pl.multiple_of((index % across) * TILE, TILE), TILE),
        )

    def by_range(index, act):
        for place, (low, high, across) in enumerate(ranges):

            @pl.when((index >= low) & (index < high))
            def _(place=place, low=low, across=across):
                act(place, block(index - low, across))

    def part_of(position, offset):
        return (
            pl.ds(pl.multiple_of(offset + (position // col_parts) * part_rows, part_rows), part_rows),
            pl.ds(pl.multiple_of((position % col_parts) * part_cols, part_cols), part_cols),
        )

    def step_load(index):
        slot = lax.rem(index, 4)

        def act(place, span):
            term = terms[place]
            pltpu.make_async_copy(term.at[:, core, span[0], span[1]], local.at[slot], sem_local.at[slot]).start()
            remote(
                term.at[:, 1 - core, span[0], span[1]], r1.at[index], send1.at[slot], recv1.at[index], core_peer
            ).start()

        by_range(index, act)

    def step_core(index):
        slot = lax.rem(index, 4)
        pltpu.make_async_copy(local.at[slot], local.at[slot], sem_local.at[slot]).wait()
        whole = remote(r1.at[index], r1.at[index], send1.at[slot], recv1.at[index], core_peer)
        whole.wait_send()
        whole.wait_recv()
        r1[index] = r1[index] + local[slot]
        remote(r1.at[index, 1 - side], r2.at[index], send2.at[slot], recv2.at[index], side_peer).start()

    half_keep = pl.ds(pl.multiple_of(grp * half, half), half)
    half_give = pl.ds(pl.multiple_of((1 - grp) * half, half), half)

    def step_side(index):
        slot = lax.rem(index, 4)
        move = remote(r1.at[index, 1 - side], r2.at[index], send2.at[slot], recv2.at[index], side_peer)
        move.wait_send()
        move.wait_recv()
        r2[index] = r2[index] + r1[index, side]
        remote(r2.at[index, half_give], r3.at[index], send3.at[slot], recv3.at[index], grp_peer).start()

    def step_grp(index):
        slot = lax.rem(index, 4)
        move = remote(r2.at[index, half_give], r3.at[index], send3.at[slot], recv3.at[index], grp_peer)
        move.wait_send()
        move.wait_recv()
        r3[index] = r3[index] + r2[index, half_keep]
        for place, peer in enumerate(ctx_peers):
            rows, cols = part_of(peer[1], 0)
            remote(r3.at[index, rows, cols], r4.at[index, place], send4.at[slot], recv4.at[index], peer).start()

    def step_ctx(index):
        slot = lax.rem(index, 4)
        move = remote(r4.at[index], r4.at[index], send4.at[slot], recv4.at[index], ctx_peers[0])
        move.wait_send()
        move.wait_recv()
        rows, cols = part_of(ctx, 0)
        total = r3[index, rows, cols].astype(jnp.float32)
        for place in range(n_ctx - 1):
            total = total + r4[index, place].astype(jnp.float32)
        rows, cols = part_of(ctx, grp * half)
        fin[index, rows, cols] = total.astype(jnp.bfloat16)
        for peer in ctx_peers:
            here = fin.at[index, rows, cols]
            remote(here, here, send5.at[slot], recv5.at[index], peer).start()

    def step_back(index):
        slot = lax.rem(index, 4)
        move = remote(r4.at[index], r4.at[index], send5.at[slot], recv5.at[index], ctx_peers[0])
        move.wait_send()
        move.wait_recv()
        here = fin.at[index, half_keep]
        remote(here, here, send6.at[slot], recv6.at[index], grp_peer).start()

    def step_out(index):
        slot = lax.rem(index, 4)
        here = fin.at[index, half_give]
        move = remote(here, here, send6.at[slot], recv6.at[index], grp_peer)
        move.wait_send()
        move.wait_recv()

        @pl.when(index >= 4)
        def _():
            pltpu.make_async_copy(stage.at[slot], stage.at[slot], sem_out.at[slot]).wait()

        stage[slot] = fin[index].astype(jnp.float32)

        def act(place, span):
            pltpu.make_async_copy(stage.at[slot], outs[place].at[span[0], span[1]], sem_out.at[slot]).start()

        by_range(index, act)

    stages = (step_core, step_side, step_grp, step_ctx, step_back, step_out)

    step_load(0)
    step_load(1)

    def body(step, carry):
        @pl.when(step + 2 < chunks)
        def _():
            step_load(step + 2)

        for lag, act in enumerate(stages):
            index = step - lag

            @pl.when((index >= 0) & (index < chunks))
            def _(act=act, index=index):
                act(index)

        return carry

    lax.fori_loop(0, chunks + len(stages) - 1, body, 0)
    for slot in range(4):
        pltpu.make_async_copy(stage.at[slot], stage.at[slot], sem_out.at[slot]).wait()


def reduce_terms(n_ctx, terms):
    widths = [(term.shape[0] // 4, term.shape[1]) for term in terms]
    chunks = sum((rows // TILE) * (cols // TILE) for rows, cols in widths)
    row_parts, col_parts = piece_parts(n_ctx)
    part = (TILE // 2 // row_parts, TILE // col_parts)
    low = jnp.bfloat16
    dma = pltpu.SemaphoreType.DMA
    hbm = pl.BlockSpec(memory_space=pl.ANY)
    return pl.pallas_call(
        functools.partial(reduce_kernel, n_ctx, widths),
        out_shape=[jax.ShapeDtypeStruct(width, jnp.float32) for width in widths],
        in_specs=[hbm] * len(terms),
        out_specs=[hbm] * len(terms),
        scratch_shapes=[
            pltpu.VMEM((chunks, 2, TILE, TILE), low),
            pltpu.VMEM((chunks, TILE, TILE), low),
            pltpu.VMEM((chunks, TILE // 2, TILE), low),
            pltpu.VMEM((chunks, n_ctx - 1) + part, low),
            pltpu.VMEM((chunks, TILE, TILE), low),
            pltpu.VMEM((4, 2, TILE, TILE), low),
            pltpu.VMEM((4, TILE, TILE), jnp.float32),
            dma((4,)),
            dma((4,)),
        ]
        + [dma((4,)), dma((chunks,))] * 6,
        compiler_params=pltpu.CompilerParams(
            collective_id=0, has_side_effects=True, vmem_limit_bytes=60 << 20
        ),
        cost_estimate=pl.CostEstimate(flops=1 << 20, bytes_accessed=256 << 20, transcendentals=0),
        name="reduce_grads",
    )(*[term.reshape(2, 2, width[0], width[1]) for term, width in zip(terms, widths)])


def per_device(n_ctx, inputs, w_qkv, w_out, w_up, w_down, norm_gains, norm_biases, block_map, out_grad):
    slots = n_ctx // 2
    raw = inputs.reshape(BLK, D)
    tokens = raw.astype(jnp.float32)
    block_entry = block_map.reshape(2)
    own_slot = block_entry[1] // BLK
    own_tag = jnp.where(block_entry[0] == 0, own_slot, n_ctx)
    slot_vec = own_slot.reshape(1)
    every_low, queries, keys_values, attn_low, lse, full_qkv, full_out, full_up, full_down = forward_part(
        n_ctx,
        jnp.stack([own_slot, own_tag]),
        norm_gains[0:1],
        norm_biases[0:1],
        raw,
        w_qkv,
        w_out,
        w_up,
        w_down,
    )
    normed_low = every_low[:BLK]
    _, first_back = jax.vjp(layer_norm, tokens, norm_gains[0], norm_biases[0])

    branch = jnp.dot(attn_low, full_out, preferred_element_type=jnp.float32)
    post_attn, attn_back = jax.vjp(layer_norm, branch, norm_gains[1], norm_biases[1])
    hidden = tokens + post_attn
    pre_ffn, ffn_back = jax.vjp(layer_norm, hidden, norm_gains[2], norm_biases[2])
    ffn_low = pre_ffn.astype(jnp.bfloat16)
    upward = jnp.dot(ffn_low, full_up, preferred_element_type=jnp.float32)
    activated, gelu_back = jax.vjp(gelu_tanh, upward)
    active_low = activated.astype(jnp.bfloat16)
    downward = jnp.dot(active_low, full_down, preferred_element_type=jnp.float32)
    post_ffn, post_back = jax.vjp(layer_norm, downward, norm_gains[3], norm_biases[3])
    result = (hidden + post_ffn).astype(jnp.bfloat16).reshape(1, 1, BLK, D)
    seed_grad = out_grad.reshape(BLK, D).astype(jnp.float32)
    grad_down_in, gain_grad3, bias_grad3 = post_back(seed_grad)
    down_low = grad_down_in.astype(jnp.bfloat16)
    term_down = contract_rows(active_low, down_low).astype(jnp.bfloat16)
    grad_active = contract_last(down_low, full_down)
    up_low = gelu_back(grad_active)[0].astype(jnp.bfloat16)
    term_up = contract_rows(ffn_low, up_low).astype(jnp.bfloat16)
    grad_pre_ffn, gain_grad2, bias_grad2 = ffn_back(contract_last(up_low, full_up))
    grad_hidden = seed_grad + grad_pre_ffn
    grad_branch, gain_grad1, bias_grad1 = attn_back(grad_hidden)
    branch_low = grad_branch.astype(jnp.bfloat16)
    term_out = contract_rows(attn_low, branch_low).astype(jnp.bfloat16)
    grad_out_low = contract_last(branch_low, full_out).astype(jnp.bfloat16)

    grad_q, grad_k, grad_v = attention_backward(
        slot_vec, queries, keys_values, attn_low, grad_out_low, lse, slots
    )
    grad_kv = jnp.concatenate([grad_k, grad_v], axis=0)
    grad_normed_kv = dot_dims(grad_kv, full_qkv[:, D:], 0, 1)
    partial = grad_normed_kv[BLK:].astype(jnp.bfloat16)
    totals = lax.psum(partial, "ctx").reshape(slots, BLK, D)
    from_others = lax.dynamic_index_in_dim(
        totals, jnp.minimum(own_slot, slots - 1), 0, keepdims=False
    ).astype(jnp.float32)
    from_others = jnp.where(own_slot < slots, from_others, 0.0)
    grad_normed = contract_last(grad_q, full_qkv[:, :D]) + grad_normed_kv[:BLK] + from_others
    term_qkv = jnp.concatenate(
        [
            contract_rows(normed_low, grad_q).astype(jnp.bfloat16),
            dot_dims(every_low, grad_kv, 0, 1).astype(jnp.bfloat16),
        ],
        axis=1,
    )
    grad_tokens, gain_grad0, bias_grad0 = first_back(grad_normed)
    grad_input = (grad_hidden + grad_tokens).reshape(1, 1, BLK, D)

    summed_down, summed_up, summed_out, summed_qkv = reduce_terms(
        n_ctx, [term_down, term_up, term_out, term_qkv]
    )
    gain_stack = jnp.stack([gain_grad0, gain_grad1, gain_grad2, gain_grad3])
    bias_stack = jnp.stack([bias_grad0, bias_grad1, bias_grad2, bias_grad3])
    gain_total, bias_total = lax.psum((gain_stack, bias_stack), ("grp", "ctx", "wsh"))
    return (
        result,
        grad_input,
        summed_qkv,
        summed_out,
        summed_up,
        summed_down,
        gain_total,
        bias_total,
    )


def solution(mesh):
    rows = P("wsh", None)
    blocks = P("grp", "wsh", "ctx", None)
    return jax.shard_map(
        functools.partial(per_device, mesh.shape["ctx"]),
        mesh=mesh,
        in_specs=(blocks, rows, rows, rows, rows, P(), P(), blocks, blocks),
        out_specs=(blocks, blocks, rows, rows, rows, rows, P(), P()),
        check_vma=False,
    )
```

```python
import functools
import math

import jax
import jax.numpy as jnp
from jax import lax
from jax.experimental import pallas as pl
from jax.experimental.pallas import tpu as pltpu
from jax.sharding import PartitionSpec as P

D = 1024
HEADS = 16
DH = 64
BLK = 512
PAIRS = HEADS // 2
QT = 256

EPS = 1e-05
ALPHA = 32.0
NEG = -1e30
LOG2E = 1.4426950408889634
C2 = ALPHA * LOG2E
MESH = pl.DeviceIdType.MESH
QSCALE = 1.0 / (ALPHA * math.sqrt(DH))


def layer_norm(values, gain_row, bias_row):
    centre = values - jnp.mean(values, axis=-1, keepdims=True)
    spread = jnp.mean(centre * centre, axis=-1, keepdims=True)
    return centre * lax.rsqrt(spread + EPS) * gain_row + bias_row


def gelu_tanh(values):
    return jax.nn.gelu(values, approximate=True)


def dot_dims(left_side, right_side, left_dim, right_dim):
    return lax.dot_general(
        left_side,
        right_side,
        (((left_dim,), (right_dim,)), ((), ())),
        preferred_element_type=jnp.float32,
    )


def contract_last(left_side, right_side):
    return dot_dims(left_side, right_side, 1, 1)


def contract_rows(left_side, right_side):
    return dot_dims(left_side, right_side, 0, 0)


def head_lanes(head, rows):
    lane = lax.broadcasted_iota(jnp.int32, (rows, 128), 1)
    return (lane >= DH) if head else (lane < DH)


def causal_tile():
    row = lax.broadcasted_iota(jnp.int32, (QT, QT), 0)
    col = lax.broadcasted_iota(jnp.int32, (QT, QT), 1)
    return col <= row


PIECE = 128
SPAN = 512
CHAIN = 64
HOP = 2
LAG = 2
GROUP = 4
AHEAD = 4


def remote(src, dst, send, recv, peer):
    return pltpu.make_async_remote_copy(
        src_ref=src, dst_ref=dst, send_sem=send, recv_sem=recv, device_id=peer, device_id_type=MESH
    )


def local_wait(ref, sem):
    pltpu.make_async_copy(ref, ref, sem).wait()


def aligned(start, size):
    return pl.ds(pl.multiple_of(start, size), size)


def softmax_block(q_ref, kv_ref, acc, top_ref, sum_ref, pair, base, own, visible):
    lanes = aligned(pair * 128, 128)
    value_lanes = aligned(D + pair * 128, 128)
    causal = causal_tile()
    first = head_lanes(0, QT)
    count = BLK // QT
    q_pair = q_ref[:, lanes]
    keys = kv_ref[pl.ds(base, BLK), lanes]
    values = kv_ref[pl.ds(base, BLK), value_lanes]
    if not own:
        old_top, old_sum, old_out = top_ref[pair], sum_ref[pair], acc[:, lanes]
        hide = jnp.where(visible, 0.0, 1e30)
    results = []
    work = [(tile, head) for tile in range(count) for head in range(2)]
    parts_of = {}
    for tile, head in work:
        q_tile = q_pair[tile * QT : (tile + 1) * QT]
        q_head = jnp.where(head_lanes(head, QT), q_tile, jnp.zeros_like(q_tile))
        span = (tile + 1) * QT if own else BLK
        parts_of[tile, head] = contract_last(q_head, keys[:span])
    top_of, expo_of, total_of = {}, {}, {}
    for tile, head in work:
        part = parts_of[tile, head]
        if own:
            diag = jnp.where(causal, part[:, tile * QT :], NEG)
            part = jnp.concatenate([part[:, : tile * QT], diag], axis=1) if tile else diag
        top = jnp.max(part, axis=-1, keepdims=True) * C2
        if own:
            shift = top
        else:
            top = jnp.maximum(
                jnp.where(visible, top, NEG), old_top[tile * QT : (tile + 1) * QT, head * DH : head * DH + 1]
            )
            shift = top + hide
        expo = jnp.exp2(part * C2 - shift)
        top_of[tile, head] = jnp.broadcast_to(top, (QT, 128))
        total_of[tile, head] = jnp.broadcast_to(jnp.sum(expo, axis=-1, keepdims=True), (QT, 128))
        expo_of[tile, head] = expo.astype(jnp.bfloat16)
    out_of = {}
    for tile, head in work:
        span = (tile + 1) * QT if own else BLK
        out_of[tile, head] = dot_dims(expo_of[tile, head], values[:span], 1, 0)
    for tile in range(count):
        rows = pl.ds(tile * QT, QT)
        new_top = jnp.where(first, top_of[tile, 0], top_of[tile, 1])
        new_sum = jnp.where(first, total_of[tile, 0], total_of[tile, 1])
        new_out = jnp.where(first, out_of[tile, 0], out_of[tile, 1])
        if not own:
            here = slice(tile * QT, (tile + 1) * QT)
            keep = jnp.exp2(old_top[here] - new_top)
            new_sum = new_sum + old_sum[here] * keep
            new_out = new_out + old_out[here] * keep
        top_ref[pair, rows, :] = new_top
        sum_ref[pair, rows, :] = new_sum
        acc[rows, lanes] = new_out


def forward_kernel(n_ctx, *refs):
    slots = n_ctx // 2
    (slot_ref, gain_ref, bias_ref, x_hbm, w_qkv, w_out, w_up, w_down) = refs[:8]
    (a_out, q_out, kv_out, o_out, lse_out, full_qkv, full_out, full_up, full_down) = refs[8:17]
    (x_own, left, right, a_all, q_all, kv_all, weight, acc, tops, sums, hop) = refs[17:28]
    (sem_in, sem_load, sem_store, sem_out, sem_a, sem_kv, side_s, side_r, grp_s, grp_r, cs_s, cs_r, cg_s, cg_r, own_s, own_r, left_s, left_r, right_s, right_r) = refs[28:]
    grp, ctx, wsh = lax.axis_index("grp"), lax.axis_index("ctx"), lax.axis_index("wsh")
    side, core = wsh // 2, wsh % 2
    core_peer = (grp, ctx, side * 2 + 1 - core)
    side_peer = (grp, ctx, (1 - side) * 2 + core)
    grp_peer = (1 - grp, ctx, wsh)
    next_ctx = (grp, lax.rem(ctx + 1, n_ctx), wsh)
    last_ctx = (grp, lax.rem(ctx + n_ctx - 1, n_ctx), wsh)

    load = pltpu.make_async_copy(x_hbm, x_own, sem_in.at[0])
    load.start()
    barrier = pltpu.get_barrier_semaphore()
    for peer in (core_peer, side_peer, grp_peer, next_ctx, last_ctx):
        pl.semaphore_signal(barrier, inc=1, device_id=peer, device_id_type=MESH)
    pl.semaphore_wait(barrier, 5)

    shards = (w_qkv, w_out, w_up, w_down)
    fulls = (weight, full_out, full_up, full_down)
    ranges, start = [], 0
    for shard in shards:
        across = shard.shape[1] // SPAN
        ranges.append((start, start + across * (shard.shape[0] // (2 * PIECE)), across))
        start = ranges[-1][1]
    pieces = start

    def by_range(index, act):
        for place, (low, high, across) in enumerate(ranges):

            @pl.when((index >= low) & (index < high))
            def _(place=place, low=low, across=across):
                act(place, (index - low) // across, aligned(((index - low) % across) * SPAN, SPAN))

    def rows_of(place, owner, half, group):
        shard_rows = shards[place].shape[0]
        return aligned(owner * shard_rows + half * (shard_rows // 2) + group * PIECE, PIECE)

    sides_owner = (1 - side) * 2 + core

    def send_piece(index, carry):
        def act(place, group, cols):
            remote(
                shards[place].at[rows_of(place, 0, grp, group), cols],
                fulls[place].at[rows_of(place, wsh, grp, group), cols],
                side_s.at[index],
                side_r.at[index],
                side_peer,
            ).start()

        by_range(index, act)
        return carry

    def own_copies():
        copies = []
        across = shards[0].shape[1] // SPAN
        for place in range(4):
            shard_rows = shards[place].shape[0]
            mine = aligned(wsh * shard_rows, shard_rows)
            steps = range(across) if place == 0 else [None]
            for step in steps:
                cols = slice(None) if step is None else pl.ds(step * SPAN, SPAN)
                number = len(copies)
                copies.append(
                    remote(
                        shards[place].at[:, cols],
                        fulls[place].at[mine, cols],
                        own_s.at[number],
                        own_r.at[number],
                        core_peer,
                    )
                )
        return copies

    for index in range(AHEAD):
        send_piece(index, 0)
    for copy in own_copies():
        copy.start()
    own_rows = aligned(wsh * w_qkv.shape[0], w_qkv.shape[0])
    own_weight = pltpu.make_async_copy(w_qkv, weight.at[own_rows, :], sem_in.at[1])
    own_weight.start()
    load.wait()

    bounces, start = [], 0
    for shard in shards[1:]:
        across = shard.shape[1] // SPAN
        bounces.append((start, start + across * (shard.shape[0] // (2 * PIECE)), across))
        start = bounces[-1][1]
    moves = start

    def bounce(index, loading):
        slot = lax.rem(index, 3)
        for place, (low, high, across) in enumerate(bounces):

            @pl.when((index >= low) & (index < high))
            def _(place=place + 1, low=low, across=across):
                group = (index - low) // across
                cols = aligned(((index - low) % across) * SPAN, SPAN)
                if loading:
                    here = shards[place].at[aligned(group * 2 * PIECE, 2 * PIECE), cols]
                    pltpu.make_async_copy(here, hop.at[slot], sem_load.at[slot]).start()
                else:
                    rows = aligned(wsh * shards[place].shape[0] + group * 2 * PIECE, 2 * PIECE)
                    local_wait(hop.at[slot], sem_load.at[slot])
                    pltpu.make_async_copy(
                        hop.at[slot], fulls[place].at[rows, cols], sem_store.at[slot]
                    ).start()

    own_tag = slot_ref[1]
    chain_chunks = slots * (BLK // CHAIN)

    def chain_step(stream, send, recv, number, is_first, is_last, target):
        slot = number // (BLK // CHAIN)
        spot = aligned((number % (BLK // CHAIN)) * CHAIN, CHAIN)
        mine = jnp.where(own_tag == slot, x_own[spot, :], jnp.zeros((CHAIN, D), jnp.bfloat16))
        here = stream.at[slot, spot]

        @pl.when(is_first)
        def _():
            stream[slot, spot, :] = mine

        @pl.when(jnp.logical_not(is_first))
        def _():
            remote(here, here, send.at[number], recv.at[number], target).wait_recv()
            stream[slot, spot, :] = stream[slot, spot, :] + mine

        @pl.when(jnp.logical_not(is_last))
        def _():
            remote(here, here, send.at[number], recv.at[number], target).start()

    def tick(step):
        @pl.when((step >= 1) & (step <= moves))
        def _():
            bounce(step - 1, False)

        @pl.when((step >= 3) & (step < moves))
        def _():
            local_wait(hop.at[lax.rem(step, 3)], sem_store.at[lax.rem(step, 3)])

        @pl.when(step < moves)
        def _():
            bounce(step, True)

        @pl.when(step + AHEAD < pieces)
        def _():
            send_piece(step + AHEAD, 0)

        number = step - HOP * ctx

        @pl.when((number >= 0) & (number < chain_chunks))
        def _():
            chain_step(left, left_s, left_r, number, ctx == 0, ctx == n_ctx - 1, next_ctx)

        back = step - HOP * (n_ctx - 1 - ctx)

        @pl.when((back >= 0) & (back < chain_chunks))
        def _():
            chain_step(right, right_s, right_r, back, ctx == n_ctx - 1, ctx == 0, last_ctx)

        @pl.when(step < pieces)
        def _():
            def act(place, group, cols):
                here = fulls[place].at[rows_of(place, sides_owner, grp, group), cols]
                remote(here, here, side_s.at[step], side_r.at[step], side_peer).wait_recv()
                remote(here, here, grp_s.at[step], grp_r.at[step], grp_peer).start()
                remote(here, here, cs_s.at[step], cs_r.at[step], core_peer).start()

            by_range(step, act)

        late = step - LAG

        @pl.when((late >= 0) & (late < pieces))
        def _():
            def act(place, group, cols):
                here = fulls[place].at[rows_of(place, sides_owner, 1 - grp, group), cols]
                remote(here, here, grp_s.at[late], grp_r.at[late], grp_peer).wait_recv()
                remote(here, here, cg_s.at[late], cg_r.at[late], core_peer).start()

            by_range(late, act)

    def normalise(source, dest):
        gain, bias = gain_ref[...], bias_ref[...]

        def body(index, carry):
            rows = aligned(index * 128, 128)
            values = source(rows).astype(jnp.float32)
            a_all[aligned(dest + index * 128, 128), :] = layer_norm(values, gain, bias).astype(
                jnp.bfloat16
            )
            return carry

        lax.fori_loop(0, BLK // 128, body, 0)

    def piece_ready(index):
        here = fulls[0].at[pl.ds(0, PIECE), pl.ds(0, SPAN)]
        remote(here, here, cs_s.at[index], cs_r.at[index], core_peer).wait_recv()
        remote(here, here, cg_s.at[index], cg_r.at[index], core_peer).wait_recv()
        whole = fulls[0].at[pl.ds(0, 2 * PIECE), pl.ds(0, SPAN)]
        remote(whole, whole, own_s.at[index], own_r.at[index], core_peer).wait_recv()

    tick(0)
    normalise(lambda rows: x_own[rows, :], 0)
    for step in range(1, LAG + 1):
        tick(step)
    own_weight.wait()

    def project_q(index, carry):
        tick(index + LAG + 1)
        piece_ready(index)
        cols = aligned(index * SPAN, SPAN)
        q_all[:, cols] = (
            jnp.dot(a_all[pl.ds(0, BLK), :], weight[:, cols], preferred_element_type=jnp.float32) * QSCALE
        ).astype(jnp.bfloat16)
        return carry

    lax.fori_loop(0, D // SPAN, project_q, 0)
    head_ticks = LAG + 1 + D // SPAN

    def project_kv(index, base):
        cols = aligned(index * SPAN, SPAN)
        rows = aligned(base, BLK)
        kv_all[rows, cols] = jnp.dot(
            a_all[rows, :], weight[:, aligned(D + index * SPAN, SPAN)], preferred_element_type=jnp.float32
        ).astype(jnp.bfloat16)

    def own_kv(index, carry):
        tick(index + head_ticks)
        piece_ready(index + D // SPAN)
        project_kv(index, 0)
        return carry

    lax.fori_loop(0, 2 * D // SPAN, own_kv, 0)
    own_ticks = head_ticks + 2 * D // SPAN

    def send_block(index):
        rows = aligned(index * BLK, BLK)
        pltpu.make_async_copy(a_all.at[rows, :], a_out.at[rows, :], sem_a.at[index]).start()
        pltpu.make_async_copy(kv_all.at[rows, :], kv_out.at[rows, :], sem_kv.at[index]).start()

    outputs = [
        pltpu.make_async_copy(weight, full_qkv, sem_out.at[0]),
        pltpu.make_async_copy(q_all, q_out, sem_out.at[1]),
    ]
    for copy in outputs:
        copy.start()

    send_block(0)

    def own_attention(group, carry):
        tick(own_ticks + 2 * group)
        tick(own_ticks + 2 * group + 1)
        for member in range(GROUP):
            softmax_block(q_all, kv_all, acc, tops, sums, group * GROUP + member, 0, True, None)
        return carry

    groups = PAIRS // GROUP
    lax.fori_loop(0, groups, own_attention, 0)
    used = own_ticks + 2 * groups
    per_slot = 2 * D // SPAN + 2 * groups

    need = BLK // CHAIN + HOP * (n_ctx - 1)
    early = max(0, need - used)
    if early:
        lax.fori_loop(0, early, lambda index, carry: (tick(used + index), carry)[1], 0)

    def each_slot(slot, carry):
        base = pl.multiple_of((slot + 1) * BLK, BLK)
        visible = slot < slot_ref[0]
        begin = early + used + slot * per_slot

        def total(rows):
            joined = left[slot, rows, :] + right[slot, rows, :]
            return jnp.where(own_tag == slot, x_own[rows, :], joined)

        normalise(total, base)

        def slot_kv(index, inner):
            tick(begin + index)
            project_kv(index, base)
            return inner

        lax.fori_loop(0, 2 * D // SPAN, slot_kv, 0)

        send_block(slot + 1)

        def slot_attention(group, inner):
            tick(begin + 2 * D // SPAN + 2 * group)
            tick(begin + 2 * D // SPAN + 2 * group + 1)
            for member in range(GROUP):
                softmax_block(
                    q_all, kv_all, acc, tops, sums, group * GROUP + member, base, False, visible
                )
            return inner

        lax.fori_loop(0, groups, slot_attention, 0)
        return carry

    lax.fori_loop(0, slots, each_slot, 0)
    done_ticks = early + used + slots * per_slot

    def finish(pair, carry):
        lanes = aligned(pair * 128, 128)
        x_own[:, lanes] = (acc[:, lanes] / sums[pair]).astype(jnp.bfloat16)
        tops[pair] = tops[pair] + jnp.log2(sums[pair])
        return carry

    lax.fori_loop(0, PAIRS, finish, 0)
    outputs += [
        pltpu.make_async_copy(x_own, o_out, sem_out.at[2]),
        pltpu.make_async_copy(tops, lse_out, sem_out.at[3]),
    ]
    for copy in outputs[2:]:
        copy.start()
    all_ticks = max(pieces + LAG, chain_chunks + HOP * (n_ctx - 1))
    if all_ticks > done_ticks:
        lax.fori_loop(done_ticks, all_ticks, lambda index, carry: (tick(index), carry)[1], 0)

    def drain(index, carry):
        here = fulls[0].at[pl.ds(0, PIECE), pl.ds(0, SPAN)]

        @pl.when(index >= ranges[0][1])
        def _():
            remote(here, here, cs_s.at[index], cs_r.at[index], core_peer).wait_recv()
            remote(here, here, cg_s.at[index], cg_r.at[index], core_peer).wait_recv()

        remote(here, here, side_s.at[index], side_r.at[index], side_peer).wait_send()
        remote(here, here, grp_s.at[index], grp_r.at[index], grp_peer).wait_send()
        remote(here, here, cs_s.at[index], cs_r.at[index], core_peer).wait_send()
        remote(here, here, cg_s.at[index], cg_r.at[index], core_peer).wait_send()
        return carry

    lax.fori_loop(0, pieces, drain, 0)
    copies = own_copies()
    for number, copy in enumerate(copies):
        copy.wait_send()
        if number >= len(copies) - 3:
            copy.wait_recv()
    for index in range(moves - 3, moves):
        local_wait(hop.at[index % 3], sem_store.at[index % 3])

    def drain_chain(index, carry):
        here = left.at[0, pl.ds(0, CHAIN)]

        @pl.when(ctx < n_ctx - 1)
        def _():
            remote(here, here, left_s.at[index], left_r.at[index], next_ctx).wait_send()

        @pl.when(ctx > 0)
        def _():
            remote(here, here, right_s.at[index], right_r.at[index], last_ctx).wait_send()

        return carry

    lax.fori_loop(0, chain_chunks, drain_chain, 0)
    for copy in outputs:
        copy.wait()

    def drain_blocks(index, carry):
        rows = aligned(index * BLK, BLK)
        local_wait(a_all.at[rows, :], sem_a.at[index])
        local_wait(kv_all.at[rows, :], sem_kv.at[index])
        return carry

    lax.fori_loop(0, slots + 1, drain_blocks, 0)


def forward_part(n_ctx, tags, gain, bias, raw, w_qkv, w_out, w_up, w_down):
    slots = n_ctx // 2
    every = (slots + 1) * BLK
    low, full = jnp.bfloat16, jnp.float32
    dma = pltpu.SemaphoreType.DMA
    hbm = pl.BlockSpec(memory_space=pl.ANY)
    vmem = pl.BlockSpec(memory_space=pltpu.VMEM)
    shards = (w_qkv, w_out, w_up, w_down)
    pieces = sum(w.shape[0] * w.shape[1] // (2 * PIECE * SPAN) for w in shards)
    own = w_qkv.shape[1] // SPAN + 3
    chain = slots * (BLK // CHAIN)
    shape = jax.ShapeDtypeStruct
    return pl.pallas_call(
        functools.partial(forward_kernel, n_ctx),
        out_shape=[
            shape((every, D), low),
            shape((BLK, D), low),
            shape((every, 2 * D), low),
            shape((BLK, D), low),
            shape((PAIRS, BLK, 128), full),
        ]
        + [shape((4 * w.shape[0], w.shape[1]), low) for w in shards],
        in_specs=[pl.BlockSpec(memory_space=pltpu.SMEM), vmem, vmem] + [hbm] * 5,
        out_specs=[hbm] * 9,
        scratch_shapes=[
            pltpu.VMEM((BLK, D), low),
            pltpu.VMEM((slots, BLK, D), low),
            pltpu.VMEM((slots, BLK, D), low),
            pltpu.VMEM((every, D), low),
            pltpu.VMEM((BLK, D), low),
            pltpu.VMEM((every, 2 * D), low),
            pltpu.VMEM((D, 3 * D), low),
            pltpu.VMEM((BLK, D), full),
            pltpu.VMEM((PAIRS, BLK, 128), full),
            pltpu.VMEM((PAIRS, BLK, 128), full),
            pltpu.VMEM((3, 2 * PIECE, SPAN), low),
            dma((2,)),
            dma((3,)),
            dma((3,)),
            dma((4,)),
            dma((slots + 1,)),
            dma((slots + 1,)),
        ]
        + [dma((pieces,))] * 8
        + [dma((own,))] * 2
        + [dma((chain,))] * 4,
        compiler_params=pltpu.CompilerParams(
            collective_id=1, has_side_effects=True, vmem_limit_bytes=63 << 20
        ),
        cost_estimate=pl.CostEstimate(flops=20 << 30, bytes_accessed=64 << 20, transcendentals=1 << 24),
        name="gather_attend",
    )(tags, gain, bias, raw, *shards)


TILE = 256
PAIRED = 2


def grad_block(q_ref, do_ref, o_ref, lse_ref, kv_ref, dq_acc, turned, pair, own, visible):
    lanes = aligned(pair * 128, 128)
    value_lanes = aligned(D + pair * 128, 128)
    size = QT if own else BLK
    count = BLK // size
    q_pair, do_pair, lse_pair = q_ref[:, lanes], do_ref[:, lanes], lse_ref[pair]
    prod = do_pair.astype(jnp.float32) * o_ref[:, lanes].astype(jnp.float32)
    keys, values = kv_ref[:, lanes], kv_ref[:, value_lanes]
    q_turned, do_turned = q_pair.T, do_pair.T
    old_dq = dq_acc[:, lanes]
    causal = causal_tile()
    hide = 0.0 if own else jnp.where(visible, 0.0, 1e30)
    lanes_of = [head_lanes(head, size) for head in range(2)]
    work = [(tile, head) for tile in range(count) for head in range(2)]
    score, dprob, dlogit, prob_low = {}, {}, {}, {}
    for tile, head in work:
        rows = slice(tile * size, (tile + 1) * size)
        span = (tile + 1) * size if own else BLK
        zero = jnp.zeros((size, 128), jnp.bfloat16)
        score[tile, head] = contract_last(jnp.where(lanes_of[head], q_pair[rows], zero), keys[:span])
        dprob[tile, head] = contract_last(jnp.where(lanes_of[head], do_pair[rows], zero), values[:span])
    for tile, head in work:
        rows = slice(tile * size, (tile + 1) * size)
        delta = jnp.sum(jnp.where(lanes_of[head], prod[rows], 0.0), axis=-1, keepdims=True)
        shift = lse_pair[rows, head * DH : head * DH + 1] + hide
        prob = jnp.exp2(score[tile, head] * C2 - shift)
        if own:
            diag = jnp.where(causal, prob[:, tile * size :], 0.0)
            prob = jnp.concatenate([prob[:, : tile * size], diag], axis=1) if tile else diag
        dlogit[tile, head] = (prob * (dprob[tile, head] - delta)).astype(jnp.bfloat16)
        prob_low[tile, head] = prob.astype(jnp.bfloat16)
    for tile in range(count):
        rows = slice(tile * size, (tile + 1) * size)
        span = (tile + 1) * size if own else BLK
        parts = [dot_dims(dlogit[tile, head], keys[:span], 1, 0) for head in range(2)]
        dq_acc[pl.ds(tile * size, size), lanes] = old_dq[rows] + jnp.where(lanes_of[0], parts[0], parts[1])
    for head in range(2):
        for offset, left_side, right_side, scale in (
            (0, q_turned, dlogit, ALPHA),
            (D, do_turned, prob_low, 1.0),
        ):
            spot = aligned(offset + pair * 128 + head * DH, DH)
            left_head = left_side[head * DH : (head + 1) * DH]
            terms = [
                dot_dims(left_head[:, tile * size : (tile + 1) * size], right_side[tile, head], 1, 0)
                for tile in range(count)
            ]
            for tile in range(count):
                cols = slice(tile * size, (tile + 1) * size)
                total = functools.reduce(
                    jnp.add, [terms[other][:, cols] for other in range(tile, count)]
                ) if own else terms[0]
                turned[spot, cols if own else slice(None)] = (total * scale).astype(jnp.bfloat16)


def backward_kernel(n_ctx, widths, *refs):
    slots = n_ctx // 2
    levels = n_ctx.bit_length() - 1
    depth = 8 + levels if levels < 3 else 6 + levels
    (slot_ref, gain_ref, norm_ref, x_hbm, q_hbm, kv_hbm, a_hbm, o_hbm, do_hbm, lse_hbm, w_hbm) = refs[:11]
    terms, outs = list(refs[11:14]), refs[14:18]
    grad_out, norm_out = refs[18:20]
    scratch = list(refs[20:])

    def take(count):
        taken = scratch[:count]
        del scratch[:count]
        return taken

    q_v, o_v, do_v, lse_v, weight, kv_b, a_b, dq_acc, turned, gkv, term, own_part, left, right, norm_v, norm_in = take(16)
    r1, r2, r3, fin, local = take(5)
    zbufs = take(levels)
    sem_in, sem_blk, sem_local, sem_out, sem_res = take(5)
    send1, recv1, send2, recv2, send3, recv3, send6, recv6 = take(8)
    rs_send, rs_recv, ag_send, ag_recv = take(levels), take(levels), take(levels), take(levels)
    left_s, left_r, right_s, right_r, norm_s, norm_r = take(6)
    terms.append(term)

    grp, ctx, wsh = lax.axis_index("grp"), lax.axis_index("ctx"), lax.axis_index("wsh")
    side, core = wsh // 2, wsh % 2
    core_peer = (grp, ctx, side * 2 + 1 - core)
    side_peer = (grp, ctx, (1 - side) * 2 + core)
    grp_peer = (1 - grp, ctx, wsh)
    next_ctx = (grp, lax.rem(ctx + 1, n_ctx), wsh)
    last_ctx = (grp, lax.rem(ctx + n_ctx - 1, n_ctx), wsh)
    bits = [(ctx // (1 << level)) % 2 for level in range(levels)]
    level_peers = [(grp, ctx + (1 - 2 * bits[level]) * (1 << level), wsh) for level in range(levels)]

    loads = [
        pltpu.make_async_copy(source, dest, sem_in.at[place])
        for place, (source, dest) in enumerate(
            ((q_hbm, q_v), (o_hbm, o_v), (do_hbm, do_v), (lse_hbm, lse_v), (w_hbm, weight))
        )
    ]
    for load in loads:
        load.start()

    def block_copies(index):
        rows = aligned(lax.rem(index, slots + 1) * BLK, BLK)
        slot = lax.rem(index, kv_b.shape[0])
        return (
            pltpu.make_async_copy(kv_hbm.at[rows, :], kv_b.at[slot], sem_blk.at[0, slot]),
            pltpu.make_async_copy(a_hbm.at[rows, :], a_b.at[slot], sem_blk.at[1, slot]),
        )

    for copy in block_copies(1):
        copy.start()

    barrier = pltpu.get_barrier_semaphore()
    peers = [core_peer, side_peer, grp_peer, next_ctx, last_ctx] + level_peers
    for peer in peers:
        pl.semaphore_signal(barrier, inc=1, device_id=peer, device_id_type=MESH)
    pl.semaphore_wait(barrier, len(peers))

    half = TILE // 2
    ranges, first = [], 0
    for rows, cols in widths:
        across = cols // TILE
        ranges.append((first, first + (rows // TILE) * across, across))
        first = ranges[-1][1]
    chunks = first

    def by_range(index, act):
        for place, (low, high, across) in enumerate(ranges):

            @pl.when((index >= low) & (index < high))
            def _(place=place, low=low, across=across):
                number = index - low
                act(place, (aligned((number // across) * TILE, TILE), aligned((number % across) * TILE, TILE)))

    def region(level, flip):
        row, rows, col, cols = 0, half, 0, TILE
        for place in range(level):
            bit = 1 - bits[place] if (flip and place == level - 1) else bits[place]
            if rows > 16:
                rows = rows // 2
                row = row + bit * rows
            else:
                cols = cols // 2
                col = col + bit * cols
        return row, rows, col, cols

    def spot(level, flip=False, base=0):
        row, rows, col, cols = region(level, flip)
        return aligned(base + row, rows), aligned(col, cols)

    def step_load(index):
        slot = lax.rem(index, depth)
        near = lax.rem(index, 4)

        def act(place, span):
            source = terms[place]
            pltpu.make_async_copy(source.at[:, core, span[0], span[1]], local.at[near], sem_local.at[near]).start()
            remote(
                source.at[:, 1 - core, span[0], span[1]], r1.at[slot], send1.at[slot], recv1.at[slot], core_peer
            ).start()

        by_range(index, act)

    def finished(move):
        move.wait_send()
        move.wait_recv()

    def step_core(index):
        slot, near = lax.rem(index, depth), lax.rem(index, 4)
        local_wait(local.at[near], sem_local.at[near])
        finished(remote(r1.at[slot], r1.at[slot], send1.at[slot], recv1.at[slot], core_peer))
        r1[slot] = r1[slot] + local[near]
        remote(r1.at[slot, 1 - side], r2.at[slot], send2.at[slot], recv2.at[slot], side_peer).start()

    keep_half = aligned(grp * half, half)
    give_half = aligned((1 - grp) * half, half)

    def step_side(index):
        slot = lax.rem(index, depth)
        finished(remote(r1.at[slot, 1 - side], r2.at[slot], send2.at[slot], recv2.at[slot], side_peer))
        r2[slot] = r2[slot] + r1[slot, side]
        remote(r2.at[slot, give_half], r3.at[slot], send3.at[slot], recv3.at[slot], grp_peer).start()

    def rs_copy(level, slot):
        rows, cols = spot(level + 1, True)
        return remote(
            r3.at[slot, rows, cols], zbufs[level].at[slot], rs_send[level].at[slot], rs_recv[level].at[slot], level_peers[level]
        )

    def ag_copy(level, slot, flip=False):
        rows, cols = spot(level + 1, flip, grp * half)
        here = fin.at[slot, rows, cols]
        return remote(here, here, ag_send[level].at[slot], ag_recv[level].at[slot], level_peers[level])

    def back_copy(slot, rows):
        here = fin.at[slot, rows]
        return remote(here, here, send6.at[slot], recv6.at[slot], grp_peer)

    def step_grp(index):
        slot = lax.rem(index, depth)
        finished(remote(r2.at[slot, give_half], r3.at[slot], send3.at[slot], recv3.at[slot], grp_peer))
        r3[slot] = r3[slot] + r2[slot, keep_half]
        rs_copy(0, slot).start()

    def step_scatter(level):
        def act(index):
            slot = lax.rem(index, depth)
            finished(rs_copy(level, slot))
            rows, cols = spot(level + 1)
            total = r3[slot, rows, cols] + zbufs[level][slot]
            if level + 1 < levels:
                r3[slot, rows, cols] = total
                rs_copy(level + 1, slot).start()
            else:
                rows, cols = spot(level + 1, False, grp * half)
                fin[slot, rows, cols] = total
                ag_copy(level, slot).start()

        return act

    def step_gather(level):
        def act(index):
            slot = lax.rem(index, depth)
            finished(ag_copy(level, slot, True))
            if level:
                ag_copy(level - 1, slot).start()
            else:
                back_copy(slot, keep_half).start()

        return act

    def out_wait(index):
        slot = lax.rem(index, depth)
        local_wait(fin.at[slot], sem_out.at[slot])

    def step_out(index):
        slot = lax.rem(index, depth)
        finished(back_copy(slot, give_half))

        def act(place, span):
            pltpu.make_async_copy(fin.at[slot], outs[place].at[span[0], span[1]], sem_out.at[slot]).start()

        by_range(index, act)

    stages = [(0, step_core), (2, step_side), (4, step_grp)]
    stages += [(5 + level, step_scatter(level)) for level in range(levels)]
    stages += [(5 + 2 * levels - 1 - level, step_gather(level)) for level in reversed(range(levels))]
    stages += [(6 + 2 * levels, step_out), (8 + 2 * levels, out_wait)]
    all_ticks = chunks + stages[-1][0]

    def tick(step):
        @pl.when(step + 2 < chunks)
        def _():
            step_load(step + 2)

        for lag, act in stages:
            index = step - lag

            @pl.when((index >= 0) & (index < chunks))
            def _(act=act, index=index):
                act(index)

    per_slot = BLK // CHAIN
    chain_chunks = slots * per_slot

    def chain_step(stream, send, recv, number, is_first, is_last, target):
        slot = number // per_slot
        rows = aligned((number % per_slot) * CHAIN, CHAIN)
        here = stream.at[slot, rows]

        @pl.when(is_first)
        def _():
            stream[slot, rows, :] = own_part[slot, rows, :]

        @pl.when(jnp.logical_not(is_first))
        def _():
            remote(here, here, send.at[number], recv.at[number], target).wait_recv()
            stream[slot, rows, :] = stream[slot, rows, :] + own_part[slot, rows, :]

        @pl.when(jnp.logical_not(is_last))
        def _():
            remote(here, here, send.at[number], recv.at[number], target).start()

    def chain_tick(step):
        number = step - HOP * ctx

        @pl.when((number >= 0) & (number < chain_chunks))
        def _():
            chain_step(left, left_s, left_r, number, ctx == 0, ctx == n_ctx - 1, next_ctx)

        back = step - HOP * (n_ctx - 1 - ctx)

        @pl.when((back >= 0) & (back < chain_chunks))
        def _():
            chain_step(right, right_s, right_r, back, ctx == n_ctx - 1, ctx == 0, last_ctx)

    chain_ticks = chain_chunks + HOP * (n_ctx - 1)

    step_load(0)
    step_load(1)
    dq_acc[...] = jnp.zeros_like(dq_acc)
    for load in loads:
        load.wait()

    groups = PAIRS // PAIRED

    def attend(kv_ref, own, visible, begin, chained, chain_from):
        def body(group, carry):
            for extra in range(2):
                tick(begin + 2 * group + extra)
            if chained is not None:

                @pl.when(chained)
                def _():
                    for extra in range(2):
                        chain_tick(chain_from + 2 * group + extra)

            for member in range(PAIRED):
                grad_block(
                    q_v, do_v, o_v, lse_v, kv_ref, dq_acc, turned, group * PAIRED + member, own, visible
                )
            return carry

        lax.fori_loop(0, groups, body, 0)

    block_ticks = 2 * groups + 2

    def each_slot(slot, carry):
        visible = slot < slot_ref[0]
        index = slot + 1
        place = lax.rem(index, kv_b.shape[0])
        for copy in block_copies(index):
            copy.wait()
        if kv_b.shape[0] > 1:
            for copy in block_copies(index + 1):
                copy.start()
        begin = slot * block_ticks
        attend(kv_b.at[place], False, visible, begin, slot > 0, (slot - 1) * per_slot)

        def weight_terms(step, inner):
            tick(begin + 2 * groups + step)
            rows = aligned(step * 512, 512)
            for part in range(2):
                cols = pl.ds(part * D, D)
                fresh = dot_dims(a_b[place, :, rows], turned[cols, :], 0, 1)

                @pl.when(slot == 0)
                def _(fresh=fresh, cols=cols):
                    gkv[rows, cols] = fresh.astype(gkv.dtype)

                @pl.when(slot > 0)
                def _(fresh=fresh, cols=cols):
                    gkv[rows, cols] = (gkv[rows, cols] + fresh).astype(gkv.dtype)

            own_part[slot, :, rows] = dot_dims(
                turned[...], weight[rows, pl.ds(D, 2 * D)], 0, 1
            ).astype(jnp.bfloat16)
            return inner

        lax.fori_loop(0, 2, weight_terms, 0)
        if kv_b.shape[0] == 1:
            for copy in block_copies(index + 1):
                copy.start()
        return carry

    lax.fori_loop(0, slots, each_slot, 0)
    begin = slots * block_ticks
    own_place = (slots + 1) % kv_b.shape[0]
    for copy in block_copies(slots + 1):
        copy.wait()
    attend(kv_b.at[own_place], True, None, begin, slots > 0, (slots - 1) * per_slot)
    dq_low = o_v
    dq_low[...] = (dq_acc[...] * ALPHA).astype(jnp.bfloat16) * jnp.bfloat16(QSCALE)
    x_load = pltpu.make_async_copy(x_hbm, do_v, sem_in.at[0])
    x_load.start()

    def last_terms(step, carry):
        tick(begin + 2 * groups + step)
        rows = aligned(step * TILE, TILE)
        a_rows = a_b[own_place, :, rows]
        up, down = step // 2, step % 2
        term[up, down, :, pl.ds(0, D)] = dot_dims(a_rows, dq_low[...], 0, 0).astype(jnp.bfloat16)
        for part in range(2):
            cols = pl.ds(part * D, D)
            term[up, down, :, pl.ds((part + 1) * D, D)] = (
                gkv[rows, cols] + dot_dims(a_rows, turned[cols, :], 0, 1)
            ).astype(jnp.bfloat16)
        return carry

    lax.fori_loop(0, 4, last_terms, 0)
    ready = begin + 2 * groups + 4
    assert ready <= ranges[-1][0] - 2 or n_ctx > 4
    da_acc = dq_acc

    def own_grad(step, carry):
        tick(ready + step)
        chain_tick(chain_chunks + step)
        rows = aligned(step * TILE, TILE)
        da_acc[:, rows] = dot_dims(dq_low[...], weight[rows, pl.ds(0, D)], 1, 1) + dot_dims(
            turned[...], weight[rows, pl.ds(D, 2 * D)], 0, 1
        )
        return carry

    lax.fori_loop(0, 4, own_grad, 0)
    ready = ready + 4

    def flush_chain(step, carry):
        tick(ready + step)
        chain_tick(chain_chunks + 4 + step)
        return carry

    left_over = max(0, chain_ticks - chain_chunks - 4)
    lax.fori_loop(0, left_over, flush_chain, 0)
    ready = ready + left_over
    x_load.wait()
    gain = gain_ref[...]

    def norm_grad(step, carry):
        gain_sum, bias_sum = carry

        @pl.when(step % 2 == 0)
        def _():
            tick(ready + step // 2)

        rows = aligned(step * CHAIN, CHAIN)
        upstream = da_acc[rows, :]
        for slot in range(slots):
            joined = left[slot, rows, :].astype(jnp.float32) + right[slot, rows, :].astype(jnp.float32)
            upstream = upstream + jnp.where(slot_ref[0] == slot, joined, 0.0)
        values = do_v[rows, :].astype(jnp.float32)
        centre = values - jnp.mean(values, axis=-1, keepdims=True)
        scale = lax.rsqrt(jnp.mean(centre * centre, axis=-1, keepdims=True) + EPS)
        centre = centre * scale
        scaled = upstream * gain
        da_acc[rows, :] = scale * (
            scaled
            - jnp.mean(scaled, axis=-1, keepdims=True)
            - centre * jnp.mean(scaled * centre, axis=-1, keepdims=True)
        )
        gain_sum = gain_sum + jnp.sum(upstream * centre, axis=0, keepdims=True)
        bias_sum = bias_sum + jnp.sum(upstream, axis=0, keepdims=True)
        return gain_sum, bias_sum

    zero = jnp.zeros((1, D), jnp.float32)
    gain_sum, bias_sum = lax.fori_loop(0, BLK // CHAIN, norm_grad, (zero, zero))
    ready = ready + BLK // CHAIN // 2
    result = pltpu.make_async_copy(da_acc, grad_out, sem_res.at[0])
    result.start()
    row = lax.broadcasted_iota(jnp.int32, (8, D), 0)
    norm_v[...] = norm_ref[...] + jnp.where(row == 0, gain_sum, 0.0) + jnp.where(row == 4, bias_sum, 0.0)
    for place, peer in enumerate([core_peer, side_peer, grp_peer] + level_peers):
        move = remote(norm_v, norm_in.at[place], norm_s.at[place], norm_r.at[place], peer)
        move.start()
        tick(ready)
        tick(ready + 1)
        ready = ready + 2
        finished(move)
        norm_v[...] = norm_v[...] + norm_in[place]
    norm_result = pltpu.make_async_copy(norm_v, norm_out, sem_res.at[1])
    norm_result.start()
    if all_ticks > ready:
        lax.fori_loop(ready, all_ticks, lambda index, carry: (tick(index), carry)[1], 0)

    def drain_chain(index, carry):
        here = left.at[0, pl.ds(0, CHAIN)]

        @pl.when(ctx < n_ctx - 1)
        def _():
            remote(here, here, left_s.at[index], left_r.at[index], next_ctx).wait_send()

        @pl.when(ctx > 0)
        def _():
            remote(here, here, right_s.at[index], right_r.at[index], last_ctx).wait_send()

        return carry

    lax.fori_loop(0, chain_chunks, drain_chain, 0)
    result.wait()
    norm_result.wait()


def backward_part(n_ctx, slot_vec, gain, norms, raw, q, kv, a, o, do, lse, weight, terms):
    slots = n_ctx // 2
    levels = n_ctx.bit_length() - 1
    depth = 8 + levels if levels < 3 else 6 + levels
    every = (slots + 1) * BLK
    widths = [(term.shape[0] // 4, term.shape[1]) for term in terms] + [(D // 4, 3 * D)]
    low, full = jnp.bfloat16, jnp.float32
    dma = pltpu.SemaphoreType.DMA
    hbm = pl.BlockSpec(memory_space=pl.ANY)
    vmem = pl.BlockSpec(memory_space=pltpu.VMEM)
    shape = jax.ShapeDtypeStruct
    buffers = 2 if slots <= 2 else 1
    chain = slots * (BLK // CHAIN)
    zshapes, rows, cols = [], TILE // 2, TILE
    for _ in range(levels):
        rows, cols = (rows // 2, cols) if rows > 16 else (rows, cols // 2)
        zshapes.append(pltpu.VMEM((depth, rows, cols), low))
    return pl.pallas_call(
        functools.partial(backward_kernel, n_ctx, widths),
        out_shape=[shape(width, low) for width in widths] + [shape((BLK, D), full), shape((8, D), full)],
        in_specs=[pl.BlockSpec(memory_space=pltpu.SMEM), vmem, vmem] + [hbm] * 11,
        out_specs=[hbm] * 6,
        scratch_shapes=[
            pltpu.VMEM((BLK, D), low),
            pltpu.VMEM((BLK, D), low),
            pltpu.VMEM((BLK, D), low),
            pltpu.VMEM((PAIRS, BLK, 128), full),
            pltpu.VMEM((D, 3 * D), low),
            pltpu.VMEM((buffers, BLK, 2 * D), low),
            pltpu.VMEM((buffers, BLK, D), low),
            pltpu.VMEM((BLK, D), full),
            pltpu.VMEM((2 * D, BLK), low),
            pltpu.VMEM((D, 2 * D), full if slots <= 2 else low),
            pltpu.VMEM((2, 2, D // 4, 3 * D), low),
            pltpu.VMEM((slots, BLK, D), low),
            pltpu.VMEM((slots, BLK, D), low),
            pltpu.VMEM((slots, BLK, D), low),
            pltpu.VMEM((8, D), full),
            pltpu.VMEM((3 + levels, 8, D), full),
            pltpu.VMEM((depth, 2, TILE, TILE), low),
            pltpu.VMEM((depth, TILE, TILE), low),
            pltpu.VMEM((depth, TILE // 2, TILE), low),
            pltpu.VMEM((depth, TILE, TILE), low),
            pltpu.VMEM((4, 2, TILE, TILE), low),
        ]
        + zshapes
        + [dma((5,)), dma((2, buffers)), dma((4,)), dma((depth,)), dma((2,))]
        + [dma((depth,))] * (8 + 4 * levels)
        + [dma((chain,))] * 4
        + [dma((3 + levels,))] * 2,
        compiler_params=pltpu.CompilerParams(
            collective_id=2, has_side_effects=True, vmem_limit_bytes=67043328
        ),
        cost_estimate=pl.CostEstimate(flops=40 << 30, bytes_accessed=64 << 20, transcendentals=1 << 24),
        name="attend_back_reduce",
    )(
        slot_vec,
        gain,
        norms,
        raw,
        q,
        kv,
        a,
        o,
        do,
        lse,
        weight,
        *[term.reshape(2, 2, width[0], width[1]) for term, width in zip(terms, widths)],
    )


def per_device(n_ctx, inputs, w_qkv, w_out, w_up, w_down, norm_gains, norm_biases, block_map, out_grad):
    slots = n_ctx // 2
    raw = inputs.reshape(BLK, D)
    tokens = raw.astype(jnp.float32)
    block_entry = block_map.reshape(2)
    own_slot = block_entry[1] // BLK
    own_tag = jnp.where(block_entry[0] == 0, own_slot, n_ctx)
    slot_vec = own_slot.reshape(1)
    every_low, queries, keys_values, attn_low, lse, full_qkv, full_out, full_up, full_down = forward_part(
        n_ctx,
        jnp.stack([own_slot, own_tag]),
        norm_gains[0:1],
        norm_biases[0:1],
        raw,
        w_qkv,
        w_out,
        w_up,
        w_down,
    )

    branch = jnp.dot(attn_low, full_out, preferred_element_type=jnp.float32)
    post_attn, attn_back = jax.vjp(layer_norm, branch, norm_gains[1], norm_biases[1])
    hidden = tokens + post_attn
    pre_ffn, ffn_back = jax.vjp(layer_norm, hidden, norm_gains[2], norm_biases[2])
    ffn_low = pre_ffn.astype(jnp.bfloat16)
    upward = jnp.dot(ffn_low, full_up, preferred_element_type=jnp.float32)
    activated, gelu_back = jax.vjp(gelu_tanh, upward)
    active_low = activated.astype(jnp.bfloat16)
    downward = jnp.dot(active_low, full_down, preferred_element_type=jnp.float32)
    post_ffn, post_back = jax.vjp(layer_norm, downward, norm_gains[3], norm_biases[3])
    result = (hidden + post_ffn).astype(jnp.bfloat16).reshape(1, 1, BLK, D)
    seed_grad = out_grad.reshape(BLK, D).astype(jnp.float32)
    grad_down_in, gain_grad3, bias_grad3 = post_back(seed_grad)
    down_low = grad_down_in.astype(jnp.bfloat16)
    term_down = contract_rows(active_low, down_low).astype(jnp.bfloat16)
    grad_active = contract_last(down_low, full_down)
    up_low = gelu_back(grad_active)[0].astype(jnp.bfloat16)
    term_up = contract_rows(ffn_low, up_low).astype(jnp.bfloat16)
    grad_pre_ffn, gain_grad2, bias_grad2 = ffn_back(contract_last(up_low, full_up))
    grad_hidden = seed_grad + grad_pre_ffn
    grad_branch, gain_grad1, bias_grad1 = attn_back(grad_hidden)
    branch_low = grad_branch.astype(jnp.bfloat16)
    term_out = contract_rows(attn_low, branch_low).astype(jnp.bfloat16)
    grad_out_low = contract_last(branch_low, full_out).astype(jnp.bfloat16)

    zero_row = jnp.zeros((D,), jnp.float32)
    norms = jnp.stack(
        [zero_row, gain_grad1, gain_grad2, gain_grad3, zero_row, bias_grad1, bias_grad2, bias_grad3]
    )
    summed_down, summed_up, summed_out, summed_qkv, grad_tokens, norm_total = backward_part(
        n_ctx,
        slot_vec,
        norm_gains[0:1],
        norms,
        raw,
        queries,
        keys_values,
        every_low,
        attn_low,
        grad_out_low,
        lse,
        full_qkv,
        [term_down, term_up, term_out],
    )
    grad_input = (grad_hidden + grad_tokens).reshape(1, 1, BLK, D)
    summed_down, summed_up, summed_out, summed_qkv = (
        total.astype(jnp.float32) for total in (summed_down, summed_up, summed_out, summed_qkv)
    )
    gain_total, bias_total = norm_total[:4], norm_total[4:]
    return (
        result,
        grad_input,
        summed_qkv,
        summed_out,
        summed_up,
        summed_down,
        gain_total,
        bias_total,
    )


def solution(mesh):
    rows = P("wsh", None)
    blocks = P("grp", "wsh", "ctx", None)
    return jax.shard_map(
        functools.partial(per_device, mesh.shape["ctx"]),
        mesh=mesh,
        in_specs=(blocks, rows, rows, rows, rows, P(), P(), blocks, blocks),
        out_specs=(blocks, blocks, rows, rows, rows, rows, P(), P()),
        check_vma=False,
    )
```

```python
import functools
import math

import jax
import jax.numpy as jnp
from jax import lax
from jax.experimental import pallas as pl
from jax.experimental.pallas import tpu as pltpu
from jax.sharding import PartitionSpec as P

D = 1024
HEADS = 16
DH = 64
BLK = 512
PAIRS = HEADS // 2
QT = 256

EPS = 1e-05
ALPHA = 32.0
NEG = -1e30
LOG2E = 1.4426950408889634
C2 = ALPHA * LOG2E
MESH = pl.DeviceIdType.MESH
QSCALE = 1.0 / (ALPHA * math.sqrt(DH))


def layer_norm(values, gain_row, bias_row):
    centre = values - jnp.mean(values, axis=-1, keepdims=True)
    spread = jnp.mean(centre * centre, axis=-1, keepdims=True)
    return centre * lax.rsqrt(spread + EPS) * gain_row + bias_row


def gelu_tanh(values):
    return jax.nn.gelu(values, approximate=True)


def dot_dims(left_side, right_side, left_dim, right_dim):
    return lax.dot_general(
        left_side,
        right_side,
        (((left_dim,), (right_dim,)), ((), ())),
        preferred_element_type=jnp.float32,
    )


def contract_last(left_side, right_side):
    return dot_dims(left_side, right_side, 1, 1)


def contract_rows(left_side, right_side):
    return dot_dims(left_side, right_side, 0, 0)


def head_lanes(head, rows):
    lane = lax.broadcasted_iota(jnp.int32, (rows, 128), 1)
    return (lane >= DH) if head else (lane < DH)


def causal_tile():
    row = lax.broadcasted_iota(jnp.int32, (QT, QT), 0)
    col = lax.broadcasted_iota(jnp.int32, (QT, QT), 1)
    return col <= row


PIECE = 128
SPAN = 512
CHAIN = 64
HOP = 2
YLAG = 2
XLAG = 2
BLAG = 2
PACE = 2
LAG = 2
GROUP = 4
AHEAD = 4


def remote(src, dst, send, recv, peer):
    return pltpu.make_async_remote_copy(
        src_ref=src, dst_ref=dst, send_sem=send, recv_sem=recv, device_id=peer, device_id_type=MESH
    )


def local_wait(ref, sem):
    pltpu.make_async_copy(ref, ref, sem).wait()


def aligned(start, size):
    return pl.ds(pl.multiple_of(start, size), size)


def softmax_block(q_ref, kv_ref, acc, top_ref, sum_ref, pair, base, own, visible):
    lanes = aligned(pair * 128, 128)
    value_lanes = aligned(D + pair * 128, 128)
    causal = causal_tile()
    first = head_lanes(0, QT)
    count = BLK // QT
    q_pair = q_ref[:, lanes]
    keys = kv_ref[pl.ds(base, BLK), lanes]
    values = kv_ref[pl.ds(base, BLK), value_lanes]
    if not own:
        old_top, old_sum, old_out = top_ref[pair], sum_ref[pair], acc[:, lanes]
        hide = jnp.where(visible, 0.0, 1e30)
    results = []
    work = [(tile, head) for tile in range(count) for head in range(2)]
    parts_of = {}
    for tile, head in work:
        q_tile = q_pair[tile * QT : (tile + 1) * QT]
        q_head = jnp.where(head_lanes(head, QT), q_tile, jnp.zeros_like(q_tile))
        span = (tile + 1) * QT if own else BLK
        parts_of[tile, head] = contract_last(q_head, keys[:span])
    top_of, expo_of, total_of = {}, {}, {}
    for tile, head in work:
        part = parts_of[tile, head]
        if own:
            diag = jnp.where(causal, part[:, tile * QT :], NEG)
            part = jnp.concatenate([part[:, : tile * QT], diag], axis=1) if tile else diag
        top = jnp.max(part, axis=-1, keepdims=True) * C2
        if own:
            shift = top
        else:
            top = jnp.maximum(
                jnp.where(visible, top, NEG), old_top[tile * QT : (tile + 1) * QT, head * DH : head * DH + 1]
            )
            shift = top + hide
        expo = jnp.exp2(part * C2 - shift)
        top_of[tile, head] = jnp.broadcast_to(top, (QT, 128))
        total_of[tile, head] = jnp.broadcast_to(jnp.sum(expo, axis=-1, keepdims=True), (QT, 128))
        expo_of[tile, head] = expo.astype(jnp.bfloat16)
    out_of = {}
    for tile, head in work:
        span = (tile + 1) * QT if own else BLK
        out_of[tile, head] = dot_dims(expo_of[tile, head], values[:span], 1, 0)
    for tile in range(count):
        rows = pl.ds(tile * QT, QT)
        new_top = jnp.where(first, top_of[tile, 0], top_of[tile, 1])
        new_sum = jnp.where(first, total_of[tile, 0], total_of[tile, 1])
        new_out = jnp.where(first, out_of[tile, 0], out_of[tile, 1])
        if not own:
            here = slice(tile * QT, (tile + 1) * QT)
            keep = jnp.exp2(old_top[here] - new_top)
            new_sum = new_sum + old_sum[here] * keep
            new_out = new_out + old_out[here] * keep
        top_ref[pair, rows, :] = new_top
        sum_ref[pair, rows, :] = new_sum
        acc[rows, lanes] = new_out


def forward_kernel(n_ctx, *refs):
    slots = n_ctx // 2
    (slot_ref, gain_ref, bias_ref, x_hbm, w_qkv, w_out, w_up, w_down) = refs[:8]
    (a_out, q_out, kv_out, o_out, lse_out, full_qkv, full_out, full_up, full_down) = refs[8:17]
    (x_own, left, right, a_all, q_all, kv_all, weight, acc, tops, sums, hop) = refs[17:28]
    (sem_in, sem_load, sem_store, sem_out, sem_a, sem_kv, side_s, side_r, grp_s, grp_r, cs_s, cs_r, cg_s, cg_r, own_s, own_r, left_s, left_r, right_s, right_r) = refs[28:]
    grp, ctx, wsh = lax.axis_index("grp"), lax.axis_index("ctx"), lax.axis_index("wsh")
    side, core = wsh // 2, wsh % 2
    core_peer = (grp, ctx, side * 2 + 1 - core)
    side_peer = (grp, ctx, (1 - side) * 2 + core)
    grp_peer = (1 - grp, ctx, wsh)
    next_ctx = (grp, lax.rem(ctx + 1, n_ctx), wsh)
    last_ctx = (grp, lax.rem(ctx + n_ctx - 1, n_ctx), wsh)

    load = pltpu.make_async_copy(x_hbm, x_own, sem_in.at[0])
    load.start()
    barrier = pltpu.get_barrier_semaphore()
    for peer in (core_peer, side_peer, grp_peer, next_ctx, last_ctx):
        pl.semaphore_signal(barrier, inc=1, device_id=peer, device_id_type=MESH)
    pl.semaphore_wait(barrier, 5)

    shards = (w_qkv, w_out, w_up, w_down)
    fulls = (weight, full_out, full_up, full_down)
    ranges, start = [], 0
    for shard in shards:
        across = shard.shape[1] // SPAN
        ranges.append((start, start + across * (shard.shape[0] // (2 * PIECE)), across))
        start = ranges[-1][1]
    pieces = start

    def by_range(index, act):
        for place, (low, high, across) in enumerate(ranges):

            @pl.when((index >= low) & (index < high))
            def _(place=place, low=low, across=across):
                act(place, (index - low) // across, aligned(((index - low) % across) * SPAN, SPAN))

    def rows_of(place, owner, half, group):
        shard_rows = shards[place].shape[0]
        return aligned(owner * shard_rows + half * (shard_rows // 2) + group * PIECE, PIECE)

    sides_owner = (1 - side) * 2 + core

    def send_piece(index, carry):
        def act(place, group, cols):
            remote(
                shards[place].at[rows_of(place, 0, grp, group), cols],
                fulls[place].at[rows_of(place, wsh, grp, group), cols],
                side_s.at[index],
                side_r.at[index],
                side_peer,
            ).start()

        by_range(index, act)
        return carry

    def own_copies():
        copies = []
        across = shards[0].shape[1] // SPAN
        for place in range(4):
            shard_rows = shards[place].shape[0]
            mine = aligned(wsh * shard_rows, shard_rows)
            steps = range(across) if place == 0 else [None]
            for step in steps:
                cols = slice(None) if step is None else pl.ds(step * SPAN, SPAN)
                number = len(copies)
                copies.append(
                    remote(
                        shards[place].at[:, cols],
                        fulls[place].at[mine, cols],
                        own_s.at[number],
                        own_r.at[number],
                        core_peer,
                    )
                )
        return copies

    for index in range(AHEAD):
        send_piece(index, 0)
    for copy in own_copies():
        copy.start()
    own_rows = aligned(wsh * w_qkv.shape[0], w_qkv.shape[0])
    own_weight = pltpu.make_async_copy(w_qkv, weight.at[own_rows, :], sem_in.at[1])
    own_weight.start()
    load.wait()

    bounces, start = [], 0
    for shard in shards[1:]:
        across = shard.shape[1] // SPAN
        bounces.append((start, start + across * (shard.shape[0] // (2 * PIECE)), across))
        start = bounces[-1][1]
    moves = start

    def bounce(index, loading):
        slot = lax.rem(index, 3)
        for place, (low, high, across) in enumerate(bounces):

            @pl.when((index >= low) & (index < high))
            def _(place=place + 1, low=low, across=across):
                group = (index - low) // across
                cols = aligned(((index - low) % across) * SPAN, SPAN)
                if loading:
                    here = shards[place].at[aligned(group * 2 * PIECE, 2 * PIECE), cols]
                    pltpu.make_async_copy(here, hop.at[slot], sem_load.at[slot]).start()
                else:
                    rows = aligned(wsh * shards[place].shape[0] + group * 2 * PIECE, 2 * PIECE)
                    local_wait(hop.at[slot], sem_load.at[slot])
                    pltpu.make_async_copy(
                        hop.at[slot], fulls[place].at[rows, cols], sem_store.at[slot]
                    ).start()

    own_tag = slot_ref[1]
    chain_chunks = slots * (BLK // CHAIN)

    def chain_step(stream, send, recv, number, is_first, is_last, target):
        slot = number // (BLK // CHAIN)
        spot = aligned((number % (BLK // CHAIN)) * CHAIN, CHAIN)
        mine = jnp.where(own_tag == slot, x_own[spot, :], jnp.zeros((CHAIN, D), jnp.bfloat16))
        here = stream.at[slot, spot]

        @pl.when(is_first)
        def _():
            stream[slot, spot, :] = mine

        @pl.when(jnp.logical_not(is_first))
        def _():
            remote(here, here, send.at[number], recv.at[number], target).wait_recv()
            stream[slot, spot, :] = stream[slot, spot, :] + mine

        @pl.when(jnp.logical_not(is_last))
        def _():
            remote(here, here, send.at[number], recv.at[number], target).start()

    def tick(step):
        @pl.when((step >= 1) & (step <= moves))
        def _():
            bounce(step - 1, False)

        @pl.when((step >= 3) & (step < moves))
        def _():
            local_wait(hop.at[lax.rem(step, 3)], sem_store.at[lax.rem(step, 3)])

        @pl.when(step < moves)
        def _():
            bounce(step, True)

        @pl.when(step + AHEAD < pieces)
        def _():
            send_piece(step + AHEAD, 0)

        number = step - HOP * ctx

        @pl.when((number >= 0) & (number < chain_chunks))
        def _():
            chain_step(left, left_s, left_r, number, ctx == 0, ctx == n_ctx - 1, next_ctx)

        back = step - HOP * (n_ctx - 1 - ctx)

        @pl.when((back >= 0) & (back < chain_chunks))
        def _():
            chain_step(right, right_s, right_r, back, ctx == n_ctx - 1, ctx == 0, last_ctx)

        @pl.when(step < pieces)
        def _():
            def act(place, group, cols):
                here = fulls[place].at[rows_of(place, sides_owner, grp, group), cols]
                remote(here, here, side_s.at[step], side_r.at[step], side_peer).wait_recv()
                remote(here, here, grp_s.at[step], grp_r.at[step], grp_peer).start()
                remote(here, here, cs_s.at[step], cs_r.at[step], core_peer).start()

            by_range(step, act)

        late = step - LAG

        @pl.when((late >= 0) & (late < pieces))
        def _():
            def act(place, group, cols):
                here = fulls[place].at[rows_of(place, sides_owner, 1 - grp, group), cols]
                remote(here, here, grp_s.at[late], grp_r.at[late], grp_peer).wait_recv()
                remote(here, here, cg_s.at[late], cg_r.at[late], core_peer).start()

            by_range(late, act)

    def normalise(source, dest):
        gain, bias = gain_ref[...], bias_ref[...]

        def body(index, carry):
            rows = aligned(index * 128, 128)
            values = source(rows).astype(jnp.float32)
            a_all[aligned(dest + index * 128, 128), :] = layer_norm(values, gain, bias).astype(
                jnp.bfloat16
            )
            return carry

        lax.fori_loop(0, BLK // 128, body, 0)

    def piece_ready(index):
        here = fulls[0].at[pl.ds(0, PIECE), pl.ds(0, SPAN)]
        remote(here, here, cs_s.at[index], cs_r.at[index], core_peer).wait_recv()
        remote(here, here, cg_s.at[index], cg_r.at[index], core_peer).wait_recv()
        whole = fulls[0].at[pl.ds(0, 2 * PIECE), pl.ds(0, SPAN)]
        remote(whole, whole, own_s.at[index], own_r.at[index], core_peer).wait_recv()

    tick(0)
    normalise(lambda rows: x_own[rows, :], 0)
    for step in range(1, LAG + 1):
        tick(step)
    own_weight.wait()

    def project_q(index, carry):
        tick(index + LAG + 1)
        piece_ready(index)
        cols = aligned(index * SPAN, SPAN)
        q_all[:, cols] = (
            jnp.dot(a_all[pl.ds(0, BLK), :], weight[:, cols], preferred_element_type=jnp.float32) * QSCALE
        ).astype(jnp.bfloat16)
        return carry

    lax.fori_loop(0, D // SPAN, project_q, 0)
    head_ticks = LAG + 1 + D // SPAN

    def project_kv(index, base):
        cols = aligned(index * SPAN, SPAN)
        rows = aligned(base, BLK)
        kv_all[rows, cols] = jnp.dot(
            a_all[rows, :], weight[:, aligned(D + index * SPAN, SPAN)], preferred_element_type=jnp.float32
        ).astype(jnp.bfloat16)

    def own_kv(index, carry):
        tick(index + head_ticks)
        piece_ready(index + D // SPAN)
        project_kv(index, 0)
        return carry

    lax.fori_loop(0, 2 * D // SPAN, own_kv, 0)
    own_ticks = head_ticks + 2 * D // SPAN

    def send_block(index):
        rows = aligned(index * BLK, BLK)
        pltpu.make_async_copy(a_all.at[rows, :], a_out.at[rows, :], sem_a.at[index]).start()
        pltpu.make_async_copy(kv_all.at[rows, :], kv_out.at[rows, :], sem_kv.at[index]).start()

    outputs = [
        pltpu.make_async_copy(weight, full_qkv, sem_out.at[0]),
        pltpu.make_async_copy(q_all, q_out, sem_out.at[1]),
    ]
    for copy in outputs:
        copy.start()

    send_block(0)

    def own_attention(group, carry):
        tick(own_ticks + 2 * group)
        tick(own_ticks + 2 * group + 1)
        for member in range(GROUP):
            softmax_block(q_all, kv_all, acc, tops, sums, group * GROUP + member, 0, True, None)
        return carry

    groups = PAIRS // GROUP
    lax.fori_loop(0, groups, own_attention, 0)
    used = own_ticks + 2 * groups
    per_slot = 2 * D // SPAN + 2 * groups

    need = BLK // CHAIN + HOP * (n_ctx - 1)
    early = max(0, need - used)
    if early:
        lax.fori_loop(0, early, lambda index, carry: (tick(used + index), carry)[1], 0)

    def each_slot(slot, carry):
        base = pl.multiple_of((slot + 1) * BLK, BLK)
        visible = slot < slot_ref[0]
        begin = early + used + slot * per_slot

        def total(rows):
            joined = left[slot, rows, :] + right[slot, rows, :]
            return jnp.where(own_tag == slot, x_own[rows, :], joined)

        normalise(total, base)

        def slot_kv(index, inner):
            tick(begin + index)
            project_kv(index, base)
            return inner

        lax.fori_loop(0, 2 * D // SPAN, slot_kv, 0)

        send_block(slot + 1)

        def slot_attention(group, inner):
            tick(begin + 2 * D // SPAN + 2 * group)
            tick(begin + 2 * D // SPAN + 2 * group + 1)
            for member in range(GROUP):
                softmax_block(
                    q_all, kv_all, acc, tops, sums, group * GROUP + member, base, False, visible
                )
            return inner

        lax.fori_loop(0, groups, slot_attention, 0)
        return carry

    lax.fori_loop(0, slots, each_slot, 0)
    done_ticks = early + used + slots * per_slot

    def finish(pair, carry):
        lanes = aligned(pair * 128, 128)
        x_own[:, lanes] = (acc[:, lanes] / sums[pair]).astype(jnp.bfloat16)
        tops[pair] = tops[pair] + jnp.log2(sums[pair])
        return carry

    lax.fori_loop(0, PAIRS, finish, 0)
    outputs += [
        pltpu.make_async_copy(x_own, o_out, sem_out.at[2]),
        pltpu.make_async_copy(tops, lse_out, sem_out.at[3]),
    ]
    for copy in outputs[2:]:
        copy.start()
    all_ticks = max(pieces + LAG, chain_chunks + HOP * (n_ctx - 1))
    if all_ticks > done_ticks:
        lax.fori_loop(done_ticks, all_ticks, lambda index, carry: (tick(index), carry)[1], 0)

    def drain(index, carry):
        here = fulls[0].at[pl.ds(0, PIECE), pl.ds(0, SPAN)]

        @pl.when(index >= ranges[0][1])
        def _():
            remote(here, here, cs_s.at[index], cs_r.at[index], core_peer).wait_recv()
            remote(here, here, cg_s.at[index], cg_r.at[index], core_peer).wait_recv()

        remote(here, here, side_s.at[index], side_r.at[index], side_peer).wait_send()
        remote(here, here, grp_s.at[index], grp_r.at[index], grp_peer).wait_send()
        remote(here, here, cs_s.at[index], cs_r.at[index], core_peer).wait_send()
        remote(here, here, cg_s.at[index], cg_r.at[index], core_peer).wait_send()
        return carry

    lax.fori_loop(0, pieces, drain, 0)
    copies = own_copies()
    for number, copy in enumerate(copies):
        copy.wait_send()
        if number >= len(copies) - 3:
            copy.wait_recv()
    for index in range(moves - 3, moves):
        local_wait(hop.at[index % 3], sem_store.at[index % 3])

    def drain_chain(index, carry):
        here = left.at[0, pl.ds(0, CHAIN)]

        @pl.when(ctx < n_ctx - 1)
        def _():
            remote(here, here, left_s.at[index], left_r.at[index], next_ctx).wait_send()

        @pl.when(ctx > 0)
        def _():
            remote(here, here, right_s.at[index], right_r.at[index], last_ctx).wait_send()

        return carry

    lax.fori_loop(0, chain_chunks, drain_chain, 0)
    for copy in outputs:
        copy.wait()

    def drain_blocks(index, carry):
        rows = aligned(index * BLK, BLK)
        local_wait(a_all.at[rows, :], sem_a.at[index])
        local_wait(kv_all.at[rows, :], sem_kv.at[index])
        return carry

    lax.fori_loop(0, slots + 1, drain_blocks, 0)


def forward_part(n_ctx, tags, gain, bias, raw, w_qkv, w_out, w_up, w_down):
    slots = n_ctx // 2
    every = (slots + 1) * BLK
    low, full = jnp.bfloat16, jnp.float32
    dma = pltpu.SemaphoreType.DMA
    hbm = pl.BlockSpec(memory_space=pl.ANY)
    vmem = pl.BlockSpec(memory_space=pltpu.VMEM)
    shards = (w_qkv, w_out, w_up, w_down)
    pieces = sum(w.shape[0] * w.shape[1] // (2 * PIECE * SPAN) for w in shards)
    own = w_qkv.shape[1] // SPAN + 3
    chain = slots * (BLK // CHAIN)
    shape = jax.ShapeDtypeStruct
    return pl.pallas_call(
        functools.partial(forward_kernel, n_ctx),
        out_shape=[
            shape((every, D), low),
            shape((BLK, D), low),
            shape((every, 2 * D), low),
            shape((BLK, D), low),
            shape((PAIRS, BLK, 128), full),
        ]
        + [shape((4 * w.shape[0], w.shape[1]), low) for w in shards],
        in_specs=[pl.BlockSpec(memory_space=pltpu.SMEM), vmem, vmem] + [hbm] * 5,
        out_specs=[hbm] * 9,
        scratch_shapes=[
            pltpu.VMEM((BLK, D), low),
            pltpu.VMEM((slots, BLK, D), low),
            pltpu.VMEM((slots, BLK, D), low),
            pltpu.VMEM((every, D), low),
            pltpu.VMEM((BLK, D), low),
            pltpu.VMEM((every, 2 * D), low),
            pltpu.VMEM((D, 3 * D), low),
            pltpu.VMEM((BLK, D), full),
            pltpu.VMEM((PAIRS, BLK, 128), full),
            pltpu.VMEM((PAIRS, BLK, 128), full),
            pltpu.VMEM((3, 2 * PIECE, SPAN), low),
            dma((2,)),
            dma((3,)),
            dma((3,)),
            dma((4,)),
            dma((slots + 1,)),
            dma((slots + 1,)),
        ]
        + [dma((pieces,))] * 8
        + [dma((own,))] * 2
        + [dma((chain,))] * 4,
        compiler_params=pltpu.CompilerParams(
            collective_id=1, has_side_effects=True, vmem_limit_bytes=63 << 20
        ),
        cost_estimate=pl.CostEstimate(flops=20 << 30, bytes_accessed=64 << 20, transcendentals=1 << 24),
        name="gather_attend",
    )(tags, gain, bias, raw, *shards)


TILE = 256
PAIRED = 2


def grad_block(q_ref, do_ref, o_ref, lse_ref, kv_ref, dq_acc, turned, pair, own, visible):
    lanes = aligned(pair * 128, 128)
    value_lanes = aligned(D + pair * 128, 128)
    size = QT if own else BLK
    count = BLK // size
    q_pair, do_pair, lse_pair = q_ref[:, lanes], do_ref[:, lanes], lse_ref[pair]
    prod = do_pair.astype(jnp.float32) * o_ref[:, lanes].astype(jnp.float32)
    keys, values = kv_ref[:, lanes], kv_ref[:, value_lanes]
    q_turned, do_turned = q_pair.T, do_pair.T
    old_dq = dq_acc[:, lanes]
    causal = causal_tile()
    hide = 0.0 if own else jnp.where(visible, 0.0, 1e30)
    lanes_of = [head_lanes(head, size) for head in range(2)]
    work = [(tile, head) for tile in range(count) for head in range(2)]
    score, dprob, dlogit, prob_low = {}, {}, {}, {}
    for tile, head in work:
        rows = slice(tile * size, (tile + 1) * size)
        span = (tile + 1) * size if own else BLK
        zero = jnp.zeros((size, 128), jnp.bfloat16)
        score[tile, head] = contract_last(jnp.where(lanes_of[head], q_pair[rows], zero), keys[:span])
        dprob[tile, head] = contract_last(jnp.where(lanes_of[head], do_pair[rows], zero), values[:span])
    for tile, head in work:
        rows = slice(tile * size, (tile + 1) * size)
        delta = jnp.sum(jnp.where(lanes_of[head], prod[rows], 0.0), axis=-1, keepdims=True)
        shift = lse_pair[rows, head * DH : head * DH + 1] + hide
        prob = jnp.exp2(score[tile, head] * C2 - shift)
        if own:
            diag = jnp.where(causal, prob[:, tile * size :], 0.0)
            prob = jnp.concatenate([prob[:, : tile * size], diag], axis=1) if tile else diag
        dlogit[tile, head] = (prob * (dprob[tile, head] - delta)).astype(jnp.bfloat16)
        prob_low[tile, head] = prob.astype(jnp.bfloat16)
    for tile in range(count):
        rows = slice(tile * size, (tile + 1) * size)
        span = (tile + 1) * size if own else BLK
        parts = [dot_dims(dlogit[tile, head], keys[:span], 1, 0) for head in range(2)]
        dq_acc[pl.ds(tile * size, size), lanes] = old_dq[rows] + jnp.where(lanes_of[0], parts[0], parts[1])
    for head in range(2):
        for offset, left_side, right_side, scale in (
            (0, q_turned, dlogit, ALPHA),
            (D, do_turned, prob_low, 1.0),
        ):
            spot = aligned(offset + pair * 128 + head * DH, DH)
            left_head = left_side[head * DH : (head + 1) * DH]
            terms = [
                dot_dims(left_head[:, tile * size : (tile + 1) * size], right_side[tile, head], 1, 0)
                for tile in range(count)
            ]
            for tile in range(count):
                cols = slice(tile * size, (tile + 1) * size)
                total = functools.reduce(
                    jnp.add, [terms[other][:, cols] for other in range(tile, count)]
                ) if own else terms[0]
                turned[spot, cols if own else slice(None)] = (total * scale).astype(jnp.bfloat16)


def backward_kernel(n_ctx, widths, *refs):
    slots = n_ctx // 2
    levels = n_ctx.bit_length() - 1
    depth = 14 if n_ctx == 4 else 10
    (slot_ref, gain_ref, norm_ref, x_hbm, q_hbm, kv_hbm, a_hbm, o_hbm, do_hbm, lse_hbm, w_hbm) = refs[:11]
    fresh = slots <= 2
    given = 5 if fresh else 3
    terms, outs = list(refs[11 : 11 + given]), refs[11 + given : 15 + given]
    grad_out, norm_out = refs[15 + given : 17 + given]
    scratch = list(refs[17 + given :])

    def take(count):
        taken = scratch[:count]
        del scratch[:count]
        return taken

    q_v, o_v, do_v, lse_v, weight, kv_b, a_b, dq_acc, turned, gkv, term, own_part, left, right, norm_v, norm_in = take(16)
    r1, r2, r3, fin, made = take(5)
    lhs, rhs = take(2) if fresh else (None, None)
    zbufs = take(levels)
    sem_in, sem_blk, sem_rhs, sem_lhs, sem_out, sem_res = take(6)
    send1, recv1, send2, recv2, send3, recv3, send6, recv6 = take(8)
    rs_send, rs_recv, ag_send, ag_recv = take(levels), take(levels), take(levels), take(levels)
    left_s, left_r, right_s, right_r, norm_s, norm_r = take(6)
    grp, ctx, wsh = lax.axis_index("grp"), lax.axis_index("ctx"), lax.axis_index("wsh")
    side, core = wsh // 2, wsh % 2
    core_peer = (grp, ctx, side * 2 + 1 - core)
    side_peer = (grp, ctx, (1 - side) * 2 + core)
    grp_peer = (1 - grp, ctx, wsh)
    next_ctx = (grp, lax.rem(ctx + 1, n_ctx), wsh)
    last_ctx = (grp, lax.rem(ctx + n_ctx - 1, n_ctx), wsh)
    bits = [(ctx // (1 << level)) % 2 for level in range(levels)]
    level_peers = [(grp, ctx + (1 - 2 * bits[level]) * (1 << level), wsh) for level in range(levels)]

    loads = [
        pltpu.make_async_copy(source, dest, sem_in.at[place])
        for place, (source, dest) in enumerate(
            ((q_hbm, q_v), (o_hbm, o_v), (do_hbm, do_v), (lse_hbm, lse_v), (w_hbm, weight))
        )
    ]
    for load in loads:
        load.start()

    def block_copies(index):
        rows = aligned(lax.rem(index, slots + 1) * BLK, BLK)
        slot = lax.rem(index, kv_b.shape[0])
        return (
            pltpu.make_async_copy(kv_hbm.at[rows, :], kv_b.at[slot], sem_blk.at[0, slot]),
            pltpu.make_async_copy(a_hbm.at[rows, :], a_b.at[slot], sem_blk.at[1, slot]),
        )

    for copy in block_copies(1):
        copy.start()

    barrier = pltpu.get_barrier_semaphore()
    peers = [core_peer, side_peer, grp_peer, next_ctx, last_ctx] + level_peers
    for peer in peers:
        pl.semaphore_signal(barrier, inc=1, device_id=peer, device_id_type=MESH)
    pl.semaphore_wait(barrier, len(peers))

    half = TILE // 2
    ranges, first = [], 0
    for rows, cols in widths:
        across = cols // TILE
        ranges.append((first, first + (rows // TILE) * across, across))
        first = ranges[-1][1]
    chunks = first

    def by_range(index, act):
        for place, (low, high, across) in enumerate(ranges):

            @pl.when((index >= low) & (index < high))
            def _(place=place, low=low, across=across):
                number = index - low
                act(place, (aligned((number // across) * TILE, TILE), aligned((number % across) * TILE, TILE)))

    def region(level, flip):
        row, rows, col, cols = 0, half, 0, TILE
        for place in range(level):
            bit = 1 - bits[place] if (flip and place == level - 1) else bits[place]
            if rows > 16:
                rows = rows // 2
                row = row + bit * rows
            else:
                cols = cols // 2
                col = col + bit * cols
        return row, rows, col, cols

    def spot(level, flip=False, base=0):
        row, rows, col, cols = region(level, flip)
        return aligned(base + row, rows), aligned(col, cols)

    last_low = ranges[-1][0]
    if fresh:
        set_of = [(0, number) for number in range(widths[0][0] // TILE)] + [(1, 0), (2, 0)]
        set_first = [number * ranges[0][2] for number in range(widths[0][0] // TILE)]
        set_first += [ranges[1][0], ranges[2][0]]
        g_hbm, dz_hbm, f_hbm, du_hbm, datt_hbm = terms
        left_of, right_of = (g_hbm, f_hbm, o_hbm), (dz_hbm, du_hbm, datt_hbm)

        def set_copies(number):
            place, group = set_of[number]
            stride = left_of[place].shape[1] // 4
            return [
                pltpu.make_async_copy(
                    left_of[place].at[:, pl.ds(owner * stride + group * TILE, TILE)],
                    lhs.at[number % 2, owner],
                    sem_lhs.at[number % 2, owner],
                )
                for owner in range(4)
            ]

    def step_fetch(index):
        near = lax.rem(index, 4)

        def act(place, span):
            if place == 3:
                return
            if fresh:
                pltpu.make_async_copy(
                    right_of[place].at[:, span[1]], rhs.at[near], sem_rhs.at[near]
                ).start()
            else:
                pltpu.make_async_copy(
                    terms[place].at[:, :, span[0], span[1]], made.at[near], sem_rhs.at[near]
                ).start()

        by_range(index, act)

    def step_make(index):
        slot = lax.rem(index, depth)
        near = lax.rem(index, 4)

        @pl.when(index < last_low)
        def _():
            if fresh:
                local_wait(rhs.at[near], sem_rhs.at[near])
                parity = jnp.int32(0)
                for number, low in enumerate(set_first):
                    parity = jnp.where(index >= low, number % 2, parity)

                    @pl.when(index == low)
                    def _(number=number):
                        for copy in set_copies(number):
                            copy.wait()
                        if number + 1 < len(set_first):
                            for copy in set_copies(number + 1):
                                copy.start()

                right_side = rhs[near]
                for owner in range(4):
                    made[near, owner // 2, owner % 2] = dot_dims(
                        lhs[parity, owner], right_side, 0, 0
                    ).astype(jnp.bfloat16)
            else:
                local_wait(made.at[near], sem_rhs.at[near])

        @pl.when(index >= last_low)
        def _():
            span = aligned((index - last_low) * TILE, TILE)
            made[near] = term[:, :, :, span]

        remote(
            made.at[near, :, 1 - core], r1.at[slot], send1.at[slot], recv1.at[slot], core_peer
        ).start()

    def finished(move):
        move.wait_send()
        move.wait_recv()

    def step_core(index):
        slot, near = lax.rem(index, depth), lax.rem(index, 4)
        finished(remote(r1.at[slot], r1.at[slot], send1.at[slot], recv1.at[slot], core_peer))
        r1[slot] = r1[slot] + made[near, :, core]
        remote(r1.at[slot, 1 - side], r2.at[slot], send2.at[slot], recv2.at[slot], side_peer).start()

    keep_half = aligned(grp * half, half)
    give_half = aligned((1 - grp) * half, half)

    def step_side(index):
        slot = lax.rem(index, depth)
        finished(remote(r1.at[slot, 1 - side], r2.at[slot], send2.at[slot], recv2.at[slot], side_peer))
        r2[slot] = r2[slot] + r1[slot, side]
        remote(r2.at[slot, give_half], r3.at[slot], send3.at[slot], recv3.at[slot], grp_peer).start()

    fold = n_ctx == 4
    if fold:
        outer = bits[0] == bits[1]
        inner = bits[0] != bits[1]
        mate, middle = level_peers[0], (grp, 3 - ctx, wsh)
        quarter = half // 2
        mine, other = aligned(bits[1] * quarter, quarter), aligned((1 - bits[1]) * quarter, quarter)
        fin_mine = aligned(grp * half + bits[1] * quarter, quarter)
        fin_other = aligned(grp * half + (1 - bits[1]) * quarter, quarter)

        def up_copy(slot):
            return remote(r3.at[slot], zbufs[0].at[slot], rs_send[0].at[slot], rs_recv[0].at[slot], mate)

        def cross_copy(slot):
            return remote(
                r3.at[slot, other], zbufs[1].at[slot], rs_send[1].at[slot], rs_recv[1].at[slot], middle
            )

        def share_copy(slot, rows):
            here = fin.at[slot, rows]
            return remote(here, here, ag_send[1].at[slot], ag_recv[1].at[slot], middle)

        def down_copy(slot):
            here = fin.at[slot, keep_half]
            return remote(here, here, ag_send[0].at[slot], ag_recv[0].at[slot], mate)

        def step_up(index):
            slot = lax.rem(index, depth)

            @pl.when(outer)
            def _():
                up_copy(slot).wait_send()

            @pl.when(inner)
            def _():
                up_copy(slot).wait_recv()
                r3[slot] = r3[slot] + zbufs[0][slot]
                cross_copy(slot).start()

        def step_cross(index):
            slot = lax.rem(index, depth)

            @pl.when(inner)
            def _():
                finished(cross_copy(slot))
                fin[slot, fin_mine] = r3[slot, mine] + zbufs[1][slot]
                share_copy(slot, fin_mine).start()

        def step_share(index):
            slot = lax.rem(index, depth)

            @pl.when(inner)
            def _():
                finished(share_copy(slot, fin_other))
                down_copy(slot).start()

        def step_down(index):
            slot = lax.rem(index, depth)

            @pl.when(inner)
            def _():
                down_copy(slot).wait_send()

            @pl.when(outer)
            def _():
                down_copy(slot).wait_recv()

            back_copy(slot, keep_half).start()

    def rs_copy(level, slot):
        rows, cols = spot(level + 1, True)
        return remote(
            r3.at[slot, rows, cols], zbufs[level].at[slot], rs_send[level].at[slot], rs_recv[level].at[slot], level_peers[level]
        )

    def ag_copy(level, slot, flip=False):
        rows, cols = spot(level + 1, flip, grp * half)
        here = fin.at[slot, rows, cols]
        return remote(here, here, ag_send[level].at[slot], ag_recv[level].at[slot], level_peers[level])

    def back_copy(slot, rows):
        here = fin.at[slot, rows]
        return remote(here, here, send6.at[slot], recv6.at[slot], grp_peer)

    def step_grp(index):
        slot = lax.rem(index, depth)
        finished(remote(r2.at[slot, give_half], r3.at[slot], send3.at[slot], recv3.at[slot], grp_peer))
        r3[slot] = r3[slot] + r2[slot, keep_half]
        if fold:

            @pl.when(outer)
            def _():
                up_copy(slot).start()
        else:
            rs_copy(0, slot).start()

    def step_scatter(level):
        def act(index):
            slot = lax.rem(index, depth)
            finished(rs_copy(level, slot))
            rows, cols = spot(level + 1)
            total = r3[slot, rows, cols] + zbufs[level][slot]
            if level + 1 < levels:
                r3[slot, rows, cols] = total
                rs_copy(level + 1, slot).start()
            else:
                rows, cols = spot(level + 1, False, grp * half)
                fin[slot, rows, cols] = total
                ag_copy(level, slot).start()

        return act

    def step_gather(level):
        def act(index):
            slot = lax.rem(index, depth)
            finished(ag_copy(level, slot, True))
            if level:
                ag_copy(level - 1, slot).start()
            else:
                back_copy(slot, keep_half).start()

        return act

    def out_wait(index):
        slot = lax.rem(index, depth)
        local_wait(fin.at[slot], sem_out.at[slot])

    def step_out(index):
        slot = lax.rem(index, depth)
        finished(back_copy(slot, give_half))

        def act(place, span):
            pltpu.make_async_copy(fin.at[slot], outs[place].at[span[0], span[1]], sem_out.at[slot]).start()

        by_range(index, act)

    z_lag = 2 if fold else 1
    order = [(YLAG, step_side), (XLAG, step_grp)]
    if fold:
        order += [(z_lag, act) for act in (step_up, step_cross, step_share, step_down)]
    else:
        order += [(z_lag, step_scatter(level)) for level in range(levels)]
        order += [(z_lag, step_gather(level)) for level in reversed(range(levels))]
    order += [(BLAG, step_out), (2, out_wait)]
    stages = [(0, step_core)]
    for lag, act in order:
        stages.append((stages[-1][0] + lag, act))
    all_ticks = chunks + stages[-1][0]

    per_slot = BLK // CHAIN
    chain_chunks = slots * per_slot

    def chain_step(stream, send, recv, number, is_first, is_last, target):
        slot = number // per_slot
        rows = aligned((number % per_slot) * CHAIN, CHAIN)
        here = stream.at[slot, rows]

        @pl.when(is_first)
        def _():
            stream[slot, rows, :] = own_part[slot, rows, :]

        @pl.when(jnp.logical_not(is_first))
        def _():
            remote(here, here, send.at[number], recv.at[number], target).wait_recv()
            stream[slot, rows, :] = stream[slot, rows, :] + own_part[slot, rows, :]

        @pl.when(jnp.logical_not(is_last))
        def _():
            remote(here, here, send.at[number], recv.at[number], target).start()

    def chain_tick(step):
        number = step - ctx

        @pl.when((number >= 0) & (number < chain_chunks))
        def _():
            chain_step(left, left_s, left_r, number, ctx == 0, ctx == n_ctx - 1, next_ctx)

        back = step - (n_ctx - 1 - ctx)

        @pl.when((back >= 0) & (back < chain_chunks))
        def _():
            chain_step(right, right_s, right_r, back, ctx == n_ctx - 1, ctx == 0, last_ctx)

    groups = PAIRS // PAIRED
    block_ticks = 2 * groups + 2
    chain_ticks = block_ticks + PACE * (chain_chunks + n_ctx - 1)

    def tick(step):
        @pl.when(step + 3 < chunks)
        def _():
            step_fetch(step + 3)

        @pl.when(step + 2 < chunks)
        def _():
            step_make(step + 2)

        for lag, act in stages:
            index = step - lag

            @pl.when((index >= 0) & (index < chunks))
            def _(act=act, index=index):
                act(index)

        beat = step - block_ticks

        @pl.when((beat >= 0) & (beat % PACE == 0))
        def _():
            chain_tick(beat // PACE)


    for index in range(3):
        step_fetch(jnp.int32(index))
    if fresh:
        for copy in set_copies(0):
            copy.start()
    for index in range(2):
        step_make(jnp.int32(index))
    dq_acc[...] = jnp.zeros_like(dq_acc)
    for load in loads:
        load.wait()

    def attend(kv_ref, own, visible, begin):
        def body(group, carry):
            for extra in range(2):
                tick(begin + 2 * group + extra)
            for member in range(PAIRED):
                grad_block(
                    q_v, do_v, o_v, lse_v, kv_ref, dq_acc, turned, group * PAIRED + member, own, visible
                )
            return carry

        lax.fori_loop(0, groups, body, 0)

    def each_slot(slot, carry):
        visible = slot < slot_ref[0]
        index = slot + 1
        place = lax.rem(index, kv_b.shape[0])
        for copy in block_copies(index):
            copy.wait()
        if kv_b.shape[0] > 1:
            for copy in block_copies(index + 1):
                copy.start()
        begin = slot * block_ticks
        attend(kv_b.at[place], False, visible, begin)

        def weight_terms(step, inner):
            tick(begin + 2 * groups + step)
            rows = aligned(step * 512, 512)
            for part in range(2):
                cols = pl.ds(part * D, D)
                product = dot_dims(a_b[place, :, rows], turned[cols, :], 0, 1)
                for down in range(2):
                    if fresh:
                        target = gkv.at[aligned(step * 512 + down * TILE, TILE), cols]
                    else:
                        target = term.at[step, down, :, pl.ds((part + 1) * D, D)]
                    piece = product[down * TILE : (down + 1) * TILE]

                    @pl.when(slot == 0)
                    def _(target=target, piece=piece):
                        target[...] = piece.astype(target.dtype)

                    @pl.when(slot > 0)
                    def _(target=target, piece=piece):
                        target[...] = (target[...] + piece).astype(target.dtype)

            own_part[slot, :, rows] = dot_dims(
                turned[...], weight[rows, pl.ds(D, 2 * D)], 0, 1
            ).astype(jnp.bfloat16)
            return inner

        lax.fori_loop(0, 2, weight_terms, 0)
        if kv_b.shape[0] == 1:
            for copy in block_copies(index + 1):
                copy.start()
        return carry

    lax.fori_loop(0, slots, each_slot, 0)
    begin = slots * block_ticks
    own_place = (slots + 1) % kv_b.shape[0]
    for copy in block_copies(slots + 1):
        copy.wait()
    attend(kv_b.at[own_place], True, None, begin)
    dq_low = o_v
    dq_low[...] = (dq_acc[...] * ALPHA).astype(jnp.bfloat16) * jnp.bfloat16(QSCALE)
    x_load = pltpu.make_async_copy(x_hbm, do_v, sem_in.at[0])
    x_load.start()

    def last_terms(step, carry):
        tick(begin + 2 * groups + step)
        rows = aligned(step * TILE, TILE)
        a_rows = a_b[own_place, :, rows]
        up, down = step // 2, step % 2
        term[up, down, :, pl.ds(0, D)] = dot_dims(a_rows, dq_low[...], 0, 0).astype(jnp.bfloat16)
        for part in range(2):
            cols = pl.ds(part * D, D)
            target = term.at[up, down, :, pl.ds((part + 1) * D, D)]
            earlier = gkv[rows, cols] if fresh else target[...]
            target[...] = (earlier + dot_dims(a_rows, turned[cols, :], 0, 1)).astype(jnp.bfloat16)
        return carry

    lax.fori_loop(0, 4, last_terms, 0)
    ready = begin + 2 * groups + 4
    assert ready <= ranges[-1][0] - 2 or n_ctx > 4
    da_acc = dq_acc

    def own_grad(step, carry):
        tick(ready + step)
        rows = aligned(step * TILE, TILE)
        da_acc[:, rows] = dot_dims(dq_low[...], weight[rows, pl.ds(0, D)], 1, 1) + dot_dims(
            turned[...], weight[rows, pl.ds(D, 2 * D)], 0, 1
        )
        return carry

    lax.fori_loop(0, 4, own_grad, 0)
    ready = ready + 4

    def flush_chain(step, carry):
        tick(ready + step)
        return carry

    left_over = max(0, chain_ticks - ready)
    lax.fori_loop(0, left_over, flush_chain, 0)
    ready = ready + left_over
    x_load.wait()
    gain = gain_ref[...]

    def norm_grad(step, carry):
        gain_sum, bias_sum = carry

        @pl.when(step % 2 == 0)
        def _():
            tick(ready + step // 2)

        rows = aligned(step * CHAIN, CHAIN)
        upstream = da_acc[rows, :]
        for slot in range(slots):
            joined = left[slot, rows, :].astype(jnp.float32) + right[slot, rows, :].astype(jnp.float32)
            upstream = upstream + jnp.where(slot_ref[0] == slot, joined, 0.0)
        values = do_v[rows, :].astype(jnp.float32)
        centre = values - jnp.mean(values, axis=-1, keepdims=True)
        scale = lax.rsqrt(jnp.mean(centre * centre, axis=-1, keepdims=True) + EPS)
        centre = centre * scale
        scaled = upstream * gain
        da_acc[rows, :] = scale * (
            scaled
            - jnp.mean(scaled, axis=-1, keepdims=True)
            - centre * jnp.mean(scaled * centre, axis=-1, keepdims=True)
        )
        gain_sum = gain_sum + jnp.sum(upstream * centre, axis=0, keepdims=True)
        bias_sum = bias_sum + jnp.sum(upstream, axis=0, keepdims=True)
        return gain_sum, bias_sum

    zero = jnp.zeros((1, D), jnp.float32)
    gain_sum, bias_sum = lax.fori_loop(0, BLK // CHAIN, norm_grad, (zero, zero))
    ready = ready + BLK // CHAIN // 2
    result = pltpu.make_async_copy(da_acc, grad_out, sem_res.at[0])
    result.start()
    row = lax.broadcasted_iota(jnp.int32, (8, D), 0)
    norm_v[...] = norm_ref[...] + jnp.where(row == 0, gain_sum, 0.0) + jnp.where(row == 4, bias_sum, 0.0)
    for place, peer in enumerate([core_peer, side_peer, grp_peer] + level_peers):
        move = remote(norm_v, norm_in.at[place], norm_s.at[place], norm_r.at[place], peer)
        move.start()
        tick(ready)
        tick(ready + 1)
        ready = ready + 2
        finished(move)
        norm_v[...] = norm_v[...] + norm_in[place]
    norm_result = pltpu.make_async_copy(norm_v, norm_out, sem_res.at[1])
    norm_result.start()
    if all_ticks > ready:
        lax.fori_loop(ready, all_ticks, lambda index, carry: (tick(index), carry)[1], 0)

    def drain_chain(index, carry):
        here = left.at[0, pl.ds(0, CHAIN)]

        @pl.when(ctx < n_ctx - 1)
        def _():
            remote(here, here, left_s.at[index], left_r.at[index], next_ctx).wait_send()

        @pl.when(ctx > 0)
        def _():
            remote(here, here, right_s.at[index], right_r.at[index], last_ctx).wait_send()

        return carry

    lax.fori_loop(0, chain_chunks, drain_chain, 0)
    result.wait()
    norm_result.wait()


def backward_part(n_ctx, slot_vec, gain, norms, raw, q, kv, a, o, do, lse, weight, pieces):
    slots = n_ctx // 2
    levels = n_ctx.bit_length() - 1
    depth = 14 if n_ctx == 4 else 10
    every = (slots + 1) * BLK
    if slots > 2:
        active, dz, ffn, du, datt = pieces
        terms = [
            contract_rows(left_side, right_side).astype(jnp.bfloat16)
            for left_side, right_side in ((active, dz), (ffn, du), (o, datt))
        ]
        widths = [(term.shape[0] // 4, term.shape[1]) for term in terms]
        pieces = [term.reshape(2, 2, width[0], width[1]) for term, width in zip(terms, widths)]
    else:
        widths = [(pieces[0].shape[1] // 4, D), (D // 4, pieces[3].shape[1]), (D // 4, D)]
    widths = widths + [(D // 4, 3 * D)]
    low, full = jnp.bfloat16, jnp.float32
    dma = pltpu.SemaphoreType.DMA
    hbm = pl.BlockSpec(memory_space=pl.ANY)
    vmem = pl.BlockSpec(memory_space=pltpu.VMEM)
    shape = jax.ShapeDtypeStruct
    buffers = 2 if slots <= 2 else 1
    chain = slots * (BLK // CHAIN)
    zshapes, rows, cols = [], TILE // 2, TILE
    if n_ctx == 4:
        zshapes = [pltpu.VMEM((depth, rows, cols), low), pltpu.VMEM((depth, rows // 2, cols), low)]
    for _ in range(0 if zshapes else levels):
        rows, cols = (rows // 2, cols) if rows > 16 else (rows, cols // 2)
        zshapes.append(pltpu.VMEM((depth, rows, cols), low))
    return pl.pallas_call(
        functools.partial(backward_kernel, n_ctx, widths),
        out_shape=[shape(width, low) for width in widths] + [shape((BLK, D), full), shape((8, D), full)],
        in_specs=[pl.BlockSpec(memory_space=pltpu.SMEM), vmem, vmem] + [hbm] * (8 + len(pieces)),
        out_specs=[hbm] * 6,
        scratch_shapes=[
            pltpu.VMEM((BLK, D), low),
            pltpu.VMEM((BLK, D), low),
            pltpu.VMEM((BLK, D), low),
            pltpu.VMEM((PAIRS, BLK, 128), full),
            pltpu.VMEM((D, 3 * D), low),
            pltpu.VMEM((buffers, BLK, 2 * D), low),
            pltpu.VMEM((buffers, BLK, D), low),
            pltpu.VMEM((BLK, D), full),
            pltpu.VMEM((2 * D, BLK), low),
            pltpu.VMEM((D, 2 * D) if slots <= 2 else (8, 128), full),
            pltpu.VMEM((2, 2, D // 4, 3 * D), low),
            pltpu.VMEM((slots, BLK, D), low),
            pltpu.VMEM((slots, BLK, D), low),
            pltpu.VMEM((slots, BLK, D), low),
            pltpu.VMEM((8, D), full),
            pltpu.VMEM((3 + levels, 8, D), full),
            pltpu.VMEM((depth, 2, TILE, TILE), low),
            pltpu.VMEM((depth, TILE, TILE), low),
            pltpu.VMEM((depth, TILE // 2, TILE), low),
            pltpu.VMEM((depth, TILE, TILE), low),
            pltpu.VMEM((4, 2, 2, TILE, TILE), low),
        ]
        + ([pltpu.VMEM((2, 4, BLK, TILE), low), pltpu.VMEM((4, BLK, TILE), low)] if slots <= 2 else [])
        + zshapes
        + [dma((5,)), dma((2, buffers)), dma((4,)), dma((2, 4)), dma((depth,)), dma((2,))]
        + [dma((depth,))] * (8 + 4 * levels)
        + [dma((chain,))] * 4
        + [dma((3 + levels,))] * 2,
        compiler_params=pltpu.CompilerParams(
            collective_id=2, has_side_effects=True, vmem_limit_bytes=67043328
        ),
        cost_estimate=pl.CostEstimate(flops=40 << 30, bytes_accessed=64 << 20, transcendentals=1 << 24),
        name="attend_back_reduce",
    )(
        slot_vec,
        gain,
        norms,
        raw,
        q,
        kv,
        a,
        o,
        do,
        lse,
        weight,
        *pieces,
    )


def per_device(n_ctx, inputs, w_qkv, w_out, w_up, w_down, norm_gains, norm_biases, block_map, out_grad):
    slots = n_ctx // 2
    raw = inputs.reshape(BLK, D)
    tokens = raw.astype(jnp.float32)
    block_entry = block_map.reshape(2)
    own_slot = block_entry[1] // BLK
    own_tag = jnp.where(block_entry[0] == 0, own_slot, n_ctx)
    slot_vec = own_slot.reshape(1)
    every_low, queries, keys_values, attn_low, lse, full_qkv, full_out, full_up, full_down = forward_part(
        n_ctx,
        jnp.stack([own_slot, own_tag]),
        norm_gains[0:1],
        norm_biases[0:1],
        raw,
        w_qkv,
        w_out,
        w_up,
        w_down,
    )

    branch = jnp.dot(attn_low, full_out, preferred_element_type=jnp.float32)
    post_attn, attn_back = jax.vjp(layer_norm, branch, norm_gains[1], norm_biases[1])
    hidden = tokens + post_attn
    pre_ffn, ffn_back = jax.vjp(layer_norm, hidden, norm_gains[2], norm_biases[2])
    ffn_low = pre_ffn.astype(jnp.bfloat16)
    upward = jnp.dot(ffn_low, full_up, preferred_element_type=jnp.float32)
    activated, gelu_back = jax.vjp(gelu_tanh, upward)
    active_low = activated.astype(jnp.bfloat16)
    downward = jnp.dot(active_low, full_down, preferred_element_type=jnp.float32)
    post_ffn, post_back = jax.vjp(layer_norm, downward, norm_gains[3], norm_biases[3])
    result = (hidden + post_ffn).astype(jnp.bfloat16).reshape(1, 1, BLK, D)
    seed_grad = out_grad.reshape(BLK, D).astype(jnp.float32)
    grad_down_in, gain_grad3, bias_grad3 = post_back(seed_grad)
    down_low = grad_down_in.astype(jnp.bfloat16)
    grad_active = contract_last(down_low, full_down)
    up_low = gelu_back(grad_active)[0].astype(jnp.bfloat16)
    grad_pre_ffn, gain_grad2, bias_grad2 = ffn_back(contract_last(up_low, full_up))
    grad_hidden = seed_grad + grad_pre_ffn
    grad_branch, gain_grad1, bias_grad1 = attn_back(grad_hidden)
    branch_low = grad_branch.astype(jnp.bfloat16)
    grad_out_low = contract_last(branch_low, full_out).astype(jnp.bfloat16)

    zero_row = jnp.zeros((D,), jnp.float32)
    norms = jnp.stack(
        [zero_row, gain_grad1, gain_grad2, gain_grad3, zero_row, bias_grad1, bias_grad2, bias_grad3]
    )
    summed_down, summed_up, summed_out, summed_qkv, grad_tokens, norm_total = backward_part(
        n_ctx,
        slot_vec,
        norm_gains[0:1],
        norms,
        raw,
        queries,
        keys_values,
        every_low,
        attn_low,
        grad_out_low,
        lse,
        full_qkv,
        [active_low, down_low, ffn_low, up_low, branch_low],
    )
    grad_input = (grad_hidden + grad_tokens).reshape(1, 1, BLK, D)
    summed_down, summed_up, summed_out, summed_qkv = (
        total.astype(jnp.float32) for total in (summed_down, summed_up, summed_out, summed_qkv)
    )
    gain_total, bias_total = norm_total[:4], norm_total[4:]
    return (
        result,
        grad_input,
        summed_qkv,
        summed_out,
        summed_up,
        summed_down,
        gain_total,
        bias_total,
    )


def solution(mesh):
    rows = P("wsh", None)
    blocks = P("grp", "wsh", "ctx", None)
    return jax.shard_map(
        functools.partial(per_device, mesh.shape["ctx"]),
        mesh=mesh,
        in_specs=(blocks, rows, rows, rows, rows, P(), P(), blocks, blocks),
        out_specs=(blocks, blocks, rows, rows, rows, rows, P(), P()),
        check_vma=False,
    )
```

```python
import functools
import math

import jax
import jax.numpy as jnp
from jax import lax
from jax.experimental import pallas as pl
from jax.experimental.pallas import tpu as pltpu
from jax.sharding import PartitionSpec as P

D = 1024
HEADS = 16
DH = 64
BLK = 512
PAIRS = HEADS // 2
QT = 256

EPS = 1e-05
ALPHA = 32.0
NEG = -1e30
LOG2E = 1.4426950408889634
C2 = ALPHA * LOG2E
MESH = pl.DeviceIdType.MESH
QSCALE = 1.0 / (ALPHA * math.sqrt(DH))


def layer_norm(values, gain_row, bias_row):
    centre = values - jnp.mean(values, axis=-1, keepdims=True)
    spread = jnp.mean(centre * centre, axis=-1, keepdims=True)
    return centre * lax.rsqrt(spread + EPS) * gain_row + bias_row


def gelu_tanh(values):
    return jax.nn.gelu(values, approximate=True)


def dot_dims(left_side, right_side, left_dim, right_dim):
    return lax.dot_general(
        left_side,
        right_side,
        (((left_dim,), (right_dim,)), ((), ())),
        preferred_element_type=jnp.float32,
    )


def contract_last(left_side, right_side):
    return dot_dims(left_side, right_side, 1, 1)


def contract_rows(left_side, right_side):
    return dot_dims(left_side, right_side, 0, 0)


def head_lanes(head, rows):
    lane = lax.broadcasted_iota(jnp.int32, (rows, 128), 1)
    return (lane >= DH) if head else (lane < DH)


def causal_tile():
    row = lax.broadcasted_iota(jnp.int32, (QT, QT), 0)
    col = lax.broadcasted_iota(jnp.int32, (QT, QT), 1)
    return col <= row


PIECE = 128
SPAN = 512
CHAIN = 64
HOP = 2
YLAG = 2
XLAG = 2
BLAG = 2
FF_TICKS = 13
GELU_A = 0.044715
GELU_C = math.sqrt(2.0 / math.pi)
PACE = 2
LAG = 2
GROUP = 4
AHEAD = 4


def remote(src, dst, send, recv, peer):
    return pltpu.make_async_remote_copy(
        src_ref=src, dst_ref=dst, send_sem=send, recv_sem=recv, device_id=peer, device_id_type=MESH
    )


def local_wait(ref, sem):
    pltpu.make_async_copy(ref, ref, sem).wait()


def aligned(start, size):
    return pl.ds(pl.multiple_of(start, size), size)


def softmax_block(q_ref, kv_ref, acc, top_ref, sum_ref, pair, base, own, visible):
    lanes = aligned(pair * 128, 128)
    value_lanes = aligned(D + pair * 128, 128)
    causal = causal_tile()
    first = head_lanes(0, QT)
    count = BLK // QT
    q_pair = q_ref[:, lanes]
    keys = kv_ref[pl.ds(base, BLK), lanes]
    values = kv_ref[pl.ds(base, BLK), value_lanes]
    if not own:
        old_top, old_sum, old_out = top_ref[pair], sum_ref[pair], acc[:, lanes]
        hide = jnp.where(visible, 0.0, 1e30)
    results = []
    work = [(tile, head) for tile in range(count) for head in range(2)]
    parts_of = {}
    for tile, head in work:
        q_tile = q_pair[tile * QT : (tile + 1) * QT]
        q_head = jnp.where(head_lanes(head, QT), q_tile, jnp.zeros_like(q_tile))
        span = (tile + 1) * QT if own else BLK
        parts_of[tile, head] = contract_last(q_head, keys[:span])
    top_of, expo_of, total_of = {}, {}, {}
    for tile, head in work:
        part = parts_of[tile, head]
        if own:
            diag = jnp.where(causal, part[:, tile * QT :], NEG)
            part = jnp.concatenate([part[:, : tile * QT], diag], axis=1) if tile else diag
        top = jnp.max(part, axis=-1, keepdims=True) * C2
        if own:
            shift = top
        else:
            top = jnp.maximum(
                jnp.where(visible, top, NEG), old_top[tile * QT : (tile + 1) * QT, head * DH : head * DH + 1]
            )
            shift = top + hide
        expo = jnp.exp2(part * C2 - shift)
        top_of[tile, head] = jnp.broadcast_to(top, (QT, 128))
        total_of[tile, head] = jnp.broadcast_to(jnp.sum(expo, axis=-1, keepdims=True), (QT, 128))
        expo_of[tile, head] = expo.astype(jnp.bfloat16)
    out_of = {}
    for tile, head in work:
        span = (tile + 1) * QT if own else BLK
        out_of[tile, head] = dot_dims(expo_of[tile, head], values[:span], 1, 0)
    for tile in range(count):
        rows = pl.ds(tile * QT, QT)
        new_top = jnp.where(first, top_of[tile, 0], top_of[tile, 1])
        new_sum = jnp.where(first, total_of[tile, 0], total_of[tile, 1])
        new_out = jnp.where(first, out_of[tile, 0], out_of[tile, 1])
        if not own:
            here = slice(tile * QT, (tile + 1) * QT)
            keep = jnp.exp2(old_top[here] - new_top)
            new_sum = new_sum + old_sum[here] * keep
            new_out = new_out + old_out[here] * keep
        top_ref[pair, rows, :] = new_top
        sum_ref[pair, rows, :] = new_sum
        acc[rows, lanes] = new_out


def forward_kernel(n_ctx, *refs):
    slots = n_ctx // 2
    (slot_ref, gain_ref, bias_ref, x_hbm, w_qkv, w_out, w_up, w_down) = refs[:8]
    (a_out, q_out, kv_out, o_out, lse_out, full_qkv, full_out, full_up, full_down) = refs[8:17]
    (x_own, left, right, a_all, q_all, kv_all, weight, acc, tops, sums, hop) = refs[17:28]
    (sem_in, sem_load, sem_store, sem_out, sem_a, sem_kv, side_s, side_r, grp_s, grp_r, cs_s, cs_r, cg_s, cg_r, own_s, own_r, left_s, left_r, right_s, right_r) = refs[28:]
    grp, ctx, wsh = lax.axis_index("grp"), lax.axis_index("ctx"), lax.axis_index("wsh")
    side, core = wsh // 2, wsh % 2
    core_peer = (grp, ctx, side * 2 + 1 - core)
    side_peer = (grp, ctx, (1 - side) * 2 + core)
    grp_peer = (1 - grp, ctx, wsh)
    next_ctx = (grp, lax.rem(ctx + 1, n_ctx), wsh)
    last_ctx = (grp, lax.rem(ctx + n_ctx - 1, n_ctx), wsh)

    load = pltpu.make_async_copy(x_hbm, x_own, sem_in.at[0])
    load.start()
    barrier = pltpu.get_barrier_semaphore()
    for peer in (core_peer, side_peer, grp_peer, next_ctx, last_ctx):
        pl.semaphore_signal(barrier, inc=1, device_id=peer, device_id_type=MESH)
    pl.semaphore_wait(barrier, 5)

    shards = (w_qkv, w_out, w_up, w_down)
    fulls = (weight, full_out, full_up, full_down)
    ranges, start = [], 0
    for shard in shards:
        across = shard.shape[1] // SPAN
        ranges.append((start, start + across * (shard.shape[0] // (2 * PIECE)), across))
        start = ranges[-1][1]
    pieces = start

    def by_range(index, act):
        for place, (low, high, across) in enumerate(ranges):

            @pl.when((index >= low) & (index < high))
            def _(place=place, low=low, across=across):
                act(place, (index - low) // across, aligned(((index - low) % across) * SPAN, SPAN))

    def rows_of(place, owner, half, group):
        shard_rows = shards[place].shape[0]
        return aligned(owner * shard_rows + half * (shard_rows // 2) + group * PIECE, PIECE)

    sides_owner = (1 - side) * 2 + core

    def send_piece(index, carry):
        def act(place, group, cols):
            remote(
                shards[place].at[rows_of(place, 0, grp, group), cols],
                fulls[place].at[rows_of(place, wsh, grp, group), cols],
                side_s.at[index],
                side_r.at[index],
                side_peer,
            ).start()

        by_range(index, act)
        return carry

    def own_copies():
        copies = []
        across = shards[0].shape[1] // SPAN
        for place in range(4):
            shard_rows = shards[place].shape[0]
            mine = aligned(wsh * shard_rows, shard_rows)
            steps = range(across) if place == 0 else [None]
            for step in steps:
                cols = slice(None) if step is None else pl.ds(step * SPAN, SPAN)
                number = len(copies)
                copies.append(
                    remote(
                        shards[place].at[:, cols],
                        fulls[place].at[mine, cols],
                        own_s.at[number],
                        own_r.at[number],
                        core_peer,
                    )
                )
        return copies

    for index in range(AHEAD):
        send_piece(index, 0)
    for copy in own_copies():
        copy.start()
    own_rows = aligned(wsh * w_qkv.shape[0], w_qkv.shape[0])
    own_weight = pltpu.make_async_copy(w_qkv, weight.at[own_rows, :], sem_in.at[1])
    own_weight.start()
    load.wait()

    bounces, start = [], 0
    for shard in shards[1:]:
        across = shard.shape[1] // SPAN
        bounces.append((start, start + across * (shard.shape[0] // (2 * PIECE)), across))
        start = bounces[-1][1]
    moves = start

    def bounce(index, loading):
        slot = lax.rem(index, 3)
        for place, (low, high, across) in enumerate(bounces):

            @pl.when((index >= low) & (index < high))
            def _(place=place + 1, low=low, across=across):
                group = (index - low) // across
                cols = aligned(((index - low) % across) * SPAN, SPAN)
                if loading:
                    here = shards[place].at[aligned(group * 2 * PIECE, 2 * PIECE), cols]
                    pltpu.make_async_copy(here, hop.at[slot], sem_load.at[slot]).start()
                else:
                    rows = aligned(wsh * shards[place].shape[0] + group * 2 * PIECE, 2 * PIECE)
                    local_wait(hop.at[slot], sem_load.at[slot])
                    pltpu.make_async_copy(
                        hop.at[slot], fulls[place].at[rows, cols], sem_store.at[slot]
                    ).start()

    own_tag = slot_ref[1]
    chain_chunks = slots * (BLK // CHAIN)

    def chain_step(stream, send, recv, number, is_first, is_last, target):
        slot = number // (BLK // CHAIN)
        spot = aligned((number % (BLK // CHAIN)) * CHAIN, CHAIN)
        mine = jnp.where(own_tag == slot, x_own[spot, :], jnp.zeros((CHAIN, D), jnp.bfloat16))
        here = stream.at[slot, spot]

        @pl.when(is_first)
        def _():
            stream[slot, spot, :] = mine

        @pl.when(jnp.logical_not(is_first))
        def _():
            remote(here, here, send.at[number], recv.at[number], target).wait_recv()
            stream[slot, spot, :] = stream[slot, spot, :] + mine

        @pl.when(jnp.logical_not(is_last))
        def _():
            remote(here, here, send.at[number], recv.at[number], target).start()

    def tick(step):
        @pl.when((step >= 1) & (step <= moves))
        def _():
            bounce(step - 1, False)

        @pl.when((step >= 3) & (step < moves))
        def _():
            local_wait(hop.at[lax.rem(step, 3)], sem_store.at[lax.rem(step, 3)])

        @pl.when(step < moves)
        def _():
            bounce(step, True)

        @pl.when(step + AHEAD < pieces)
        def _():
            send_piece(step + AHEAD, 0)

        number = step - HOP * ctx

        @pl.when((number >= 0) & (number < chain_chunks))
        def _():
            chain_step(left, left_s, left_r, number, ctx == 0, ctx == n_ctx - 1, next_ctx)

        back = step - HOP * (n_ctx - 1 - ctx)

        @pl.when((back >= 0) & (back < chain_chunks))
        def _():
            chain_step(right, right_s, right_r, back, ctx == n_ctx - 1, ctx == 0, last_ctx)

        @pl.when(step < pieces)
        def _():
            def act(place, group, cols):
                here = fulls[place].at[rows_of(place, sides_owner, grp, group), cols]
                remote(here, here, side_s.at[step], side_r.at[step], side_peer).wait_recv()
                remote(here, here, grp_s.at[step], grp_r.at[step], grp_peer).start()
                remote(here, here, cs_s.at[step], cs_r.at[step], core_peer).start()

            by_range(step, act)

        late = step - LAG

        @pl.when((late >= 0) & (late < pieces))
        def _():
            def act(place, group, cols):
                here = fulls[place].at[rows_of(place, sides_owner, 1 - grp, group), cols]
                remote(here, here, grp_s.at[late], grp_r.at[late], grp_peer).wait_recv()
                remote(here, here, cg_s.at[late], cg_r.at[late], core_peer).start()

            by_range(late, act)

    def normalise(source, dest):
        gain, bias = gain_ref[...], bias_ref[...]

        def body(index, carry):
            rows = aligned(index * 128, 128)
            values = source(rows).astype(jnp.float32)
            a_all[aligned(dest + index * 128, 128), :] = layer_norm(values, gain, bias).astype(
                jnp.bfloat16
            )
            return carry

        lax.fori_loop(0, BLK // 128, body, 0)

    def piece_ready(index):
        here = fulls[0].at[pl.ds(0, PIECE), pl.ds(0, SPAN)]
        remote(here, here, cs_s.at[index], cs_r.at[index], core_peer).wait_recv()
        remote(here, here, cg_s.at[index], cg_r.at[index], core_peer).wait_recv()
        whole = fulls[0].at[pl.ds(0, 2 * PIECE), pl.ds(0, SPAN)]
        remote(whole, whole, own_s.at[index], own_r.at[index], core_peer).wait_recv()

    tick(0)
    normalise(lambda rows: x_own[rows, :], 0)
    for step in range(1, LAG + 1):
        tick(step)
    own_weight.wait()

    def project_q(index, carry):
        tick(index + LAG + 1)
        piece_ready(index)
        cols = aligned(index * SPAN, SPAN)
        q_all[:, cols] = (
            jnp.dot(a_all[pl.ds(0, BLK), :], weight[:, cols], preferred_element_type=jnp.float32) * QSCALE
        ).astype(jnp.bfloat16)
        return carry

    lax.fori_loop(0, D // SPAN, project_q, 0)
    head_ticks = LAG + 1 + D // SPAN

    def project_kv(index, base):
        cols = aligned(index * SPAN, SPAN)
        rows = aligned(base, BLK)
        kv_all[rows, cols] = jnp.dot(
            a_all[rows, :], weight[:, aligned(D + index * SPAN, SPAN)], preferred_element_type=jnp.float32
        ).astype(jnp.bfloat16)

    def own_kv(index, carry):
        tick(index + head_ticks)
        piece_ready(index + D // SPAN)
        project_kv(index, 0)
        return carry

    lax.fori_loop(0, 2 * D // SPAN, own_kv, 0)
    own_ticks = head_ticks + 2 * D // SPAN

    def send_block(index):
        rows = aligned(index * BLK, BLK)
        pltpu.make_async_copy(a_all.at[rows, :], a_out.at[rows, :], sem_a.at[index]).start()
        pltpu.make_async_copy(kv_all.at[rows, :], kv_out.at[rows, :], sem_kv.at[index]).start()

    outputs = [
        pltpu.make_async_copy(weight, full_qkv, sem_out.at[0]),
        pltpu.make_async_copy(q_all, q_out, sem_out.at[1]),
    ]
    for copy in outputs:
        copy.start()

    send_block(0)

    def own_attention(group, carry):
        tick(own_ticks + 2 * group)
        tick(own_ticks + 2 * group + 1)
        for member in range(GROUP):
            softmax_block(q_all, kv_all, acc, tops, sums, group * GROUP + member, 0, True, None)
        return carry

    groups = PAIRS // GROUP
    lax.fori_loop(0, groups, own_attention, 0)
    used = own_ticks + 2 * groups
    per_slot = 2 * D // SPAN + 2 * groups

    need = BLK // CHAIN + HOP * (n_ctx - 1)
    early = max(0, need - used)
    if early:
        lax.fori_loop(0, early, lambda index, carry: (tick(used + index), carry)[1], 0)

    def each_slot(slot, carry):
        base = pl.multiple_of((slot + 1) * BLK, BLK)
        visible = slot < slot_ref[0]
        begin = early + used + slot * per_slot

        def total(rows):
            joined = left[slot, rows, :] + right[slot, rows, :]
            return jnp.where(own_tag == slot, x_own[rows, :], joined)

        normalise(total, base)

        def slot_kv(index, inner):
            tick(begin + index)
            project_kv(index, base)
            return inner

        lax.fori_loop(0, 2 * D // SPAN, slot_kv, 0)

        send_block(slot + 1)

        def slot_attention(group, inner):
            tick(begin + 2 * D // SPAN + 2 * group)
            tick(begin + 2 * D // SPAN + 2 * group + 1)
            for member in range(GROUP):
                softmax_block(
                    q_all, kv_all, acc, tops, sums, group * GROUP + member, base, False, visible
                )
            return inner

        lax.fori_loop(0, groups, slot_attention, 0)
        return carry

    lax.fori_loop(0, slots, each_slot, 0)
    done_ticks = early + used + slots * per_slot

    def finish(pair, carry):
        lanes = aligned(pair * 128, 128)
        x_own[:, lanes] = (acc[:, lanes] / sums[pair]).astype(jnp.bfloat16)
        tops[pair] = tops[pair] + jnp.log2(sums[pair])
        return carry

    lax.fori_loop(0, PAIRS, finish, 0)
    outputs += [
        pltpu.make_async_copy(x_own, o_out, sem_out.at[2]),
        pltpu.make_async_copy(tops, lse_out, sem_out.at[3]),
    ]
    for copy in outputs[2:]:
        copy.start()
    all_ticks = max(pieces + LAG, chain_chunks + HOP * (n_ctx - 1))
    if all_ticks > done_ticks:
        lax.fori_loop(done_ticks, all_ticks, lambda index, carry: (tick(index), carry)[1], 0)

    def drain(index, carry):
        here = fulls[0].at[pl.ds(0, PIECE), pl.ds(0, SPAN)]

        @pl.when(index >= ranges[0][1])
        def _():
            remote(here, here, cs_s.at[index], cs_r.at[index], core_peer).wait_recv()
            remote(here, here, cg_s.at[index], cg_r.at[index], core_peer).wait_recv()

        remote(here, here, side_s.at[index], side_r.at[index], side_peer).wait_send()
        remote(here, here, grp_s.at[index], grp_r.at[index], grp_peer).wait_send()
        remote(here, here, cs_s.at[index], cs_r.at[index], core_peer).wait_send()
        remote(here, here, cg_s.at[index], cg_r.at[index], core_peer).wait_send()
        return carry

    lax.fori_loop(0, pieces, drain, 0)
    copies = own_copies()
    for number, copy in enumerate(copies):
        copy.wait_send()
        if number >= len(copies) - 3:
            copy.wait_recv()
    for index in range(moves - 3, moves):
        local_wait(hop.at[index % 3], sem_store.at[index % 3])

    def drain_chain(index, carry):
        here = left.at[0, pl.ds(0, CHAIN)]

        @pl.when(ctx < n_ctx - 1)
        def _():
            remote(here, here, left_s.at[index], left_r.at[index], next_ctx).wait_send()

        @pl.when(ctx > 0)
        def _():
            remote(here, here, right_s.at[index], right_r.at[index], last_ctx).wait_send()

        return carry

    lax.fori_loop(0, chain_chunks, drain_chain, 0)
    for copy in outputs:
        copy.wait()

    def drain_blocks(index, carry):
        rows = aligned(index * BLK, BLK)
        local_wait(a_all.at[rows, :], sem_a.at[index])
        local_wait(kv_all.at[rows, :], sem_kv.at[index])
        return carry

    lax.fori_loop(0, slots + 1, drain_blocks, 0)


def forward_part(n_ctx, tags, gain, bias, raw, w_qkv, w_out, w_up, w_down):
    slots = n_ctx // 2
    every = (slots + 1) * BLK
    low, full = jnp.bfloat16, jnp.float32
    dma = pltpu.SemaphoreType.DMA
    hbm = pl.BlockSpec(memory_space=pl.ANY)
    vmem = pl.BlockSpec(memory_space=pltpu.VMEM)
    shards = (w_qkv, w_out, w_up, w_down)
    pieces = sum(w.shape[0] * w.shape[1] // (2 * PIECE * SPAN) for w in shards)
    own = w_qkv.shape[1] // SPAN + 3
    chain = slots * (BLK // CHAIN)
    shape = jax.ShapeDtypeStruct
    return pl.pallas_call(
        functools.partial(forward_kernel, n_ctx),
        out_shape=[
            shape((every, D), low),
            shape((BLK, D), low),
            shape((every, 2 * D), low),
            shape((BLK, D), low),
            shape((PAIRS, BLK, 128), full),
        ]
        + [shape((4 * w.shape[0], w.shape[1]), low) for w in shards],
        in_specs=[pl.BlockSpec(memory_space=pltpu.SMEM), vmem, vmem] + [hbm] * 5,
        out_specs=[hbm] * 9,
        scratch_shapes=[
            pltpu.VMEM((BLK, D), low),
            pltpu.VMEM((slots, BLK, D), low),
            pltpu.VMEM((slots, BLK, D), low),
            pltpu.VMEM((every, D), low),
            pltpu.VMEM((BLK, D), low),
            pltpu.VMEM((every, 2 * D), low),
            pltpu.VMEM((D, 3 * D), low),
            pltpu.VMEM((BLK, D), full),
            pltpu.VMEM((PAIRS, BLK, 128), full),
            pltpu.VMEM((PAIRS, BLK, 128), full),
            pltpu.VMEM((3, 2 * PIECE, SPAN), low),
            dma((2,)),
            dma((3,)),
            dma((3,)),
            dma((4,)),
            dma((slots + 1,)),
            dma((slots + 1,)),
        ]
        + [dma((pieces,))] * 8
        + [dma((own,))] * 2
        + [dma((chain,))] * 4,
        compiler_params=pltpu.CompilerParams(
            collective_id=1, has_side_effects=True, vmem_limit_bytes=63 << 20
        ),
        cost_estimate=pl.CostEstimate(flops=20 << 30, bytes_accessed=64 << 20, transcendentals=1 << 24),
        name="gather_attend",
    )(tags, gain, bias, raw, *shards)


TILE = 256
PAIRED = 2


def grad_block(q_ref, do_ref, o_ref, lse_ref, kv_ref, dq_acc, turned, pair, own, visible):
    lanes = aligned(pair * 128, 128)
    value_lanes = aligned(D + pair * 128, 128)
    size = QT if own else BLK
    count = BLK // size
    q_pair, do_pair, lse_pair = q_ref[:, lanes], do_ref[:, lanes], lse_ref[pair]
    prod = do_pair.astype(jnp.float32) * o_ref[:, lanes].astype(jnp.float32)
    keys, values = kv_ref[:, lanes], kv_ref[:, value_lanes]
    q_turned, do_turned = q_pair.T, do_pair.T
    old_dq = dq_acc[:, lanes]
    causal = causal_tile()
    hide = 0.0 if own else jnp.where(visible, 0.0, 1e30)
    lanes_of = [head_lanes(head, size) for head in range(2)]
    work = [(tile, head) for tile in range(count) for head in range(2)]
    score, dprob, dlogit, prob_low = {}, {}, {}, {}
    for tile, head in work:
        rows = slice(tile * size, (tile + 1) * size)
        span = (tile + 1) * size if own else BLK
        zero = jnp.zeros((size, 128), jnp.bfloat16)
        score[tile, head] = contract_last(jnp.where(lanes_of[head], q_pair[rows], zero), keys[:span])
        dprob[tile, head] = contract_last(jnp.where(lanes_of[head], do_pair[rows], zero), values[:span])
    for tile, head in work:
        rows = slice(tile * size, (tile + 1) * size)
        delta = jnp.sum(jnp.where(lanes_of[head], prod[rows], 0.0), axis=-1, keepdims=True)
        shift = lse_pair[rows, head * DH : head * DH + 1] + hide
        prob = jnp.exp2(score[tile, head] * C2 - shift)
        if own:
            diag = jnp.where(causal, prob[:, tile * size :], 0.0)
            prob = jnp.concatenate([prob[:, : tile * size], diag], axis=1) if tile else diag
        dlogit[tile, head] = (prob * (dprob[tile, head] - delta)).astype(jnp.bfloat16)
        prob_low[tile, head] = prob.astype(jnp.bfloat16)
    for tile in range(count):
        rows = slice(tile * size, (tile + 1) * size)
        span = (tile + 1) * size if own else BLK
        parts = [dot_dims(dlogit[tile, head], keys[:span], 1, 0) for head in range(2)]
        dq_acc[pl.ds(tile * size, size), lanes] = old_dq[rows] + jnp.where(lanes_of[0], parts[0], parts[1])
    for head in range(2):
        for offset, left_side, right_side, scale in (
            (0, q_turned, dlogit, ALPHA),
            (D, do_turned, prob_low, 1.0),
        ):
            spot = aligned(offset + pair * 128 + head * DH, DH)
            left_head = left_side[head * DH : (head + 1) * DH]
            terms = [
                dot_dims(left_head[:, tile * size : (tile + 1) * size], right_side[tile, head], 1, 0)
                for tile in range(count)
            ]
            for tile in range(count):
                cols = slice(tile * size, (tile + 1) * size)
                total = functools.reduce(
                    jnp.add, [terms[other][:, cols] for other in range(tile, count)]
                ) if own else terms[0]
                turned[spot, cols if own else slice(None)] = (total * scale).astype(jnp.bfloat16)


def backward_kernel(n_ctx, widths, *refs):
    slots = n_ctx // 2
    levels = n_ctx.bit_length() - 1
    depth = 14 if n_ctx == 4 else 10
    shallow = slots <= 2
    (slot_ref, gain_ref, norm_ref, x_hbm, q_hbm, kv_hbm, a_hbm, o_hbm, lse_hbm, w_hbm) = refs[:10]
    (w_out, w_up, w_down, g_hbm, dz_hbm, f_hbm, u_hbm, hat1_hbm, hat2_hbm, rstd_hbm, dy_hbm) = refs[10:21]
    outs = refs[21:25]
    grad_out, norm_out, dh_hbm, du_hbm, datt_hbm = refs[25:30]
    scratch = list(refs[30:])

    def take(count):
        taken = scratch[:count]
        del scratch[:count]
        return taken

    q_v, o_v, do_v, lse_v, weight, kv_b, a_b, dq_acc, turned, gkv, term, own_part, left, right, norm_v, norm_in = take(16)
    r1, r2, r3, fin, made = take(5)
    lhs, rhs = take(2)
    zbufs = take(levels)
    sem_in, sem_blk, sem_rhs, sem_lhs, sem_ff, sem_out, sem_res = take(7)
    send1, recv1, send2, recv2, send3, recv3, send6, recv6 = take(8)
    rs_send, rs_recv, ag_send, ag_recv = take(levels), take(levels), take(levels), take(levels)
    left_s, left_r, right_s, right_r, norm_s, norm_r = take(6)
    grp, ctx, wsh = lax.axis_index("grp"), lax.axis_index("ctx"), lax.axis_index("wsh")
    side, core = wsh // 2, wsh % 2
    core_peer = (grp, ctx, side * 2 + 1 - core)
    side_peer = (grp, ctx, (1 - side) * 2 + core)
    grp_peer = (1 - grp, ctx, wsh)
    next_ctx = (grp, lax.rem(ctx + 1, n_ctx), wsh)
    last_ctx = (grp, lax.rem(ctx + n_ctx - 1, n_ctx), wsh)
    bits = [(ctx // (1 << level)) % 2 for level in range(levels)]
    level_peers = [(grp, ctx + (1 - 2 * bits[level]) * (1 << level), wsh) for level in range(levels)]

    def block_copies(index):
        rows = aligned(lax.rem(index, slots + 1) * BLK, BLK)
        slot = lax.rem(index, kv_b.shape[0])
        return (
            pltpu.make_async_copy(kv_hbm.at[rows, :], kv_b.at[slot], sem_blk.at[0, slot]),
            pltpu.make_async_copy(a_hbm.at[rows, :], a_b.at[slot], sem_blk.at[1, slot]),
        )

    barrier = pltpu.get_barrier_semaphore()
    peers = [core_peer, side_peer, grp_peer, next_ctx, last_ctx] + level_peers
    for peer in peers:
        pl.semaphore_signal(barrier, inc=1, device_id=peer, device_id_type=MESH)
    pl.semaphore_wait(barrier, len(peers))

    half = TILE // 2
    ranges, first = [], 0
    for rows, cols in widths:
        across = cols // TILE
        ranges.append((first, first + (rows // TILE) * across, across))
        first = ranges[-1][1]
    chunks = first

    def by_range(index, act):
        for place, (low, high, across) in enumerate(ranges):

            @pl.when((index >= low) & (index < high))
            def _(place=place, low=low, across=across):
                number = index - low
                act(place, (aligned((number // across) * TILE, TILE), aligned((number % across) * TILE, TILE)))

    def region(level, flip):
        row, rows, col, cols = 0, half, 0, TILE
        for place in range(level):
            bit = 1 - bits[place] if (flip and place == level - 1) else bits[place]
            if rows > 16:
                rows = rows // 2
                row = row + bit * rows
            else:
                cols = cols // 2
                col = col + bit * cols
        return row, rows, col, cols

    def spot(level, flip=False, base=0):
        row, rows, col, cols = region(level, flip)
        return aligned(base + row, rows), aligned(col, cols)

    last_low = ranges[-1][0]
    set_of = [(0, number) for number in range(widths[0][0] // TILE)] + [(1, 0), (2, 0)]
    set_first = [number * ranges[0][2] for number in range(widths[0][0] // TILE)]
    set_first += [ranges[1][0], ranges[2][0]]
    left_of, right_of = (g_hbm, f_hbm, o_hbm), (dz_hbm, du_hbm, datt_hbm)

    def set_copies(number):
        place, group = set_of[number]
        stride = left_of[place].shape[1] // 4
        return [
            pltpu.make_async_copy(
                left_of[place].at[:, pl.ds(owner * stride + group * TILE, TILE)],
                lhs.at[number % 2, owner],
                sem_lhs.at[number % 2, owner],
            )
            for owner in range(4)
        ]

    def step_fetch(index):
        near = lax.rem(index, 4)

        def act(place, span):
            if place < 3:
                pltpu.make_async_copy(
                    right_of[place].at[:, span[1]], rhs.at[near], sem_rhs.at[near]
                ).start()

        by_range(index, act)

    def step_make(index):
        slot = lax.rem(index, depth)
        near = lax.rem(index, 4)

        @pl.when(index < last_low)
        def _():
            local_wait(rhs.at[near], sem_rhs.at[near])
            parity = jnp.int32(0)
            for number, low in enumerate(set_first):
                parity = jnp.where(index >= low, number % 2, parity)

                @pl.when(index == low)
                def _(number=number):
                    for copy in set_copies(number):
                        copy.wait()
                    if number + 1 < len(set_first):
                        for copy in set_copies(number + 1):
                            copy.start()

            right_side = rhs[near]
            for owner in range(4):
                made[near, owner // 2, owner % 2] = dot_dims(
                    lhs[parity, owner], right_side, 0, 0
                ).astype(jnp.bfloat16)

        @pl.when(index >= last_low)
        def _():
            span = aligned((index - last_low) * TILE, TILE)
            made[near] = term[:, :, :, span]

        remote(
            made.at[near, :, 1 - core], r1.at[slot], send1.at[slot], recv1.at[slot], core_peer
        ).start()

    def finished(move):
        move.wait_send()
        move.wait_recv()

    def step_core(index):
        slot, near = lax.rem(index, depth), lax.rem(index, 4)
        finished(remote(r1.at[slot], r1.at[slot], send1.at[slot], recv1.at[slot], core_peer))
        r1[slot] = r1[slot] + made[near, :, core]
        remote(r1.at[slot, 1 - side], r2.at[slot], send2.at[slot], recv2.at[slot], side_peer).start()

    keep_half = aligned(grp * half, half)
    give_half = aligned((1 - grp) * half, half)

    def step_side(index):
        slot = lax.rem(index, depth)
        finished(remote(r1.at[slot, 1 - side], r2.at[slot], send2.at[slot], recv2.at[slot], side_peer))
        r2[slot] = r2[slot] + r1[slot, side]
        remote(r2.at[slot, give_half], r3.at[slot], send3.at[slot], recv3.at[slot], grp_peer).start()

    fold = n_ctx == 4
    if fold:
        outer = bits[0] == bits[1]
        inner = bits[0] != bits[1]
        mate, middle = level_peers[0], (grp, 3 - ctx, wsh)
        quarter = half // 2
        mine, other = aligned(bits[1] * quarter, quarter), aligned((1 - bits[1]) * quarter, quarter)
        fin_mine = aligned(grp * half + bits[1] * quarter, quarter)
        fin_other = aligned(grp * half + (1 - bits[1]) * quarter, quarter)

        def up_copy(slot):
            return remote(r3.at[slot], zbufs[0].at[slot], rs_send[0].at[slot], rs_recv[0].at[slot], mate)

        def cross_copy(slot):
            return remote(
                r3.at[slot, other], zbufs[1].at[slot], rs_send[1].at[slot], rs_recv[1].at[slot], middle
            )

        def share_copy(slot, rows):
            here = fin.at[slot, rows]
            return remote(here, here, ag_send[1].at[slot], ag_recv[1].at[slot], middle)

        def down_copy(slot):
            here = fin.at[slot, keep_half]
            return remote(here, here, ag_send[0].at[slot], ag_recv[0].at[slot], mate)

        def step_up(index):
            slot = lax.rem(index, depth)

            @pl.when(outer)
            def _():
                up_copy(slot).wait_send()

            @pl.when(inner)
            def _():
                up_copy(slot).wait_recv()
                r3[slot] = r3[slot] + zbufs[0][slot]
                cross_copy(slot).start()

        def step_cross(index):
            slot = lax.rem(index, depth)

            @pl.when(inner)
            def _():
                finished(cross_copy(slot))
                fin[slot, fin_mine] = r3[slot, mine] + zbufs[1][slot]
                share_copy(slot, fin_mine).start()

        def step_share(index):
            slot = lax.rem(index, depth)

            @pl.when(inner)
            def _():
                finished(share_copy(slot, fin_other))
                down_copy(slot).start()

        def step_down(index):
            slot = lax.rem(index, depth)

            @pl.when(inner)
            def _():
                down_copy(slot).wait_send()

            @pl.when(outer)
            def _():
                down_copy(slot).wait_recv()

            back_copy(slot, keep_half).start()

    def rs_copy(level, slot):
        rows, cols = spot(level + 1, True)
        return remote(
            r3.at[slot, rows, cols], zbufs[level].at[slot], rs_send[level].at[slot], rs_recv[level].at[slot], level_peers[level]
        )

    def ag_copy(level, slot, flip=False):
        rows, cols = spot(level + 1, flip, grp * half)
        here = fin.at[slot, rows, cols]
        return remote(here, here, ag_send[level].at[slot], ag_recv[level].at[slot], level_peers[level])

    def back_copy(slot, rows):
        here = fin.at[slot, rows]
        return remote(here, here, send6.at[slot], recv6.at[slot], grp_peer)

    def step_grp(index):
        slot = lax.rem(index, depth)
        finished(remote(r2.at[slot, give_half], r3.at[slot], send3.at[slot], recv3.at[slot], grp_peer))
        r3[slot] = r3[slot] + r2[slot, keep_half]
        if fold:

            @pl.when(outer)
            def _():
                up_copy(slot).start()
        else:
            rs_copy(0, slot).start()

    def step_scatter(level):
        def act(index):
            slot = lax.rem(index, depth)
            finished(rs_copy(level, slot))
            rows, cols = spot(level + 1)
            total = r3[slot, rows, cols] + zbufs[level][slot]
            if level + 1 < levels:
                r3[slot, rows, cols] = total
                rs_copy(level + 1, slot).start()
            else:
                rows, cols = spot(level + 1, False, grp * half)
                fin[slot, rows, cols] = total
                ag_copy(level, slot).start()

        return act

    def step_gather(level):
        def act(index):
            slot = lax.rem(index, depth)
            finished(ag_copy(level, slot, True))
            if level:
                ag_copy(level - 1, slot).start()
            else:
                back_copy(slot, keep_half).start()

        return act

    def out_wait(index):
        slot = lax.rem(index, depth)
        local_wait(fin.at[slot], sem_out.at[slot])

    def step_out(index):
        slot = lax.rem(index, depth)
        finished(back_copy(slot, give_half))

        def act(place, span):
            pltpu.make_async_copy(fin.at[slot], outs[place].at[span[0], span[1]], sem_out.at[slot]).start()

        by_range(index, act)

    z_lag = 2 if fold else 1
    order = [(YLAG, step_side), (XLAG, step_grp)]
    if fold:
        order += [(z_lag, act) for act in (step_up, step_cross, step_share, step_down)]
    else:
        order += [(z_lag, step_scatter(level)) for level in range(levels)]
        order += [(z_lag, step_gather(level)) for level in reversed(range(levels))]
    order += [(BLAG, step_out), (2, out_wait)]
    stages = [(0, step_core)]
    for lag, act in order:
        stages.append((stages[-1][0] + lag, act))
    all_ticks = chunks + stages[-1][0]

    per_slot = BLK // CHAIN
    chain_chunks = slots * per_slot

    def chain_step(stream, send, recv, number, is_first, is_last, target):
        slot = number // per_slot
        rows = aligned((number % per_slot) * CHAIN, CHAIN)
        here = stream.at[slot, rows]

        @pl.when(is_first)
        def _():
            stream[slot, rows, :] = own_part[slot, rows, :]

        @pl.when(jnp.logical_not(is_first))
        def _():
            remote(here, here, send.at[number], recv.at[number], target).wait_recv()
            stream[slot, rows, :] = stream[slot, rows, :] + own_part[slot, rows, :]

        @pl.when(jnp.logical_not(is_last))
        def _():
            remote(here, here, send.at[number], recv.at[number], target).start()

    def chain_tick(step):
        number = step - ctx

        @pl.when((number >= 0) & (number < chain_chunks))
        def _():
            chain_step(left, left_s, left_r, number, ctx == 0, ctx == n_ctx - 1, next_ctx)

        back = step - (n_ctx - 1 - ctx)

        @pl.when((back >= 0) & (back < chain_chunks))
        def _():
            chain_step(right, right_s, right_r, back, ctx == n_ctx - 1, ctx == 0, last_ctx)

    groups = PAIRS // PAIRED
    block_ticks = groups + 2
    chain_first = FF_TICKS + block_ticks
    paced = max(0, -(-(chunks - chain_first) // PACE))
    chain_ticks = max(chunks, chain_first) + max(0, chain_chunks + n_ctx - 1 - paced)

    def tick(step):
        @pl.when(step + 3 < chunks)
        def _():
            step_fetch(step + 3)

        @pl.when(step + 2 < chunks)
        def _():
            step_make(step + 2)

        for lag, act in stages:
            index = step - lag

            @pl.when((index >= 0) & (index < chunks))
            def _(act=act, index=index):
                act(index)

        beat = step - chain_first

        @pl.when((beat >= 0) & (step < chunks) & (beat % PACE == 0))
        def _():
            chain_tick(beat // PACE)

        @pl.when((beat >= 0) & (step >= chunks))
        def _():
            chain_tick(paced + step - max(chunks, chain_first))


    for index in range(3):
        step_fetch(jnp.int32(index))
    for copy in set_copies(0):
        copy.start()

    hidden_tiles = u_hbm.shape[1] // SPAN
    datt_v, dz_v, dy_v, hat1_v, hat2_v = own_part.at[0], do_v, left.at[1], right.at[0], right.at[1]

    def tile_copies(tile, parity):
        cols = aligned(tile * SPAN, SPAN)
        return (
            pltpu.make_async_copy(w_down.at[cols, :], own_part.at[parity], sem_ff.at[0, parity]),
            pltpu.make_async_copy(
                w_up.at[:, cols], turned.at[aligned(parity * D, D), :], sem_ff.at[1, parity]
            ),
            pltpu.make_async_copy(
                u_hbm.at[:, cols], left.at[0, :, aligned(parity * SPAN, SPAN)], sem_ff.at[2, parity]
            ),
        )

    def du_store(tile, parity):
        return pltpu.make_async_copy(
            kv_b.at[0, :, aligned(parity * SPAN, SPAN)],
            du_hbm.at[:, aligned(tile * SPAN, SPAN)],
            sem_ff.at[3, parity],
        )

    dz_load = pltpu.make_async_copy(dz_hbm, dz_v, sem_in.at[0])
    dz_load.start()
    for copy in tile_copies(0, 0):
        copy.start()
    wide_loads = [
        pltpu.make_async_copy(source, dest, sem_in.at[place + 1])
        for place, (source, dest) in enumerate(
            (
                (dy_hbm, dy_v),
                (hat1_hbm, hat1_v),
                (hat2_hbm, hat2_v),
                (rstd_hbm, lse_v.at[pl.ds(0, 2)]),
                (q_hbm, q_v),
                (o_hbm, o_v),
                (w_hbm, weight),
            )
        )
    ]
    out_loads = [
        pltpu.make_async_copy(
            w_out.at[pl.ds(place * TILE, TILE), :],
            term.at[place // 2, place % 2, :, pl.ds(0, D)],
            sem_in.at[8 + place],
        )
        for place in range(4)
    ]
    for index in range(2):
        step_make(jnp.int32(index))
    dz_load.wait()

    def ff_tile(tile, carry):
        start = tile + (tile + 1) // 2
        tick(start)

        @pl.when(tile % 2 == 0)
        def _():
            tick(start + 1)

        parity = tile % 2
        for copy in tile_copies(tile, parity):
            copy.wait()

        @pl.when(tile + 1 < hidden_tiles)
        def _():
            for copy in tile_copies(tile + 1, 1 - parity):
                copy.start()

        @pl.when(tile == 0)
        def _():
            for copy in wide_loads + out_loads:
                copy.start()

        @pl.when(tile >= 2)
        def _():
            du_store(tile - 2, parity).wait()

        u_cols = aligned(parity * SPAN, SPAN)
        u_tile = left[0, :, u_cols].astype(jnp.float32)
        square = u_tile * u_tile
        bend = jnp.tanh(GELU_C * u_tile * (1.0 + GELU_A * square))
        slope = 0.5 * (1.0 + bend) + (0.5 * GELU_C) * u_tile * (1.0 - bend * bend) * (
            1.0 + 3.0 * GELU_A * square
        )
        du_tile = (contract_last(dz_v[...], own_part[parity]) * slope).astype(jnp.bfloat16)
        kv_b[0, :, u_cols] = du_tile
        du_store(tile, parity).start()
        fresh = contract_last(du_tile, turned[aligned(parity * D, D), :])

        @pl.when(tile == 0)
        def _():
            dq_acc[...] = fresh

        @pl.when(tile > 0)
        def _():
            dq_acc[...] = dq_acc[...] + fresh

        return carry

    lax.fori_loop(0, hidden_tiles, ff_tile, 0)
    for tile in range(hidden_tiles - 2, hidden_tiles):
        du_store(tile, tile % 2).wait()
    for copy in wide_loads:
        copy.wait()
    for copy in block_copies(1):
        copy.start()

    def row_back(upstream, hat, scale, gain):
        scaled = upstream * gain
        return scale * (
            scaled
            - jnp.mean(scaled, axis=-1, keepdims=True)
            - hat * jnp.mean(scaled * hat, axis=-1, keepdims=True)
        )

    def column_sum(values):
        return jnp.sum(values, axis=0, keepdims=True)

    def hidden_back(step, carry):
        gain1, gain2, bias1, bias2 = carry
        rows = aligned(step * CHAIN, CHAIN)
        upstream = dq_acc[rows, :]
        hat = hat2_v[rows, :].astype(jnp.float32)
        grad_h = dy_v[rows, :].astype(jnp.float32) + row_back(
            upstream, hat, lse_v[1, rows, 0:1], gain_ref[2:3, :]
        )
        gain2, bias2 = gain2 + column_sum(upstream * hat), bias2 + column_sum(upstream)
        dq_acc[rows, :] = grad_h
        hat = hat1_v[rows, :].astype(jnp.float32)
        datt_v[rows, :] = row_back(grad_h, hat, lse_v[0, rows, 0:1], gain_ref[1:2, :]).astype(
            jnp.bfloat16
        )
        return gain1 + column_sum(grad_h * hat), gain2, bias1 + column_sum(grad_h), bias2

    zero = jnp.zeros((1, D), jnp.float32)
    sums = lax.fori_loop(0, BLK // CHAIN, hidden_back, (zero,) * 4)
    row = lax.broadcasted_iota(jnp.int32, (8, D), 0)
    norm_v[...] = norm_ref[...]
    for place, value in zip((1, 2, 5, 6), sums):
        norm_v[...] = norm_v[...] + jnp.where(row == place, value, 0.0)
    tick(FF_TICKS - 1)
    stores = [
        pltpu.make_async_copy(dq_acc, dh_hbm, sem_res.at[0]),
        pltpu.make_async_copy(datt_v, datt_hbm, sem_res.at[1]),
    ]
    lse_load = pltpu.make_async_copy(lse_hbm, lse_v, sem_in.at[0])
    for copy in stores + [lse_load]:
        copy.start()
    for place in range(4):
        out_loads[place].wait()
        do_v[:, pl.ds(place * TILE, TILE)] = contract_last(
            datt_v[...], term[place // 2, place % 2, :, pl.ds(0, D)]
        ).astype(jnp.bfloat16)
    for copy in stores + [lse_load]:
        copy.wait()
    dq_acc[...] = jnp.zeros_like(dq_acc)

    def attend(kv_ref, own, visible, begin):
        def body(group, carry):
            tick(begin + group)
            for member in range(PAIRED):
                grad_block(
                    q_v, do_v, o_v, lse_v, kv_ref, dq_acc, turned, group * PAIRED + member, own, visible
                )
            return carry

        lax.fori_loop(0, groups, body, 0)

    def each_slot(slot, carry):
        visible = slot < slot_ref[0]
        index = slot + 1
        place = lax.rem(index, kv_b.shape[0])
        for copy in block_copies(index):
            copy.wait()
        if kv_b.shape[0] > 1:
            for copy in block_copies(index + 1):
                copy.start()
        begin = FF_TICKS + slot * block_ticks
        attend(kv_b.at[place], False, visible, begin)

        def weight_terms(step, inner):
            tick(begin + groups + step)
            rows = aligned(step * 512, 512)
            for part in range(2):
                cols = pl.ds(part * D, D)
                product = dot_dims(a_b[place, :, rows], turned[cols, :], 0, 1)
                for down in range(2):
                    if shallow:
                        target = gkv.at[aligned(step * 512 + down * TILE, TILE), cols]
                    else:
                        target = term.at[step, down, :, pl.ds((part + 1) * D, D)]
                    piece = product[down * TILE : (down + 1) * TILE]

                    @pl.when(slot == 0)
                    def _(target=target, piece=piece):
                        target[...] = piece.astype(target.dtype)

                    @pl.when(slot > 0)
                    def _(target=target, piece=piece):
                        target[...] = (target[...] + piece).astype(target.dtype)

            own_part[slot, :, rows] = dot_dims(
                turned[...], weight[rows, pl.ds(D, 2 * D)], 0, 1
            ).astype(jnp.bfloat16)
            return inner

        lax.fori_loop(0, 2, weight_terms, 0)
        if kv_b.shape[0] == 1:
            for copy in block_copies(index + 1):
                copy.start()
        return carry

    lax.fori_loop(0, slots, each_slot, 0)
    begin = FF_TICKS + slots * block_ticks
    own_place = (slots + 1) % kv_b.shape[0]
    for copy in block_copies(slots + 1):
        copy.wait()
    attend(kv_b.at[own_place], True, None, begin)
    dq_low = o_v
    dq_low[...] = (dq_acc[...] * ALPHA).astype(jnp.bfloat16) * jnp.bfloat16(QSCALE)
    x_load = pltpu.make_async_copy(x_hbm, do_v, sem_in.at[0])
    x_load.start()

    def last_terms(step, carry):
        tick(begin + groups + step)
        rows = aligned(step * TILE, TILE)
        a_rows = a_b[own_place, :, rows]
        up, down = step // 2, step % 2
        term[up, down, :, pl.ds(0, D)] = dot_dims(a_rows, dq_low[...], 0, 0).astype(jnp.bfloat16)
        for part in range(2):
            cols = pl.ds(part * D, D)
            target = term.at[up, down, :, pl.ds((part + 1) * D, D)]
            earlier = gkv[rows, cols] if shallow else target[...]
            target[...] = (earlier + dot_dims(a_rows, turned[cols, :], 0, 1)).astype(jnp.bfloat16)
        return carry

    lax.fori_loop(0, 4, last_terms, 0)
    ready = begin + groups + 4
    assert ready <= ranges[-1][0] - 2 or n_ctx > 4
    da_acc = dq_acc

    def own_grad(step, carry):
        tick(ready + step)
        rows = aligned(step * TILE, TILE)
        da_acc[:, rows] = dot_dims(dq_low[...], weight[rows, pl.ds(0, D)], 1, 1) + dot_dims(
            turned[...], weight[rows, pl.ds(D, 2 * D)], 0, 1
        )
        return carry

    lax.fori_loop(0, 4, own_grad, 0)
    ready = ready + 4

    def flush_chain(step, carry):
        tick(ready + step)
        return carry

    left_over = max(0, chain_ticks - ready)
    lax.fori_loop(0, left_over, flush_chain, 0)
    ready = ready + left_over
    x_load.wait()
    gain = gain_ref[0:1, :]

    def norm_grad(step, carry):
        gain_sum, bias_sum = carry

        @pl.when(step % 2 == 0)
        def _():
            tick(ready + step // 2)

        rows = aligned(step * CHAIN, CHAIN)
        upstream = da_acc[rows, :]
        for slot in range(slots):
            joined = left[slot, rows, :].astype(jnp.float32) + right[slot, rows, :].astype(jnp.float32)
            upstream = upstream + jnp.where(slot_ref[0] == slot, joined, 0.0)
        values = do_v[rows, :].astype(jnp.float32)
        centre = values - jnp.mean(values, axis=-1, keepdims=True)
        scale = lax.rsqrt(jnp.mean(centre * centre, axis=-1, keepdims=True) + EPS)
        centre = centre * scale
        da_acc[rows, :] = row_back(upstream, centre, scale, gain)
        return gain_sum + column_sum(upstream * centre), bias_sum + column_sum(upstream)

    gain_sum, bias_sum = lax.fori_loop(0, BLK // CHAIN, norm_grad, (zero, zero))
    ready = ready + BLK // CHAIN // 2
    result = pltpu.make_async_copy(da_acc, grad_out, sem_res.at[0])
    result.start()
    norm_v[...] = norm_v[...] + jnp.where(row == 0, gain_sum, 0.0) + jnp.where(row == 4, bias_sum, 0.0)
    for place, peer in enumerate([core_peer, side_peer, grp_peer] + level_peers):
        move = remote(norm_v, norm_in.at[place], norm_s.at[place], norm_r.at[place], peer)
        move.start()
        tick(ready)
        tick(ready + 1)
        ready = ready + 2
        finished(move)
        norm_v[...] = norm_v[...] + norm_in[place]
    norm_result = pltpu.make_async_copy(norm_v, norm_out, sem_res.at[1])
    norm_result.start()
    if all_ticks > ready:
        lax.fori_loop(ready, all_ticks, lambda index, carry: (tick(index), carry)[1], 0)

    def drain_chain(index, carry):
        here = left.at[0, pl.ds(0, CHAIN)]

        @pl.when(ctx < n_ctx - 1)
        def _():
            remote(here, here, left_s.at[index], left_r.at[index], next_ctx).wait_send()

        @pl.when(ctx > 0)
        def _():
            remote(here, here, right_s.at[index], right_r.at[index], last_ctx).wait_send()

        return carry

    lax.fori_loop(0, chain_chunks, drain_chain, 0)
    result.wait()
    norm_result.wait()


def backward_part(n_ctx, slot_vec, gains, norms, saved, weights, ffn):
    slots = n_ctx // 2
    levels = n_ctx.bit_length() - 1
    depth = 14 if n_ctx == 4 else 10
    hidden = weights[1].shape[1]
    widths = [(hidden // 4, D), (D // 4, hidden), (D // 4, D), (D // 4, 3 * D)]
    low, full = jnp.bfloat16, jnp.float32
    dma = pltpu.SemaphoreType.DMA
    hbm = pl.BlockSpec(memory_space=pl.ANY)
    vmem = pl.BlockSpec(memory_space=pltpu.VMEM)
    shape = jax.ShapeDtypeStruct
    buffers = 2 if slots <= 2 else 1
    chain = slots * (BLK // CHAIN)
    zshapes, rows, cols = [], TILE // 2, TILE
    if n_ctx == 4:
        zshapes = [pltpu.VMEM((depth, rows, cols), low), pltpu.VMEM((depth, rows // 2, cols), low)]
    for _ in range(0 if zshapes else levels):
        rows, cols = (rows // 2, cols) if rows > 16 else (rows, cols // 2)
        zshapes.append(pltpu.VMEM((depth, rows, cols), low))
    return pl.pallas_call(
        functools.partial(backward_kernel, n_ctx, widths),
        out_shape=[shape(width, low) for width in widths] + [
            shape((BLK, D), full),
            shape((8, D), full),
            shape((BLK, D), full),
            shape((BLK, hidden), low),
            shape((BLK, D), low),
        ],
        in_specs=[pl.BlockSpec(memory_space=pltpu.SMEM), vmem, vmem]
        + [hbm] * (len(saved) + len(weights) + len(ffn)),
        out_specs=[hbm] * 9,
        scratch_shapes=[
            pltpu.VMEM((BLK, D), low),
            pltpu.VMEM((BLK, D), low),
            pltpu.VMEM((BLK, D), low),
            pltpu.VMEM((PAIRS, BLK, 128), full),
            pltpu.VMEM((D, 3 * D), low),
            pltpu.VMEM((buffers, BLK, 2 * D), low),
            pltpu.VMEM((buffers, BLK, D), low),
            pltpu.VMEM((BLK, D), full),
            pltpu.VMEM((2 * D, BLK), low),
            pltpu.VMEM((D, 2 * D) if slots <= 2 else (8, 128), full),
            pltpu.VMEM((2, 2, D // 4, 3 * D), low),
            pltpu.VMEM((slots, BLK, D), low),
            pltpu.VMEM((slots, BLK, D), low),
            pltpu.VMEM((slots, BLK, D), low),
            pltpu.VMEM((8, D), full),
            pltpu.VMEM((3 + levels, 8, D), full),
            pltpu.VMEM((depth, 2, TILE, TILE), low),
            pltpu.VMEM((depth, TILE, TILE), low),
            pltpu.VMEM((depth, TILE // 2, TILE), low),
            pltpu.VMEM((depth, TILE, TILE), low),
            pltpu.VMEM((4, 2, 2, TILE, TILE), low),
        ]
        + [pltpu.VMEM((2, 4, BLK, TILE), low), pltpu.VMEM((4, BLK, TILE), low)]
        + zshapes
        + [dma((12,)), dma((2, buffers)), dma((4,)), dma((2, 4)), dma((4, 2)), dma((depth,)), dma((2,))]
        + [dma((depth,))] * (8 + 4 * levels)
        + [dma((chain,))] * 4
        + [dma((3 + levels,))] * 2,
        compiler_params=pltpu.CompilerParams(
            collective_id=2, has_side_effects=True, vmem_limit_bytes=67043328
        ),
        cost_estimate=pl.CostEstimate(flops=40 << 30, bytes_accessed=64 << 20, transcendentals=1 << 24),
        name="attend_back_reduce",
    )(
        slot_vec,
        gains,
        norms,
        *saved,
        *weights,
        *ffn,
    )


def per_device(n_ctx, inputs, w_qkv, w_out, w_up, w_down, norm_gains, norm_biases, block_map, out_grad):
    slots = n_ctx // 2
    raw = inputs.reshape(BLK, D)
    tokens = raw.astype(jnp.float32)
    block_entry = block_map.reshape(2)
    own_slot = block_entry[1] // BLK
    own_tag = jnp.where(block_entry[0] == 0, own_slot, n_ctx)
    slot_vec = own_slot.reshape(1)
    every_low, queries, keys_values, attn_low, lse, full_qkv, full_out, full_up, full_down = forward_part(
        n_ctx,
        jnp.stack([own_slot, own_tag]),
        norm_gains[0:1],
        norm_biases[0:1],
        raw,
        w_qkv,
        w_out,
        w_up,
        w_down,
    )

    def normalised(values):
        centre = values - jnp.mean(values, axis=-1, keepdims=True)
        scale = lax.rsqrt(jnp.mean(centre * centre, axis=-1, keepdims=True) + EPS)
        return centre * scale, jnp.broadcast_to(scale, (BLK, 128))

    branch = jnp.dot(attn_low, full_out, preferred_element_type=jnp.float32)
    hat1, rstd1 = normalised(branch)
    hidden = tokens + hat1 * norm_gains[1] + norm_biases[1]
    hat2, rstd2 = normalised(hidden)
    ffn_low = (hat2 * norm_gains[2] + norm_biases[2]).astype(jnp.bfloat16)
    upward = jnp.dot(ffn_low, full_up, preferred_element_type=jnp.float32)
    active_low = gelu_tanh(upward).astype(jnp.bfloat16)
    downward = jnp.dot(active_low, full_down, preferred_element_type=jnp.float32)
    post_ffn, post_back = jax.vjp(layer_norm, downward, norm_gains[3], norm_biases[3])
    result = (hidden + post_ffn).astype(jnp.bfloat16).reshape(1, 1, BLK, D)
    seed_low = out_grad.reshape(BLK, D)
    grad_down_in, gain_grad3, bias_grad3 = post_back(seed_low.astype(jnp.float32))
    zero_row = jnp.zeros((D,), jnp.float32)
    norms = jnp.stack([zero_row] * 3 + [gain_grad3] + [zero_row] * 3 + [bias_grad3])
    summed_down, summed_up, summed_out, summed_qkv, grad_tokens, norm_total, grad_hidden = backward_part(
        n_ctx,
        slot_vec,
        norm_gains,
        norms,
        [raw, queries, keys_values, every_low, attn_low, lse, full_qkv],
        [full_out, full_up, full_down],
        [
            active_low,
            grad_down_in.astype(jnp.bfloat16),
            ffn_low,
            upward.astype(jnp.bfloat16),
            hat1.astype(jnp.bfloat16),
            hat2.astype(jnp.bfloat16),
            jnp.stack([rstd1, rstd2]),
            seed_low,
        ],
    )[:7]
    grad_input = (grad_hidden + grad_tokens).reshape(1, 1, BLK, D)
    summed_down, summed_up, summed_out, summed_qkv = (
        total.astype(jnp.float32) for total in (summed_down, summed_up, summed_out, summed_qkv)
    )
    gain_total, bias_total = norm_total[:4], norm_total[4:]
    return (
        result,
        grad_input,
        summed_qkv,
        summed_out,
        summed_up,
        summed_down,
        gain_total,
        bias_total,
    )


def solution(mesh):
    rows = P("wsh", None)
    blocks = P("grp", "wsh", "ctx", None)
    return jax.shard_map(
        functools.partial(per_device, mesh.shape["ctx"]),
        mesh=mesh,
        in_specs=(blocks, rows, rows, rows, rows, P(), P(), blocks, blocks),
        out_specs=(blocks, blocks, rows, rows, rows, rows, P(), P()),
        check_vma=False,
    )
```

```python
import functools
import math

import jax
import jax.numpy as jnp
from jax import lax
from jax.experimental import pallas as pl
from jax.experimental.pallas import tpu as pltpu
from jax.sharding import PartitionSpec as P

D = 1024
HEADS = 16
DH = 64
BLK = 512
PAIRS = HEADS // 2
QT = 256

EPS = 1e-05
ALPHA = 32.0
NEG = -1e30
LOG2E = 1.4426950408889634
C2 = ALPHA * LOG2E
MESH = pl.DeviceIdType.MESH
QSCALE = 1.0 / (ALPHA * math.sqrt(DH))


def layer_norm(values, gain_row, bias_row):
    centre = values - jnp.mean(values, axis=-1, keepdims=True)
    spread = jnp.mean(centre * centre, axis=-1, keepdims=True)
    return centre * lax.rsqrt(spread + EPS) * gain_row + bias_row


def dot_dims(left_side, right_side, left_dim, right_dim):
    return lax.dot_general(
        left_side,
        right_side,
        (((left_dim,), (right_dim,)), ((), ())),
        preferred_element_type=jnp.float32,
    )


def contract_last(left_side, right_side):
    return dot_dims(left_side, right_side, 1, 1)


def contract_rows(left_side, right_side):
    return dot_dims(left_side, right_side, 0, 0)


def standard_rows(values):
    centre = values - jnp.mean(values, axis=-1, keepdims=True)
    scale = lax.rsqrt(jnp.mean(centre * centre, axis=-1, keepdims=True) + EPS)
    return centre * scale, scale


def row_back(upstream, hat, scale, gain):
    scaled = upstream * gain
    return scale * (
        scaled
        - jnp.mean(scaled, axis=-1, keepdims=True)
        - hat * jnp.mean(scaled * hat, axis=-1, keepdims=True)
    )


def column_sum(values):
    return jnp.sum(values, axis=0, keepdims=True)


def head_lanes(head, rows):
    lane = lax.broadcasted_iota(jnp.int32, (rows, 128), 1)
    return (lane >= DH) if head else (lane < DH)


def causal_tile():
    row = lax.broadcasted_iota(jnp.int32, (QT, QT), 0)
    col = lax.broadcasted_iota(jnp.int32, (QT, QT), 1)
    return col <= row


PIECE = 128
SPAN = 512
CHAIN = 64
HOP = 2
YLAG = 3
XLAG = 2
BLAG = 2
FF_TICKS = 13
GELU_A = 0.044715
GELU_C = math.sqrt(2.0 / math.pi)
PACE = 2
LAG = 2
GROUP = 4
AHEAD = 4


def remote(src, dst, send, recv, peer):
    return pltpu.make_async_remote_copy(
        src_ref=src, dst_ref=dst, send_sem=send, recv_sem=recv, device_id=peer, device_id_type=MESH
    )


def local_wait(ref, sem):
    pltpu.make_async_copy(ref, ref, sem).wait()


def aligned(start, size):
    return pl.ds(pl.multiple_of(start, size), size)


def softmax_block(q_ref, kv_ref, acc, top_ref, sum_ref, pair, base, own, visible):
    lanes = aligned(pair * 128, 128)
    value_lanes = aligned(D + pair * 128, 128)
    causal = causal_tile()
    first = head_lanes(0, QT)
    count = BLK // QT
    q_pair = q_ref[:, lanes]
    keys = kv_ref[pl.ds(base, BLK), lanes]
    values = kv_ref[pl.ds(base, BLK), value_lanes]
    if not own:
        old_top, old_sum, old_out = top_ref[pair], sum_ref[pair], acc[:, lanes]
        hide = jnp.where(visible, 0.0, 1e30)
    results = []
    work = [(tile, head) for tile in range(count) for head in range(2)]
    parts_of = {}
    for tile, head in work:
        q_tile = q_pair[tile * QT : (tile + 1) * QT]
        q_head = jnp.where(head_lanes(head, QT), q_tile, jnp.zeros_like(q_tile))
        span = (tile + 1) * QT if own else BLK
        parts_of[tile, head] = contract_last(q_head, keys[:span])
    top_of, expo_of, total_of = {}, {}, {}
    for tile, head in work:
        part = parts_of[tile, head]
        if own:
            diag = jnp.where(causal, part[:, tile * QT :], NEG)
            part = jnp.concatenate([part[:, : tile * QT], diag], axis=1) if tile else diag
        top = jnp.max(part, axis=-1, keepdims=True) * C2
        if own:
            shift = top
        else:
            top = jnp.maximum(
                jnp.where(visible, top, NEG), old_top[tile * QT : (tile + 1) * QT, head * DH : head * DH + 1]
            )
            shift = top + hide
        expo = jnp.exp2(part * C2 - shift)
        top_of[tile, head] = jnp.broadcast_to(top, (QT, 128))
        total_of[tile, head] = jnp.broadcast_to(jnp.sum(expo, axis=-1, keepdims=True), (QT, 128))
        expo_of[tile, head] = expo.astype(jnp.bfloat16)
    out_of = {}
    for tile, head in work:
        span = (tile + 1) * QT if own else BLK
        out_of[tile, head] = dot_dims(expo_of[tile, head], values[:span], 1, 0)
    for tile in range(count):
        rows = pl.ds(tile * QT, QT)
        new_top = jnp.where(first, top_of[tile, 0], top_of[tile, 1])
        new_sum = jnp.where(first, total_of[tile, 0], total_of[tile, 1])
        new_out = jnp.where(first, out_of[tile, 0], out_of[tile, 1])
        if not own:
            here = slice(tile * QT, (tile + 1) * QT)
            keep = jnp.exp2(old_top[here] - new_top)
            new_sum = new_sum + old_sum[here] * keep
            new_out = new_out + old_out[here] * keep
        top_ref[pair, rows, :] = new_top
        sum_ref[pair, rows, :] = new_sum
        acc[rows, lanes] = new_out


def forward_kernel(n_ctx, *refs):
    slots = n_ctx // 2
    (slot_ref, gain_ref, bias_ref, x_hbm, dy_hbm, w_qkv, w_out, w_up, w_down) = refs[:9]
    (a_out, q_out, kv_out, o_out, lse_out, full_qkv, full_out, full_up, full_down) = refs[9:18]
    (y_out, g_out, dz_out, f_out, u_out, hat1_out, hat2_out, rstd_out, norm_out) = refs[18:27]
    (x_own, left, right, a_all, q_all, kv_all, weight, acc, z_acc, norm_v, tops, sums, hop) = refs[27:40]
    (sem_in, sem_load, sem_store, sem_ff, sem_out, sem_a, sem_kv, side_s, side_r, grp_s, grp_r, cs_s, cs_r, cg_s, cg_r, own_s, own_r, left_s, left_r, right_s, right_r) = refs[40:]
    grp, ctx, wsh = lax.axis_index("grp"), lax.axis_index("ctx"), lax.axis_index("wsh")
    side, core = wsh // 2, wsh % 2
    core_peer = (grp, ctx, side * 2 + 1 - core)
    side_peer = (grp, ctx, (1 - side) * 2 + core)
    grp_peer = (1 - grp, ctx, wsh)
    next_ctx = (grp, lax.rem(ctx + 1, n_ctx), wsh)
    last_ctx = (grp, lax.rem(ctx + n_ctx - 1, n_ctx), wsh)

    load = pltpu.make_async_copy(x_hbm, x_own, sem_in.at[0])
    load.start()
    barrier = pltpu.get_barrier_semaphore()
    for peer in (core_peer, side_peer, grp_peer, next_ctx, last_ctx):
        pl.semaphore_signal(barrier, inc=1, device_id=peer, device_id_type=MESH)
    pl.semaphore_wait(barrier, 5)

    shards = (w_qkv, w_out, w_up, w_down)
    fulls = (weight, full_out, full_up, full_down)
    ranges, start = [], 0
    for shard in shards:
        across = shard.shape[1] // SPAN
        ranges.append((start, start + across * (shard.shape[0] // (2 * PIECE)), across))
        start = ranges[-1][1]
    pieces = start

    def by_range(index, act):
        for place, (low, high, across) in enumerate(ranges):

            @pl.when((index >= low) & (index < high))
            def _(place=place, low=low, across=across):
                act(place, (index - low) // across, aligned(((index - low) % across) * SPAN, SPAN))

    def rows_of(place, owner, half, group):
        shard_rows = shards[place].shape[0]
        return aligned(owner * shard_rows + half * (shard_rows // 2) + group * PIECE, PIECE)

    sides_owner = (1 - side) * 2 + core

    def send_piece(index, carry):
        def act(place, group, cols):
            remote(
                shards[place].at[rows_of(place, 0, grp, group), cols],
                fulls[place].at[rows_of(place, wsh, grp, group), cols],
                side_s.at[index],
                side_r.at[index],
                side_peer,
            ).start()

        by_range(index, act)
        return carry

    def own_copies():
        copies = []
        across = shards[0].shape[1] // SPAN
        for place in range(4):
            shard_rows = shards[place].shape[0]
            mine = aligned(wsh * shard_rows, shard_rows)
            steps = range(across) if place == 0 else [None]
            for step in steps:
                cols = slice(None) if step is None else pl.ds(step * SPAN, SPAN)
                number = len(copies)
                copies.append(
                    remote(
                        shards[place].at[:, cols],
                        fulls[place].at[mine, cols],
                        own_s.at[number],
                        own_r.at[number],
                        core_peer,
                    )
                )
        return copies

    for index in range(AHEAD):
        send_piece(index, 0)
    for copy in own_copies():
        copy.start()
    own_rows = aligned(wsh * w_qkv.shape[0], w_qkv.shape[0])
    own_weight = pltpu.make_async_copy(w_qkv, weight.at[own_rows, :], sem_in.at[1])
    own_weight.start()
    load.wait()

    bounces, start = [], 0
    for shard in shards[1:]:
        across = shard.shape[1] // SPAN
        bounces.append((start, start + across * (shard.shape[0] // (2 * PIECE)), across))
        start = bounces[-1][1]
    moves = start

    def bounce(index, loading):
        slot = lax.rem(index, 3)
        for place, (low, high, across) in enumerate(bounces):

            @pl.when((index >= low) & (index < high))
            def _(place=place + 1, low=low, across=across):
                group = (index - low) // across
                cols = aligned(((index - low) % across) * SPAN, SPAN)
                if loading:
                    here = shards[place].at[aligned(group * 2 * PIECE, 2 * PIECE), cols]
                    pltpu.make_async_copy(here, hop.at[slot], sem_load.at[slot]).start()
                else:
                    rows = aligned(wsh * shards[place].shape[0] + group * 2 * PIECE, 2 * PIECE)
                    local_wait(hop.at[slot], sem_load.at[slot])
                    pltpu.make_async_copy(
                        hop.at[slot], fulls[place].at[rows, cols], sem_store.at[slot]
                    ).start()

    own_tag = slot_ref[1]
    chain_chunks = slots * (BLK // CHAIN)

    def chain_step(stream, send, recv, number, is_first, is_last, target):
        slot = number // (BLK // CHAIN)
        spot = aligned((number % (BLK // CHAIN)) * CHAIN, CHAIN)
        mine = jnp.where(own_tag == slot, x_own[spot, :], jnp.zeros((CHAIN, D), jnp.bfloat16))
        here = stream.at[slot, spot]

        @pl.when(is_first)
        def _():
            stream[slot, spot, :] = mine

        @pl.when(jnp.logical_not(is_first))
        def _():
            remote(here, here, send.at[number], recv.at[number], target).wait_recv()
            stream[slot, spot, :] = stream[slot, spot, :] + mine

        @pl.when(jnp.logical_not(is_last))
        def _():
            remote(here, here, send.at[number], recv.at[number], target).start()

    def tick(step):
        @pl.when((step >= 1) & (step <= moves))
        def _():
            bounce(step - 1, False)

        @pl.when((step >= 3) & (step < moves))
        def _():
            local_wait(hop.at[lax.rem(step, 3)], sem_store.at[lax.rem(step, 3)])

        @pl.when(step < moves)
        def _():
            bounce(step, True)

        @pl.when(step + AHEAD < pieces)
        def _():
            send_piece(step + AHEAD, 0)

        number = step - HOP * ctx

        @pl.when((number >= 0) & (number < chain_chunks))
        def _():
            chain_step(left, left_s, left_r, number, ctx == 0, ctx == n_ctx - 1, next_ctx)

        back = step - HOP * (n_ctx - 1 - ctx)

        @pl.when((back >= 0) & (back < chain_chunks))
        def _():
            chain_step(right, right_s, right_r, back, ctx == n_ctx - 1, ctx == 0, last_ctx)

        @pl.when(step < pieces)
        def _():
            def act(place, group, cols):
                here = fulls[place].at[rows_of(place, sides_owner, grp, group), cols]
                remote(here, here, side_s.at[step], side_r.at[step], side_peer).wait_recv()
                remote(here, here, grp_s.at[step], grp_r.at[step], grp_peer).start()
                remote(here, here, cs_s.at[step], cs_r.at[step], core_peer).start()

            by_range(step, act)

        late = step - LAG

        @pl.when((late >= 0) & (late < pieces))
        def _():
            def act(place, group, cols):
                here = fulls[place].at[rows_of(place, sides_owner, 1 - grp, group), cols]
                remote(here, here, grp_s.at[late], grp_r.at[late], grp_peer).wait_recv()
                remote(here, here, cg_s.at[late], cg_r.at[late], core_peer).start()

            by_range(late, act)

    def normalise(source, dest):
        gain, bias = gain_ref[0:1, :], bias_ref[0:1, :]

        def body(index, carry):
            rows = aligned(index * 128, 128)
            values = source(rows).astype(jnp.float32)
            a_all[aligned(dest + index * 128, 128), :] = layer_norm(values, gain, bias).astype(
                jnp.bfloat16
            )
            return carry

        lax.fori_loop(0, BLK // 128, body, 0)

    def piece_ready(index):
        here = fulls[0].at[pl.ds(0, PIECE), pl.ds(0, SPAN)]
        remote(here, here, cs_s.at[index], cs_r.at[index], core_peer).wait_recv()
        remote(here, here, cg_s.at[index], cg_r.at[index], core_peer).wait_recv()
        whole = fulls[0].at[pl.ds(0, 2 * PIECE), pl.ds(0, SPAN)]
        remote(whole, whole, own_s.at[index], own_r.at[index], core_peer).wait_recv()

    tick(0)
    normalise(lambda rows: x_own[rows, :], 0)
    for step in range(1, LAG + 1):
        tick(step)
    own_weight.wait()

    def project_q(index, carry):
        tick(index + LAG + 1)
        piece_ready(index)
        cols = aligned(index * SPAN, SPAN)
        q_all[:, cols] = (
            jnp.dot(a_all[pl.ds(0, BLK), :], weight[:, cols], preferred_element_type=jnp.float32) * QSCALE
        ).astype(jnp.bfloat16)
        return carry

    lax.fori_loop(0, D // SPAN, project_q, 0)
    head_ticks = LAG + 1 + D // SPAN

    def project_kv(index, base):
        cols = aligned(index * SPAN, SPAN)
        rows = aligned(base, BLK)
        kv_all[rows, cols] = jnp.dot(
            a_all[rows, :], weight[:, aligned(D + index * SPAN, SPAN)], preferred_element_type=jnp.float32
        ).astype(jnp.bfloat16)

    def own_kv(index, carry):
        tick(index + head_ticks)
        piece_ready(index + D // SPAN)
        project_kv(index, 0)
        return carry

    lax.fori_loop(0, 2 * D // SPAN, own_kv, 0)
    own_ticks = head_ticks + 2 * D // SPAN

    def send_block(index):
        rows = aligned(index * BLK, BLK)
        pltpu.make_async_copy(a_all.at[rows, :], a_out.at[rows, :], sem_a.at[index]).start()
        pltpu.make_async_copy(kv_all.at[rows, :], kv_out.at[rows, :], sem_kv.at[index]).start()

    outputs = [
        pltpu.make_async_copy(weight, full_qkv, sem_out.at[0]),
        pltpu.make_async_copy(q_all, q_out, sem_out.at[1]),
    ]
    for copy in outputs:
        copy.start()

    send_block(0)

    def own_attention(group, carry):
        tick(own_ticks + 2 * group)
        tick(own_ticks + 2 * group + 1)
        for member in range(GROUP):
            softmax_block(q_all, kv_all, acc, tops, sums, group * GROUP + member, 0, True, None)
        return carry

    groups = PAIRS // GROUP
    lax.fori_loop(0, groups, own_attention, 0)
    used = own_ticks + 2 * groups
    per_slot = 2 * D // SPAN + 2 * groups

    need = BLK // CHAIN + HOP * (n_ctx - 1)
    early = max(0, need - used)
    if early:
        lax.fori_loop(0, early, lambda index, carry: (tick(used + index), carry)[1], 0)

    def each_slot(slot, carry):
        base = pl.multiple_of((slot + 1) * BLK, BLK)
        visible = slot < slot_ref[0]
        begin = early + used + slot * per_slot

        def total(rows):
            joined = left[slot, rows, :] + right[slot, rows, :]
            return jnp.where(own_tag == slot, x_own[rows, :], joined)

        normalise(total, base)

        def slot_kv(index, inner):
            tick(begin + index)
            project_kv(index, base)
            return inner

        lax.fori_loop(0, 2 * D // SPAN, slot_kv, 0)

        send_block(slot + 1)

        def slot_attention(group, inner):
            tick(begin + 2 * D // SPAN + 2 * group)
            tick(begin + 2 * D // SPAN + 2 * group + 1)
            for member in range(GROUP):
                softmax_block(
                    q_all, kv_all, acc, tops, sums, group * GROUP + member, base, False, visible
                )
            return inner

        lax.fori_loop(0, groups, slot_attention, 0)
        return carry

    lax.fori_loop(0, slots, each_slot, 0)
    done_ticks = early + used + slots * per_slot

    def finish(pair, carry):
        lanes = aligned(pair * 128, 128)
        x_own[:, lanes] = (acc[:, lanes] / sums[pair]).astype(jnp.bfloat16)
        tops[pair] = tops[pair] + jnp.log2(sums[pair])
        return carry

    lax.fori_loop(0, PAIRS, finish, 0)
    outputs += [
        pltpu.make_async_copy(x_own, o_out, sem_out.at[2]),
        pltpu.make_async_copy(tops, lse_out, sem_out.at[3]),
    ]
    for copy in outputs[2:]:
        copy.start()
    all_ticks = max(pieces + LAG, chain_chunks + HOP * (n_ctx - 1))
    if all_ticks > done_ticks:
        lax.fori_loop(done_ticks, all_ticks, lambda index, carry: (tick(index), carry)[1], 0)

    def drain(index, carry):
        here = fulls[0].at[pl.ds(0, PIECE), pl.ds(0, SPAN)]

        @pl.when(index >= ranges[0][1])
        def _():
            remote(here, here, cs_s.at[index], cs_r.at[index], core_peer).wait_recv()
            remote(here, here, cg_s.at[index], cg_r.at[index], core_peer).wait_recv()

        remote(here, here, side_s.at[index], side_r.at[index], side_peer).wait_send()
        remote(here, here, grp_s.at[index], grp_r.at[index], grp_peer).wait_send()
        remote(here, here, cs_s.at[index], cs_r.at[index], core_peer).wait_send()
        remote(here, here, cg_s.at[index], cg_r.at[index], core_peer).wait_send()
        return carry

    lax.fori_loop(0, pieces, drain, 0)
    copies = own_copies()
    for number, copy in enumerate(copies):
        copy.wait_send()
        if number >= len(copies) - 3:
            copy.wait_recv()
    for index in range(moves - 3, moves):
        local_wait(hop.at[index % 3], sem_store.at[index % 3])

    def drain_chain(index, carry):
        here = left.at[0, pl.ds(0, CHAIN)]

        @pl.when(ctx < n_ctx - 1)
        def _():
            remote(here, here, left_s.at[index], left_r.at[index], next_ctx).wait_send()

        @pl.when(ctx > 0)
        def _():
            remote(here, here, right_s.at[index], right_r.at[index], last_ctx).wait_send()

        return carry

    lax.fori_loop(0, chain_chunks, drain_chain, 0)
    for copy in outputs[:2]:
        copy.wait()
    shallow_tiles = full_up.shape[1] // SPAN

    def tile_loads(tile, parity):
        cols = aligned(tile * SPAN, SPAN)
        return (
            pltpu.make_async_copy(
                full_up.at[:, cols], weight.at[:, aligned(D + parity * SPAN, SPAN)], sem_ff.at[0, parity]
            ),
            pltpu.make_async_copy(full_down.at[cols, :], left.at[parity], sem_ff.at[1, parity]),
        )

    def tile_stores(tile, parity):
        cols = aligned(tile * SPAN, SPAN)
        return [
            pltpu.make_async_copy(
                kv_all.at[pl.ds(0, BLK), aligned(base + parity * SPAN, SPAN)],
                dest.at[:, cols],
                sem_ff.at[2 + place, parity],
            )
            for place, (base, dest) in enumerate(((0, u_out), (D, g_out)))
        ]

    out_load = pltpu.make_async_copy(full_out, weight.at[:, pl.ds(0, D)], sem_in.at[0])
    x_load = pltpu.make_async_copy(x_hbm, right.at[1], sem_in.at[1])
    for copy in (out_load, x_load) + tile_loads(0, 0):
        copy.start()

    def drain_blocks(index, carry):
        rows = aligned(index * BLK, BLK)
        local_wait(a_all.at[rows, :], sem_a.at[index])
        local_wait(kv_all.at[rows, :], sem_kv.at[index])
        return carry

    lax.fori_loop(0, slots + 1, drain_blocks, 0)
    out_load.wait()
    for half_cols in range(2):
        cols = pl.ds(half_cols * SPAN, SPAN)
        acc[:, cols] = jnp.dot(x_own[...], weight[:, cols], preferred_element_type=jnp.float32)
    x_load.wait()
    for copy in outputs[2:]:
        copy.wait()
    dy_load = pltpu.make_async_copy(dy_hbm, x_own, sem_in.at[0])
    dy_load.start()

    def inner_rows(step, carry):
        rows = aligned(step * CHAIN, CHAIN)
        hat, scale = standard_rows(acc[rows, :])
        a_all[rows, :] = hat.astype(jnp.bfloat16)
        sums[0, rows, :] = jnp.broadcast_to(scale, (CHAIN, 128))
        hidden = right[1, rows, :].astype(jnp.float32) + hat * gain_ref[1:2, :] + bias_ref[1:2, :]
        acc[rows, :] = hidden
        hat, scale = standard_rows(hidden)
        a_all[aligned(BLK + step * CHAIN, CHAIN), :] = hat.astype(jnp.bfloat16)
        sums[1, rows, :] = jnp.broadcast_to(scale, (CHAIN, 128))
        q_all[rows, :] = (hat * gain_ref[2:3, :] + bias_ref[2:3, :]).astype(jnp.bfloat16)
        return carry

    lax.fori_loop(0, BLK // CHAIN, inner_rows, 0)
    saves = [
        pltpu.make_async_copy(a_all.at[pl.ds(0, BLK), :], hat1_out, sem_out.at[0]),
        pltpu.make_async_copy(a_all.at[pl.ds(BLK, BLK), :], hat2_out, sem_out.at[1]),
        pltpu.make_async_copy(sums.at[pl.ds(0, 2)], rstd_out, sem_out.at[2]),
        pltpu.make_async_copy(q_all, f_out, sem_out.at[3]),
    ]
    for copy in saves:
        copy.start()

    def ff_tile(tile, carry):
        parity = tile % 2
        for copy in tile_loads(tile, parity):
            copy.wait()

        @pl.when(tile + 1 < shallow_tiles)
        def _():
            for copy in tile_loads(tile + 1, 1 - parity):
                copy.start()

        @pl.when(tile >= 2)
        def _():
            for copy in tile_stores(tile - 2, parity):
                copy.wait()

        upward = jnp.dot(
            q_all[...], weight[:, aligned(D + parity * SPAN, SPAN)], preferred_element_type=jnp.float32
        )
        kv_all[pl.ds(0, BLK), aligned(parity * SPAN, SPAN)] = upward.astype(jnp.bfloat16)
        active = (
            0.5 * upward * (1.0 + jnp.tanh(GELU_C * upward * (1.0 + GELU_A * upward * upward)))
        ).astype(jnp.bfloat16)
        kv_all[pl.ds(0, BLK), aligned(D + parity * SPAN, SPAN)] = active
        for copy in tile_stores(tile, parity):
            copy.start()
        fresh = jnp.dot(active, left[parity], preferred_element_type=jnp.float32)

        @pl.when(tile == 0)
        def _():
            z_acc[...] = fresh

        @pl.when(tile > 0)
        def _():
            z_acc[...] = z_acc[...] + fresh

        return carry

    lax.fori_loop(0, shallow_tiles, ff_tile, 0)
    dy_load.wait()

    def outer_rows(step, carry):
        gain_sum, bias_sum = carry
        rows = aligned(step * CHAIN, CHAIN)
        hat, scale = standard_rows(z_acc[rows, :])
        right[0, rows, :] = (acc[rows, :] + hat * gain_ref[3:4, :] + bias_ref[3:4, :]).astype(jnp.bfloat16)
        upstream = x_own[rows, :].astype(jnp.float32)
        a_all[aligned(2 * BLK + step * CHAIN, CHAIN), :] = row_back(
            upstream, hat, scale, gain_ref[3:4, :]
        ).astype(jnp.bfloat16)
        return gain_sum + column_sum(upstream * hat), bias_sum + column_sum(upstream)

    zero = jnp.zeros((1, D), jnp.float32)
    gain_sum, bias_sum = lax.fori_loop(0, BLK // CHAIN, outer_rows, (zero, zero))
    row = lax.broadcasted_iota(jnp.int32, (8, D), 0)
    norm_v[...] = jnp.where(row == 3, gain_sum, 0.0) + jnp.where(row == 7, bias_sum, 0.0)
    ends = [
        pltpu.make_async_copy(right.at[0], y_out, sem_in.at[0]),
        pltpu.make_async_copy(a_all.at[pl.ds(2 * BLK, BLK), :], dz_out, sem_in.at[1]),
        pltpu.make_async_copy(norm_v, norm_out, sem_in.at[2]),
    ]
    for copy in ends:
        copy.start()
    for tile in range(shallow_tiles - 2, shallow_tiles):
        for copy in tile_stores(tile, tile % 2):
            copy.wait()
    for copy in saves + ends:
        copy.wait()


def forward_part(n_ctx, tags, gains, biases, raw, dy, w_qkv, w_out, w_up, w_down):
    slots = n_ctx // 2
    every = (slots + 1) * BLK
    low, full = jnp.bfloat16, jnp.float32
    dma = pltpu.SemaphoreType.DMA
    hbm = pl.BlockSpec(memory_space=pl.ANY)
    vmem = pl.BlockSpec(memory_space=pltpu.VMEM)
    shards = (w_qkv, w_out, w_up, w_down)
    pieces = sum(w.shape[0] * w.shape[1] // (2 * PIECE * SPAN) for w in shards)
    own = w_qkv.shape[1] // SPAN + 3
    chain = slots * (BLK // CHAIN)
    shape = jax.ShapeDtypeStruct
    return pl.pallas_call(
        functools.partial(forward_kernel, n_ctx),
        out_shape=[
            shape((every, D), low),
            shape((BLK, D), low),
            shape((every, 2 * D), low),
            shape((BLK, D), low),
            shape((PAIRS, BLK, 128), full),
        ]
        + [shape((4 * w.shape[0], w.shape[1]), low) for w in shards]
        + [
            shape((BLK, D), low),
            shape((BLK, w_up.shape[1]), low),
            shape((BLK, D), low),
            shape((BLK, D), low),
            shape((BLK, w_up.shape[1]), low),
            shape((BLK, D), low),
            shape((BLK, D), low),
            shape((2, BLK, 128), full),
            shape((8, D), full),
        ],
        in_specs=[pl.BlockSpec(memory_space=pltpu.SMEM), vmem, vmem] + [hbm] * 6,
        out_specs=[hbm] * 18,
        scratch_shapes=[
            pltpu.VMEM((BLK, D), low),
            pltpu.VMEM((slots, BLK, D), low),
            pltpu.VMEM((slots, BLK, D), low),
            pltpu.VMEM((every, D), low),
            pltpu.VMEM((BLK, D), low),
            pltpu.VMEM((every, 2 * D), low),
            pltpu.VMEM((D, 3 * D), low),
            pltpu.VMEM((BLK, D), full),
            pltpu.VMEM((BLK, D), full),
            pltpu.VMEM((8, D), full),
            pltpu.VMEM((PAIRS, BLK, 128), full),
            pltpu.VMEM((PAIRS, BLK, 128), full),
            pltpu.VMEM((3, 2 * PIECE, SPAN), low),
            dma((3,)),
            dma((3,)),
            dma((3,)),
            dma((4, 2)),
            dma((4,)),
            dma((slots + 1,)),
            dma((slots + 1,)),
        ]
        + [dma((pieces,))] * 8
        + [dma((own,))] * 2
        + [dma((chain,))] * 4,
        compiler_params=pltpu.CompilerParams(
            collective_id=1, has_side_effects=True, vmem_limit_bytes=67043328
        ),
        cost_estimate=pl.CostEstimate(flops=20 << 30, bytes_accessed=64 << 20, transcendentals=1 << 24),
        name="gather_attend",
    )(tags, gains, biases, raw, dy, *shards)


TILE = 256
PAIRED = 2


def grad_block(q_ref, do_ref, o_ref, lse_ref, kv_ref, dq_acc, turned, pair, own, visible):
    lanes = aligned(pair * 128, 128)
    value_lanes = aligned(D + pair * 128, 128)
    size = QT if own else BLK
    count = BLK // size
    q_pair, do_pair, lse_pair = q_ref[:, lanes], do_ref[:, lanes], lse_ref[pair]
    prod = do_pair.astype(jnp.float32) * o_ref[:, lanes].astype(jnp.float32)
    keys, values = kv_ref[:, lanes], kv_ref[:, value_lanes]
    q_turned, do_turned = q_pair.T, do_pair.T
    old_dq = dq_acc[:, lanes]
    causal = causal_tile()
    hide = 0.0 if own else jnp.where(visible, 0.0, 1e30)
    lanes_of = [head_lanes(head, size) for head in range(2)]
    work = [(tile, head) for tile in range(count) for head in range(2)]
    score, dprob, dlogit, prob_low = {}, {}, {}, {}
    for tile, head in work:
        rows = slice(tile * size, (tile + 1) * size)
        span = (tile + 1) * size if own else BLK
        zero = jnp.zeros((size, 128), jnp.bfloat16)
        score[tile, head] = contract_last(jnp.where(lanes_of[head], q_pair[rows], zero), keys[:span])
        dprob[tile, head] = contract_last(jnp.where(lanes_of[head], do_pair[rows], zero), values[:span])
    for tile, head in work:
        rows = slice(tile * size, (tile + 1) * size)
        delta = jnp.sum(jnp.where(lanes_of[head], prod[rows], 0.0), axis=-1, keepdims=True)
        shift = lse_pair[rows, head * DH : head * DH + 1] + hide
        prob = jnp.exp2(score[tile, head] * C2 - shift)
        if own:
            diag = jnp.where(causal, prob[:, tile * size :], 0.0)
            prob = jnp.concatenate([prob[:, : tile * size], diag], axis=1) if tile else diag
        dlogit[tile, head] = (prob * (dprob[tile, head] - delta)).astype(jnp.bfloat16)
        prob_low[tile, head] = prob.astype(jnp.bfloat16)
    for tile in range(count):
        rows = slice(tile * size, (tile + 1) * size)
        span = (tile + 1) * size if own else BLK
        parts = [dot_dims(dlogit[tile, head], keys[:span], 1, 0) for head in range(2)]
        dq_acc[pl.ds(tile * size, size), lanes] = old_dq[rows] + jnp.where(lanes_of[0], parts[0], parts[1])
    for head in range(2):
        for offset, left_side, right_side, scale in (
            (0, q_turned, dlogit, ALPHA),
            (D, do_turned, prob_low, 1.0),
        ):
            spot = aligned(offset + pair * 128 + head * DH, DH)
            left_head = left_side[head * DH : (head + 1) * DH]
            terms = [
                dot_dims(left_head[:, tile * size : (tile + 1) * size], right_side[tile, head], 1, 0)
                for tile in range(count)
            ]
            for tile in range(count):
                cols = slice(tile * size, (tile + 1) * size)
                total = functools.reduce(
                    jnp.add, [terms[other][:, cols] for other in range(tile, count)]
                ) if own else terms[0]
                turned[spot, cols if own else slice(None)] = (total * scale).astype(jnp.bfloat16)


def backward_kernel(n_ctx, widths, *refs):
    slots = n_ctx // 2
    levels = n_ctx.bit_length() - 1
    depth = 16 if n_ctx == 4 else 10
    shallow = slots <= 2
    (slot_ref, gain_ref, norm_ref, x_hbm, q_hbm, kv_hbm, a_hbm, o_hbm, lse_hbm, w_hbm) = refs[:10]
    (w_out, w_up, w_down, g_hbm, dz_hbm, f_hbm, u_hbm, hat1_hbm, hat2_hbm, rstd_hbm, dy_hbm) = refs[10:21]
    outs = refs[21:25]
    grad_out, norm_out, dh_hbm, du_hbm, datt_hbm = refs[25:30]
    scratch = list(refs[30:])

    def take(count):
        taken = scratch[:count]
        del scratch[:count]
        return taken

    q_v, o_v, do_v, lse_v, weight, kv_b, a_b, dq_acc, turned, gkv, term, own_part, left, right, norm_v, norm_in = take(16)
    r1, r2, r3, fin, made = take(5)
    lhs, rhs = take(2)
    zbufs = take(levels)
    sem_in, sem_blk, sem_rhs, sem_lhs, sem_ff, sem_out, sem_res = take(7)
    send1, recv1, send2, recv2, send3, recv3, send6, recv6 = take(8)
    rs_send, rs_recv, ag_send, ag_recv = take(levels), take(levels), take(levels), take(levels)
    left_s, left_r, right_s, right_r, norm_s, norm_r = take(6)
    grp, ctx, wsh = lax.axis_index("grp"), lax.axis_index("ctx"), lax.axis_index("wsh")
    side, core = wsh // 2, wsh % 2
    core_peer = (grp, ctx, side * 2 + 1 - core)
    side_peer = (grp, ctx, (1 - side) * 2 + core)
    grp_peer = (1 - grp, ctx, wsh)
    next_ctx = (grp, lax.rem(ctx + 1, n_ctx), wsh)
    last_ctx = (grp, lax.rem(ctx + n_ctx - 1, n_ctx), wsh)
    bits = [(ctx // (1 << level)) % 2 for level in range(levels)]
    level_peers = [(grp, ctx + (1 - 2 * bits[level]) * (1 << level), wsh) for level in range(levels)]

    def block_copies(index):
        rows = aligned(lax.rem(index, slots + 1) * BLK, BLK)
        slot = lax.rem(index, kv_b.shape[0])
        return (
            pltpu.make_async_copy(kv_hbm.at[rows, :], kv_b.at[slot], sem_blk.at[0, slot]),
            pltpu.make_async_copy(a_hbm.at[rows, :], a_b.at[slot], sem_blk.at[1, slot]),
        )

    barrier = pltpu.get_barrier_semaphore()
    peers = [core_peer, side_peer, grp_peer, next_ctx, last_ctx] + level_peers
    for peer in peers:
        pl.semaphore_signal(barrier, inc=1, device_id=peer, device_id_type=MESH)
    pl.semaphore_wait(barrier, len(peers))

    half = TILE // 2
    ranges, first = [], 0
    for rows, cols in widths:
        across = cols // TILE
        ranges.append((first, first + (rows // TILE) * across, across))
        first = ranges[-1][1]
    chunks = first

    def by_range(index, act):
        for place, (low, high, across) in enumerate(ranges):

            @pl.when((index >= low) & (index < high))
            def _(place=place, low=low, across=across):
                number = index - low
                act(place, (aligned((number // across) * TILE, TILE), aligned((number % across) * TILE, TILE)))

    def region(level, flip):
        row, rows, col, cols = 0, half, 0, TILE
        for place in range(level):
            bit = 1 - bits[place] if (flip and place == level - 1) else bits[place]
            if rows > 16:
                rows = rows // 2
                row = row + bit * rows
            else:
                cols = cols // 2
                col = col + bit * cols
        return row, rows, col, cols

    def spot(level, flip=False, base=0):
        row, rows, col, cols = region(level, flip)
        return aligned(base + row, rows), aligned(col, cols)

    last_low = ranges[-1][0]
    set_of = [(0, number) for number in range(widths[0][0] // TILE)] + [(1, 0), (2, 0)]
    set_first = [number * ranges[0][2] for number in range(widths[0][0] // TILE)]
    set_first += [ranges[1][0], ranges[2][0]]
    left_of, right_of = (g_hbm, f_hbm, o_hbm), (dz_hbm, du_hbm, datt_hbm)

    def set_copies(number):
        place, group = set_of[number]
        stride = left_of[place].shape[1] // 4
        return [
            pltpu.make_async_copy(
                left_of[place].at[:, pl.ds(owner * stride + group * TILE, TILE)],
                lhs.at[number % 2, owner],
                sem_lhs.at[number % 2, owner],
            )
            for owner in range(4)
        ]

    def step_fetch(index):
        near = lax.rem(index, 4)

        def act(place, span):
            if place < 3:
                pltpu.make_async_copy(
                    right_of[place].at[:, span[1]], rhs.at[near], sem_rhs.at[near]
                ).start()

        by_range(index, act)

    def step_make(index):
        slot = lax.rem(index, depth)
        near = lax.rem(index, 4)

        @pl.when(index < last_low)
        def _():
            local_wait(rhs.at[near], sem_rhs.at[near])
            parity = jnp.int32(0)
            for number, low in enumerate(set_first):
                parity = jnp.where(index >= low, number % 2, parity)

                @pl.when(index == low)
                def _(number=number):
                    for copy in set_copies(number):
                        copy.wait()
                    if number + 1 < len(set_first):
                        for copy in set_copies(number + 1):
                            copy.start()

            right_side = rhs[near]
            for owner in range(4):
                made[near, owner // 2, owner % 2] = dot_dims(
                    lhs[parity, owner], right_side, 0, 0
                ).astype(jnp.bfloat16)

        @pl.when(index >= last_low)
        def _():
            span = aligned((index - last_low) * TILE, TILE)
            made[near] = term[:, :, :, span]

        remote(
            made.at[near, :, 1 - core], r1.at[slot], send1.at[slot], recv1.at[slot], core_peer
        ).start()

    def finished(move):
        move.wait_send()
        move.wait_recv()

    def step_core(index):
        slot, near = lax.rem(index, depth), lax.rem(index, 4)
        finished(remote(r1.at[slot], r1.at[slot], send1.at[slot], recv1.at[slot], core_peer))
        r1[slot] = r1[slot] + made[near, :, core]
        remote(r1.at[slot, 1 - side], r2.at[slot], send2.at[slot], recv2.at[slot], side_peer).start()

    keep_half = aligned(grp * half, half)
    give_half = aligned((1 - grp) * half, half)

    def step_side(index):
        slot = lax.rem(index, depth)
        finished(remote(r1.at[slot, 1 - side], r2.at[slot], send2.at[slot], recv2.at[slot], side_peer))
        r2[slot] = r2[slot] + r1[slot, side]
        remote(r2.at[slot, give_half], r3.at[slot], send3.at[slot], recv3.at[slot], grp_peer).start()

    fold = n_ctx == 4
    if fold:
        outer = bits[0] == bits[1]
        inner = bits[0] != bits[1]
        mate, middle = level_peers[0], (grp, 3 - ctx, wsh)
        quarter = half // 2
        mine, other = aligned(bits[1] * quarter, quarter), aligned((1 - bits[1]) * quarter, quarter)
        fin_mine = aligned(grp * half + bits[1] * quarter, quarter)
        fin_other = aligned(grp * half + (1 - bits[1]) * quarter, quarter)

        def up_copy(slot):
            return remote(r3.at[slot], zbufs[0].at[slot], rs_send[0].at[slot], rs_recv[0].at[slot], mate)

        def cross_copy(slot):
            return remote(
                r3.at[slot, other], zbufs[1].at[slot], rs_send[1].at[slot], rs_recv[1].at[slot], middle
            )

        def share_copy(slot, rows):
            here = fin.at[slot, rows]
            return remote(here, here, ag_send[1].at[slot], ag_recv[1].at[slot], middle)

        def down_copy(slot):
            here = fin.at[slot, keep_half]
            return remote(here, here, ag_send[0].at[slot], ag_recv[0].at[slot], mate)

        def step_up(index):
            slot = lax.rem(index, depth)

            @pl.when(outer)
            def _():
                up_copy(slot).wait_send()

            @pl.when(inner)
            def _():
                up_copy(slot).wait_recv()
                r3[slot] = r3[slot] + zbufs[0][slot]
                cross_copy(slot).start()

        def step_cross(index):
            slot = lax.rem(index, depth)

            @pl.when(inner)
            def _():
                finished(cross_copy(slot))
                fin[slot, fin_mine] = r3[slot, mine] + zbufs[1][slot]
                share_copy(slot, fin_mine).start()

        def step_share(index):
            slot = lax.rem(index, depth)

            @pl.when(inner)
            def _():
                finished(share_copy(slot, fin_other))
                down_copy(slot).start()

        def step_down(index):
            slot = lax.rem(index, depth)

            @pl.when(inner)
            def _():
                down_copy(slot).wait_send()

            @pl.when(outer)
            def _():
                down_copy(slot).wait_recv()

            back_copy(slot, keep_half).start()

    def rs_copy(level, slot):
        rows, cols = spot(level + 1, True)
        return remote(
            r3.at[slot, rows, cols], zbufs[level].at[slot], rs_send[level].at[slot], rs_recv[level].at[slot], level_peers[level]
        )

    def ag_copy(level, slot, flip=False):
        rows, cols = spot(level + 1, flip, grp * half)
        here = fin.at[slot, rows, cols]
        return remote(here, here, ag_send[level].at[slot], ag_recv[level].at[slot], level_peers[level])

    def back_copy(slot, rows):
        here = fin.at[slot, rows]
        return remote(here, here, send6.at[slot], recv6.at[slot], grp_peer)

    def step_grp(index):
        slot = lax.rem(index, depth)
        finished(remote(r2.at[slot, give_half], r3.at[slot], send3.at[slot], recv3.at[slot], grp_peer))
        r3[slot] = r3[slot] + r2[slot, keep_half]
        if fold:

            @pl.when(outer)
            def _():
                up_copy(slot).start()
        else:
            rs_copy(0, slot).start()

    def step_scatter(level):
        def act(index):
            slot = lax.rem(index, depth)
            finished(rs_copy(level, slot))
            rows, cols = spot(level + 1)
            total = r3[slot, rows, cols] + zbufs[level][slot]
            if level + 1 < levels:
                r3[slot, rows, cols] = total
                rs_copy(level + 1, slot).start()
            else:
                rows, cols = spot(level + 1, False, grp * half)
                fin[slot, rows, cols] = total
                ag_copy(level, slot).start()

        return act

    def step_gather(level):
        def act(index):
            slot = lax.rem(index, depth)
            finished(ag_copy(level, slot, True))
            if level:
                ag_copy(level - 1, slot).start()
            else:
                back_copy(slot, keep_half).start()

        return act

    def out_wait(index):
        slot = lax.rem(index, depth)
        local_wait(fin.at[slot], sem_out.at[slot])

    def step_out(index):
        slot = lax.rem(index, depth)
        finished(back_copy(slot, give_half))

        def act(place, span):
            pltpu.make_async_copy(fin.at[slot], outs[place].at[span[0], span[1]], sem_out.at[slot]).start()

        by_range(index, act)

    z_lag = 2 if fold else 1
    order = [(YLAG, step_side), (XLAG, step_grp)]
    if fold:
        order += [(z_lag, act) for act in (step_up, step_cross, step_share, step_down)]
    else:
        order += [(z_lag, step_scatter(level)) for level in range(levels)]
        order += [(z_lag, step_gather(level)) for level in reversed(range(levels))]
    order += [(BLAG, step_out), (2, out_wait)]
    stages = [(0, step_core)]
    for lag, act in order:
        stages.append((stages[-1][0] + lag, act))
    all_ticks = chunks + stages[-1][0]

    per_slot = BLK // CHAIN
    chain_chunks = slots * per_slot

    def chain_step(stream, send, recv, number, is_first, is_last, target):
        slot = number // per_slot
        rows = aligned((number % per_slot) * CHAIN, CHAIN)
        here = stream.at[slot, rows]

        @pl.when(is_first)
        def _():
            stream[slot, rows, :] = own_part[slot, rows, :]

        @pl.when(jnp.logical_not(is_first))
        def _():
            remote(here, here, send.at[number], recv.at[number], target).wait_recv()
            stream[slot, rows, :] = stream[slot, rows, :] + own_part[slot, rows, :]

        @pl.when(jnp.logical_not(is_last))
        def _():
            remote(here, here, send.at[number], recv.at[number], target).start()

    def chain_tick(step):
        number = step - ctx

        @pl.when((number >= 0) & (number < chain_chunks))
        def _():
            chain_step(left, left_s, left_r, number, ctx == 0, ctx == n_ctx - 1, next_ctx)

        back = step - (n_ctx - 1 - ctx)

        @pl.when((back >= 0) & (back < chain_chunks))
        def _():
            chain_step(right, right_s, right_r, back, ctx == n_ctx - 1, ctx == 0, last_ctx)

    groups = PAIRS // PAIRED
    block_ticks = groups + 2
    chain_first = FF_TICKS + block_ticks
    paced = max(0, -(-(chunks - chain_first) // PACE))
    chain_ticks = max(chunks, chain_first) + max(0, chain_chunks + n_ctx - 1 - paced)

    def tick(step):
        @pl.when(step + 3 < chunks)
        def _():
            step_fetch(step + 3)

        @pl.when(step + 2 < chunks)
        def _():
            step_make(step + 2)

        for lag, act in stages:
            index = step - lag

            @pl.when((index >= 0) & (index < chunks))
            def _(act=act, index=index):
                act(index)

        beat = step - chain_first

        @pl.when((beat >= 0) & (step < chunks) & (beat % PACE == 0))
        def _():
            chain_tick(beat // PACE)

        @pl.when((beat >= 0) & (step >= chunks))
        def _():
            chain_tick(paced + step - max(chunks, chain_first))


    for index in range(3):
        step_fetch(jnp.int32(index))
    for copy in set_copies(0):
        copy.start()

    hidden_tiles = u_hbm.shape[1] // SPAN
    datt_v, dz_v, dy_v, hat1_v, hat2_v = own_part.at[0], do_v, left.at[1], right.at[0], right.at[1]

    def tile_copies(tile, parity):
        cols = aligned(tile * SPAN, SPAN)
        return (
            pltpu.make_async_copy(w_down.at[cols, :], own_part.at[parity], sem_ff.at[0, parity]),
            pltpu.make_async_copy(
                w_up.at[:, cols], turned.at[aligned(parity * D, D), :], sem_ff.at[1, parity]
            ),
            pltpu.make_async_copy(
                u_hbm.at[:, cols], left.at[0, :, aligned(parity * SPAN, SPAN)], sem_ff.at[2, parity]
            ),
        )

    def du_store(tile, parity):
        return pltpu.make_async_copy(
            kv_b.at[0, :, aligned(parity * SPAN, SPAN)],
            du_hbm.at[:, aligned(tile * SPAN, SPAN)],
            sem_ff.at[3, parity],
        )

    dz_load = pltpu.make_async_copy(dz_hbm, dz_v, sem_in.at[0])
    dz_load.start()
    for copy in tile_copies(0, 0):
        copy.start()
    wide_loads = [
        pltpu.make_async_copy(source, dest, sem_in.at[place + 1])
        for place, (source, dest) in enumerate(
            (
                (dy_hbm, dy_v),
                (hat1_hbm, hat1_v),
                (hat2_hbm, hat2_v),
                (rstd_hbm, lse_v.at[pl.ds(0, 2)]),
                (q_hbm, q_v),
                (o_hbm, o_v),
                (w_hbm, weight),
            )
        )
    ]
    out_loads = [
        pltpu.make_async_copy(
            w_out.at[pl.ds(place * TILE, TILE), :],
            term.at[place // 2, place % 2, :, pl.ds(0, D)],
            sem_in.at[8 + place],
        )
        for place in range(4)
    ]
    for index in range(2):
        step_make(jnp.int32(index))
    dz_load.wait()

    def ff_tile(tile, carry):
        start = tile + (tile + 1) // 2
        tick(start)

        @pl.when(tile % 2 == 0)
        def _():
            tick(start + 1)

        parity = tile % 2
        for copy in tile_copies(tile, parity):
            copy.wait()

        @pl.when(tile + 1 < hidden_tiles)
        def _():
            for copy in tile_copies(tile + 1, 1 - parity):
                copy.start()

        @pl.when(tile == 0)
        def _():
            for copy in wide_loads + out_loads:
                copy.start()

        @pl.when(tile >= 2)
        def _():
            du_store(tile - 2, parity).wait()

        u_cols = aligned(parity * SPAN, SPAN)
        u_tile = left[0, :, u_cols].astype(jnp.float32)
        square = u_tile * u_tile
        bend = jnp.tanh(GELU_C * u_tile * (1.0 + GELU_A * square))
        slope = 0.5 * (1.0 + bend) + (0.5 * GELU_C) * u_tile * (1.0 - bend * bend) * (
            1.0 + 3.0 * GELU_A * square
        )
        du_tile = (contract_last(dz_v[...], own_part[parity]) * slope).astype(jnp.bfloat16)
        kv_b[0, :, u_cols] = du_tile
        du_store(tile, parity).start()
        fresh = contract_last(du_tile, turned[aligned(parity * D, D), :])

        @pl.when(tile == 0)
        def _():
            dq_acc[...] = fresh

        @pl.when(tile > 0)
        def _():
            dq_acc[...] = dq_acc[...] + fresh

        return carry

    lax.fori_loop(0, hidden_tiles, ff_tile, 0)
    for tile in range(hidden_tiles - 2, hidden_tiles):
        du_store(tile, tile % 2).wait()
    for copy in wide_loads:
        copy.wait()
    for copy in block_copies(1):
        copy.start()

    def hidden_back(step, carry):
        gain1, gain2, bias1, bias2 = carry
        rows = aligned(step * CHAIN, CHAIN)
        upstream = dq_acc[rows, :]
        hat = hat2_v[rows, :].astype(jnp.float32)
        grad_h = dy_v[rows, :].astype(jnp.float32) + row_back(
            upstream, hat, lse_v[1, rows, 0:1], gain_ref[2:3, :]
        )
        gain2, bias2 = gain2 + column_sum(upstream * hat), bias2 + column_sum(upstream)
        dq_acc[rows, :] = grad_h
        hat = hat1_v[rows, :].astype(jnp.float32)
        datt_v[rows, :] = row_back(grad_h, hat, lse_v[0, rows, 0:1], gain_ref[1:2, :]).astype(
            jnp.bfloat16
        )
        return gain1 + column_sum(grad_h * hat), gain2, bias1 + column_sum(grad_h), bias2

    zero = jnp.zeros((1, D), jnp.float32)
    sums = lax.fori_loop(0, BLK // CHAIN, hidden_back, (zero,) * 4)
    row = lax.broadcasted_iota(jnp.int32, (8, D), 0)
    norm_v[...] = norm_ref[...]
    for place, value in zip((1, 2, 5, 6), sums):
        norm_v[...] = norm_v[...] + jnp.where(row == place, value, 0.0)
    tick(FF_TICKS - 1)
    stores = [
        pltpu.make_async_copy(dq_acc, dh_hbm, sem_res.at[0]),
        pltpu.make_async_copy(datt_v, datt_hbm, sem_res.at[1]),
    ]
    lse_load = pltpu.make_async_copy(lse_hbm, lse_v, sem_in.at[0])
    for copy in stores + [lse_load]:
        copy.start()
    for place in range(4):
        out_loads[place].wait()
        do_v[:, pl.ds(place * TILE, TILE)] = contract_last(
            datt_v[...], term[place // 2, place % 2, :, pl.ds(0, D)]
        ).astype(jnp.bfloat16)
    for copy in stores + [lse_load]:
        copy.wait()
    dq_acc[...] = jnp.zeros_like(dq_acc)

    def attend(kv_ref, own, visible, begin):
        def body(group, carry):
            tick(begin + group)
            for member in range(PAIRED):
                grad_block(
                    q_v, do_v, o_v, lse_v, kv_ref, dq_acc, turned, group * PAIRED + member, own, visible
                )
            return carry

        lax.fori_loop(0, groups, body, 0)

    def each_slot(slot, carry):
        visible = slot < slot_ref[0]
        index = slot + 1
        place = lax.rem(index, kv_b.shape[0])
        for copy in block_copies(index):
            copy.wait()
        if kv_b.shape[0] > 1:
            for copy in block_copies(index + 1):
                copy.start()
        begin = FF_TICKS + slot * block_ticks
        attend(kv_b.at[place], False, visible, begin)

        def weight_terms(step, inner):
            tick(begin + groups + step)
            rows = aligned(step * 512, 512)
            for part in range(2):
                cols = pl.ds(part * D, D)
                product = dot_dims(a_b[place, :, rows], turned[cols, :], 0, 1)
                for down in range(2):
                    if shallow:
                        target = gkv.at[aligned(step * 512 + down * TILE, TILE), cols]
                    else:
                        target = term.at[step, down, :, pl.ds((part + 1) * D, D)]
                    piece = product[down * TILE : (down + 1) * TILE]

                    @pl.when(slot == 0)
                    def _(target=target, piece=piece):
                        target[...] = piece.astype(target.dtype)

                    @pl.when(slot > 0)
                    def _(target=target, piece=piece):
                        target[...] = (target[...] + piece).astype(target.dtype)

            own_part[slot, :, rows] = dot_dims(
                turned[...], weight[rows, pl.ds(D, 2 * D)], 0, 1
            ).astype(jnp.bfloat16)
            return inner

        lax.fori_loop(0, 2, weight_terms, 0)
        if kv_b.shape[0] == 1:
            for copy in block_copies(index + 1):
                copy.start()
        return carry

    lax.fori_loop(0, slots, each_slot, 0)
    begin = FF_TICKS + slots * block_ticks
    own_place = (slots + 1) % kv_b.shape[0]
    for copy in block_copies(slots + 1):
        copy.wait()
    attend(kv_b.at[own_place], True, None, begin)
    dq_low = o_v
    dq_low[...] = (dq_acc[...] * ALPHA).astype(jnp.bfloat16) * jnp.bfloat16(QSCALE)
    x_load = pltpu.make_async_copy(x_hbm, do_v, sem_in.at[0])
    x_load.start()
    if shallow:
        hidden_load = pltpu.make_async_copy(dh_hbm, gkv.at[pl.ds(0, BLK), pl.ds(0, D)], sem_in.at[1])

    def last_terms(step, carry):
        tick(begin + groups + step)
        rows = aligned(step * TILE, TILE)
        a_rows = a_b[own_place, :, rows]
        up, down = step // 2, step % 2
        term[up, down, :, pl.ds(0, D)] = dot_dims(a_rows, dq_low[...], 0, 0).astype(jnp.bfloat16)
        for part in range(2):
            cols = pl.ds(part * D, D)
            target = term.at[up, down, :, pl.ds((part + 1) * D, D)]
            earlier = gkv[rows, cols] if shallow else target[...]
            target[...] = (earlier + dot_dims(a_rows, turned[cols, :], 0, 1)).astype(jnp.bfloat16)
        return carry

    lax.fori_loop(0, 4, last_terms, 0)
    if shallow:
        hidden_load.start()
    ready = begin + groups + 4
    assert ready <= ranges[-1][0] - 2 or n_ctx > 4
    da_acc = dq_acc

    def own_grad(step, carry):
        tick(ready + step)
        rows = aligned(step * TILE, TILE)
        da_acc[:, rows] = dot_dims(dq_low[...], weight[rows, pl.ds(0, D)], 1, 1) + dot_dims(
            turned[...], weight[rows, pl.ds(D, 2 * D)], 0, 1
        )
        return carry

    lax.fori_loop(0, 4, own_grad, 0)
    ready = ready + 4

    def flush_chain(step, carry):
        tick(ready + step)
        return carry

    left_over = max(0, chain_ticks - ready)
    lax.fori_loop(0, left_over, flush_chain, 0)
    ready = ready + left_over
    x_load.wait()
    if shallow:
        hidden_load.wait()
    gain = gain_ref[0:1, :]

    def norm_grad(step, carry):
        gain_sum, bias_sum = carry

        @pl.when(step % 2 == 0)
        def _():
            tick(ready + step // 2)

        rows = aligned(step * CHAIN, CHAIN)
        upstream = da_acc[rows, :]
        for slot in range(slots):
            joined = left[slot, rows, :].astype(jnp.float32) + right[slot, rows, :].astype(jnp.float32)
            upstream = upstream + jnp.where(slot_ref[0] == slot, joined, 0.0)
        values = do_v[rows, :].astype(jnp.float32)
        centre = values - jnp.mean(values, axis=-1, keepdims=True)
        scale = lax.rsqrt(jnp.mean(centre * centre, axis=-1, keepdims=True) + EPS)
        centre = centre * scale
        grad = row_back(upstream, centre, scale, gain)
        da_acc[rows, :] = grad + gkv[rows, pl.ds(0, D)] if shallow else grad
        return gain_sum + column_sum(upstream * centre), bias_sum + column_sum(upstream)

    gain_sum, bias_sum = lax.fori_loop(0, BLK // CHAIN, norm_grad, (zero, zero))
    ready = ready + BLK // CHAIN // 2
    result = pltpu.make_async_copy(da_acc, grad_out, sem_res.at[0])
    result.start()
    norm_v[...] = norm_v[...] + jnp.where(row == 0, gain_sum, 0.0) + jnp.where(row == 4, bias_sum, 0.0)
    for place, peer in enumerate([core_peer, side_peer, grp_peer] + level_peers):
        move = remote(norm_v, norm_in.at[place], norm_s.at[place], norm_r.at[place], peer)
        move.start()
        tick(ready)
        tick(ready + 1)
        ready = ready + 2
        finished(move)
        norm_v[...] = norm_v[...] + norm_in[place]
    norm_result = pltpu.make_async_copy(norm_v, norm_out, sem_res.at[1])
    norm_result.start()
    if all_ticks > ready:
        lax.fori_loop(ready, all_ticks, lambda index, carry: (tick(index), carry)[1], 0)

    def drain_chain(index, carry):
        here = left.at[0, pl.ds(0, CHAIN)]

        @pl.when(ctx < n_ctx - 1)
        def _():
            remote(here, here, left_s.at[index], left_r.at[index], next_ctx).wait_send()

        @pl.when(ctx > 0)
        def _():
            remote(here, here, right_s.at[index], right_r.at[index], last_ctx).wait_send()

        return carry

    lax.fori_loop(0, chain_chunks, drain_chain, 0)
    result.wait()
    norm_result.wait()


def backward_part(n_ctx, slot_vec, gains, norms, saved, weights, ffn):
    slots = n_ctx // 2
    levels = n_ctx.bit_length() - 1
    depth = 16 if n_ctx == 4 else 10
    hidden = weights[1].shape[1]
    widths = [(hidden // 4, D), (D // 4, hidden), (D // 4, D), (D // 4, 3 * D)]
    low, full = jnp.bfloat16, jnp.float32
    dma = pltpu.SemaphoreType.DMA
    hbm = pl.BlockSpec(memory_space=pl.ANY)
    vmem = pl.BlockSpec(memory_space=pltpu.VMEM)
    shape = jax.ShapeDtypeStruct
    buffers = 2 if slots <= 2 else 1
    chain = slots * (BLK // CHAIN)
    zshapes, rows, cols = [], TILE // 2, TILE
    if n_ctx == 4:
        zshapes = [pltpu.VMEM((depth, rows, cols), low), pltpu.VMEM((depth, rows // 2, cols), low)]
    for _ in range(0 if zshapes else levels):
        rows, cols = (rows // 2, cols) if rows > 16 else (rows, cols // 2)
        zshapes.append(pltpu.VMEM((depth, rows, cols), low))
    return pl.pallas_call(
        functools.partial(backward_kernel, n_ctx, widths),
        out_shape=[shape(width, low) for width in widths] + [
            shape((BLK, D), full),
            shape((8, D), full),
            shape((BLK, D), full),
            shape((BLK, hidden), low),
            shape((BLK, D), low),
        ],
        in_specs=[pl.BlockSpec(memory_space=pltpu.SMEM), vmem, vmem]
        + [hbm] * (len(saved) + len(weights) + len(ffn)),
        out_specs=[hbm] * 9,
        scratch_shapes=[
            pltpu.VMEM((BLK, D), low),
            pltpu.VMEM((BLK, D), low),
            pltpu.VMEM((BLK, D), low),
            pltpu.VMEM((PAIRS, BLK, 128), full),
            pltpu.VMEM((D, 3 * D), low),
            pltpu.VMEM((buffers, BLK, 2 * D), low),
            pltpu.VMEM((buffers, BLK, D), low),
            pltpu.VMEM((BLK, D), full),
            pltpu.VMEM((2 * D, BLK), low),
            pltpu.VMEM((D, 2 * D) if slots <= 2 else (8, 128), full),
            pltpu.VMEM((2, 2, D // 4, 3 * D), low),
            pltpu.VMEM((slots, BLK, D), low),
            pltpu.VMEM((slots, BLK, D), low),
            pltpu.VMEM((slots, BLK, D), low),
            pltpu.VMEM((8, D), full),
            pltpu.VMEM((3 + levels, 8, D), full),
            pltpu.VMEM((depth, 2, TILE, TILE), low),
            pltpu.VMEM((depth, TILE, TILE), low),
            pltpu.VMEM((depth, TILE // 2, TILE), low),
            pltpu.VMEM((depth, TILE, TILE), low),
            pltpu.VMEM((4, 2, 2, TILE, TILE), low),
        ]
        + [pltpu.VMEM((2, 4, BLK, TILE), low), pltpu.VMEM((4, BLK, TILE), low)]
        + zshapes
        + [dma((12,)), dma((2, buffers)), dma((4,)), dma((2, 4)), dma((4, 2)), dma((depth,)), dma((2,))]
        + [dma((depth,))] * (8 + 4 * levels)
        + [dma((chain,))] * 4
        + [dma((3 + levels,))] * 2,
        compiler_params=pltpu.CompilerParams(
            collective_id=2, has_side_effects=True, vmem_limit_bytes=67043328
        ),
        cost_estimate=pl.CostEstimate(flops=40 << 30, bytes_accessed=64 << 20, transcendentals=1 << 24),
        name="attend_back_reduce",
    )(
        slot_vec,
        gains,
        norms,
        *saved,
        *weights,
        *ffn,
    )


def per_device(n_ctx, inputs, w_qkv, w_out, w_up, w_down, norm_gains, norm_biases, block_map, out_grad):
    slots = n_ctx // 2
    raw, seed_low = inputs.reshape(BLK, D), out_grad.reshape(BLK, D)
    block_entry = block_map.reshape(2)
    own_slot = block_entry[1] // BLK
    own_tag = jnp.where(block_entry[0] == 0, own_slot, n_ctx)
    forward = forward_part(
        n_ctx,
        jnp.stack([own_slot, own_tag]),
        norm_gains,
        norm_biases,
        raw,
        seed_low,
        w_qkv,
        w_out,
        w_up,
        w_down,
    )
    every_low, queries, keys_values, attn_low, lse, full_qkv, full_out, full_up, full_down = forward[:9]
    result, active_low, down_low, ffn_low, upward, hat1, hat2, rstd, norms = forward[9:]
    backward = backward_part(
        n_ctx,
        own_slot.reshape(1),
        norm_gains,
        norms,
        [raw, queries, keys_values, every_low, attn_low, lse, full_qkv],
        [full_out, full_up, full_down],
        [active_low, down_low, ffn_low, upward, hat1, hat2, rstd, seed_low],
    )
    summed_down, summed_up, summed_out, summed_qkv = (
        total.astype(jnp.float32) for total in backward[:4]
    )
    grad_tokens, norm_total, grad_hidden = backward[4:7]
    grad_input = grad_tokens if slots <= 2 else grad_tokens + grad_hidden
    return (
        result.reshape(1, 1, BLK, D),
        grad_input.reshape(1, 1, BLK, D),
        summed_qkv,
        summed_out,
        summed_up,
        summed_down,
        norm_total[:4],
        norm_total[4:],
    )


def solution(mesh):
    rows = P("wsh", None)
    blocks = P("grp", "wsh", "ctx", None)
    return jax.shard_map(
        functools.partial(per_device, mesh.shape["ctx"]),
        mesh=mesh,
        in_specs=(blocks, rows, rows, rows, rows, P(), P(), blocks, blocks),
        out_specs=(blocks, blocks, rows, rows, rows, rows, P(), P()),
        check_vma=False,
    )
```

```python
import functools
import math

import jax
import jax.numpy as jnp
from jax import lax
from jax.experimental import pallas as pl
from jax.experimental.pallas import tpu as pltpu
from jax.sharding import PartitionSpec as P

D = 1024
HEADS = 16
DH = 64
BLK = 512
PAIRS = HEADS // 2
QT = 256

EPS = 1e-05
ALPHA = 32.0
NEG = -1e30
LOG2E = 1.4426950408889634
C2 = ALPHA * LOG2E
MESH = pl.DeviceIdType.MESH
QSCALE = 1.0 / (ALPHA * math.sqrt(DH))


def layer_norm(values, gain_row, bias_row):
    centre = values - jnp.mean(values, axis=-1, keepdims=True)
    spread = jnp.mean(centre * centre, axis=-1, keepdims=True)
    return centre * lax.rsqrt(spread + EPS) * gain_row + bias_row


def dot_dims(left_side, right_side, left_dim, right_dim):
    return lax.dot_general(
        left_side,
        right_side,
        (((left_dim,), (right_dim,)), ((), ())),
        preferred_element_type=jnp.float32,
    )


def contract_last(left_side, right_side):
    return dot_dims(left_side, right_side, 1, 1)


def contract_rows(left_side, right_side):
    return dot_dims(left_side, right_side, 0, 0)


def standard_rows(values):
    centre = values - jnp.mean(values, axis=-1, keepdims=True)
    scale = lax.rsqrt(jnp.mean(centre * centre, axis=-1, keepdims=True) + EPS)
    return centre * scale, scale


def row_back(upstream, hat, scale, gain):
    scaled = upstream * gain
    return scale * (
        scaled
        - jnp.mean(scaled, axis=-1, keepdims=True)
        - hat * jnp.mean(scaled * hat, axis=-1, keepdims=True)
    )


def column_sum(values):
    return jnp.sum(values, axis=0, keepdims=True)


def head_lanes(head, rows):
    lane = lax.broadcasted_iota(jnp.int32, (rows, 128), 1)
    return (lane >= DH) if head else (lane < DH)


def causal_tile():
    row = lax.broadcasted_iota(jnp.int32, (QT, QT), 0)
    col = lax.broadcasted_iota(jnp.int32, (QT, QT), 1)
    return col <= row


PIECE = 128
SPAN = 512
CHAIN = 64
HOP = 2
YLAG = 3
XLAG = 2
BLAG = 2
FF_TICKS = 13
TAIL_PACE = 3
GELU_A = 0.044715
GELU_C = math.sqrt(2.0 / math.pi)
PACE = 2
LAG = 2
GROUP = 4
AHEAD = 4


def remote(src, dst, send, recv, peer):
    return pltpu.make_async_remote_copy(
        src_ref=src, dst_ref=dst, send_sem=send, recv_sem=recv, device_id=peer, device_id_type=MESH
    )


def local_wait(ref, sem):
    pltpu.make_async_copy(ref, ref, sem).wait()


def aligned(start, size):
    return pl.ds(pl.multiple_of(start, size), size)


def softmax_block(q_ref, kv_ref, acc, top_ref, sum_ref, pair, base, own, visible):
    lanes = aligned(pair * 128, 128)
    value_lanes = aligned(D + pair * 128, 128)
    causal = causal_tile()
    first = head_lanes(0, QT)
    count = BLK // QT
    q_pair = q_ref[:, lanes]
    keys = kv_ref[pl.ds(base, BLK), lanes]
    values = kv_ref[pl.ds(base, BLK), value_lanes]
    if not own:
        old_top, old_sum, old_out = top_ref[pair], sum_ref[pair], acc[:, lanes]
        hide = jnp.where(visible, 0.0, 1e30)
    results = []
    work = [(tile, head) for tile in range(count) for head in range(2)]
    parts_of = {}
    for tile, head in work:
        q_tile = q_pair[tile * QT : (tile + 1) * QT]
        q_head = jnp.where(head_lanes(head, QT), q_tile, jnp.zeros_like(q_tile))
        span = (tile + 1) * QT if own else BLK
        parts_of[tile, head] = contract_last(q_head, keys[:span])
    top_of, expo_of, total_of = {}, {}, {}
    for tile, head in work:
        part = parts_of[tile, head]
        if own:
            diag = jnp.where(causal, part[:, tile * QT :], NEG)
            part = jnp.concatenate([part[:, : tile * QT], diag], axis=1) if tile else diag
        top = jnp.max(part, axis=-1, keepdims=True) * C2
        if own:
            shift = top
        else:
            top = jnp.maximum(
                jnp.where(visible, top, NEG), old_top[tile * QT : (tile + 1) * QT, head * DH : head * DH + 1]
            )
            shift = top + hide
        expo = jnp.exp2(part * C2 - shift)
        top_of[tile, head] = jnp.broadcast_to(top, (QT, 128))
        total_of[tile, head] = jnp.broadcast_to(jnp.sum(expo, axis=-1, keepdims=True), (QT, 128))
        expo_of[tile, head] = expo.astype(jnp.bfloat16)
    out_of = {}
    for tile, head in work:
        span = (tile + 1) * QT if own else BLK
        out_of[tile, head] = dot_dims(expo_of[tile, head], values[:span], 1, 0)
    for tile in range(count):
        rows = pl.ds(tile * QT, QT)
        new_top = jnp.where(first, top_of[tile, 0], top_of[tile, 1])
        new_sum = jnp.where(first, total_of[tile, 0], total_of[tile, 1])
        new_out = jnp.where(first, out_of[tile, 0], out_of[tile, 1])
        if not own:
            here = slice(tile * QT, (tile + 1) * QT)
            keep = jnp.exp2(old_top[here] - new_top)
            new_sum = new_sum + old_sum[here] * keep
            new_out = new_out + old_out[here] * keep
        top_ref[pair, rows, :] = new_top
        sum_ref[pair, rows, :] = new_sum
        acc[rows, lanes] = new_out


def forward_kernel(n_ctx, *refs):
    slots = n_ctx // 2
    (slot_ref, gain_ref, bias_ref, x_hbm, dy_hbm, w_qkv, w_out, w_up, w_down) = refs[:9]
    (a_out, q_out, kv_out, o_out, lse_out, full_qkv, full_out, full_up, full_down) = refs[9:18]
    (y_out, g_out, dz_out, f_out, u_out, hat1_out, hat2_out, rstd_out, norm_out) = refs[18:27]
    (x_own, left, right, a_all, q_all, kv_all, weight, acc, z_acc, norm_v, tops, sums, hop) = refs[27:40]
    (sem_in, sem_load, sem_store, sem_ff, sem_out, sem_a, sem_kv, side_s, side_r, grp_s, grp_r, cs_s, cs_r, cg_s, cg_r, own_s, own_r, left_s, left_r, right_s, right_r) = refs[40:]
    grp, ctx, wsh = lax.axis_index("grp"), lax.axis_index("ctx"), lax.axis_index("wsh")
    side, core = wsh // 2, wsh % 2
    core_peer = (grp, ctx, side * 2 + 1 - core)
    side_peer = (grp, ctx, (1 - side) * 2 + core)
    grp_peer = (1 - grp, ctx, wsh)
    next_ctx = (grp, lax.rem(ctx + 1, n_ctx), wsh)
    last_ctx = (grp, lax.rem(ctx + n_ctx - 1, n_ctx), wsh)

    load = pltpu.make_async_copy(x_hbm, x_own, sem_in.at[0])
    load.start()
    barrier = pltpu.get_barrier_semaphore()
    for peer in (core_peer, side_peer, grp_peer, next_ctx, last_ctx):
        pl.semaphore_signal(barrier, inc=1, device_id=peer, device_id_type=MESH)
    pl.semaphore_wait(barrier, 5)

    shards = (w_qkv, w_out, w_up, w_down)
    fulls = (weight, full_out, full_up, full_down)
    ranges, start = [], 0
    for shard in shards:
        across = shard.shape[1] // SPAN
        ranges.append((start, start + across * (shard.shape[0] // (2 * PIECE)), across))
        start = ranges[-1][1]
    pieces = start

    def by_range(index, act):
        for place, (low, high, across) in enumerate(ranges):

            @pl.when((index >= low) & (index < high))
            def _(place=place, low=low, across=across):
                act(place, (index - low) // across, aligned(((index - low) % across) * SPAN, SPAN))

    def rows_of(place, owner, half, group):
        shard_rows = shards[place].shape[0]
        return aligned(owner * shard_rows + half * (shard_rows // 2) + group * PIECE, PIECE)

    sides_owner = (1 - side) * 2 + core

    def send_piece(index, carry):
        def act(place, group, cols):
            remote(
                shards[place].at[rows_of(place, 0, grp, group), cols],
                fulls[place].at[rows_of(place, wsh, grp, group), cols],
                side_s.at[index],
                side_r.at[index],
                side_peer,
            ).start()

        by_range(index, act)
        return carry

    def own_copies():
        copies = []
        across = shards[0].shape[1] // SPAN
        for place in range(4):
            shard_rows = shards[place].shape[0]
            mine = aligned(wsh * shard_rows, shard_rows)
            steps = range(across) if place == 0 else [None]
            for step in steps:
                cols = slice(None) if step is None else pl.ds(step * SPAN, SPAN)
                number = len(copies)
                copies.append(
                    remote(
                        shards[place].at[:, cols],
                        fulls[place].at[mine, cols],
                        own_s.at[number],
                        own_r.at[number],
                        core_peer,
                    )
                )
        return copies

    for index in range(AHEAD):
        send_piece(index, 0)
    for copy in own_copies():
        copy.start()
    own_rows = aligned(wsh * w_qkv.shape[0], w_qkv.shape[0])
    own_weight = pltpu.make_async_copy(w_qkv, weight.at[own_rows, :], sem_in.at[1])
    own_weight.start()
    load.wait()

    bounces, start = [], 0
    for shard in shards[1:]:
        across = shard.shape[1] // SPAN
        bounces.append((start, start + across * (shard.shape[0] // (2 * PIECE)), across))
        start = bounces[-1][1]
    moves = start

    def bounce(index, loading):
        slot = lax.rem(index, 3)
        for place, (low, high, across) in enumerate(bounces):

            @pl.when((index >= low) & (index < high))
            def _(place=place + 1, low=low, across=across):
                group = (index - low) // across
                cols = aligned(((index - low) % across) * SPAN, SPAN)
                if loading:
                    here = shards[place].at[aligned(group * 2 * PIECE, 2 * PIECE), cols]
                    pltpu.make_async_copy(here, hop.at[slot], sem_load.at[slot]).start()
                else:
                    rows = aligned(wsh * shards[place].shape[0] + group * 2 * PIECE, 2 * PIECE)
                    local_wait(hop.at[slot], sem_load.at[slot])
                    pltpu.make_async_copy(
                        hop.at[slot], fulls[place].at[rows, cols], sem_store.at[slot]
                    ).start()

    own_slot = slot_ref[1] // BLK
    own_tag = jnp.where(slot_ref[0] == 0, own_slot, n_ctx)
    chain_chunks = slots * (BLK // CHAIN)

    def chain_step(stream, send, recv, number, is_first, is_last, target):
        slot = number // (BLK // CHAIN)
        spot = aligned((number % (BLK // CHAIN)) * CHAIN, CHAIN)
        mine = jnp.where(own_tag == slot, x_own[spot, :], jnp.zeros((CHAIN, D), jnp.bfloat16))
        here = stream.at[slot, spot]

        @pl.when(is_first)
        def _():
            stream[slot, spot, :] = mine

        @pl.when(jnp.logical_not(is_first))
        def _():
            remote(here, here, send.at[number], recv.at[number], target).wait_recv()
            stream[slot, spot, :] = stream[slot, spot, :] + mine

        @pl.when(jnp.logical_not(is_last))
        def _():
            remote(here, here, send.at[number], recv.at[number], target).start()

    def tick(step):
        @pl.when((step >= 1) & (step <= moves))
        def _():
            bounce(step - 1, False)

        @pl.when((step >= 3) & (step < moves))
        def _():
            local_wait(hop.at[lax.rem(step, 3)], sem_store.at[lax.rem(step, 3)])

        @pl.when(step < moves)
        def _():
            bounce(step, True)

        @pl.when(step + AHEAD < pieces)
        def _():
            send_piece(step + AHEAD, 0)

        number = step - HOP * ctx

        @pl.when((number >= 0) & (number < chain_chunks))
        def _():
            chain_step(left, left_s, left_r, number, ctx == 0, ctx == n_ctx - 1, next_ctx)

        back = step - HOP * (n_ctx - 1 - ctx)

        @pl.when((back >= 0) & (back < chain_chunks))
        def _():
            chain_step(right, right_s, right_r, back, ctx == n_ctx - 1, ctx == 0, last_ctx)

        @pl.when(step < pieces)
        def _():
            def act(place, group, cols):
                here = fulls[place].at[rows_of(place, sides_owner, grp, group), cols]
                remote(here, here, side_s.at[step], side_r.at[step], side_peer).wait_recv()
                remote(here, here, grp_s.at[step], grp_r.at[step], grp_peer).start()
                remote(here, here, cs_s.at[step], cs_r.at[step], core_peer).start()

            by_range(step, act)

        late = step - LAG

        @pl.when((late >= 0) & (late < pieces))
        def _():
            def act(place, group, cols):
                here = fulls[place].at[rows_of(place, sides_owner, 1 - grp, group), cols]
                remote(here, here, grp_s.at[late], grp_r.at[late], grp_peer).wait_recv()
                remote(here, here, cg_s.at[late], cg_r.at[late], core_peer).start()

            by_range(late, act)

    def normalise(source, dest):
        gain, bias = gain_ref[0:1, :], bias_ref[0:1, :]

        def body(index, carry):
            rows = aligned(index * 128, 128)
            values = source(rows).astype(jnp.float32)
            a_all[aligned(dest + index * 128, 128), :] = layer_norm(values, gain, bias).astype(
                jnp.bfloat16
            )
            return carry

        lax.fori_loop(0, BLK // 128, body, 0)

    def piece_ready(index):
        here = fulls[0].at[pl.ds(0, PIECE), pl.ds(0, SPAN)]
        remote(here, here, cs_s.at[index], cs_r.at[index], core_peer).wait_recv()
        remote(here, here, cg_s.at[index], cg_r.at[index], core_peer).wait_recv()
        whole = fulls[0].at[pl.ds(0, 2 * PIECE), pl.ds(0, SPAN)]
        remote(whole, whole, own_s.at[index], own_r.at[index], core_peer).wait_recv()

    tick(0)
    normalise(lambda rows: x_own[rows, :], 0)
    for step in range(1, LAG + 1):
        tick(step)
    own_weight.wait()

    def project_q(index, carry):
        tick(index + LAG + 1)
        piece_ready(index)
        cols = aligned(index * SPAN, SPAN)
        q_all[:, cols] = (
            jnp.dot(a_all[pl.ds(0, BLK), :], weight[:, cols], preferred_element_type=jnp.float32) * QSCALE
        ).astype(jnp.bfloat16)
        return carry

    lax.fori_loop(0, D // SPAN, project_q, 0)
    head_ticks = LAG + 1 + D // SPAN

    def project_kv(index, base):
        cols = aligned(index * SPAN, SPAN)
        rows = aligned(base, BLK)
        kv_all[rows, cols] = jnp.dot(
            a_all[rows, :], weight[:, aligned(D + index * SPAN, SPAN)], preferred_element_type=jnp.float32
        ).astype(jnp.bfloat16)

    def own_kv(index, carry):
        tick(index + head_ticks)
        piece_ready(index + D // SPAN)
        project_kv(index, 0)
        return carry

    lax.fori_loop(0, 2 * D // SPAN, own_kv, 0)
    own_ticks = head_ticks + 2 * D // SPAN

    def send_block(index):
        rows = aligned(index * BLK, BLK)
        pltpu.make_async_copy(a_all.at[rows, :], a_out.at[rows, :], sem_a.at[index]).start()
        pltpu.make_async_copy(kv_all.at[rows, :], kv_out.at[rows, :], sem_kv.at[index]).start()

    outputs = [
        pltpu.make_async_copy(weight, full_qkv, sem_out.at[0]),
        pltpu.make_async_copy(q_all, q_out, sem_out.at[1]),
    ]
    for copy in outputs:
        copy.start()

    send_block(0)

    def own_attention(group, carry):
        tick(own_ticks + 2 * group)
        tick(own_ticks + 2 * group + 1)
        for member in range(GROUP):
            softmax_block(q_all, kv_all, acc, tops, sums, group * GROUP + member, 0, True, None)
        return carry

    groups = PAIRS // GROUP
    lax.fori_loop(0, groups, own_attention, 0)
    used = own_ticks + 2 * groups
    per_slot = 2 * D // SPAN + 2 * groups

    need = BLK // CHAIN + HOP * (n_ctx - 1)
    early = max(0, need - used)
    if early:
        lax.fori_loop(0, early, lambda index, carry: (tick(used + index), carry)[1], 0)

    def each_slot(slot, carry):
        base = pl.multiple_of((slot + 1) * BLK, BLK)
        visible = slot < own_slot
        begin = early + used + slot * per_slot

        def total(rows):
            joined = left[slot, rows, :] + right[slot, rows, :]
            return jnp.where(own_tag == slot, x_own[rows, :], joined)

        normalise(total, base)

        def slot_kv(index, inner):
            tick(begin + index)
            project_kv(index, base)
            return inner

        lax.fori_loop(0, 2 * D // SPAN, slot_kv, 0)

        send_block(slot + 1)

        def slot_attention(group, inner):
            tick(begin + 2 * D // SPAN + 2 * group)
            tick(begin + 2 * D // SPAN + 2 * group + 1)
            for member in range(GROUP):
                softmax_block(
                    q_all, kv_all, acc, tops, sums, group * GROUP + member, base, False, visible
                )
            return inner

        lax.fori_loop(0, groups, slot_attention, 0)
        return carry

    lax.fori_loop(0, slots, each_slot, 0)
    done_ticks = early + used + slots * per_slot

    def finish(pair, carry):
        lanes = aligned(pair * 128, 128)
        x_own[:, lanes] = (acc[:, lanes] / sums[pair]).astype(jnp.bfloat16)
        tops[pair] = tops[pair] + jnp.log2(sums[pair])
        return carry

    lax.fori_loop(0, PAIRS, finish, 0)
    outputs += [
        pltpu.make_async_copy(x_own, o_out, sem_out.at[2]),
        pltpu.make_async_copy(tops, lse_out, sem_out.at[3]),
    ]
    for copy in outputs[2:]:
        copy.start()
    all_ticks = max(pieces + LAG, chain_chunks + HOP * (n_ctx - 1))
    if all_ticks > done_ticks:
        lax.fori_loop(done_ticks, all_ticks, lambda index, carry: (tick(index), carry)[1], 0)

    def drain(index, carry):
        here = fulls[0].at[pl.ds(0, PIECE), pl.ds(0, SPAN)]

        @pl.when(index >= ranges[0][1])
        def _():
            remote(here, here, cs_s.at[index], cs_r.at[index], core_peer).wait_recv()
            remote(here, here, cg_s.at[index], cg_r.at[index], core_peer).wait_recv()

        remote(here, here, side_s.at[index], side_r.at[index], side_peer).wait_send()
        remote(here, here, grp_s.at[index], grp_r.at[index], grp_peer).wait_send()
        remote(here, here, cs_s.at[index], cs_r.at[index], core_peer).wait_send()
        remote(here, here, cg_s.at[index], cg_r.at[index], core_peer).wait_send()
        return carry

    lax.fori_loop(0, pieces, drain, 0)
    copies = own_copies()
    for number, copy in enumerate(copies):
        copy.wait_send()
        if number >= len(copies) - 3:
            copy.wait_recv()
    for index in range(moves - 3, moves):
        local_wait(hop.at[index % 3], sem_store.at[index % 3])

    def drain_chain(index, carry):
        here = left.at[0, pl.ds(0, CHAIN)]

        @pl.when(ctx < n_ctx - 1)
        def _():
            remote(here, here, left_s.at[index], left_r.at[index], next_ctx).wait_send()

        @pl.when(ctx > 0)
        def _():
            remote(here, here, right_s.at[index], right_r.at[index], last_ctx).wait_send()

        return carry

    lax.fori_loop(0, chain_chunks, drain_chain, 0)
    for copy in outputs[:2]:
        copy.wait()
    shallow_tiles = full_up.shape[1] // SPAN

    def tile_loads(tile, parity):
        cols = aligned(tile * SPAN, SPAN)
        return (
            pltpu.make_async_copy(
                full_up.at[:, cols], weight.at[:, aligned(D + parity * SPAN, SPAN)], sem_ff.at[0, parity]
            ),
            pltpu.make_async_copy(full_down.at[cols, :], left.at[parity], sem_ff.at[1, parity]),
        )

    def tile_stores(tile, parity):
        cols = aligned(tile * SPAN, SPAN)
        return [
            pltpu.make_async_copy(
                kv_all.at[pl.ds(0, BLK), aligned(base + parity * SPAN, SPAN)],
                dest.at[:, cols],
                sem_ff.at[2 + place, parity],
            )
            for place, (base, dest) in enumerate(((0, u_out), (D, g_out)))
        ]

    out_load = pltpu.make_async_copy(full_out, weight.at[:, pl.ds(0, D)], sem_in.at[0])
    x_load = pltpu.make_async_copy(x_hbm, right.at[1], sem_in.at[1])
    for copy in (out_load, x_load) + tile_loads(0, 0):
        copy.start()

    def drain_blocks(index, carry):
        rows = aligned(index * BLK, BLK)
        local_wait(a_all.at[rows, :], sem_a.at[index])
        local_wait(kv_all.at[rows, :], sem_kv.at[index])
        return carry

    lax.fori_loop(0, slots + 1, drain_blocks, 0)
    out_load.wait()
    for half_cols in range(2):
        cols = pl.ds(half_cols * SPAN, SPAN)
        acc[:, cols] = jnp.dot(x_own[...], weight[:, cols], preferred_element_type=jnp.float32)
    x_load.wait()
    for copy in outputs[2:]:
        copy.wait()
    dy_load = pltpu.make_async_copy(dy_hbm, x_own, sem_in.at[0])
    dy_load.start()

    def inner_rows(step, carry):
        rows = aligned(step * CHAIN, CHAIN)
        hat, scale = standard_rows(acc[rows, :])
        a_all[rows, :] = hat.astype(jnp.bfloat16)
        sums[0, rows, :] = jnp.broadcast_to(scale, (CHAIN, 128))
        hidden = right[1, rows, :].astype(jnp.float32) + hat * gain_ref[1:2, :] + bias_ref[1:2, :]
        acc[rows, :] = hidden
        hat, scale = standard_rows(hidden)
        a_all[aligned(BLK + step * CHAIN, CHAIN), :] = hat.astype(jnp.bfloat16)
        sums[1, rows, :] = jnp.broadcast_to(scale, (CHAIN, 128))
        q_all[rows, :] = (hat * gain_ref[2:3, :] + bias_ref[2:3, :]).astype(jnp.bfloat16)
        return carry

    lax.fori_loop(0, BLK // CHAIN, inner_rows, 0)
    saves = [
        pltpu.make_async_copy(a_all.at[pl.ds(0, BLK), :], hat1_out, sem_out.at[0]),
        pltpu.make_async_copy(a_all.at[pl.ds(BLK, BLK), :], hat2_out, sem_out.at[1]),
        pltpu.make_async_copy(sums.at[pl.ds(0, 2)], rstd_out, sem_out.at[2]),
        pltpu.make_async_copy(q_all, f_out, sem_out.at[3]),
    ]
    for copy in saves:
        copy.start()

    def ff_tile(tile, carry):
        parity = tile % 2
        for copy in tile_loads(tile, parity):
            copy.wait()

        @pl.when(tile + 1 < shallow_tiles)
        def _():
            for copy in tile_loads(tile + 1, 1 - parity):
                copy.start()

        @pl.when(tile >= 2)
        def _():
            for copy in tile_stores(tile - 2, parity):
                copy.wait()

        upward = jnp.dot(
            q_all[...], weight[:, aligned(D + parity * SPAN, SPAN)], preferred_element_type=jnp.float32
        )
        kv_all[pl.ds(0, BLK), aligned(parity * SPAN, SPAN)] = upward.astype(jnp.bfloat16)
        active = (
            0.5 * upward * (1.0 + jnp.tanh(GELU_C * upward * (1.0 + GELU_A * upward * upward)))
        ).astype(jnp.bfloat16)
        kv_all[pl.ds(0, BLK), aligned(D + parity * SPAN, SPAN)] = active
        for copy in tile_stores(tile, parity):
            copy.start()
        fresh = jnp.dot(active, left[parity], preferred_element_type=jnp.float32)

        @pl.when(tile == 0)
        def _():
            z_acc[...] = fresh

        @pl.when(tile > 0)
        def _():
            z_acc[...] = z_acc[...] + fresh

        return carry

    lax.fori_loop(0, shallow_tiles, ff_tile, 0)
    dy_load.wait()

    def outer_rows(step, carry):
        gain_sum, bias_sum = carry
        rows = aligned(step * CHAIN, CHAIN)
        hat, scale = standard_rows(z_acc[rows, :])
        right[0, rows, :] = (acc[rows, :] + hat * gain_ref[3:4, :] + bias_ref[3:4, :]).astype(jnp.bfloat16)
        upstream = x_own[rows, :].astype(jnp.float32)
        a_all[aligned(2 * BLK + step * CHAIN, CHAIN), :] = row_back(
            upstream, hat, scale, gain_ref[3:4, :]
        ).astype(jnp.bfloat16)
        return gain_sum + column_sum(upstream * hat), bias_sum + column_sum(upstream)

    zero = jnp.zeros((1, D), jnp.float32)
    gain_sum, bias_sum = lax.fori_loop(0, BLK // CHAIN, outer_rows, (zero, zero))
    row = lax.broadcasted_iota(jnp.int32, (8, D), 0)
    norm_v[...] = jnp.where(row == 3, gain_sum, 0.0) + jnp.where(row == 7, bias_sum, 0.0)
    ends = [
        pltpu.make_async_copy(right.at[0], y_out, sem_in.at[0]),
        pltpu.make_async_copy(a_all.at[pl.ds(2 * BLK, BLK), :], dz_out, sem_in.at[1]),
        pltpu.make_async_copy(norm_v, norm_out, sem_in.at[2]),
    ]
    for copy in ends:
        copy.start()
    for tile in range(shallow_tiles - 2, shallow_tiles):
        for copy in tile_stores(tile, tile % 2):
            copy.wait()
    for copy in saves + ends:
        copy.wait()


def forward_part(n_ctx, tags, gains, biases, raw, dy, w_qkv, w_out, w_up, w_down):
    slots = n_ctx // 2
    every = (slots + 1) * BLK
    low, full = jnp.bfloat16, jnp.float32
    dma = pltpu.SemaphoreType.DMA
    hbm = pl.BlockSpec(memory_space=pl.ANY)
    vmem = pl.BlockSpec(memory_space=pltpu.VMEM)
    shards = (w_qkv, w_out, w_up, w_down)
    pieces = sum(w.shape[0] * w.shape[1] // (2 * PIECE * SPAN) for w in shards)
    own = w_qkv.shape[1] // SPAN + 3
    chain = slots * (BLK // CHAIN)
    shape = jax.ShapeDtypeStruct
    return pl.pallas_call(
        functools.partial(forward_kernel, n_ctx),
        out_shape=[
            shape((every, D), low),
            shape((BLK, D), low),
            shape((every, 2 * D), low),
            shape((BLK, D), low),
            shape((PAIRS, BLK, 128), full),
        ]
        + [shape((4 * w.shape[0], w.shape[1]), low) for w in shards]
        + [
            shape((BLK, D), low),
            shape((BLK, w_up.shape[1]), low),
            shape((BLK, D), low),
            shape((BLK, D), low),
            shape((BLK, w_up.shape[1]), low),
            shape((BLK, D), low),
            shape((BLK, D), low),
            shape((2, BLK, 128), full),
            shape((8, D), full),
        ],
        in_specs=[pl.BlockSpec(memory_space=pltpu.SMEM), vmem, vmem] + [hbm] * 6,
        out_specs=[hbm] * 18,
        scratch_shapes=[
            pltpu.VMEM((BLK, D), low),
            pltpu.VMEM((slots, BLK, D), low),
            pltpu.VMEM((slots, BLK, D), low),
            pltpu.VMEM((every, D), low),
            pltpu.VMEM((BLK, D), low),
            pltpu.VMEM((every, 2 * D), low),
            pltpu.VMEM((D, 3 * D), low),
            pltpu.VMEM((BLK, D), full),
            pltpu.VMEM((BLK, D), full),
            pltpu.VMEM((8, D), full),
            pltpu.VMEM((PAIRS, BLK, 128), full),
            pltpu.VMEM((PAIRS, BLK, 128), full),
            pltpu.VMEM((3, 2 * PIECE, SPAN), low),
            dma((3,)),
            dma((3,)),
            dma((3,)),
            dma((4, 2)),
            dma((4,)),
            dma((slots + 1,)),
            dma((slots + 1,)),
        ]
        + [dma((pieces,))] * 8
        + [dma((own,))] * 2
        + [dma((chain,))] * 4,
        compiler_params=pltpu.CompilerParams(
            collective_id=1, has_side_effects=True, vmem_limit_bytes=67043328
        ),
        cost_estimate=pl.CostEstimate(flops=20 << 30, bytes_accessed=64 << 20, transcendentals=1 << 24),
        name="gather_attend",
    )(tags, gains, biases, raw, dy, *shards)


TILE = 256
PAIRED = 2


def grad_block(q_ref, do_ref, o_ref, lse_ref, kv_ref, dq_acc, turned, pair, own, visible):
    lanes = aligned(pair * 128, 128)
    value_lanes = aligned(D + pair * 128, 128)
    size = QT if own else BLK
    count = BLK // size
    q_pair, do_pair, lse_pair = q_ref[:, lanes], do_ref[:, lanes], lse_ref[pair]
    prod = do_pair.astype(jnp.float32) * o_ref[:, lanes].astype(jnp.float32)
    keys, values = kv_ref[:, lanes], kv_ref[:, value_lanes]
    q_turned, do_turned = q_pair.T, do_pair.T
    old_dq = dq_acc[:, lanes]
    causal = causal_tile()
    hide = 0.0 if own else jnp.where(visible, 0.0, 1e30)
    lanes_of = [head_lanes(head, size) for head in range(2)]
    work = [(tile, head) for tile in range(count) for head in range(2)]
    score, dprob, dlogit, prob_low = {}, {}, {}, {}
    for tile, head in work:
        rows = slice(tile * size, (tile + 1) * size)
        span = (tile + 1) * size if own else BLK
        zero = jnp.zeros((size, 128), jnp.bfloat16)
        score[tile, head] = contract_last(jnp.where(lanes_of[head], q_pair[rows], zero), keys[:span])
        dprob[tile, head] = contract_last(jnp.where(lanes_of[head], do_pair[rows], zero), values[:span])
    for tile, head in work:
        rows = slice(tile * size, (tile + 1) * size)
        delta = jnp.sum(jnp.where(lanes_of[head], prod[rows], 0.0), axis=-1, keepdims=True)
        shift = lse_pair[rows, head * DH : head * DH + 1] + hide
        prob = jnp.exp2(score[tile, head] * C2 - shift)
        if own:
            diag = jnp.where(causal, prob[:, tile * size :], 0.0)
            prob = jnp.concatenate([prob[:, : tile * size], diag], axis=1) if tile else diag
        dlogit[tile, head] = (prob * (dprob[tile, head] - delta)).astype(jnp.bfloat16)
        prob_low[tile, head] = prob.astype(jnp.bfloat16)
    for tile in range(count):
        rows = slice(tile * size, (tile + 1) * size)
        span = (tile + 1) * size if own else BLK
        parts = [dot_dims(dlogit[tile, head], keys[:span], 1, 0) for head in range(2)]
        dq_acc[pl.ds(tile * size, size), lanes] = old_dq[rows] + jnp.where(lanes_of[0], parts[0], parts[1])
    for head in range(2):
        for offset, left_side, right_side, scale in (
            (0, q_turned, dlogit, ALPHA),
            (D, do_turned, prob_low, 1.0),
        ):
            spot = aligned(offset + pair * 128 + head * DH, DH)
            left_head = left_side[head * DH : (head + 1) * DH]
            terms = [
                dot_dims(left_head[:, tile * size : (tile + 1) * size], right_side[tile, head], 1, 0)
                for tile in range(count)
            ]
            for tile in range(count):
                cols = slice(tile * size, (tile + 1) * size)
                total = functools.reduce(
                    jnp.add, [terms[other][:, cols] for other in range(tile, count)]
                ) if own else terms[0]
                turned[spot, cols if own else slice(None)] = (total * scale).astype(jnp.bfloat16)


def backward_kernel(n_ctx, widths, *refs):
    slots = n_ctx // 2
    levels = n_ctx.bit_length() - 1
    depth = 16 if n_ctx == 4 else 10
    shallow = slots <= 2
    (slot_ref, gain_ref, bias_ref, norm_ref, x_hbm, q_hbm, kv_hbm, a_hbm, o_hbm, lse_hbm, w_hbm) = refs[:11]
    (w_out, w_up, w_down, g_hbm, dz_hbm, f_hbm, u_hbm, hat1_hbm, hat2_hbm, rstd_hbm, dy_hbm) = refs[11:22]
    outs = refs[22:26]
    grad_out, norm_out, dh_hbm, du_hbm, datt_hbm = refs[26:31]
    scratch = list(refs[31:])
    own_slot = slot_ref[1] // BLK

    def take(count):
        taken = scratch[:count]
        del scratch[:count]
        return taken

    q_v, o_v, do_v, lse_v, weight, kv_b, a_b, dq_acc, turned, gkv, term, own_part, left, right, norm_v, norm_in, gain_sum, bias_sum = take(18)
    r1, r2, r3, fin, made = take(5)
    lhs, rhs = take(2)
    zbufs = take(levels)
    sem_in, sem_blk, sem_rhs, sem_lhs, sem_ff, sem_out, sem_res = take(7)
    send1, recv1, send2, recv2, send3, recv3, send6, recv6 = take(8)
    rs_send, rs_recv, ag_send, ag_recv = take(levels), take(levels), take(levels), take(levels)
    left_s, left_r, right_s, right_r, norm_s, norm_r = take(6)
    grp, ctx, wsh = lax.axis_index("grp"), lax.axis_index("ctx"), lax.axis_index("wsh")
    side, core = wsh // 2, wsh % 2
    core_peer = (grp, ctx, side * 2 + 1 - core)
    side_peer = (grp, ctx, (1 - side) * 2 + core)
    grp_peer = (1 - grp, ctx, wsh)
    next_ctx = (grp, lax.rem(ctx + 1, n_ctx), wsh)
    last_ctx = (grp, lax.rem(ctx + n_ctx - 1, n_ctx), wsh)
    bits = [(ctx // (1 << level)) % 2 for level in range(levels)]
    level_peers = [(grp, ctx + (1 - 2 * bits[level]) * (1 << level), wsh) for level in range(levels)]

    def block_copies(index):
        rows = aligned(lax.rem(index, slots + 1) * BLK, BLK)
        slot = lax.rem(index, kv_b.shape[0])
        return (
            pltpu.make_async_copy(kv_hbm.at[rows, :], kv_b.at[slot], sem_blk.at[0, slot]),
            pltpu.make_async_copy(a_hbm.at[rows, :], a_b.at[slot], sem_blk.at[1, slot]),
        )

    barrier = pltpu.get_barrier_semaphore()
    peers = [core_peer, side_peer, grp_peer, next_ctx, last_ctx] + level_peers
    for peer in peers:
        pl.semaphore_signal(barrier, inc=1, device_id=peer, device_id_type=MESH)
    pl.semaphore_wait(barrier, len(peers))

    half = TILE // 2
    ranges, first = [], 0
    for rows, cols in widths:
        across = cols // TILE
        ranges.append((first, first + (rows // TILE) * across, across))
        first = ranges[-1][1]
    chunks = first

    def by_range(index, act):
        for place, (low, high, across) in enumerate(ranges):

            @pl.when((index >= low) & (index < high))
            def _(place=place, low=low, across=across):
                number = index - low
                act(place, (aligned((number // across) * TILE, TILE), aligned((number % across) * TILE, TILE)))

    def region(level, flip):
        row, rows, col, cols = 0, half, 0, TILE
        for place in range(level):
            bit = 1 - bits[place] if (flip and place == level - 1) else bits[place]
            if rows > 16:
                rows = rows // 2
                row = row + bit * rows
            else:
                cols = cols // 2
                col = col + bit * cols
        return row, rows, col, cols

    def spot(level, flip=False, base=0):
        row, rows, col, cols = region(level, flip)
        return aligned(base + row, rows), aligned(col, cols)

    last_low = ranges[-1][0]
    set_of = [(0, number) for number in range(widths[0][0] // TILE)] + [(1, 0), (2, 0)]
    set_first = [number * ranges[0][2] for number in range(widths[0][0] // TILE)]
    set_first += [ranges[1][0], ranges[2][0]]
    left_of, right_of = (g_hbm, f_hbm, o_hbm), (dz_hbm, du_hbm, datt_hbm)

    def set_copies(number):
        place, group = set_of[number]
        stride = left_of[place].shape[1] // 4
        return [
            pltpu.make_async_copy(
                left_of[place].at[:, pl.ds(owner * stride + group * TILE, TILE)],
                lhs.at[number % 2, owner],
                sem_lhs.at[number % 2, owner],
            )
            for owner in range(4)
        ]

    def step_fetch(index):
        near = lax.rem(index, 4)

        def act(place, span):
            if place < 3:
                pltpu.make_async_copy(
                    right_of[place].at[:, span[1]], rhs.at[near], sem_rhs.at[near]
                ).start()

        by_range(index, act)

    def step_make(index):
        slot = lax.rem(index, depth)
        near = lax.rem(index, 4)

        @pl.when(index < last_low)
        def _():
            local_wait(rhs.at[near], sem_rhs.at[near])
            parity = jnp.int32(0)
            for number, low in enumerate(set_first):
                parity = jnp.where(index >= low, number % 2, parity)

                @pl.when(index == low)
                def _(number=number):
                    for copy in set_copies(number):
                        copy.wait()
                    if number + 1 < len(set_first):
                        for copy in set_copies(number + 1):
                            copy.start()

            right_side = rhs[near]
            for owner in range(4):
                made[near, owner // 2, owner % 2] = dot_dims(
                    lhs[parity, owner], right_side, 0, 0
                ).astype(jnp.bfloat16)

        @pl.when(index >= last_low)
        def _():
            span = aligned((index - last_low) * TILE, TILE)
            made[near] = term[:, :, :, span]

        remote(
            made.at[near, :, 1 - core], r1.at[slot], send1.at[slot], recv1.at[slot], core_peer
        ).start()

    def finished(move):
        move.wait_send()
        move.wait_recv()

    def step_core(index):
        slot, near = lax.rem(index, depth), lax.rem(index, 4)
        finished(remote(r1.at[slot], r1.at[slot], send1.at[slot], recv1.at[slot], core_peer))
        r1[slot] = r1[slot] + made[near, :, core]
        remote(r1.at[slot, 1 - side], r2.at[slot], send2.at[slot], recv2.at[slot], side_peer).start()

    keep_half = aligned(grp * half, half)
    give_half = aligned((1 - grp) * half, half)

    def step_side(index):
        slot = lax.rem(index, depth)
        finished(remote(r1.at[slot, 1 - side], r2.at[slot], send2.at[slot], recv2.at[slot], side_peer))
        r2[slot] = r2[slot] + r1[slot, side]
        remote(r2.at[slot, give_half], r3.at[slot], send3.at[slot], recv3.at[slot], grp_peer).start()

    fold = n_ctx == 4
    if fold:
        outer = bits[0] == bits[1]
        inner = bits[0] != bits[1]
        mate, middle = level_peers[0], (grp, 3 - ctx, wsh)
        quarter = half // 2
        mine, other = aligned(bits[1] * quarter, quarter), aligned((1 - bits[1]) * quarter, quarter)
        fin_mine = aligned(grp * half + bits[1] * quarter, quarter)
        fin_other = aligned(grp * half + (1 - bits[1]) * quarter, quarter)

        def up_copy(slot):
            return remote(r3.at[slot], zbufs[0].at[slot], rs_send[0].at[slot], rs_recv[0].at[slot], mate)

        def cross_copy(slot):
            return remote(
                r3.at[slot, other], zbufs[1].at[slot], rs_send[1].at[slot], rs_recv[1].at[slot], middle
            )

        def share_copy(slot, rows):
            here = fin.at[slot, rows]
            return remote(here, here, ag_send[1].at[slot], ag_recv[1].at[slot], middle)

        def down_copy(slot):
            here = fin.at[slot, keep_half]
            return remote(here, here, ag_send[0].at[slot], ag_recv[0].at[slot], mate)

        def step_up(index):
            slot = lax.rem(index, depth)

            @pl.when(outer)
            def _():
                up_copy(slot).wait_send()

            @pl.when(inner)
            def _():
                up_copy(slot).wait_recv()
                r3[slot] = r3[slot] + zbufs[0][slot]
                cross_copy(slot).start()

        def step_cross(index):
            slot = lax.rem(index, depth)

            @pl.when(inner)
            def _():
                finished(cross_copy(slot))
                fin[slot, fin_mine] = r3[slot, mine] + zbufs[1][slot]
                share_copy(slot, fin_mine).start()

        def step_share(index):
            slot = lax.rem(index, depth)

            @pl.when(inner)
            def _():
                finished(share_copy(slot, fin_other))
                down_copy(slot).start()

        def step_down(index):
            slot = lax.rem(index, depth)

            @pl.when(inner)
            def _():
                down_copy(slot).wait_send()

            @pl.when(outer)
            def _():
                down_copy(slot).wait_recv()

            back_copy(slot, keep_half).start()

    def rs_copy(level, slot):
        rows, cols = spot(level + 1, True)
        return remote(
            r3.at[slot, rows, cols], zbufs[level].at[slot], rs_send[level].at[slot], rs_recv[level].at[slot], level_peers[level]
        )

    def ag_copy(level, slot, flip=False):
        rows, cols = spot(level + 1, flip, grp * half)
        here = fin.at[slot, rows, cols]
        return remote(here, here, ag_send[level].at[slot], ag_recv[level].at[slot], level_peers[level])

    def back_copy(slot, rows):
        here = fin.at[slot, rows]
        return remote(here, here, send6.at[slot], recv6.at[slot], grp_peer)

    def step_grp(index):
        slot = lax.rem(index, depth)
        finished(remote(r2.at[slot, give_half], r3.at[slot], send3.at[slot], recv3.at[slot], grp_peer))
        r3[slot] = r3[slot] + r2[slot, keep_half]
        if fold:

            @pl.when(outer)
            def _():
                up_copy(slot).start()
        else:
            rs_copy(0, slot).start()

    def step_scatter(level):
        def act(index):
            slot = lax.rem(index, depth)
            finished(rs_copy(level, slot))
            rows, cols = spot(level + 1)
            total = r3[slot, rows, cols] + zbufs[level][slot]
            if level + 1 < levels:
                r3[slot, rows, cols] = total
                rs_copy(level + 1, slot).start()
            else:
                rows, cols = spot(level + 1, False, grp * half)
                fin[slot, rows, cols] = total
                ag_copy(level, slot).start()

        return act

    def step_gather(level):
        def act(index):
            slot = lax.rem(index, depth)
            finished(ag_copy(level, slot, True))
            if level:
                ag_copy(level - 1, slot).start()
            else:
                back_copy(slot, keep_half).start()

        return act

    def out_wait(index):
        slot = lax.rem(index, depth)
        local_wait(fin.at[slot], sem_out.at[slot])

    def step_out(index):
        slot = lax.rem(index, depth)
        finished(back_copy(slot, give_half))

        def act(place, span):
            pltpu.make_async_copy(fin.at[slot], outs[place].at[span[0], span[1]], sem_out.at[slot]).start()

        by_range(index, act)

    z_lag = 2 if fold else 1
    order = [(YLAG, step_side), (XLAG, step_grp)]
    if fold:
        order += [(z_lag, act) for act in (step_up, step_cross, step_share, step_down)]
    else:
        order += [(z_lag, step_scatter(level)) for level in range(levels)]
        order += [(z_lag, step_gather(level)) for level in reversed(range(levels))]
    order += [(BLAG, step_out), (2, out_wait)]
    stages = [(0, step_core)]
    for lag, act in order:
        stages.append((stages[-1][0] + lag, act))
    all_ticks = chunks + stages[-1][0]

    per_slot = BLK // CHAIN
    chain_chunks = slots * per_slot

    def chain_step(stream, send, recv, number, is_first, is_last, target):
        slot = number // per_slot
        rows = aligned((number % per_slot) * CHAIN, CHAIN)
        here = stream.at[slot, rows]

        @pl.when(is_first)
        def _():
            stream[slot, rows, :] = own_part[slot, rows, :]

        @pl.when(jnp.logical_not(is_first))
        def _():
            remote(here, here, send.at[number], recv.at[number], target).wait_recv()
            stream[slot, rows, :] = stream[slot, rows, :] + own_part[slot, rows, :]

        @pl.when(jnp.logical_not(is_last))
        def _():
            remote(here, here, send.at[number], recv.at[number], target).start()

    def chain_tick(step):
        number = step - ctx

        @pl.when((number >= 0) & (number < chain_chunks))
        def _():
            chain_step(left, left_s, left_r, number, ctx == 0, ctx == n_ctx - 1, next_ctx)

        back = step - (n_ctx - 1 - ctx)

        @pl.when((back >= 0) & (back < chain_chunks))
        def _():
            chain_step(right, right_s, right_r, back, ctx == n_ctx - 1, ctx == 0, last_ctx)

    groups = PAIRS // PAIRED
    block_ticks = groups + 2
    chain_first = FF_TICKS + block_ticks
    paced = max(0, -(-(chunks - chain_first) // PACE))
    late_first = max(chunks, chain_first)
    late_beats = max(0, chain_chunks + n_ctx - 1 - paced)
    chain_ticks = late_first + TAIL_PACE * max(0, late_beats - 1) + 1

    def tick(step):
        @pl.when(step + 3 < chunks)
        def _():
            step_fetch(step + 3)

        @pl.when(step + 2 < chunks)
        def _():
            step_make(step + 2)

        for lag, act in stages:
            index = step - lag

            @pl.when((index >= 0) & (index < chunks))
            def _(act=act, index=index):
                act(index)

        beat = step - chain_first

        @pl.when((beat >= 0) & (step < chunks) & (beat % PACE == 0))
        def _():
            chain_tick(beat // PACE)

        late = step - late_first

        @pl.when((late >= 0) & (late % TAIL_PACE == 0))
        def _():
            chain_tick(paced + late // TAIL_PACE)


    for index in range(3):
        step_fetch(jnp.int32(index))
    for copy in set_copies(0):
        copy.start()

    hidden_tiles = u_hbm.shape[1] // SPAN
    datt_v, dz_v, dy_v, hat1_v, hat2_v = own_part.at[0], do_v, left.at[1], right.at[0], right.at[1]

    def tile_copies(tile, parity):
        cols = aligned(tile * SPAN, SPAN)
        return (
            pltpu.make_async_copy(w_down.at[cols, :], own_part.at[parity], sem_ff.at[0, parity]),
            pltpu.make_async_copy(
                w_up.at[:, cols], turned.at[aligned(parity * D, D), :], sem_ff.at[1, parity]
            ),
            pltpu.make_async_copy(
                u_hbm.at[:, cols], left.at[0, :, aligned(parity * SPAN, SPAN)], sem_ff.at[2, parity]
            ),
        )

    def du_store(tile, parity):
        return pltpu.make_async_copy(
            kv_b.at[0, :, aligned(parity * SPAN, SPAN)],
            du_hbm.at[:, aligned(tile * SPAN, SPAN)],
            sem_ff.at[3, parity],
        )

    dz_load = pltpu.make_async_copy(dz_hbm, dz_v, sem_in.at[0])
    dz_load.start()
    for copy in tile_copies(0, 0):
        copy.start()
    wide_loads = [
        pltpu.make_async_copy(source, dest, sem_in.at[place + 1])
        for place, (source, dest) in enumerate(
            (
                (dy_hbm, dy_v),
                (hat1_hbm, hat1_v),
                (hat2_hbm, hat2_v),
                (rstd_hbm, lse_v.at[pl.ds(0, 2)]),
                (q_hbm, q_v),
                (o_hbm, o_v),
                (w_hbm, weight),
            )
        )
    ]
    out_loads = [
        pltpu.make_async_copy(
            w_out.at[pl.ds(place * TILE, TILE), :],
            term.at[place // 2, place % 2, :, pl.ds(0, D)],
            sem_in.at[8 + place],
        )
        for place in range(4)
    ]
    for index in range(2):
        step_make(jnp.int32(index))
    dz_load.wait()

    def ff_tile(tile, carry):
        start = tile + (tile + 1) // 2
        tick(start)

        @pl.when(tile % 2 == 0)
        def _():
            tick(start + 1)

        parity = tile % 2
        for copy in tile_copies(tile, parity):
            copy.wait()

        @pl.when(tile + 1 < hidden_tiles)
        def _():
            for copy in tile_copies(tile + 1, 1 - parity):
                copy.start()

        @pl.when(tile == 0)
        def _():
            for copy in wide_loads + out_loads:
                copy.start()

        @pl.when(tile >= 2)
        def _():
            du_store(tile - 2, parity).wait()

        u_cols = aligned(parity * SPAN, SPAN)
        u_tile = left[0, :, u_cols].astype(jnp.float32)
        square = u_tile * u_tile
        bend = jnp.tanh(GELU_C * u_tile * (1.0 + GELU_A * square))
        slope = 0.5 * (1.0 + bend) + (0.5 * GELU_C) * u_tile * (1.0 - bend * bend) * (
            1.0 + 3.0 * GELU_A * square
        )
        du_tile = (contract_last(dz_v[...], own_part[parity]) * slope).astype(jnp.bfloat16)
        kv_b[0, :, u_cols] = du_tile
        du_store(tile, parity).start()
        fresh = contract_last(du_tile, turned[aligned(parity * D, D), :])

        @pl.when(tile == 0)
        def _():
            dq_acc[...] = fresh

        @pl.when(tile > 0)
        def _():
            dq_acc[...] = dq_acc[...] + fresh

        return carry

    lax.fori_loop(0, hidden_tiles, ff_tile, 0)
    for tile in range(hidden_tiles - 2, hidden_tiles):
        du_store(tile, tile % 2).wait()
    for copy in wide_loads:
        copy.wait()
    for copy in block_copies(1):
        copy.start()

    def hidden_back(step, carry):
        gain1, gain2, bias1, bias2 = carry
        rows = aligned(step * CHAIN, CHAIN)
        upstream = dq_acc[rows, :]
        hat = hat2_v[rows, :].astype(jnp.float32)
        grad_h = dy_v[rows, :].astype(jnp.float32) + row_back(
            upstream, hat, lse_v[1, rows, 0:1], gain_ref[2:3, :]
        )
        gain2, bias2 = gain2 + column_sum(upstream * hat), bias2 + column_sum(upstream)
        dq_acc[rows, :] = grad_h
        hat = hat1_v[rows, :].astype(jnp.float32)
        datt_v[rows, :] = row_back(grad_h, hat, lse_v[0, rows, 0:1], gain_ref[1:2, :]).astype(
            jnp.bfloat16
        )
        return gain1 + column_sum(grad_h * hat), gain2, bias1 + column_sum(grad_h), bias2

    zero = jnp.zeros((1, D), jnp.float32)
    sums = lax.fori_loop(0, BLK // CHAIN, hidden_back, (zero,) * 4)
    row = lax.broadcasted_iota(jnp.int32, (8, D), 0)
    norm_v[...] = norm_ref[...]
    for place, value in zip((1, 2, 5, 6), sums):
        norm_v[...] = norm_v[...] + jnp.where(row == place, value, 0.0)
    tick(FF_TICKS - 1)
    stores = [
        pltpu.make_async_copy(dq_acc, dh_hbm, sem_res.at[0]),
        pltpu.make_async_copy(datt_v, datt_hbm, sem_res.at[1]),
    ]
    lse_load = pltpu.make_async_copy(lse_hbm, lse_v, sem_in.at[0])
    for copy in stores + [lse_load]:
        copy.start()
    for place in range(4):
        out_loads[place].wait()
        do_v[:, pl.ds(place * TILE, TILE)] = contract_last(
            datt_v[...], term[place // 2, place % 2, :, pl.ds(0, D)]
        ).astype(jnp.bfloat16)
    for copy in stores + [lse_load]:
        copy.wait()
    dq_acc[...] = jnp.zeros_like(dq_acc)

    def attend(kv_ref, own, visible, begin):
        def body(group, carry):
            tick(begin + group)
            for member in range(PAIRED):
                grad_block(
                    q_v, do_v, o_v, lse_v, kv_ref, dq_acc, turned, group * PAIRED + member, own, visible
                )
            return carry

        lax.fori_loop(0, groups, body, 0)

    def first_sums(piece, normed, cols):
        gain_sum[:, cols] = gain_sum[:, cols] + column_sum(piece * normed.astype(jnp.float32))
        bias_sum[:, cols] = bias_sum[:, cols] + column_sum(piece)

    gain_sum[...] = jnp.zeros_like(gain_sum)
    bias_sum[...] = jnp.zeros_like(bias_sum)

    def each_slot(slot, carry):
        visible = slot < own_slot
        index = slot + 1
        place = lax.rem(index, kv_b.shape[0])
        for copy in block_copies(index):
            copy.wait()
        if kv_b.shape[0] > 1:
            for copy in block_copies(index + 1):
                copy.start()
        begin = FF_TICKS + slot * block_ticks
        attend(kv_b.at[place], False, visible, begin)

        def weight_terms(step, inner):
            tick(begin + groups + step)
            rows = aligned(step * 512, 512)
            for part in range(2):
                cols = pl.ds(part * D, D)
                product = dot_dims(a_b[place, :, rows], turned[cols, :], 0, 1)
                for down in range(2):
                    if shallow:
                        target = gkv.at[aligned(step * 512 + down * TILE, TILE), cols]
                    else:
                        target = term.at[step, down, :, pl.ds((part + 1) * D, D)]
                    piece = product[down * TILE : (down + 1) * TILE]

                    @pl.when(slot == 0)
                    def _(target=target, piece=piece):
                        target[...] = piece.astype(target.dtype)

                    @pl.when(slot > 0)
                    def _(target=target, piece=piece):
                        target[...] = (target[...] + piece).astype(target.dtype)

            piece = dot_dims(turned[...], weight[rows, pl.ds(D, 2 * D)], 0, 1)
            own_part[slot, :, rows] = piece.astype(jnp.bfloat16)
            first_sums(piece, a_b[place, :, rows], rows)
            return inner

        lax.fori_loop(0, 2, weight_terms, 0)
        if kv_b.shape[0] == 1:
            for copy in block_copies(index + 1):
                copy.start()
        return carry

    lax.fori_loop(0, slots, each_slot, 0)
    begin = FF_TICKS + slots * block_ticks
    own_place = (slots + 1) % kv_b.shape[0]
    for copy in block_copies(slots + 1):
        copy.wait()
    attend(kv_b.at[own_place], True, None, begin)
    dq_low = o_v
    dq_low[...] = (dq_acc[...] * ALPHA).astype(jnp.bfloat16) * jnp.bfloat16(QSCALE)
    x_load = pltpu.make_async_copy(x_hbm, do_v, sem_in.at[0])
    x_load.start()
    if shallow:
        hidden_load = pltpu.make_async_copy(dh_hbm, gkv.at[pl.ds(0, BLK), pl.ds(0, D)], sem_in.at[1])

    def last_terms(step, carry):
        tick(begin + groups + step)
        rows = aligned(step * TILE, TILE)
        a_rows = a_b[own_place, :, rows]
        up, down = step // 2, step % 2
        term[up, down, :, pl.ds(0, D)] = dot_dims(a_rows, dq_low[...], 0, 0).astype(jnp.bfloat16)
        for part in range(2):
            cols = pl.ds(part * D, D)
            target = term.at[up, down, :, pl.ds((part + 1) * D, D)]
            earlier = gkv[rows, cols] if shallow else target[...]
            target[...] = (earlier + dot_dims(a_rows, turned[cols, :], 0, 1)).astype(jnp.bfloat16)
        return carry

    lax.fori_loop(0, 4, last_terms, 0)
    if shallow:
        hidden_load.start()
    ready = begin + groups + 4
    assert ready <= ranges[-1][0] - 2 or n_ctx > 4
    da_acc = dq_acc

    def own_grad(step, carry):
        tick(ready + step)
        rows = aligned(step * TILE, TILE)
        piece = dot_dims(dq_low[...], weight[rows, pl.ds(0, D)], 1, 1) + dot_dims(
            turned[...], weight[rows, pl.ds(D, 2 * D)], 0, 1
        )
        da_acc[:, rows] = piece
        first_sums(piece, a_b[own_place, :, rows], rows)
        return carry

    lax.fori_loop(0, 4, own_grad, 0)
    ready = ready + 4

    first_gain = (gain_sum[...] - bias_ref[0:1, :] * bias_sum[...]) / gain_ref[0:1, :]
    norm_v[...] = (
        norm_v[...] + jnp.where(row == 0, first_gain, 0.0) + jnp.where(row == 4, bias_sum[...], 0.0)
    )

    def run_ticks(first, last):
        if last > first:
            lax.fori_loop(first, last, lambda index, carry: (tick(index), carry)[1], 0)
        return last

    for place, peer in enumerate([core_peer, side_peer, grp_peer] + level_peers):
        move = remote(norm_v, norm_in.at[place], norm_s.at[place], norm_r.at[place], peer)
        move.start()
        ready = run_ticks(ready, ready + 3)
        finished(move)
        norm_v[...] = norm_v[...] + norm_in[place]
    norm_result = pltpu.make_async_copy(norm_v, norm_out, sem_res.at[1])
    norm_result.start()
    ready = run_ticks(ready, max(ready, chain_ticks))
    x_load.wait()
    if shallow:
        hidden_load.wait()
    gain = gain_ref[0:1, :]

    def norm_grad(step, carry):
        @pl.when(step % 2 == 0)
        def _():
            tick(ready + step // 2)

        rows = aligned(step * CHAIN, CHAIN)
        upstream = da_acc[rows, :]
        for slot in range(slots):
            joined = left[slot, rows, :].astype(jnp.float32) + right[slot, rows, :].astype(jnp.float32)
            upstream = upstream + jnp.where(own_slot == slot, joined, 0.0)
        values = do_v[rows, :].astype(jnp.float32)
        centre = values - jnp.mean(values, axis=-1, keepdims=True)
        scale = lax.rsqrt(jnp.mean(centre * centre, axis=-1, keepdims=True) + EPS)
        centre = centre * scale
        grad = row_back(upstream, centre, scale, gain)
        da_acc[rows, :] = grad + gkv[rows, pl.ds(0, D)] if shallow else grad
        return carry

    lax.fori_loop(0, BLK // CHAIN, norm_grad, 0)
    ready = ready + BLK // CHAIN // 2
    result = pltpu.make_async_copy(da_acc, grad_out, sem_res.at[0])
    result.start()
    run_ticks(ready, all_ticks)

    def drain_chain(index, carry):
        here = left.at[0, pl.ds(0, CHAIN)]

        @pl.when(ctx < n_ctx - 1)
        def _():
            remote(here, here, left_s.at[index], left_r.at[index], next_ctx).wait_send()

        @pl.when(ctx > 0)
        def _():
            remote(here, here, right_s.at[index], right_r.at[index], last_ctx).wait_send()

        return carry

    lax.fori_loop(0, chain_chunks, drain_chain, 0)
    result.wait()
    norm_result.wait()


def backward_part(n_ctx, slot_vec, gains, biases, norms, saved, weights, ffn):
    slots = n_ctx // 2
    levels = n_ctx.bit_length() - 1
    depth = 16 if n_ctx == 4 else 10
    hidden = weights[1].shape[1]
    widths = [(hidden // 4, D), (D // 4, hidden), (D // 4, D), (D // 4, 3 * D)]
    low, full = jnp.bfloat16, jnp.float32
    dma = pltpu.SemaphoreType.DMA
    hbm = pl.BlockSpec(memory_space=pl.ANY)
    vmem = pl.BlockSpec(memory_space=pltpu.VMEM)
    shape = jax.ShapeDtypeStruct
    buffers = 2 if slots <= 2 else 1
    chain = slots * (BLK // CHAIN)
    zshapes, rows, cols = [], TILE // 2, TILE
    if n_ctx == 4:
        zshapes = [pltpu.VMEM((depth, rows, cols), low), pltpu.VMEM((depth, rows // 2, cols), low)]
    for _ in range(0 if zshapes else levels):
        rows, cols = (rows // 2, cols) if rows > 16 else (rows, cols // 2)
        zshapes.append(pltpu.VMEM((depth, rows, cols), low))
    return pl.pallas_call(
        functools.partial(backward_kernel, n_ctx, widths),
        out_shape=[shape(width, low) for width in widths] + [
            shape((BLK, D), full),
            shape((8, D), full),
            shape((BLK, D), full),
            shape((BLK, hidden), low),
            shape((BLK, D), low),
        ],
        in_specs=[pl.BlockSpec(memory_space=pltpu.SMEM), vmem, vmem, vmem]
        + [hbm] * (len(saved) + len(weights) + len(ffn)),
        out_specs=[hbm] * 9,
        scratch_shapes=[
            pltpu.VMEM((BLK, D), low),
            pltpu.VMEM((BLK, D), low),
            pltpu.VMEM((BLK, D), low),
            pltpu.VMEM((PAIRS, BLK, 128), full),
            pltpu.VMEM((D, 3 * D), low),
            pltpu.VMEM((buffers, BLK, 2 * D), low),
            pltpu.VMEM((buffers, BLK, D), low),
            pltpu.VMEM((BLK, D), full),
            pltpu.VMEM((2 * D, BLK), low),
            pltpu.VMEM((D, 2 * D) if slots <= 2 else (8, 128), full),
            pltpu.VMEM((2, 2, D // 4, 3 * D), low),
            pltpu.VMEM((slots, BLK, D), low),
            pltpu.VMEM((slots, BLK, D), low),
            pltpu.VMEM((slots, BLK, D), low),
            pltpu.VMEM((8, D), full),
            pltpu.VMEM((3 + levels, 8, D), full),
            pltpu.VMEM((1, D), full),
            pltpu.VMEM((1, D), full),
            pltpu.VMEM((depth, 2, TILE, TILE), low),
            pltpu.VMEM((depth, TILE, TILE), low),
            pltpu.VMEM((depth, TILE // 2, TILE), low),
            pltpu.VMEM((depth, TILE, TILE), low),
            pltpu.VMEM((4, 2, 2, TILE, TILE), low),
        ]
        + [pltpu.VMEM((2, 4, BLK, TILE), low), pltpu.VMEM((4, BLK, TILE), low)]
        + zshapes
        + [dma((12,)), dma((2, buffers)), dma((4,)), dma((2, 4)), dma((4, 2)), dma((depth,)), dma((2,))]
        + [dma((depth,))] * (8 + 4 * levels)
        + [dma((chain,))] * 4
        + [dma((3 + levels,))] * 2,
        compiler_params=pltpu.CompilerParams(
            collective_id=2, has_side_effects=True, vmem_limit_bytes=67043328
        ),
        cost_estimate=pl.CostEstimate(flops=40 << 30, bytes_accessed=64 << 20, transcendentals=1 << 24),
        name="attend_back_reduce",
    )(
        slot_vec,
        gains,
        biases,
        norms,
        *saved,
        *weights,
        *ffn,
    )


def widen_kernel(*refs):
    count = len(refs) // 2
    for source, dest in zip(refs[:count], refs[count:]):
        dest[...] = source[...].astype(jnp.float32)


def widen(arrays):
    steps = 8
    specs = [pl.BlockSpec((x.shape[0] // steps, x.shape[1]), lambda i: (i, 0)) for x in arrays]
    return pl.pallas_call(
        widen_kernel,
        out_shape=[jax.ShapeDtypeStruct(x.shape, jnp.float32) for x in arrays],
        grid=(steps,),
        in_specs=specs,
        out_specs=specs,
        compiler_params=pltpu.CompilerParams(vmem_limit_bytes=32 << 20),
        name="widen",
    )(*arrays)


def per_device(n_ctx, inputs, w_qkv, w_out, w_up, w_down, norm_gains, norm_biases, block_map, out_grad):
    slots = n_ctx // 2
    raw, seed_low = inputs.reshape(BLK, D), out_grad.reshape(BLK, D)
    block_entry = block_map.reshape(2)
    forward = forward_part(
        n_ctx,
        block_entry,
        norm_gains,
        norm_biases,
        raw,
        seed_low,
        w_qkv,
        w_out,
        w_up,
        w_down,
    )
    every_low, queries, keys_values, attn_low, lse, full_qkv, full_out, full_up, full_down = forward[:9]
    result, active_low, down_low, ffn_low, upward, hat1, hat2, rstd, norms = forward[9:]
    backward = backward_part(
        n_ctx,
        block_entry,
        norm_gains,
        norm_biases,
        norms,
        [raw, queries, keys_values, every_low, attn_low, lse, full_qkv],
        [full_out, full_up, full_down],
        [active_low, down_low, ffn_low, upward, hat1, hat2, rstd, seed_low],
    )
    grad_tokens, norm_total, grad_hidden = backward[4:7]
    if slots > 2:
        grad_tokens = grad_tokens + grad_hidden
    summed_down, summed_up, summed_out, summed_qkv, grad_input = widen(
        list(backward[:4]) + [grad_tokens]
    )
    return (
        result.reshape(1, 1, BLK, D),
        grad_input.reshape(1, 1, BLK, D),
        summed_qkv,
        summed_out,
        summed_up,
        summed_down,
        norm_total[:4],
        norm_total[4:],
    )


def solution(mesh):
    rows = P("wsh", None)
    blocks = P("grp", "wsh", "ctx", None)
    return jax.shard_map(
        functools.partial(per_device, mesh.shape["ctx"]),
        mesh=mesh,
        in_specs=(blocks, rows, rows, rows, rows, P(), P(), blocks, blocks),
        out_specs=(blocks, blocks, rows, rows, rows, rows, P(), P()),
        check_vma=False,
    )
```

```python
import functools
import math

import jax
import jax.numpy as jnp
from jax import lax
from jax.experimental import pallas as pl
from jax.experimental.pallas import tpu as pltpu
from jax.sharding import PartitionSpec as P

D = 1024
HEADS = 16
DH = 64
BLK = 512
PAIRS = HEADS // 2
QT = 256

EPS = 1e-05
ALPHA = 32.0
NEG = -1e30
LOG2E = 1.4426950408889634
C2 = ALPHA * LOG2E
MESH = pl.DeviceIdType.MESH
QSCALE = 1.0 / (ALPHA * math.sqrt(DH))


def layer_norm(values, gain_row, bias_row):
    centre = values - jnp.mean(values, axis=-1, keepdims=True)
    spread = jnp.mean(centre * centre, axis=-1, keepdims=True)
    return centre * lax.rsqrt(spread + EPS) * gain_row + bias_row


def dot_dims(left_side, right_side, left_dim, right_dim):
    return lax.dot_general(
        left_side,
        right_side,
        (((left_dim,), (right_dim,)), ((), ())),
        preferred_element_type=jnp.float32,
    )


def contract_last(left_side, right_side):
    return dot_dims(left_side, right_side, 1, 1)


def contract_rows(left_side, right_side):
    return dot_dims(left_side, right_side, 0, 0)


def standard_rows(values):
    centre = values - jnp.mean(values, axis=-1, keepdims=True)
    scale = lax.rsqrt(jnp.mean(centre * centre, axis=-1, keepdims=True) + EPS)
    return centre * scale, scale


def row_back(upstream, hat, scale, gain):
    scaled = upstream * gain
    return scale * (
        scaled
        - jnp.mean(scaled, axis=-1, keepdims=True)
        - hat * jnp.mean(scaled * hat, axis=-1, keepdims=True)
    )


def column_sum(values):
    return jnp.sum(values, axis=0, keepdims=True)


def head_lanes(head, rows):
    lane = lax.broadcasted_iota(jnp.int32, (rows, 128), 1)
    return (lane >= DH) if head else (lane < DH)


def causal_tile():
    row = lax.broadcasted_iota(jnp.int32, (QT, QT), 0)
    col = lax.broadcasted_iota(jnp.int32, (QT, QT), 1)
    return col <= row


PIECE = 128
SPAN = 512
CHAIN = 64
HOP = 2
YLAG = 3
XLAG = 2
BLAG = 2
FF_TICKS = 13
TAIL_PACE = 3
GELU_A = 0.044715
GELU_C = math.sqrt(2.0 / math.pi)
PACE = 2
LAG = 2
GROUP = 4
AHEAD = 4


def remote(src, dst, send, recv, peer):
    return pltpu.make_async_remote_copy(
        src_ref=src, dst_ref=dst, send_sem=send, recv_sem=recv, device_id=peer, device_id_type=MESH
    )


def local_wait(ref, sem):
    pltpu.make_async_copy(ref, ref, sem).wait()


def aligned(start, size):
    return pl.ds(pl.multiple_of(start, size), size)


def softmax_block(q_ref, kv_ref, acc, top_ref, sum_ref, pair, base, own, visible):
    lanes = aligned(pair * 128, 128)
    value_lanes = aligned(D + pair * 128, 128)
    causal = causal_tile()
    first = head_lanes(0, QT)
    count = BLK // QT
    q_pair = q_ref[:, lanes]
    keys = kv_ref[pl.ds(base, BLK), lanes]
    values = kv_ref[pl.ds(base, BLK), value_lanes]
    if not own:
        old_top, old_sum, old_out = top_ref[pair], sum_ref[pair], acc[:, lanes]
        hide = jnp.where(visible, 0.0, 1e30)
    results = []
    work = [(tile, head) for tile in range(count) for head in range(2)]
    parts_of = {}
    for tile, head in work:
        q_tile = q_pair[tile * QT : (tile + 1) * QT]
        q_head = jnp.where(head_lanes(head, QT), q_tile, jnp.zeros_like(q_tile))
        span = (tile + 1) * QT if own else BLK
        parts_of[tile, head] = contract_last(q_head, keys[:span])
    top_of, expo_of, total_of = {}, {}, {}
    for tile, head in work:
        part = parts_of[tile, head]
        if own:
            diag = jnp.where(causal, part[:, tile * QT :], NEG)
            part = jnp.concatenate([part[:, : tile * QT], diag], axis=1) if tile else diag
        top = jnp.max(part, axis=-1, keepdims=True) * C2
        if own:
            shift = top
        else:
            top = jnp.maximum(
                jnp.where(visible, top, NEG), old_top[tile * QT : (tile + 1) * QT, head * DH : head * DH + 1]
            )
            shift = top + hide
        expo = jnp.exp2(part * C2 - shift)
        top_of[tile, head] = jnp.broadcast_to(top, (QT, 128))
        total_of[tile, head] = jnp.broadcast_to(jnp.sum(expo, axis=-1, keepdims=True), (QT, 128))
        expo_of[tile, head] = expo.astype(jnp.bfloat16)
    out_of = {}
    for tile, head in work:
        span = (tile + 1) * QT if own else BLK
        out_of[tile, head] = dot_dims(expo_of[tile, head], values[:span], 1, 0)
    for tile in range(count):
        rows = pl.ds(tile * QT, QT)
        new_top = jnp.where(first, top_of[tile, 0], top_of[tile, 1])
        new_sum = jnp.where(first, total_of[tile, 0], total_of[tile, 1])
        new_out = jnp.where(first, out_of[tile, 0], out_of[tile, 1])
        if not own:
            here = slice(tile * QT, (tile + 1) * QT)
            keep = jnp.exp2(old_top[here] - new_top)
            new_sum = new_sum + old_sum[here] * keep
            new_out = new_out + old_out[here] * keep
        top_ref[pair, rows, :] = new_top
        sum_ref[pair, rows, :] = new_sum
        acc[rows, lanes] = new_out


def forward_kernel(n_ctx, *refs):
    slots = n_ctx // 2
    (slot_ref, gain_ref, bias_ref, x_hbm, dy_hbm, w_qkv, w_out, w_up, w_down) = refs[:9]
    (a_out, q_out, kv_out, o_out, lse_out, full_qkv, full_out, full_up, full_down) = refs[9:18]
    (y_out, g_out, dz_out, f_out, u_out, hat1_out, hat2_out, rstd_out, norm_out) = refs[18:27]
    (x_own, left, right, a_all, q_all, kv_all, weight, acc, z_acc, norm_v, tops, sums, hop) = refs[27:40]
    (sem_in, sem_load, sem_store, sem_ff, sem_out, sem_a, sem_kv, side_s, side_r, grp_s, grp_r, cs_s, cs_r, cg_s, cg_r, own_s, own_r, left_s, left_r, right_s, right_r) = refs[40:]
    grp, ctx, wsh = lax.axis_index("grp"), lax.axis_index("ctx"), lax.axis_index("wsh")
    side, core = wsh // 2, wsh % 2
    core_peer = (grp, ctx, side * 2 + 1 - core)
    side_peer = (grp, ctx, (1 - side) * 2 + core)
    grp_peer = (1 - grp, ctx, wsh)
    next_ctx = (grp, lax.rem(ctx + 1, n_ctx), wsh)
    last_ctx = (grp, lax.rem(ctx + n_ctx - 1, n_ctx), wsh)

    load = pltpu.make_async_copy(x_hbm, x_own, sem_in.at[0])
    load.start()
    barrier = pltpu.get_barrier_semaphore()
    for peer in (core_peer, side_peer, grp_peer, next_ctx, last_ctx):
        pl.semaphore_signal(barrier, inc=1, device_id=peer, device_id_type=MESH)
    pl.semaphore_wait(barrier, 5)

    shards = (w_qkv, w_out, w_up, w_down)
    fulls = (weight, full_out, full_up, full_down)
    ranges, start = [], 0
    for shard in shards:
        across = shard.shape[1] // SPAN
        ranges.append((start, start + across * (shard.shape[0] // (2 * PIECE)), across))
        start = ranges[-1][1]
    pieces = start

    def by_range(index, act):
        for place, (low, high, across) in enumerate(ranges):

            @pl.when((index >= low) & (index < high))
            def _(place=place, low=low, across=across):
                act(place, (index - low) // across, aligned(((index - low) % across) * SPAN, SPAN))

    def rows_of(place, owner, half, group):
        shard_rows = shards[place].shape[0]
        return aligned(owner * shard_rows + half * (shard_rows // 2) + group * PIECE, PIECE)

    sides_owner = (1 - side) * 2 + core

    def send_piece(index, carry):
        def act(place, group, cols):
            remote(
                shards[place].at[rows_of(place, 0, grp, group), cols],
                fulls[place].at[rows_of(place, wsh, grp, group), cols],
                side_s.at[index],
                side_r.at[index],
                side_peer,
            ).start()

        by_range(index, act)
        return carry

    def own_copies():
        copies = []
        across = shards[0].shape[1] // SPAN
        for place in range(4):
            shard_rows = shards[place].shape[0]
            mine = aligned(wsh * shard_rows, shard_rows)
            steps = range(across) if place == 0 else [None]
            for step in steps:
                cols = slice(None) if step is None else pl.ds(step * SPAN, SPAN)
                number = len(copies)
                copies.append(
                    remote(
                        shards[place].at[:, cols],
                        fulls[place].at[mine, cols],
                        own_s.at[number],
                        own_r.at[number],
                        core_peer,
                    )
                )
        return copies

    for index in range(AHEAD):
        send_piece(index, 0)
    for copy in own_copies():
        copy.start()
    own_rows = aligned(wsh * w_qkv.shape[0], w_qkv.shape[0])
    own_weight = pltpu.make_async_copy(w_qkv, weight.at[own_rows, :], sem_in.at[1])
    own_weight.start()
    load.wait()

    bounces, start = [], 0
    for shard in shards[1:]:
        across = shard.shape[1] // SPAN
        bounces.append((start, start + across * (shard.shape[0] // (2 * PIECE)), across))
        start = bounces[-1][1]
    moves = start

    def bounce(index, loading):
        slot = lax.rem(index, 3)
        for place, (low, high, across) in enumerate(bounces):

            @pl.when((index >= low) & (index < high))
            def _(place=place + 1, low=low, across=across):
                group = (index - low) // across
                cols = aligned(((index - low) % across) * SPAN, SPAN)
                if loading:
                    here = shards[place].at[aligned(group * 2 * PIECE, 2 * PIECE), cols]
                    pltpu.make_async_copy(here, hop.at[slot], sem_load.at[slot]).start()
                else:
                    rows = aligned(wsh * shards[place].shape[0] + group * 2 * PIECE, 2 * PIECE)
                    local_wait(hop.at[slot], sem_load.at[slot])
                    pltpu.make_async_copy(
                        hop.at[slot], fulls[place].at[rows, cols], sem_store.at[slot]
                    ).start()

    own_slot = slot_ref[1] // BLK
    own_tag = jnp.where(slot_ref[0] == 0, own_slot, n_ctx)
    chain_chunks = slots * (BLK // CHAIN)

    def chain_step(stream, send, recv, number, is_first, is_last, target):
        slot = number // (BLK // CHAIN)
        spot = aligned((number % (BLK // CHAIN)) * CHAIN, CHAIN)
        mine = jnp.where(own_tag == slot, x_own[spot, :], jnp.zeros((CHAIN, D), jnp.bfloat16))
        here = stream.at[slot, spot]

        @pl.when(is_first)
        def _():
            stream[slot, spot, :] = mine

        @pl.when(jnp.logical_not(is_first))
        def _():
            remote(here, here, send.at[number], recv.at[number], target).wait_recv()
            stream[slot, spot, :] = stream[slot, spot, :] + mine

        @pl.when(jnp.logical_not(is_last))
        def _():
            remote(here, here, send.at[number], recv.at[number], target).start()

    def tick(step):
        @pl.when((step >= 1) & (step <= moves))
        def _():
            bounce(step - 1, False)

        @pl.when((step >= 3) & (step < moves))
        def _():
            local_wait(hop.at[lax.rem(step, 3)], sem_store.at[lax.rem(step, 3)])

        @pl.when(step < moves)
        def _():
            bounce(step, True)

        @pl.when(step + AHEAD < pieces)
        def _():
            send_piece(step + AHEAD, 0)

        number = step - HOP * ctx

        @pl.when((number >= 0) & (number < chain_chunks))
        def _():
            chain_step(left, left_s, left_r, number, ctx == 0, ctx == n_ctx - 1, next_ctx)

        back = step - HOP * (n_ctx - 1 - ctx)

        @pl.when((back >= 0) & (back < chain_chunks))
        def _():
            chain_step(right, right_s, right_r, back, ctx == n_ctx - 1, ctx == 0, last_ctx)

        @pl.when(step < pieces)
        def _():
            def act(place, group, cols):
                here = fulls[place].at[rows_of(place, sides_owner, grp, group), cols]
                remote(here, here, side_s.at[step], side_r.at[step], side_peer).wait_recv()
                remote(here, here, grp_s.at[step], grp_r.at[step], grp_peer).start()
                remote(here, here, cs_s.at[step], cs_r.at[step], core_peer).start()

            by_range(step, act)

        late = step - LAG

        @pl.when((late >= 0) & (late < pieces))
        def _():
            def act(place, group, cols):
                here = fulls[place].at[rows_of(place, sides_owner, 1 - grp, group), cols]
                remote(here, here, grp_s.at[late], grp_r.at[late], grp_peer).wait_recv()
                remote(here, here, cg_s.at[late], cg_r.at[late], core_peer).start()

            by_range(late, act)

    def normalise(source, dest):
        gain, bias = gain_ref[0:1, :], bias_ref[0:1, :]

        def body(index, carry):
            rows = aligned(index * 128, 128)
            values = source(rows).astype(jnp.float32)
            a_all[aligned(dest + index * 128, 128), :] = layer_norm(values, gain, bias).astype(
                jnp.bfloat16
            )
            return carry

        lax.fori_loop(0, BLK // 128, body, 0)

    def piece_ready(index):
        here = fulls[0].at[pl.ds(0, PIECE), pl.ds(0, SPAN)]
        remote(here, here, cs_s.at[index], cs_r.at[index], core_peer).wait_recv()
        remote(here, here, cg_s.at[index], cg_r.at[index], core_peer).wait_recv()
        whole = fulls[0].at[pl.ds(0, 2 * PIECE), pl.ds(0, SPAN)]
        remote(whole, whole, own_s.at[index], own_r.at[index], core_peer).wait_recv()

    tick(0)
    normalise(lambda rows: x_own[rows, :], 0)
    for step in range(1, LAG + 1):
        tick(step)
    own_weight.wait()

    def project_q(index, carry):
        tick(index + LAG + 1)
        piece_ready(index)
        cols = aligned(index * SPAN, SPAN)
        q_all[:, cols] = (
            jnp.dot(a_all[pl.ds(0, BLK), :], weight[:, cols], preferred_element_type=jnp.float32) * QSCALE
        ).astype(jnp.bfloat16)
        return carry

    lax.fori_loop(0, D // SPAN, project_q, 0)
    head_ticks = LAG + 1 + D // SPAN

    def project_kv(index, base):
        cols = aligned(index * SPAN, SPAN)
        rows = aligned(base, BLK)
        kv_all[rows, cols] = jnp.dot(
            a_all[rows, :], weight[:, aligned(D + index * SPAN, SPAN)], preferred_element_type=jnp.float32
        ).astype(jnp.bfloat16)

    def own_kv(index, carry):
        tick(index + head_ticks)
        piece_ready(index + D // SPAN)
        project_kv(index, 0)
        return carry

    lax.fori_loop(0, 2 * D // SPAN, own_kv, 0)
    own_ticks = head_ticks + 2 * D // SPAN

    def send_block(index):
        rows = aligned(index * BLK, BLK)
        pltpu.make_async_copy(a_all.at[rows, :], a_out.at[rows, :], sem_a.at[index]).start()
        pltpu.make_async_copy(kv_all.at[rows, :], kv_out.at[rows, :], sem_kv.at[index]).start()

    outputs = [
        pltpu.make_async_copy(weight, full_qkv, sem_out.at[0]),
        pltpu.make_async_copy(q_all, q_out, sem_out.at[1]),
    ]
    for copy in outputs:
        copy.start()

    send_block(0)

    def own_attention(group, carry):
        tick(own_ticks + 2 * group)
        tick(own_ticks + 2 * group + 1)
        for member in range(GROUP):
            softmax_block(q_all, kv_all, acc, tops, sums, group * GROUP + member, 0, True, None)
        return carry

    groups = PAIRS // GROUP
    lax.fori_loop(0, groups, own_attention, 0)
    used = own_ticks + 2 * groups
    per_slot = 2 * D // SPAN + 2 * groups

    need = BLK // CHAIN + HOP * (n_ctx - 1)
    early = max(0, need - used)
    if early:
        lax.fori_loop(0, early, lambda index, carry: (tick(used + index), carry)[1], 0)

    def each_slot(slot, carry):
        base = pl.multiple_of((slot + 1) * BLK, BLK)
        visible = slot < own_slot
        begin = early + used + slot * per_slot

        def total(rows):
            joined = left[slot, rows, :] + right[slot, rows, :]
            return jnp.where(own_tag == slot, x_own[rows, :], joined)

        normalise(total, base)

        def slot_kv(index, inner):
            tick(begin + index)
            project_kv(index, base)
            return inner

        lax.fori_loop(0, 2 * D // SPAN, slot_kv, 0)

        send_block(slot + 1)

        def slot_attention(group, inner):
            tick(begin + 2 * D // SPAN + 2 * group)
            tick(begin + 2 * D // SPAN + 2 * group + 1)
            for member in range(GROUP):
                softmax_block(
                    q_all, kv_all, acc, tops, sums, group * GROUP + member, base, False, visible
                )
            return inner

        lax.fori_loop(0, groups, slot_attention, 0)
        return carry

    lax.fori_loop(0, slots, each_slot, 0)
    done_ticks = early + used + slots * per_slot

    def finish(pair, carry):
        lanes = aligned(pair * 128, 128)
        x_own[:, lanes] = (acc[:, lanes] / sums[pair]).astype(jnp.bfloat16)
        tops[pair] = tops[pair] + jnp.log2(sums[pair])
        return carry

    lax.fori_loop(0, PAIRS, finish, 0)
    outputs += [
        pltpu.make_async_copy(x_own, o_out, sem_out.at[2]),
        pltpu.make_async_copy(tops, lse_out, sem_out.at[3]),
    ]
    for copy in outputs[2:]:
        copy.start()
    all_ticks = max(pieces + LAG, chain_chunks + HOP * (n_ctx - 1))
    if all_ticks > done_ticks:
        lax.fori_loop(done_ticks, all_ticks, lambda index, carry: (tick(index), carry)[1], 0)

    def drain(index, carry):
        here = fulls[0].at[pl.ds(0, PIECE), pl.ds(0, SPAN)]

        @pl.when(index >= ranges[0][1])
        def _():
            remote(here, here, cs_s.at[index], cs_r.at[index], core_peer).wait_recv()
            remote(here, here, cg_s.at[index], cg_r.at[index], core_peer).wait_recv()

        remote(here, here, side_s.at[index], side_r.at[index], side_peer).wait_send()
        remote(here, here, grp_s.at[index], grp_r.at[index], grp_peer).wait_send()
        remote(here, here, cs_s.at[index], cs_r.at[index], core_peer).wait_send()
        remote(here, here, cg_s.at[index], cg_r.at[index], core_peer).wait_send()
        return carry

    lax.fori_loop(0, pieces, drain, 0)
    copies = own_copies()
    for number, copy in enumerate(copies):
        copy.wait_send()
        if number >= len(copies) - 3:
            copy.wait_recv()
    for index in range(moves - 3, moves):
        local_wait(hop.at[index % 3], sem_store.at[index % 3])

    def drain_chain(index, carry):
        here = left.at[0, pl.ds(0, CHAIN)]

        @pl.when(ctx < n_ctx - 1)
        def _():
            remote(here, here, left_s.at[index], left_r.at[index], next_ctx).wait_send()

        @pl.when(ctx > 0)
        def _():
            remote(here, here, right_s.at[index], right_r.at[index], last_ctx).wait_send()

        return carry

    lax.fori_loop(0, chain_chunks, drain_chain, 0)
    for copy in outputs[:2]:
        copy.wait()
    shallow_tiles = full_up.shape[1] // SPAN

    def tile_loads(tile, parity):
        cols = aligned(tile * SPAN, SPAN)
        return (
            pltpu.make_async_copy(
                full_up.at[:, cols], weight.at[:, aligned(D + parity * SPAN, SPAN)], sem_ff.at[0, parity]
            ),
            pltpu.make_async_copy(full_down.at[cols, :], left.at[parity], sem_ff.at[1, parity]),
        )

    def tile_stores(tile, parity):
        cols = aligned(tile * SPAN, SPAN)
        return [
            pltpu.make_async_copy(
                kv_all.at[pl.ds(0, BLK), aligned(base + parity * SPAN, SPAN)],
                dest.at[:, cols],
                sem_ff.at[2 + place, parity],
            )
            for place, (base, dest) in enumerate(((0, u_out), (D, g_out)))
        ]

    out_load = pltpu.make_async_copy(full_out, weight.at[:, pl.ds(0, D)], sem_in.at[0])
    x_load = pltpu.make_async_copy(x_hbm, right.at[1], sem_in.at[1])
    for copy in (out_load, x_load) + tile_loads(0, 0):
        copy.start()

    def drain_blocks(index, carry):
        rows = aligned(index * BLK, BLK)
        local_wait(a_all.at[rows, :], sem_a.at[index])
        local_wait(kv_all.at[rows, :], sem_kv.at[index])
        return carry

    lax.fori_loop(0, slots + 1, drain_blocks, 0)
    out_load.wait()
    for half_cols in range(2):
        cols = pl.ds(half_cols * SPAN, SPAN)
        acc[:, cols] = jnp.dot(x_own[...], weight[:, cols], preferred_element_type=jnp.float32)
    x_load.wait()
    for copy in outputs[2:]:
        copy.wait()
    dy_load = pltpu.make_async_copy(dy_hbm, x_own, sem_in.at[0])
    dy_load.start()

    def inner_rows(step, carry):
        rows = aligned(step * CHAIN, CHAIN)
        hat, scale = standard_rows(acc[rows, :])
        a_all[rows, :] = hat.astype(jnp.bfloat16)
        sums[0, rows, :] = jnp.broadcast_to(scale, (CHAIN, 128))
        hidden = right[1, rows, :].astype(jnp.float32) + hat * gain_ref[1:2, :] + bias_ref[1:2, :]
        acc[rows, :] = hidden
        hat, scale = standard_rows(hidden)
        a_all[aligned(BLK + step * CHAIN, CHAIN), :] = hat.astype(jnp.bfloat16)
        sums[1, rows, :] = jnp.broadcast_to(scale, (CHAIN, 128))
        q_all[rows, :] = (hat * gain_ref[2:3, :] + bias_ref[2:3, :]).astype(jnp.bfloat16)
        return carry

    lax.fori_loop(0, BLK // CHAIN, inner_rows, 0)
    saves = [
        pltpu.make_async_copy(a_all.at[pl.ds(0, BLK), :], hat1_out, sem_out.at[0]),
        pltpu.make_async_copy(a_all.at[pl.ds(BLK, BLK), :], hat2_out, sem_out.at[1]),
        pltpu.make_async_copy(sums.at[pl.ds(0, 2)], rstd_out, sem_out.at[2]),
        pltpu.make_async_copy(q_all, f_out, sem_out.at[3]),
    ]
    for copy in saves:
        copy.start()

    def ff_tile(tile, carry):
        parity = tile % 2
        for copy in tile_loads(tile, parity):
            copy.wait()

        @pl.when(tile + 1 < shallow_tiles)
        def _():
            for copy in tile_loads(tile + 1, 1 - parity):
                copy.start()

        @pl.when(tile >= 2)
        def _():
            for copy in tile_stores(tile - 2, parity):
                copy.wait()

        upward = jnp.dot(
            q_all[...], weight[:, aligned(D + parity * SPAN, SPAN)], preferred_element_type=jnp.float32
        )
        kv_all[pl.ds(0, BLK), aligned(parity * SPAN, SPAN)] = upward.astype(jnp.bfloat16)
        active = (
            0.5 * upward * (1.0 + jnp.tanh(GELU_C * upward * (1.0 + GELU_A * upward * upward)))
        ).astype(jnp.bfloat16)
        kv_all[pl.ds(0, BLK), aligned(D + parity * SPAN, SPAN)] = active
        for copy in tile_stores(tile, parity):
            copy.start()
        fresh = jnp.dot(active, left[parity], preferred_element_type=jnp.float32)

        @pl.when(tile == 0)
        def _():
            z_acc[...] = fresh

        @pl.when(tile > 0)
        def _():
            z_acc[...] = z_acc[...] + fresh

        return carry

    lax.fori_loop(0, shallow_tiles, ff_tile, 0)
    dy_load.wait()

    def outer_rows(step, carry):
        gain_sum, bias_sum = carry
        rows = aligned(step * CHAIN, CHAIN)
        hat, scale = standard_rows(z_acc[rows, :])
        right[0, rows, :] = (acc[rows, :] + hat * gain_ref[3:4, :] + bias_ref[3:4, :]).astype(jnp.bfloat16)
        upstream = x_own[rows, :].astype(jnp.float32)
        a_all[aligned(2 * BLK + step * CHAIN, CHAIN), :] = row_back(
            upstream, hat, scale, gain_ref[3:4, :]
        ).astype(jnp.bfloat16)
        return gain_sum + column_sum(upstream * hat), bias_sum + column_sum(upstream)

    zero = jnp.zeros((1, D), jnp.float32)
    gain_sum, bias_sum = lax.fori_loop(0, BLK // CHAIN, outer_rows, (zero, zero))
    row = lax.broadcasted_iota(jnp.int32, (8, D), 0)
    norm_v[...] = jnp.where(row == 3, gain_sum, 0.0) + jnp.where(row == 7, bias_sum, 0.0)
    ends = [
        pltpu.make_async_copy(right.at[0], y_out, sem_in.at[0]),
        pltpu.make_async_copy(a_all.at[pl.ds(2 * BLK, BLK), :], dz_out, sem_in.at[1]),
        pltpu.make_async_copy(norm_v, norm_out, sem_in.at[2]),
    ]
    for copy in ends:
        copy.start()
    for tile in range(shallow_tiles - 2, shallow_tiles):
        for copy in tile_stores(tile, tile % 2):
            copy.wait()
    for copy in saves + ends:
        copy.wait()


def forward_part(n_ctx, tags, gains, biases, raw, dy, w_qkv, w_out, w_up, w_down):
    slots = n_ctx // 2
    every = (slots + 1) * BLK
    low, full = jnp.bfloat16, jnp.float32
    dma = pltpu.SemaphoreType.DMA
    hbm = pl.BlockSpec(memory_space=pl.ANY)
    vmem = pl.BlockSpec(memory_space=pltpu.VMEM)
    shards = (w_qkv, w_out, w_up, w_down)
    pieces = sum(w.shape[0] * w.shape[1] // (2 * PIECE * SPAN) for w in shards)
    own = w_qkv.shape[1] // SPAN + 3
    chain = slots * (BLK // CHAIN)
    shape = jax.ShapeDtypeStruct
    return pl.pallas_call(
        functools.partial(forward_kernel, n_ctx),
        out_shape=[
            shape((every, D), low),
            shape((BLK, D), low),
            shape((every, 2 * D), low),
            shape((BLK, D), low),
            shape((PAIRS, BLK, 128), full),
        ]
        + [shape((4 * w.shape[0], w.shape[1]), low) for w in shards]
        + [
            shape((BLK, D), low),
            shape((BLK, w_up.shape[1]), low),
            shape((BLK, D), low),
            shape((BLK, D), low),
            shape((BLK, w_up.shape[1]), low),
            shape((BLK, D), low),
            shape((BLK, D), low),
            shape((2, BLK, 128), full),
            shape((8, D), full),
        ],
        in_specs=[pl.BlockSpec(memory_space=pltpu.SMEM), vmem, vmem] + [hbm] * 6,
        out_specs=[hbm] * 18,
        scratch_shapes=[
            pltpu.VMEM((BLK, D), low),
            pltpu.VMEM((slots, BLK, D), low),
            pltpu.VMEM((slots, BLK, D), low),
            pltpu.VMEM((every, D), low),
            pltpu.VMEM((BLK, D), low),
            pltpu.VMEM((every, 2 * D), low),
            pltpu.VMEM((D, 3 * D), low),
            pltpu.VMEM((BLK, D), full),
            pltpu.VMEM((BLK, D), full),
            pltpu.VMEM((8, D), full),
            pltpu.VMEM((PAIRS, BLK, 128), full),
            pltpu.VMEM((PAIRS, BLK, 128), full),
            pltpu.VMEM((3, 2 * PIECE, SPAN), low),
            dma((3,)),
            dma((3,)),
            dma((3,)),
            dma((4, 2)),
            dma((4,)),
            dma((slots + 1,)),
            dma((slots + 1,)),
        ]
        + [dma((pieces,))] * 8
        + [dma((own,))] * 2
        + [dma((chain,))] * 4,
        compiler_params=pltpu.CompilerParams(
            collective_id=1, has_side_effects=True, vmem_limit_bytes=67043328
        ),
        cost_estimate=pl.CostEstimate(flops=20 << 30, bytes_accessed=64 << 20, transcendentals=1 << 24),
        name="gather_attend",
    )(tags, gains, biases, raw, dy, *shards)


TILE = 256
PAIRED = 2


def grad_block(q_ref, do_ref, o_ref, lse_ref, kv_ref, dq_acc, turned, pair, own, visible):
    lanes = aligned(pair * 128, 128)
    value_lanes = aligned(D + pair * 128, 128)
    size = QT if own else BLK
    count = BLK // size
    q_pair, do_pair, lse_pair = q_ref[:, lanes], do_ref[:, lanes], lse_ref[pair]
    prod = do_pair.astype(jnp.float32) * o_ref[:, lanes].astype(jnp.float32)
    keys, values = kv_ref[:, lanes], kv_ref[:, value_lanes]
    q_turned, do_turned = q_pair.T, do_pair.T
    old_dq = dq_acc[:, lanes]
    causal = causal_tile()
    hide = 0.0 if own else jnp.where(visible, 0.0, 1e30)
    lanes_of = [head_lanes(head, size) for head in range(2)]
    work = [(tile, head) for tile in range(count) for head in range(2)]
    score, dprob, dlogit, prob_low = {}, {}, {}, {}
    for tile, head in work:
        rows = slice(tile * size, (tile + 1) * size)
        span = (tile + 1) * size if own else BLK
        zero = jnp.zeros((size, 128), jnp.bfloat16)
        score[tile, head] = contract_last(jnp.where(lanes_of[head], q_pair[rows], zero), keys[:span])
        dprob[tile, head] = contract_last(jnp.where(lanes_of[head], do_pair[rows], zero), values[:span])
    for tile, head in work:
        rows = slice(tile * size, (tile + 1) * size)
        delta = jnp.sum(jnp.where(lanes_of[head], prod[rows], 0.0), axis=-1, keepdims=True)
        shift = lse_pair[rows, head * DH : head * DH + 1] + hide
        prob = jnp.exp2(score[tile, head] * C2 - shift)
        if own:
            diag = jnp.where(causal, prob[:, tile * size :], 0.0)
            prob = jnp.concatenate([prob[:, : tile * size], diag], axis=1) if tile else diag
        dlogit[tile, head] = (prob * (dprob[tile, head] - delta)).astype(jnp.bfloat16)
        prob_low[tile, head] = prob.astype(jnp.bfloat16)
    for tile in range(count):
        rows = slice(tile * size, (tile + 1) * size)
        span = (tile + 1) * size if own else BLK
        parts = [dot_dims(dlogit[tile, head], keys[:span], 1, 0) for head in range(2)]
        dq_acc[pl.ds(tile * size, size), lanes] = old_dq[rows] + jnp.where(lanes_of[0], parts[0], parts[1])
    for head in range(2):
        for offset, left_side, right_side, scale in (
            (0, q_turned, dlogit, ALPHA),
            (D, do_turned, prob_low, 1.0),
        ):
            spot = aligned(offset + pair * 128 + head * DH, DH)
            left_head = left_side[head * DH : (head + 1) * DH]
            terms = [
                dot_dims(left_head[:, tile * size : (tile + 1) * size], right_side[tile, head], 1, 0)
                for tile in range(count)
            ]
            for tile in range(count):
                cols = slice(tile * size, (tile + 1) * size)
                total = functools.reduce(
                    jnp.add, [terms[other][:, cols] for other in range(tile, count)]
                ) if own else terms[0]
                turned[spot, cols if own else slice(None)] = (total * scale).astype(jnp.bfloat16)


def backward_kernel(n_ctx, widths, *refs):
    slots = n_ctx // 2
    levels = n_ctx.bit_length() - 1
    depth = 16 if n_ctx == 4 else 10
    shallow = slots <= 2
    (slot_ref, gain_ref, bias_ref, norm_ref, x_hbm, q_hbm, kv_hbm, a_hbm, o_hbm, lse_hbm, w_hbm) = refs[:11]
    (w_out, w_up, w_down, g_hbm, dz_hbm, f_hbm, u_hbm, hat1_hbm, hat2_hbm, rstd_hbm, dy_hbm) = refs[11:22]
    outs = refs[22:26]
    grad_out, norm_out, dh_hbm, du_hbm, datt_hbm = refs[26:31]
    scratch = list(refs[31:])
    own_slot = slot_ref[1] // BLK

    def take(count):
        taken = scratch[:count]
        del scratch[:count]
        return taken

    q_v, o_v, do_v, lse_v, weight, kv_b, a_b, dq_acc, turned, gkv, term, own_part, left, right, norm_v, norm_in, gain_sum, bias_sum = take(18)
    r1, r2, r3, fin, made = take(5)
    lhs, rhs = take(2)
    zbufs = take(levels)
    sem_in, sem_blk, sem_rhs, sem_lhs, sem_ff, sem_out, sem_res = take(7)
    send1, recv1, send2, recv2, send3, recv3, send6, recv6 = take(8)
    rs_send, rs_recv, ag_send, ag_recv = take(levels), take(levels), take(levels), take(levels)
    left_s, left_r, right_s, right_r, norm_s, norm_r = take(6)
    grp, ctx, wsh = lax.axis_index("grp"), lax.axis_index("ctx"), lax.axis_index("wsh")
    side, core = wsh // 2, wsh % 2
    core_peer = (grp, ctx, side * 2 + 1 - core)
    side_peer = (grp, ctx, (1 - side) * 2 + core)
    grp_peer = (1 - grp, ctx, wsh)
    next_ctx = (grp, lax.rem(ctx + 1, n_ctx), wsh)
    last_ctx = (grp, lax.rem(ctx + n_ctx - 1, n_ctx), wsh)
    bits = [(ctx // (1 << level)) % 2 for level in range(levels)]
    level_peers = [(grp, ctx + (1 - 2 * bits[level]) * (1 << level), wsh) for level in range(levels)]

    def block_copies(index):
        rows = aligned(lax.rem(index, slots + 1) * BLK, BLK)
        slot = lax.rem(index, kv_b.shape[0])
        a_slot = index - 1 if shallow else 0
        return (
            pltpu.make_async_copy(kv_hbm.at[rows, :], kv_b.at[slot], sem_blk.at[0, slot]),
            pltpu.make_async_copy(a_hbm.at[rows, :], a_b.at[a_slot], sem_blk.at[1, slot]),
        )

    barrier = pltpu.get_barrier_semaphore()
    peers = [core_peer, side_peer, grp_peer, next_ctx, last_ctx] + level_peers
    for peer in peers:
        pl.semaphore_signal(barrier, inc=1, device_id=peer, device_id_type=MESH)
    pl.semaphore_wait(barrier, len(peers))

    half = TILE // 2
    ranges, first = [], 0
    for rows, cols in widths:
        across = cols // TILE
        ranges.append((first, first + (rows // TILE) * across, across))
        first = ranges[-1][1]
    chunks = first

    def by_range(index, act):
        for place, (low, high, across) in enumerate(ranges):

            @pl.when((index >= low) & (index < high))
            def _(place=place, low=low, across=across):
                number = index - low
                act(place, (aligned((number // across) * TILE, TILE), aligned((number % across) * TILE, TILE)))

    def region(level, flip):
        row, rows, col, cols = 0, half, 0, TILE
        for place in range(level):
            bit = 1 - bits[place] if (flip and place == level - 1) else bits[place]
            if rows > 16:
                rows = rows // 2
                row = row + bit * rows
            else:
                cols = cols // 2
                col = col + bit * cols
        return row, rows, col, cols

    def spot(level, flip=False, base=0):
        row, rows, col, cols = region(level, flip)
        return aligned(base + row, rows), aligned(col, cols)

    last_low = ranges[-1][0]
    dq_low = o_v
    set_of = [(0, number) for number in range(widths[0][0] // TILE)] + [(1, 0), (2, 0)]
    set_first = [number * ranges[0][2] for number in range(widths[0][0] // TILE)]
    set_first += [ranges[1][0], ranges[2][0]]
    left_of, right_of = (g_hbm, f_hbm, o_hbm), (dz_hbm, du_hbm, datt_hbm)

    def set_copies(number):
        place, group = set_of[number]
        stride = left_of[place].shape[1] // 4
        return [
            pltpu.make_async_copy(
                left_of[place].at[:, pl.ds(owner * stride + group * TILE, TILE)],
                lhs.at[number % 2, owner],
                sem_lhs.at[number % 2, owner],
            )
            for owner in range(4)
        ]

    def step_fetch(index):
        near = lax.rem(index, 4)

        def act(place, span):
            if place < 3:
                pltpu.make_async_copy(
                    right_of[place].at[:, span[1]], rhs.at[near], sem_rhs.at[near]
                ).start()

        by_range(index, act)

    def step_make(index, kinds):
        slot = lax.rem(index, depth)
        near = lax.rem(index, 4)

        def low_piece():
            local_wait(rhs.at[near], sem_rhs.at[near])
            parity = jnp.int32(0)
            for number, low in enumerate(set_first):
                parity = jnp.where(index >= low, number % 2, parity)

                @pl.when(index == low)
                def _(number=number):
                    for copy in set_copies(number):
                        copy.wait()
                    if number + 1 < len(set_first):
                        for copy in set_copies(number + 1):
                            copy.start()

            right_side = rhs[near]
            for owner in range(4):
                made[near, owner // 2, owner % 2] = dot_dims(
                    lhs[parity, owner], right_side, 0, 0
                ).astype(jnp.bfloat16)

        def high_piece():
            number = index - last_low
            if not shallow:
                made[near] = term[:, :, :, aligned(number * TILE, TILE)]
                return

            @pl.when(number < D // TILE)
            def _():
                right_side = dq_low[:, aligned(number * TILE, TILE)]
                for owner in range(4):
                    made[near, owner // 2, owner % 2] = dot_dims(
                        a_b[slots, :, pl.ds(owner * TILE, TILE)], right_side, 0, 0
                    ).astype(jnp.bfloat16)

            @pl.when(number >= D // TILE)
            def _():
                cols = aligned((number - D // TILE) * TILE, TILE)
                for owner in range(4):
                    total = functools.reduce(
                        jnp.add,
                        [
                            dot_dims(a_b[block, :, pl.ds(owner * TILE, TILE)], turned[block, cols, :], 0, 1)
                            for block in range(slots + 1)
                        ],
                    )
                    made[near, owner // 2, owner % 2] = total.astype(jnp.bfloat16)

        if kinds == "low":
            low_piece()
        elif kinds == "high":
            high_piece()
        else:
            pl.when(index < last_low)(low_piece)
            pl.when(index >= last_low)(high_piece)
        remote(
            made.at[near, :, 1 - core], r1.at[slot], send1.at[slot], recv1.at[slot], core_peer
        ).start()

    def finished(move):
        move.wait_send()
        move.wait_recv()

    def step_core(index):
        slot, near = lax.rem(index, depth), lax.rem(index, 4)
        finished(remote(r1.at[slot], r1.at[slot], send1.at[slot], recv1.at[slot], core_peer))
        r1[slot] = r1[slot] + made[near, :, core]
        remote(r1.at[slot, 1 - side], r2.at[slot], send2.at[slot], recv2.at[slot], side_peer).start()

    keep_half = aligned(grp * half, half)
    give_half = aligned((1 - grp) * half, half)

    def step_side(index):
        slot = lax.rem(index, depth)
        finished(remote(r1.at[slot, 1 - side], r2.at[slot], send2.at[slot], recv2.at[slot], side_peer))
        r2[slot] = r2[slot] + r1[slot, side]
        remote(r2.at[slot, give_half], r3.at[slot], send3.at[slot], recv3.at[slot], grp_peer).start()

    fold = n_ctx == 4
    if fold:
        outer = bits[0] == bits[1]
        inner = bits[0] != bits[1]
        mate, middle = level_peers[0], (grp, 3 - ctx, wsh)
        quarter = half // 2
        mine, other = aligned(bits[1] * quarter, quarter), aligned((1 - bits[1]) * quarter, quarter)
        fin_mine = aligned(grp * half + bits[1] * quarter, quarter)
        fin_other = aligned(grp * half + (1 - bits[1]) * quarter, quarter)

        def up_copy(slot):
            return remote(r3.at[slot], zbufs[0].at[slot], rs_send[0].at[slot], rs_recv[0].at[slot], mate)

        def cross_copy(slot):
            return remote(
                r3.at[slot, other], zbufs[1].at[slot], rs_send[1].at[slot], rs_recv[1].at[slot], middle
            )

        def share_copy(slot, rows):
            here = fin.at[slot, rows]
            return remote(here, here, ag_send[1].at[slot], ag_recv[1].at[slot], middle)

        def down_copy(slot):
            here = fin.at[slot, keep_half]
            return remote(here, here, ag_send[0].at[slot], ag_recv[0].at[slot], mate)

        def step_up(index):
            slot = lax.rem(index, depth)

            @pl.when(outer)
            def _():
                up_copy(slot).wait_send()

            @pl.when(inner)
            def _():
                up_copy(slot).wait_recv()
                r3[slot] = r3[slot] + zbufs[0][slot]
                cross_copy(slot).start()

        def step_cross(index):
            slot = lax.rem(index, depth)

            @pl.when(inner)
            def _():
                finished(cross_copy(slot))
                fin[slot, fin_mine] = r3[slot, mine] + zbufs[1][slot]
                share_copy(slot, fin_mine).start()

        def step_share(index):
            slot = lax.rem(index, depth)

            @pl.when(inner)
            def _():
                finished(share_copy(slot, fin_other))
                down_copy(slot).start()

        def step_down(index):
            slot = lax.rem(index, depth)

            @pl.when(inner)
            def _():
                down_copy(slot).wait_send()

            @pl.when(outer)
            def _():
                down_copy(slot).wait_recv()

            back_copy(slot, keep_half).start()

    def rs_copy(level, slot):
        rows, cols = spot(level + 1, True)
        return remote(
            r3.at[slot, rows, cols], zbufs[level].at[slot], rs_send[level].at[slot], rs_recv[level].at[slot], level_peers[level]
        )

    def ag_copy(level, slot, flip=False):
        rows, cols = spot(level + 1, flip, grp * half)
        here = fin.at[slot, rows, cols]
        return remote(here, here, ag_send[level].at[slot], ag_recv[level].at[slot], level_peers[level])

    def back_copy(slot, rows):
        here = fin.at[slot, rows]
        return remote(here, here, send6.at[slot], recv6.at[slot], grp_peer)

    def step_grp(index):
        slot = lax.rem(index, depth)
        finished(remote(r2.at[slot, give_half], r3.at[slot], send3.at[slot], recv3.at[slot], grp_peer))
        r3[slot] = r3[slot] + r2[slot, keep_half]
        if fold:

            @pl.when(outer)
            def _():
                up_copy(slot).start()
        else:
            rs_copy(0, slot).start()

    def step_scatter(level):
        def act(index):
            slot = lax.rem(index, depth)
            finished(rs_copy(level, slot))
            rows, cols = spot(level + 1)
            total = r3[slot, rows, cols] + zbufs[level][slot]
            if level + 1 < levels:
                r3[slot, rows, cols] = total
                rs_copy(level + 1, slot).start()
            else:
                rows, cols = spot(level + 1, False, grp * half)
                fin[slot, rows, cols] = total
                ag_copy(level, slot).start()

        return act

    def step_gather(level):
        def act(index):
            slot = lax.rem(index, depth)
            finished(ag_copy(level, slot, True))
            if level:
                ag_copy(level - 1, slot).start()
            else:
                back_copy(slot, keep_half).start()

        return act

    def out_wait(index):
        slot = lax.rem(index, depth)
        local_wait(fin.at[slot], sem_out.at[slot])

    def step_out(index):
        slot = lax.rem(index, depth)
        finished(back_copy(slot, give_half))

        def act(place, span):
            pltpu.make_async_copy(fin.at[slot], outs[place].at[span[0], span[1]], sem_out.at[slot]).start()

        by_range(index, act)

    z_lag = 2 if fold else 1
    order = [(YLAG, step_side), (XLAG, step_grp)]
    if fold:
        order += [(z_lag, act) for act in (step_up, step_cross, step_share, step_down)]
    else:
        order += [(z_lag, step_scatter(level)) for level in range(levels)]
        order += [(z_lag, step_gather(level)) for level in reversed(range(levels))]
    order += [(BLAG, step_out), (2, out_wait)]
    stages = [(0, step_core)]
    for lag, act in order:
        stages.append((stages[-1][0] + lag, act))
    all_ticks = chunks + stages[-1][0]

    per_slot = BLK // CHAIN
    chain_chunks = slots * per_slot

    def chain_step(stream, send, recv, number, is_first, is_last, target):
        slot = number // per_slot
        rows = aligned((number % per_slot) * CHAIN, CHAIN)
        here = stream.at[slot, rows]

        @pl.when(is_first)
        def _():
            stream[slot, rows, :] = own_part[slot, rows, :]

        @pl.when(jnp.logical_not(is_first))
        def _():
            remote(here, here, send.at[number], recv.at[number], target).wait_recv()
            stream[slot, rows, :] = stream[slot, rows, :] + own_part[slot, rows, :]

        @pl.when(jnp.logical_not(is_last))
        def _():
            remote(here, here, send.at[number], recv.at[number], target).start()

    def chain_tick(step):
        number = step - ctx

        @pl.when((number >= 0) & (number < chain_chunks))
        def _():
            chain_step(left, left_s, left_r, number, ctx == 0, ctx == n_ctx - 1, next_ctx)

        back = step - (n_ctx - 1 - ctx)

        @pl.when((back >= 0) & (back < chain_chunks))
        def _():
            chain_step(right, right_s, right_r, back, ctx == n_ctx - 1, ctx == 0, last_ctx)

    groups = PAIRS // PAIRED
    group_ticks = groups if shallow else 0
    block_ticks = group_ticks + 2
    chain_first = FF_TICKS + block_ticks
    paced = max(0, -(-(chunks - chain_first) // PACE))
    late_first = max(chunks, chain_first)
    late_beats = max(0, chain_chunks + n_ctx - 1 - paced)
    chain_ticks = late_first + TAIL_PACE * max(0, late_beats - 1) + 1

    def tick(step, kinds):
        kinds = kinds if shallow or kinds == "none" else "both"
        if kinds in ("low", "both"):

            @pl.when(step + 3 < chunks)
            def _():
                step_fetch(step + 3)

        if kinds != "none":

            @pl.when(step + 2 < chunks)
            def _():
                step_make(step + 2, kinds)

        for lag, act in stages:
            index = step - lag

            @pl.when((index >= 0) & (index < chunks))
            def _(act=act, index=index):
                act(index)

        beat = step - chain_first

        @pl.when((beat >= 0) & (step < chunks) & (beat % PACE == 0))
        def _():
            chain_tick(beat // PACE)

        late = step - late_first

        @pl.when((late >= 0) & (late % TAIL_PACE == 0))
        def _():
            chain_tick(paced + late // TAIL_PACE)


    for index in range(3):
        step_fetch(jnp.int32(index))
    for copy in set_copies(0):
        copy.start()

    hidden_tiles = u_hbm.shape[1] // SPAN
    datt_v, dz_v, dy_v, hat1_v, hat2_v = own_part.at[0], do_v, left.at[1], right.at[0], right.at[1]

    def tile_copies(tile, parity):
        cols = aligned(tile * SPAN, SPAN)
        return (
            pltpu.make_async_copy(w_down.at[cols, :], own_part.at[parity], sem_ff.at[0, parity]),
            pltpu.make_async_copy(
                w_up.at[:, cols], turned.at[0, aligned(parity * D, D), :], sem_ff.at[1, parity]
            ),
            pltpu.make_async_copy(
                u_hbm.at[:, cols], left.at[0, :, aligned(parity * SPAN, SPAN)], sem_ff.at[2, parity]
            ),
        )

    def du_store(tile, parity):
        return pltpu.make_async_copy(
            kv_b.at[0, :, aligned(parity * SPAN, SPAN)],
            du_hbm.at[:, aligned(tile * SPAN, SPAN)],
            sem_ff.at[3, parity],
        )

    dz_load = pltpu.make_async_copy(dz_hbm, dz_v, sem_in.at[0])
    dz_load.start()
    for copy in tile_copies(0, 0):
        copy.start()
    wide_loads = [
        pltpu.make_async_copy(source, dest, sem_in.at[place + 1])
        for place, (source, dest) in enumerate(
            (
                (dy_hbm, dy_v),
                (hat1_hbm, hat1_v),
                (hat2_hbm, hat2_v),
                (rstd_hbm, lse_v.at[pl.ds(0, 2)]),
                (q_hbm, q_v),
                (o_hbm, o_v),
                (w_hbm, weight),
            )
        )
    ]
    out_loads = [
        pltpu.make_async_copy(
            w_out.at[pl.ds(place * TILE, TILE), :],
            term.at[place // 2, place % 2, :, pl.ds(0, D)],
            sem_in.at[8 + place],
        )
        for place in range(4)
    ]
    for index in range(2):
        step_make(jnp.int32(index), "low")
    dz_load.wait()

    def ff_tile(tile, carry):
        start = tile + (tile + 1) // 2
        extra = 1 - tile % 2
        lax.fori_loop(start, start + 1 + extra, lambda index, inner: (tick(index, "low"), inner)[1], 0)

        parity = tile % 2
        for copy in tile_copies(tile, parity):
            copy.wait()

        @pl.when(tile + 1 < hidden_tiles)
        def _():
            for copy in tile_copies(tile + 1, 1 - parity):
                copy.start()

        @pl.when(tile == 0)
        def _():
            for copy in wide_loads + out_loads:
                copy.start()

        @pl.when(tile >= 2)
        def _():
            du_store(tile - 2, parity).wait()

        u_cols = aligned(parity * SPAN, SPAN)
        u_tile = left[0, :, u_cols].astype(jnp.float32)
        square = u_tile * u_tile
        bend = jnp.tanh(GELU_C * u_tile * (1.0 + GELU_A * square))
        slope = 0.5 * (1.0 + bend) + (0.5 * GELU_C) * u_tile * (1.0 - bend * bend) * (
            1.0 + 3.0 * GELU_A * square
        )
        du_tile = (contract_last(dz_v[...], own_part[parity]) * slope).astype(jnp.bfloat16)
        kv_b[0, :, u_cols] = du_tile
        du_store(tile, parity).start()
        fresh = contract_last(du_tile, turned[0, aligned(parity * D, D), :])

        @pl.when(tile == 0)
        def _():
            dq_acc[...] = fresh

        @pl.when(tile > 0)
        def _():
            dq_acc[...] = dq_acc[...] + fresh

        return carry

    lax.fori_loop(0, hidden_tiles, ff_tile, 0)
    for tile in range(hidden_tiles - 2, hidden_tiles):
        du_store(tile, tile % 2).wait()
    for copy in wide_loads:
        copy.wait()
    for copy in block_copies(1):
        copy.start()

    def hidden_back(step, carry):
        gain1, gain2, bias1, bias2 = carry
        rows = aligned(step * CHAIN, CHAIN)
        upstream = dq_acc[rows, :]
        hat = hat2_v[rows, :].astype(jnp.float32)
        grad_h = dy_v[rows, :].astype(jnp.float32) + row_back(
            upstream, hat, lse_v[1, rows, 0:1], gain_ref[2:3, :]
        )
        gain2, bias2 = gain2 + column_sum(upstream * hat), bias2 + column_sum(upstream)
        dq_acc[rows, :] = grad_h
        if shallow:
            gkv[rows, :] = grad_h
        hat = hat1_v[rows, :].astype(jnp.float32)
        datt_v[rows, :] = row_back(grad_h, hat, lse_v[0, rows, 0:1], gain_ref[1:2, :]).astype(
            jnp.bfloat16
        )
        return gain1 + column_sum(grad_h * hat), gain2, bias1 + column_sum(grad_h), bias2

    zero = jnp.zeros((1, D), jnp.float32)
    sums = lax.fori_loop(0, BLK // CHAIN, hidden_back, (zero,) * 4)
    row = lax.broadcasted_iota(jnp.int32, (8, D), 0)
    norm_v[...] = norm_ref[...]
    for place, value in zip((1, 2, 5, 6), sums):
        norm_v[...] = norm_v[...] + jnp.where(row == place, value, 0.0)
    tick(FF_TICKS - 1, "low")
    stores = [
        pltpu.make_async_copy(dq_acc, dh_hbm, sem_res.at[0]),
        pltpu.make_async_copy(datt_v, datt_hbm, sem_res.at[1]),
    ]
    lse_load = pltpu.make_async_copy(lse_hbm, lse_v, sem_in.at[0])
    for copy in stores + [lse_load]:
        copy.start()
    for place in range(4):
        out_loads[place].wait()
        do_v[:, pl.ds(place * TILE, TILE)] = contract_last(
            datt_v[...], term[place // 2, place % 2, :, pl.ds(0, D)]
        ).astype(jnp.bfloat16)
    for copy in stores + [lse_load]:
        copy.wait()
    dq_acc[...] = jnp.zeros_like(dq_acc)

    def attend(kv_ref, turned_ref, own, visible, begin):
        def body(group, carry):
            if shallow:
                tick(begin + group, "low")
            for member in range(PAIRED):
                grad_block(
                    q_v, do_v, o_v, lse_v, kv_ref, dq_acc, turned_ref, group * PAIRED + member, own, visible
                )
            return carry

        lax.fori_loop(0, groups, body, 0)

    def first_sums(piece, normed, cols):
        gain_sum[:, cols] = gain_sum[:, cols] + column_sum(piece * normed.astype(jnp.float32))
        bias_sum[:, cols] = bias_sum[:, cols] + column_sum(piece)

    gain_sum[...] = jnp.zeros_like(gain_sum)
    bias_sum[...] = jnp.zeros_like(bias_sum)

    def each_slot(slot, carry):
        visible = slot < own_slot
        index = slot + 1
        place = lax.rem(index, kv_b.shape[0])
        for copy in block_copies(index):
            copy.wait()
        if kv_b.shape[0] > 1:
            for copy in block_copies(index + 1):
                copy.start()
        begin = FF_TICKS + slot * block_ticks
        a_place = slot if shallow else 0
        attend(kv_b.at[place], turned.at[a_place], False, visible, begin)

        def weight_terms(step, inner):
            tick(begin + group_ticks + step, "low")
            rows = aligned(step * 512, 512)
            for part in range(0 if shallow else 2):
                cols = pl.ds(part * D, D)
                product = dot_dims(a_b[a_place, :, rows], turned[a_place, cols, :], 0, 1)
                for down in range(2):
                    target = term.at[step, down, :, pl.ds((part + 1) * D, D)]
                    piece = product[down * TILE : (down + 1) * TILE]

                    @pl.when(slot == 0)
                    def _(target=target, piece=piece):
                        target[...] = piece.astype(target.dtype)

                    @pl.when(slot > 0)
                    def _(target=target, piece=piece):
                        target[...] = (target[...] + piece).astype(target.dtype)

            piece = dot_dims(turned[a_place], weight[rows, pl.ds(D, 2 * D)], 0, 1)
            own_part[slot, :, rows] = piece.astype(jnp.bfloat16)
            first_sums(piece, a_b[a_place, :, rows], rows)
            return inner

        lax.fori_loop(0, 2, weight_terms, 0)
        if kv_b.shape[0] == 1:
            for copy in block_copies(index + 1):
                copy.start()
        return carry

    lax.fori_loop(0, slots, each_slot, 0)
    begin = FF_TICKS + slots * block_ticks
    own_place = (slots + 1) % kv_b.shape[0]
    for copy in block_copies(slots + 1):
        copy.wait()
    own_a = slots if shallow else 0
    attend(kv_b.at[own_place], turned.at[own_a], True, None, begin)
    dq_low[...] = (dq_acc[...] * ALPHA).astype(jnp.bfloat16) * jnp.bfloat16(QSCALE)
    x_load = pltpu.make_async_copy(x_hbm, do_v, sem_in.at[0])
    x_load.start()
    ready = begin + group_ticks

    def last_terms(step, carry):
        tick(begin + group_ticks + step, "both")
        rows = aligned(step * TILE, TILE)
        a_rows = a_b[0, :, rows]
        up, down = step // 2, step % 2
        term[up, down, :, pl.ds(0, D)] = dot_dims(a_rows, dq_low[...], 0, 0).astype(jnp.bfloat16)
        for part in range(2):
            cols = pl.ds(part * D, D)
            target = term.at[up, down, :, pl.ds((part + 1) * D, D)]
            target[...] = (target[...] + dot_dims(a_rows, turned[0, cols, :], 0, 1)).astype(jnp.bfloat16)
        return carry

    if not shallow:
        lax.fori_loop(0, 4, last_terms, 0)
        ready = ready + 4
    assert ready <= last_low - 2
    da_acc = dq_acc

    def own_grad(step, carry):
        tick(ready + step, "low")
        rows = aligned(step * TILE, TILE)
        piece = dot_dims(dq_low[...], weight[rows, pl.ds(0, D)], 1, 1) + dot_dims(
            turned[own_a], weight[rows, pl.ds(D, 2 * D)], 0, 1
        )
        da_acc[:, rows] = piece
        first_sums(piece, a_b[own_a, :, rows], rows)
        return carry

    lax.fori_loop(0, 4, own_grad, 0)
    ready = ready + 4

    first_gain = (gain_sum[...] - bias_ref[0:1, :] * bias_sum[...]) / gain_ref[0:1, :]
    norm_v[...] = (
        norm_v[...] + jnp.where(row == 0, first_gain, 0.0) + jnp.where(row == 4, bias_sum[...], 0.0)
    )

    def run_ticks(first, last, kinds):
        if last > first:
            lax.fori_loop(first, last, lambda index, carry: (tick(index, kinds), carry)[1], 0)
        return max(first, last)

    if shallow:
        assert ready <= last_low - 2
        ready = run_ticks(ready, last_low - 2, "low")
    norm_peers = [core_peer, side_peer, grp_peer] + level_peers
    norm_base = ready
    norm_result = pltpu.make_async_copy(norm_v, norm_out, sem_res.at[1])

    def norm_move(place):
        return remote(norm_v, norm_in.at[place], norm_s.at[place], norm_r.at[place], norm_peers[place])

    def norm_ticks(step, carry):
        for place in range(len(norm_peers) + 1):

            @pl.when(step == norm_base + 3 * place)
            def _(place=place):
                if place:
                    finished(norm_move(place - 1))
                    norm_v[...] = norm_v[...] + norm_in[place - 1]
                if place < len(norm_peers):
                    norm_move(place).start()
                else:
                    norm_result.start()

        tick(step, "high")
        return carry

    last_tick = max(ready + 3 * len(norm_peers) + 1, chain_ticks)
    lax.fori_loop(ready, last_tick, norm_ticks, 0)
    ready = last_tick
    x_load.wait()
    gain = gain_ref[0:1, :]

    def norm_grad(step, carry):
        @pl.when(step % 2 == 0)
        def _():
            tick(ready + step // 2, "none")

        rows = aligned(step * CHAIN, CHAIN)
        upstream = da_acc[rows, :]
        for slot in range(slots):
            joined = left[slot, rows, :].astype(jnp.float32) + right[slot, rows, :].astype(jnp.float32)
            upstream = upstream + jnp.where(own_slot == slot, joined, 0.0)
        values = do_v[rows, :].astype(jnp.float32)
        centre = values - jnp.mean(values, axis=-1, keepdims=True)
        scale = lax.rsqrt(jnp.mean(centre * centre, axis=-1, keepdims=True) + EPS)
        centre = centre * scale
        grad = row_back(upstream, centre, scale, gain)
        da_acc[rows, :] = grad + gkv[rows, :] if shallow else grad
        return carry

    lax.fori_loop(0, BLK // CHAIN, norm_grad, 0)
    ready = ready + BLK // CHAIN // 2
    result = pltpu.make_async_copy(da_acc, grad_out, sem_res.at[0])
    result.start()
    run_ticks(ready, all_ticks, "none")

    def drain_chain(index, carry):
        here = left.at[0, pl.ds(0, CHAIN)]

        @pl.when(ctx < n_ctx - 1)
        def _():
            remote(here, here, left_s.at[index], left_r.at[index], next_ctx).wait_send()

        @pl.when(ctx > 0)
        def _():
            remote(here, here, right_s.at[index], right_r.at[index], last_ctx).wait_send()

        return carry

    lax.fori_loop(0, chain_chunks, drain_chain, 0)
    result.wait()
    norm_result.wait()


def backward_part(n_ctx, slot_vec, gains, biases, norms, saved, weights, ffn):
    slots = n_ctx // 2
    levels = n_ctx.bit_length() - 1
    depth = 16 if n_ctx == 4 else 10
    hidden = weights[1].shape[1]
    widths = [(hidden // 4, D), (D // 4, hidden), (D // 4, D), (D // 4, 3 * D)]
    low, full = jnp.bfloat16, jnp.float32
    dma = pltpu.SemaphoreType.DMA
    hbm = pl.BlockSpec(memory_space=pl.ANY)
    vmem = pl.BlockSpec(memory_space=pltpu.VMEM)
    shape = jax.ShapeDtypeStruct
    buffers = 2 if slots <= 2 else 1
    chain = slots * (BLK // CHAIN)
    zshapes, rows, cols = [], TILE // 2, TILE
    if n_ctx == 4:
        zshapes = [pltpu.VMEM((depth, rows, cols), low), pltpu.VMEM((depth, rows // 2, cols), low)]
    for _ in range(0 if zshapes else levels):
        rows, cols = (rows // 2, cols) if rows > 16 else (rows, cols // 2)
        zshapes.append(pltpu.VMEM((depth, rows, cols), low))
    return pl.pallas_call(
        functools.partial(backward_kernel, n_ctx, widths),
        out_shape=[shape(width, low) for width in widths] + [
            shape((BLK, D), full),
            shape((8, D), full),
            shape((BLK, D), full),
            shape((BLK, hidden), low),
            shape((BLK, D), low),
        ],
        in_specs=[pl.BlockSpec(memory_space=pltpu.SMEM), vmem, vmem, vmem]
        + [hbm] * (len(saved) + len(weights) + len(ffn)),
        out_specs=[hbm] * 9,
        scratch_shapes=[
            pltpu.VMEM((BLK, D), low),
            pltpu.VMEM((BLK, D), low),
            pltpu.VMEM((BLK, D), low),
            pltpu.VMEM((PAIRS, BLK, 128), full),
            pltpu.VMEM((D, 3 * D), low),
            pltpu.VMEM((buffers, BLK, 2 * D), low),
            pltpu.VMEM((slots + 1 if slots <= 2 else 1, BLK, D), low),
            pltpu.VMEM((BLK, D), full),
            pltpu.VMEM((slots + 1 if slots <= 2 else 1, 2 * D, BLK), low),
            pltpu.VMEM((BLK, D) if slots <= 2 else (8, 128), full),
            pltpu.VMEM((2, 2, D // 4, D if slots <= 2 else 3 * D), low),
            pltpu.VMEM((slots, BLK, D), low),
            pltpu.VMEM((slots, BLK, D), low),
            pltpu.VMEM((slots, BLK, D), low),
            pltpu.VMEM((8, D), full),
            pltpu.VMEM((3 + levels, 8, D), full),
            pltpu.VMEM((1, D), full),
            pltpu.VMEM((1, D), full),
            pltpu.VMEM((depth, 2, TILE, TILE), low),
            pltpu.VMEM((depth, TILE, TILE), low),
            pltpu.VMEM((depth, TILE // 2, TILE), low),
            pltpu.VMEM((depth, TILE, TILE), low),
            pltpu.VMEM((4, 2, 2, TILE, TILE), low),
        ]
        + [pltpu.VMEM((2, 4, BLK, TILE), low), pltpu.VMEM((4, BLK, TILE), low)]
        + zshapes
        + [dma((12,)), dma((2, buffers)), dma((4,)), dma((2, 4)), dma((4, 2)), dma((depth,)), dma((2,))]
        + [dma((depth,))] * (8 + 4 * levels)
        + [dma((chain,))] * 4
        + [dma((3 + levels,))] * 2,
        compiler_params=pltpu.CompilerParams(
            collective_id=2, has_side_effects=True, vmem_limit_bytes=67043328
        ),
        cost_estimate=pl.CostEstimate(flops=40 << 30, bytes_accessed=64 << 20, transcendentals=1 << 24),
        name="attend_back_reduce",
    )(
        slot_vec,
        gains,
        biases,
        norms,
        *saved,
        *weights,
        *ffn,
    )


def widen_kernel(*refs):
    count = len(refs) // 2
    for source, dest in zip(refs[: count - 1], refs[count:]):
        dest[...] = source[...].astype(dest.dtype)
    refs[-2][...] = refs[count - 1][0:4, :]
    refs[-1][...] = refs[count - 1][4:8, :]


def widen(arrays, types, norms):
    steps = 8
    specs = [pl.BlockSpec((x.shape[0] // steps, x.shape[1]), lambda i: (i, 0)) for x in arrays]
    shape = jax.ShapeDtypeStruct
    pair = [pl.BlockSpec((4, D), lambda i: (0, 0))] * 2
    return pl.pallas_call(
        widen_kernel,
        out_shape=[shape(x.shape, kind) for x, kind in zip(arrays, types)]
        + [shape((4, D), jnp.float32)] * 2,
        grid=(steps,),
        in_specs=specs + [pl.BlockSpec((8, D), lambda i: (0, 0))],
        out_specs=specs + pair,
        compiler_params=pltpu.CompilerParams(vmem_limit_bytes=67043328),
        name="widen",
    )(*arrays, norms)


def per_device(n_ctx, inputs, w_qkv, w_out, w_up, w_down, norm_gains, norm_biases, block_map, out_grad):
    slots = n_ctx // 2
    raw, seed_low = inputs.reshape(BLK, D), out_grad.reshape(BLK, D)
    block_entry = block_map.reshape(2)
    forward = forward_part(
        n_ctx,
        block_entry,
        norm_gains,
        norm_biases,
        raw,
        seed_low,
        w_qkv,
        w_out,
        w_up,
        w_down,
    )
    every_low, queries, keys_values, attn_low, lse, full_qkv, full_out, full_up, full_down = forward[:9]
    result, active_low, down_low, ffn_low, upward, hat1, hat2, rstd, norms = forward[9:]
    backward = backward_part(
        n_ctx,
        block_entry,
        norm_gains,
        norm_biases,
        norms,
        [raw, queries, keys_values, every_low, attn_low, lse, full_qkv],
        [full_out, full_up, full_down],
        [active_low, down_low, ffn_low, upward, hat1, hat2, rstd, seed_low],
    )
    grad_tokens, norm_total, grad_hidden = backward[4:7]
    if slots > 2:
        grad_tokens = grad_tokens + grad_hidden
    full = jnp.float32
    summed_down, summed_up, summed_out, summed_qkv, grad_input, result, gain_total, bias_total = widen(
        list(backward[:4]) + [grad_tokens, result],
        [full] * 5 + [jnp.bfloat16],
        norm_total,
    )
    return (
        result.reshape(1, 1, BLK, D),
        grad_input.reshape(1, 1, BLK, D),
        summed_qkv,
        summed_out,
        summed_up,
        summed_down,
        gain_total,
        bias_total,
    )


def solution(mesh):
    rows = P("wsh", None)
    blocks = P("grp", "wsh", "ctx", None)
    return jax.shard_map(
        functools.partial(per_device, mesh.shape["ctx"]),
        mesh=mesh,
        in_specs=(blocks, rows, rows, rows, rows, P(), P(), blocks, blocks),
        out_specs=(blocks, blocks, rows, rows, rows, rows, P(), P()),
        check_vma=False,
    )
```

```python
import functools
import math

import jax
import jax.numpy as jnp
from jax import lax
from jax.experimental import pallas as pl
from jax.experimental.pallas import tpu as pltpu
from jax.sharding import PartitionSpec as P

D = 1024
HEADS = 16
DH = 64
BLK = 512
PAIRS = HEADS // 2
QT = 256

EPS = 1e-05
ALPHA = 32.0
NEG = -1e30
LOG2E = 1.4426950408889634
C2 = ALPHA * LOG2E
MESH = pl.DeviceIdType.MESH
QSCALE = 1.0 / (ALPHA * math.sqrt(DH))


def layer_norm(values, gain_row, bias_row):
    centre = values - jnp.mean(values, axis=-1, keepdims=True)
    spread = jnp.mean(centre * centre, axis=-1, keepdims=True)
    return centre * lax.rsqrt(spread + EPS) * gain_row + bias_row


def dot_dims(left_side, right_side, left_dim, right_dim):
    return lax.dot_general(
        left_side,
        right_side,
        (((left_dim,), (right_dim,)), ((), ())),
        preferred_element_type=jnp.float32,
    )


def contract_last(left_side, right_side):
    return dot_dims(left_side, right_side, 1, 1)


def contract_rows(left_side, right_side):
    return dot_dims(left_side, right_side, 0, 0)


def standard_rows(values):
    centre = values - jnp.mean(values, axis=-1, keepdims=True)
    scale = lax.rsqrt(jnp.mean(centre * centre, axis=-1, keepdims=True) + EPS)
    return centre * scale, scale


def row_back(upstream, hat, scale, gain):
    scaled = upstream * gain
    return scale * (
        scaled
        - jnp.mean(scaled, axis=-1, keepdims=True)
        - hat * jnp.mean(scaled * hat, axis=-1, keepdims=True)
    )


def column_sum(values):
    return jnp.sum(values, axis=0, keepdims=True)


def head_lanes(head, rows):
    lane = lax.broadcasted_iota(jnp.int32, (rows, 128), 1)
    return (lane >= DH) if head else (lane < DH)


def causal_tile():
    row = lax.broadcasted_iota(jnp.int32, (QT, QT), 0)
    col = lax.broadcasted_iota(jnp.int32, (QT, QT), 1)
    return col <= row


PIECE = 128
SPAN = 512
CHAIN = 64
HOP = 2
YLAG = 3
XLAG = 2
BLAG = 2
FF_TICKS = 13
TAIL_PACE = 3
GELU_A = 0.044715
GELU_C = math.sqrt(2.0 / math.pi)
PACE = 2
LAG = 2
GROUP = 4
AHEAD = 4


def remote(src, dst, send, recv, peer):
    return pltpu.make_async_remote_copy(
        src_ref=src, dst_ref=dst, send_sem=send, recv_sem=recv, device_id=peer, device_id_type=MESH
    )


def local_wait(ref, sem):
    pltpu.make_async_copy(ref, ref, sem).wait()


def aligned(start, size):
    return pl.ds(pl.multiple_of(start, size), size)


def softmax_block(q_ref, kv_ref, acc, top_ref, sum_ref, pair, base, own, visible):
    lanes = aligned(pair * 128, 128)
    value_lanes = aligned(D + pair * 128, 128)
    causal = causal_tile()
    first = head_lanes(0, QT)
    count = BLK // QT
    q_pair = q_ref[:, lanes]
    keys = kv_ref[pl.ds(base, BLK), lanes]
    values = kv_ref[pl.ds(base, BLK), value_lanes]
    if not own:
        old_top, old_sum, old_out = top_ref[pair], sum_ref[pair], acc[:, lanes]
        hide = jnp.where(visible, 0.0, 1e30)
    results = []
    work = [(tile, head) for tile in range(count) for head in range(2)]
    parts_of = {}
    for tile, head in work:
        q_tile = q_pair[tile * QT : (tile + 1) * QT]
        q_head = jnp.where(head_lanes(head, QT), q_tile, jnp.zeros_like(q_tile))
        span = (tile + 1) * QT if own else BLK
        parts_of[tile, head] = contract_last(q_head, keys[:span])
    top_of, expo_of, total_of = {}, {}, {}
    for tile, head in work:
        part = parts_of[tile, head]
        if own:
            diag = jnp.where(causal, part[:, tile * QT :], NEG)
            part = jnp.concatenate([part[:, : tile * QT], diag], axis=1) if tile else diag
        top = jnp.max(part, axis=-1, keepdims=True) * C2
        if own:
            shift = top
        else:
            top = jnp.maximum(
                jnp.where(visible, top, NEG), old_top[tile * QT : (tile + 1) * QT, head * DH : head * DH + 1]
            )
            shift = top + hide
        expo = jnp.exp2(part * C2 - shift)
        top_of[tile, head] = jnp.broadcast_to(top, (QT, 128))
        total_of[tile, head] = jnp.broadcast_to(jnp.sum(expo, axis=-1, keepdims=True), (QT, 128))
        expo_of[tile, head] = expo.astype(jnp.bfloat16)
    out_of = {}
    for tile, head in work:
        span = (tile + 1) * QT if own else BLK
        out_of[tile, head] = dot_dims(expo_of[tile, head], values[:span], 1, 0)
    for tile in range(count):
        rows = pl.ds(tile * QT, QT)
        new_top = jnp.where(first, top_of[tile, 0], top_of[tile, 1])
        new_sum = jnp.where(first, total_of[tile, 0], total_of[tile, 1])
        new_out = jnp.where(first, out_of[tile, 0], out_of[tile, 1])
        if not own:
            here = slice(tile * QT, (tile + 1) * QT)
            keep = jnp.exp2(old_top[here] - new_top)
            new_sum = new_sum + old_sum[here] * keep
            new_out = new_out + old_out[here] * keep
        top_ref[pair, rows, :] = new_top
        sum_ref[pair, rows, :] = new_sum
        acc[rows, lanes] = new_out


def forward_kernel(n_ctx, *refs):
    slots = n_ctx // 2
    (slot_ref, gain_ref, bias_ref, x_hbm, dy_hbm, w_qkv, w_out, w_up, w_down) = refs[:9]
    (a_out, q_out, kv_out, o_out, lse_out, full_qkv, full_out, full_up, full_down) = refs[9:18]
    (y_out, g_out, dz_out, f_out, u_out, hat1_out, hat2_out, rstd_out, norm_out) = refs[18:27]
    (x_own, left, right, a_all, q_all, kv_all, weight, acc, z_acc, norm_v, tops, sums, hop) = refs[27:40]
    (sem_in, sem_load, sem_store, sem_ff, sem_out, sem_a, sem_kv, side_s, side_r, grp_s, grp_r, cs_s, cs_r, cg_s, cg_r, own_s, own_r, left_s, left_r, right_s, right_r) = refs[40:]
    grp, ctx, wsh = lax.axis_index("grp"), lax.axis_index("ctx"), lax.axis_index("wsh")
    side, core = wsh // 2, wsh % 2
    core_peer = (grp, ctx, side * 2 + 1 - core)
    side_peer = (grp, ctx, (1 - side) * 2 + core)
    grp_peer = (1 - grp, ctx, wsh)
    next_ctx = (grp, lax.rem(ctx + 1, n_ctx), wsh)
    last_ctx = (grp, lax.rem(ctx + n_ctx - 1, n_ctx), wsh)

    load = pltpu.make_async_copy(x_hbm, x_own, sem_in.at[0])
    load.start()
    barrier = pltpu.get_barrier_semaphore()
    for peer in (core_peer, side_peer, grp_peer, next_ctx, last_ctx):
        pl.semaphore_signal(barrier, inc=1, device_id=peer, device_id_type=MESH)
    pl.semaphore_wait(barrier, 5)

    shards = (w_qkv, w_out, w_up, w_down)
    fulls = (weight, full_out, full_up, full_down)
    ranges, start = [], 0
    for shard in shards:
        across = shard.shape[1] // SPAN
        ranges.append((start, start + across * (shard.shape[0] // (2 * PIECE)), across))
        start = ranges[-1][1]
    pieces = start

    def by_range(index, act):
        for place, (low, high, across) in enumerate(ranges):

            @pl.when((index >= low) & (index < high))
            def _(place=place, low=low, across=across):
                act(place, (index - low) // across, aligned(((index - low) % across) * SPAN, SPAN))

    def rows_of(place, owner, half, group):
        shard_rows = shards[place].shape[0]
        return aligned(owner * shard_rows + half * (shard_rows // 2) + group * PIECE, PIECE)

    sides_owner = (1 - side) * 2 + core

    def send_piece(index, carry):
        def act(place, group, cols):
            remote(
                shards[place].at[rows_of(place, 0, grp, group), cols],
                fulls[place].at[rows_of(place, wsh, grp, group), cols],
                side_s.at[index],
                side_r.at[index],
                side_peer,
            ).start()

        by_range(index, act)
        return carry

    def own_copies():
        copies = []
        across = shards[0].shape[1] // SPAN
        for place in range(4):
            shard_rows = shards[place].shape[0]
            mine = aligned(wsh * shard_rows, shard_rows)
            steps = range(across) if place == 0 else [None]
            for step in steps:
                cols = slice(None) if step is None else pl.ds(step * SPAN, SPAN)
                number = len(copies)
                copies.append(
                    remote(
                        shards[place].at[:, cols],
                        fulls[place].at[mine, cols],
                        own_s.at[number],
                        own_r.at[number],
                        core_peer,
                    )
                )
        return copies

    for index in range(AHEAD):
        send_piece(index, 0)
    for copy in own_copies():
        copy.start()
    own_rows = aligned(wsh * w_qkv.shape[0], w_qkv.shape[0])
    own_weight = pltpu.make_async_copy(w_qkv, weight.at[own_rows, :], sem_in.at[1])
    own_weight.start()
    load.wait()

    bounces, start = [], 0
    for shard in shards[1:]:
        across = shard.shape[1] // SPAN
        bounces.append((start, start + across * (shard.shape[0] // (2 * PIECE)), across))
        start = bounces[-1][1]
    moves = start

    def bounce(index, loading):
        slot = lax.rem(index, 3)
        for place, (low, high, across) in enumerate(bounces):

            @pl.when((index >= low) & (index < high))
            def _(place=place + 1, low=low, across=across):
                group = (index - low) // across
                cols = aligned(((index - low) % across) * SPAN, SPAN)
                if loading:
                    here = shards[place].at[aligned(group * 2 * PIECE, 2 * PIECE), cols]
                    pltpu.make_async_copy(here, hop.at[slot], sem_load.at[slot]).start()
                else:
                    rows = aligned(wsh * shards[place].shape[0] + group * 2 * PIECE, 2 * PIECE)
                    local_wait(hop.at[slot], sem_load.at[slot])
                    pltpu.make_async_copy(
                        hop.at[slot], fulls[place].at[rows, cols], sem_store.at[slot]
                    ).start()

    own_slot = slot_ref[1] // BLK
    own_tag = jnp.where(slot_ref[0] == 0, own_slot, n_ctx)
    chain_chunks = slots * (BLK // CHAIN)

    def chain_step(stream, send, recv, number, is_first, is_last, target):
        slot = number // (BLK // CHAIN)
        spot = aligned((number % (BLK // CHAIN)) * CHAIN, CHAIN)
        mine = jnp.where(own_tag == slot, x_own[spot, :], jnp.zeros((CHAIN, D), jnp.bfloat16))
        here = stream.at[slot, spot]

        @pl.when(is_first)
        def _():
            stream[slot, spot, :] = mine

        @pl.when(jnp.logical_not(is_first))
        def _():
            remote(here, here, send.at[number], recv.at[number], target).wait_recv()
            stream[slot, spot, :] = stream[slot, spot, :] + mine

        @pl.when(jnp.logical_not(is_last))
        def _():
            remote(here, here, send.at[number], recv.at[number], target).start()

    def tick(step):
        @pl.when((step >= 1) & (step <= moves))
        def _():
            bounce(step - 1, False)

        @pl.when((step >= 3) & (step < moves))
        def _():
            local_wait(hop.at[lax.rem(step, 3)], sem_store.at[lax.rem(step, 3)])

        @pl.when(step < moves)
        def _():
            bounce(step, True)

        @pl.when(step + AHEAD < pieces)
        def _():
            send_piece(step + AHEAD, 0)

        number = step - HOP * ctx

        @pl.when((number >= 0) & (number < chain_chunks))
        def _():
            chain_step(left, left_s, left_r, number, ctx == 0, ctx == n_ctx - 1, next_ctx)

        back = step - HOP * (n_ctx - 1 - ctx)

        @pl.when((back >= 0) & (back < chain_chunks))
        def _():
            chain_step(right, right_s, right_r, back, ctx == n_ctx - 1, ctx == 0, last_ctx)

        @pl.when(step < pieces)
        def _():
            def act(place, group, cols):
                here = fulls[place].at[rows_of(place, sides_owner, grp, group), cols]
                remote(here, here, side_s.at[step], side_r.at[step], side_peer).wait_recv()
                remote(here, here, grp_s.at[step], grp_r.at[step], grp_peer).start()
                remote(here, here, cs_s.at[step], cs_r.at[step], core_peer).start()

            by_range(step, act)

        late = step - LAG

        @pl.when((late >= 0) & (late < pieces))
        def _():
            def act(place, group, cols):
                here = fulls[place].at[rows_of(place, sides_owner, 1 - grp, group), cols]
                remote(here, here, grp_s.at[late], grp_r.at[late], grp_peer).wait_recv()
                remote(here, here, cg_s.at[late], cg_r.at[late], core_peer).start()

            by_range(late, act)

    def ticks(first, last):
        lax.fori_loop(first, last, lambda index, carry: (tick(index), carry)[1], 0)

    def normalise(source, dest):
        gain, bias = gain_ref[0:1, :], bias_ref[0:1, :]

        def body(index, carry):
            rows = aligned(index * 128, 128)
            values = source(rows).astype(jnp.float32)
            a_all[aligned(dest + index * 128, 128), :] = layer_norm(values, gain, bias).astype(
                jnp.bfloat16
            )
            return carry

        lax.fori_loop(0, BLK // 128, body, 0)

    def piece_ready(index):
        here = fulls[0].at[pl.ds(0, PIECE), pl.ds(0, SPAN)]
        remote(here, here, cs_s.at[index], cs_r.at[index], core_peer).wait_recv()
        remote(here, here, cg_s.at[index], cg_r.at[index], core_peer).wait_recv()
        whole = fulls[0].at[pl.ds(0, 2 * PIECE), pl.ds(0, SPAN)]
        remote(whole, whole, own_s.at[index], own_r.at[index], core_peer).wait_recv()

    tick(0)
    normalise(lambda rows: x_own[rows, :], 0)
    ticks(1, LAG + 1)
    own_weight.wait()

    def project_q(index, carry):
        tick(index + LAG + 1)
        piece_ready(index)
        cols = aligned(index * SPAN, SPAN)
        q_all[:, cols] = (
            jnp.dot(a_all[pl.ds(0, BLK), :], weight[:, cols], preferred_element_type=jnp.float32) * QSCALE
        ).astype(jnp.bfloat16)
        return carry

    lax.fori_loop(0, D // SPAN, project_q, 0)
    head_ticks = LAG + 1 + D // SPAN

    def project_kv(index, base):
        cols = aligned(index * SPAN, SPAN)
        rows = aligned(base, BLK)
        kv_all[rows, cols] = jnp.dot(
            a_all[rows, :], weight[:, aligned(D + index * SPAN, SPAN)], preferred_element_type=jnp.float32
        ).astype(jnp.bfloat16)

    def own_kv(index, carry):
        tick(index + head_ticks)
        piece_ready(index + D // SPAN)
        project_kv(index, 0)
        return carry

    lax.fori_loop(0, 2 * D // SPAN, own_kv, 0)
    own_ticks = head_ticks + 2 * D // SPAN

    def send_block(index):
        rows = aligned(index * BLK, BLK)
        pltpu.make_async_copy(a_all.at[rows, :], a_out.at[rows, :], sem_a.at[index]).start()
        pltpu.make_async_copy(kv_all.at[rows, :], kv_out.at[rows, :], sem_kv.at[index]).start()

    outputs = [
        pltpu.make_async_copy(weight, full_qkv, sem_out.at[0]),
        pltpu.make_async_copy(q_all, q_out, sem_out.at[1]),
    ]
    for copy in outputs:
        copy.start()

    send_block(0)

    def own_attention(group, carry):
        ticks(own_ticks + 2 * group, own_ticks + 2 * group + 2)
        for member in range(GROUP):
            softmax_block(q_all, kv_all, acc, tops, sums, group * GROUP + member, 0, True, None)
        return carry

    groups = PAIRS // GROUP
    lax.fori_loop(0, groups, own_attention, 0)
    used = own_ticks + 2 * groups
    per_slot = 2 * D // SPAN + 2 * groups

    need = BLK // CHAIN + HOP * (n_ctx - 1)
    early = max(0, need - used)
    if early:
        lax.fori_loop(0, early, lambda index, carry: (tick(used + index), carry)[1], 0)

    def each_slot(slot, carry):
        base = pl.multiple_of((slot + 1) * BLK, BLK)
        visible = slot < own_slot
        begin = early + used + slot * per_slot

        def total(rows):
            joined = left[slot, rows, :] + right[slot, rows, :]
            return jnp.where(own_tag == slot, x_own[rows, :], joined)

        normalise(total, base)

        def slot_kv(index, inner):
            tick(begin + index)
            project_kv(index, base)
            return inner

        lax.fori_loop(0, 2 * D // SPAN, slot_kv, 0)

        send_block(slot + 1)

        def slot_attention(group, inner):
            start = begin + 2 * D // SPAN + 2 * group
            ticks(start, start + 2)
            for member in range(GROUP):
                softmax_block(
                    q_all, kv_all, acc, tops, sums, group * GROUP + member, base, False, visible
                )
            return inner

        lax.fori_loop(0, groups, slot_attention, 0)
        return carry

    lax.fori_loop(0, slots, each_slot, 0)
    done_ticks = early + used + slots * per_slot

    def finish(pair, carry):
        lanes = aligned(pair * 128, 128)
        x_own[:, lanes] = (acc[:, lanes] / sums[pair]).astype(jnp.bfloat16)
        tops[pair] = tops[pair] + jnp.log2(sums[pair])
        return carry

    lax.fori_loop(0, PAIRS, finish, 0)
    outputs += [
        pltpu.make_async_copy(x_own, o_out, sem_out.at[2]),
        pltpu.make_async_copy(tops, lse_out, sem_out.at[3]),
    ]
    for copy in outputs[2:]:
        copy.start()
    all_ticks = max(pieces + LAG, chain_chunks + HOP * (n_ctx - 1))
    if all_ticks > done_ticks:
        lax.fori_loop(done_ticks, all_ticks, lambda index, carry: (tick(index), carry)[1], 0)

    def drain(index, carry):
        here = fulls[0].at[pl.ds(0, PIECE), pl.ds(0, SPAN)]

        @pl.when(index >= ranges[0][1])
        def _():
            remote(here, here, cs_s.at[index], cs_r.at[index], core_peer).wait_recv()
            remote(here, here, cg_s.at[index], cg_r.at[index], core_peer).wait_recv()

        remote(here, here, side_s.at[index], side_r.at[index], side_peer).wait_send()
        remote(here, here, grp_s.at[index], grp_r.at[index], grp_peer).wait_send()
        remote(here, here, cs_s.at[index], cs_r.at[index], core_peer).wait_send()
        remote(here, here, cg_s.at[index], cg_r.at[index], core_peer).wait_send()
        return carry

    lax.fori_loop(0, pieces, drain, 0)
    copies = own_copies()
    for number, copy in enumerate(copies):
        copy.wait_send()
        if number >= len(copies) - 3:
            copy.wait_recv()
    for index in range(moves - 3, moves):
        local_wait(hop.at[index % 3], sem_store.at[index % 3])

    def drain_chain(index, carry):
        here = left.at[0, pl.ds(0, CHAIN)]

        @pl.when(ctx < n_ctx - 1)
        def _():
            remote(here, here, left_s.at[index], left_r.at[index], next_ctx).wait_send()

        @pl.when(ctx > 0)
        def _():
            remote(here, here, right_s.at[index], right_r.at[index], last_ctx).wait_send()

        return carry

    lax.fori_loop(0, chain_chunks, drain_chain, 0)
    for copy in outputs[:2]:
        copy.wait()
    shallow_tiles = full_up.shape[1] // SPAN

    def tile_loads(tile, parity):
        cols = aligned(tile * SPAN, SPAN)
        return (
            pltpu.make_async_copy(
                full_up.at[:, cols], weight.at[:, aligned(D + parity * SPAN, SPAN)], sem_ff.at[0, parity]
            ),
            pltpu.make_async_copy(full_down.at[cols, :], left.at[parity], sem_ff.at[1, parity]),
        )

    def tile_stores(tile, parity):
        cols = aligned(tile * SPAN, SPAN)
        return [
            pltpu.make_async_copy(
                kv_all.at[pl.ds(0, BLK), aligned(base + parity * SPAN, SPAN)],
                dest.at[:, cols],
                sem_ff.at[2 + place, parity],
            )
            for place, (base, dest) in enumerate(((0, u_out), (D, g_out)))
        ]

    out_load = pltpu.make_async_copy(full_out, weight.at[:, pl.ds(0, D)], sem_in.at[0])
    x_load = pltpu.make_async_copy(x_hbm, right.at[1], sem_in.at[1])
    for copy in (out_load, x_load) + tile_loads(0, 0):
        copy.start()

    def drain_blocks(index, carry):
        rows = aligned(index * BLK, BLK)
        local_wait(a_all.at[rows, :], sem_a.at[index])
        local_wait(kv_all.at[rows, :], sem_kv.at[index])
        return carry

    lax.fori_loop(0, slots + 1, drain_blocks, 0)
    out_load.wait()
    for half_cols in range(2):
        cols = pl.ds(half_cols * SPAN, SPAN)
        acc[:, cols] = jnp.dot(x_own[...], weight[:, cols], preferred_element_type=jnp.float32)
    x_load.wait()
    for copy in outputs[2:]:
        copy.wait()
    dy_load = pltpu.make_async_copy(dy_hbm, x_own, sem_in.at[0])
    dy_load.start()

    def inner_rows(step, carry):
        rows = aligned(step * CHAIN, CHAIN)
        hat, scale = standard_rows(acc[rows, :])
        a_all[rows, :] = hat.astype(jnp.bfloat16)
        sums[0, rows, :] = jnp.broadcast_to(scale, (CHAIN, 128))
        hidden = right[1, rows, :].astype(jnp.float32) + hat * gain_ref[1:2, :] + bias_ref[1:2, :]
        acc[rows, :] = hidden
        hat, scale = standard_rows(hidden)
        a_all[aligned(BLK + step * CHAIN, CHAIN), :] = hat.astype(jnp.bfloat16)
        sums[1, rows, :] = jnp.broadcast_to(scale, (CHAIN, 128))
        q_all[rows, :] = (hat * gain_ref[2:3, :] + bias_ref[2:3, :]).astype(jnp.bfloat16)
        return carry

    lax.fori_loop(0, BLK // CHAIN, inner_rows, 0)
    saves = [
        pltpu.make_async_copy(a_all.at[pl.ds(0, BLK), :], hat1_out, sem_out.at[0]),
        pltpu.make_async_copy(a_all.at[pl.ds(BLK, BLK), :], hat2_out, sem_out.at[1]),
        pltpu.make_async_copy(sums.at[pl.ds(0, 2)], rstd_out, sem_out.at[2]),
        pltpu.make_async_copy(q_all, f_out, sem_out.at[3]),
    ]
    for copy in saves:
        copy.start()

    def ff_tile(tile, carry):
        parity = tile % 2
        for copy in tile_loads(tile, parity):
            copy.wait()

        @pl.when(tile + 1 < shallow_tiles)
        def _():
            for copy in tile_loads(tile + 1, 1 - parity):
                copy.start()

        @pl.when(tile >= 2)
        def _():
            for copy in tile_stores(tile - 2, parity):
                copy.wait()

        upward = jnp.dot(
            q_all[...], weight[:, aligned(D + parity * SPAN, SPAN)], preferred_element_type=jnp.float32
        )
        kv_all[pl.ds(0, BLK), aligned(parity * SPAN, SPAN)] = upward.astype(jnp.bfloat16)
        active = (
            0.5 * upward * (1.0 + jnp.tanh(GELU_C * upward * (1.0 + GELU_A * upward * upward)))
        ).astype(jnp.bfloat16)
        kv_all[pl.ds(0, BLK), aligned(D + parity * SPAN, SPAN)] = active
        for copy in tile_stores(tile, parity):
            copy.start()
        fresh = jnp.dot(active, left[parity], preferred_element_type=jnp.float32)

        @pl.when(tile == 0)
        def _():
            z_acc[...] = fresh

        @pl.when(tile > 0)
        def _():
            z_acc[...] = z_acc[...] + fresh

        return carry

    lax.fori_loop(0, shallow_tiles, ff_tile, 0)
    dy_load.wait()

    def outer_rows(step, carry):
        gain_sum, bias_sum = carry
        rows = aligned(step * CHAIN, CHAIN)
        hat, scale = standard_rows(z_acc[rows, :])
        right[0, rows, :] = (acc[rows, :] + hat * gain_ref[3:4, :] + bias_ref[3:4, :]).astype(jnp.bfloat16)
        upstream = x_own[rows, :].astype(jnp.float32)
        a_all[aligned(2 * BLK + step * CHAIN, CHAIN), :] = row_back(
            upstream, hat, scale, gain_ref[3:4, :]
        ).astype(jnp.bfloat16)
        return gain_sum + column_sum(upstream * hat), bias_sum + column_sum(upstream)

    zero = jnp.zeros((1, D), jnp.float32)
    gain_sum, bias_sum = lax.fori_loop(0, BLK // CHAIN, outer_rows, (zero, zero))
    row = lax.broadcasted_iota(jnp.int32, (8, D), 0)
    norm_v[...] = jnp.where(row == 3, gain_sum, 0.0) + jnp.where(row == 7, bias_sum, 0.0)
    ends = [
        pltpu.make_async_copy(right.at[0], y_out, sem_in.at[0]),
        pltpu.make_async_copy(a_all.at[pl.ds(2 * BLK, BLK), :], dz_out, sem_in.at[1]),
        pltpu.make_async_copy(norm_v, norm_out, sem_in.at[2]),
    ]
    for copy in ends:
        copy.start()
    for tile in range(shallow_tiles - 2, shallow_tiles):
        for copy in tile_stores(tile, tile % 2):
            copy.wait()
    for copy in saves + ends:
        copy.wait()


def forward_part(n_ctx, tags, gains, biases, raw, dy, w_qkv, w_out, w_up, w_down):
    slots = n_ctx // 2
    every = (slots + 1) * BLK
    low, full = jnp.bfloat16, jnp.float32
    dma = pltpu.SemaphoreType.DMA
    hbm = pl.BlockSpec(memory_space=pl.ANY)
    vmem = pl.BlockSpec(memory_space=pltpu.VMEM)
    shards = (w_qkv, w_out, w_up, w_down)
    pieces = sum(w.shape[0] * w.shape[1] // (2 * PIECE * SPAN) for w in shards)
    own = w_qkv.shape[1] // SPAN + 3
    chain = slots * (BLK // CHAIN)
    shape = jax.ShapeDtypeStruct
    return pl.pallas_call(
        functools.partial(forward_kernel, n_ctx),
        out_shape=[
            shape((every, D), low),
            shape((BLK, D), low),
            shape((every, 2 * D), low),
            shape((BLK, D), low),
            shape((PAIRS, BLK, 128), full),
        ]
        + [shape((4 * w.shape[0], w.shape[1]), low) for w in shards]
        + [
            shape((BLK, D), low),
            shape((BLK, w_up.shape[1]), low),
            shape((BLK, D), low),
            shape((BLK, D), low),
            shape((BLK, w_up.shape[1]), low),
            shape((BLK, D), low),
            shape((BLK, D), low),
            shape((2, BLK, 128), full),
            shape((8, D), full),
        ],
        in_specs=[pl.BlockSpec(memory_space=pltpu.SMEM), vmem, vmem] + [hbm] * 6,
        out_specs=[hbm] * 18,
        scratch_shapes=[
            pltpu.VMEM((BLK, D), low),
            pltpu.VMEM((slots, BLK, D), low),
            pltpu.VMEM((slots, BLK, D), low),
            pltpu.VMEM((every, D), low),
            pltpu.VMEM((BLK, D), low),
            pltpu.VMEM((every, 2 * D), low),
            pltpu.VMEM((D, 3 * D), low),
            pltpu.VMEM((BLK, D), full),
            pltpu.VMEM((BLK, D), full),
            pltpu.VMEM((8, D), full),
            pltpu.VMEM((PAIRS, BLK, 128), full),
            pltpu.VMEM((PAIRS, BLK, 128), full),
            pltpu.VMEM((3, 2 * PIECE, SPAN), low),
            dma((3,)),
            dma((3,)),
            dma((3,)),
            dma((4, 2)),
            dma((4,)),
            dma((slots + 1,)),
            dma((slots + 1,)),
        ]
        + [dma((pieces,))] * 8
        + [dma((own,))] * 2
        + [dma((chain,))] * 4,
        compiler_params=pltpu.CompilerParams(
            collective_id=1, has_side_effects=True, vmem_limit_bytes=67043328
        ),
        cost_estimate=pl.CostEstimate(flops=20 << 30, bytes_accessed=64 << 20, transcendentals=1 << 24),
        name="gather_attend",
    )(tags, gains, biases, raw, dy, *shards)


TILE = 256
PAIRED = 2


def grad_block(q_ref, do_ref, o_ref, lse_ref, kv_ref, dq_acc, turned, pair, own, visible):
    lanes = aligned(pair * 128, 128)
    value_lanes = aligned(D + pair * 128, 128)
    size = QT if own else BLK
    count = BLK // size
    q_pair, do_pair, lse_pair = q_ref[:, lanes], do_ref[:, lanes], lse_ref[pair]
    prod = do_pair.astype(jnp.float32) * o_ref[:, lanes].astype(jnp.float32)
    keys, values = kv_ref[:, lanes], kv_ref[:, value_lanes]
    q_turned, do_turned = q_pair.T, do_pair.T
    old_dq = dq_acc[:, lanes]
    causal = causal_tile()
    hide = 0.0 if own else jnp.where(visible, 0.0, 1e30)
    lanes_of = [head_lanes(head, size) for head in range(2)]
    work = [(tile, head) for tile in range(count) for head in range(2)]
    score, dprob, dlogit, prob_low = {}, {}, {}, {}
    for tile, head in work:
        rows = slice(tile * size, (tile + 1) * size)
        span = (tile + 1) * size if own else BLK
        zero = jnp.zeros((size, 128), jnp.bfloat16)
        score[tile, head] = contract_last(jnp.where(lanes_of[head], q_pair[rows], zero), keys[:span])
        dprob[tile, head] = contract_last(jnp.where(lanes_of[head], do_pair[rows], zero), values[:span])
    for tile, head in work:
        rows = slice(tile * size, (tile + 1) * size)
        delta = jnp.sum(jnp.where(lanes_of[head], prod[rows], 0.0), axis=-1, keepdims=True)
        shift = lse_pair[rows, head * DH : head * DH + 1] + hide
        prob = jnp.exp2(score[tile, head] * C2 - shift)
        if own:
            diag = jnp.where(causal, prob[:, tile * size :], 0.0)
            prob = jnp.concatenate([prob[:, : tile * size], diag], axis=1) if tile else diag
        dlogit[tile, head] = (prob * (dprob[tile, head] - delta)).astype(jnp.bfloat16)
        prob_low[tile, head] = prob.astype(jnp.bfloat16)
    for tile in range(count):
        rows = slice(tile * size, (tile + 1) * size)
        span = (tile + 1) * size if own else BLK
        parts = [dot_dims(dlogit[tile, head], keys[:span], 1, 0) for head in range(2)]
        dq_acc[pl.ds(tile * size, size), lanes] = old_dq[rows] + jnp.where(lanes_of[0], parts[0], parts[1])
    for head in range(2):
        for offset, left_side, right_side, scale in (
            (0, q_turned, dlogit, ALPHA),
            (D, do_turned, prob_low, 1.0),
        ):
            spot = aligned(offset + pair * 128 + head * DH, DH)
            left_head = left_side[head * DH : (head + 1) * DH]
            terms = [
                dot_dims(left_head[:, tile * size : (tile + 1) * size], right_side[tile, head], 1, 0)
                for tile in range(count)
            ]
            for tile in range(count):
                cols = slice(tile * size, (tile + 1) * size)
                total = functools.reduce(
                    jnp.add, [terms[other][:, cols] for other in range(tile, count)]
                ) if own else terms[0]
                turned[spot, cols if own else slice(None)] = (total * scale).astype(jnp.bfloat16)


def backward_kernel(n_ctx, widths, *refs):
    slots = n_ctx // 2
    levels = n_ctx.bit_length() - 1
    depth = 16 if n_ctx == 4 else 10
    shallow = slots <= 2
    (slot_ref, gain_ref, bias_ref, norm_ref, x_hbm, q_hbm, kv_hbm, a_hbm, o_hbm, lse_hbm, w_hbm) = refs[:11]
    (w_out, w_up, w_down, g_hbm, dz_hbm, f_hbm, u_hbm, hat1_hbm, hat2_hbm, rstd_hbm, dy_hbm) = refs[11:22]
    outs = refs[22:26]
    grad_out, norm_out, dh_hbm, du_hbm, datt_hbm = refs[26:31]
    scratch = list(refs[31:])
    own_slot = slot_ref[1] // BLK

    def take(count):
        taken = scratch[:count]
        del scratch[:count]
        return taken

    q_v, o_v, do_v, lse_v, weight, kv_b, a_b, dq_acc, turned, gkv, term, own_part, left, right, norm_v, norm_in, gain_sum, bias_sum = take(18)
    r1, r2, r3, fin, made = take(5)
    lhs, rhs = take(2)
    zbufs = take(levels)
    sem_in, sem_blk, sem_rhs, sem_lhs, sem_ff, sem_out, sem_res = take(7)
    send1, recv1, send2, recv2, send3, recv3, send6, recv6 = take(8)
    rs_send, rs_recv, ag_send, ag_recv = take(levels), take(levels), take(levels), take(levels)
    left_s, left_r, right_s, right_r, norm_s, norm_r = take(6)
    grp, ctx, wsh = lax.axis_index("grp"), lax.axis_index("ctx"), lax.axis_index("wsh")
    side, core = wsh // 2, wsh % 2
    core_peer = (grp, ctx, side * 2 + 1 - core)
    side_peer = (grp, ctx, (1 - side) * 2 + core)
    grp_peer = (1 - grp, ctx, wsh)
    next_ctx = (grp, lax.rem(ctx + 1, n_ctx), wsh)
    last_ctx = (grp, lax.rem(ctx + n_ctx - 1, n_ctx), wsh)
    bits = [(ctx // (1 << level)) % 2 for level in range(levels)]
    level_peers = [(grp, ctx + (1 - 2 * bits[level]) * (1 << level), wsh) for level in range(levels)]

    def block_copies(index):
        rows = aligned(lax.rem(index, slots + 1) * BLK, BLK)
        slot = lax.rem(index, kv_b.shape[0])
        a_slot = index - 1 if shallow else 0
        return (
            pltpu.make_async_copy(kv_hbm.at[rows, :], kv_b.at[slot], sem_blk.at[0, slot]),
            pltpu.make_async_copy(a_hbm.at[rows, :], a_b.at[a_slot], sem_blk.at[1, slot]),
        )

    barrier = pltpu.get_barrier_semaphore()
    peers = [core_peer, side_peer, grp_peer, next_ctx, last_ctx] + level_peers
    for peer in peers:
        pl.semaphore_signal(barrier, inc=1, device_id=peer, device_id_type=MESH)
    pl.semaphore_wait(barrier, len(peers))

    half = TILE // 2
    ranges, first = [], 0
    for rows, cols in widths:
        across = cols // TILE
        ranges.append((first, first + (rows // TILE) * across, across))
        first = ranges[-1][1]
    chunks = first

    def by_range(index, act):
        for place, (low, high, across) in enumerate(ranges):

            @pl.when((index >= low) & (index < high))
            def _(place=place, low=low, across=across):
                number = index - low
                act(place, (aligned((number // across) * TILE, TILE), aligned((number % across) * TILE, TILE)))

    def region(level, flip):
        row, rows, col, cols = 0, half, 0, TILE
        for place in range(level):
            bit = 1 - bits[place] if (flip and place == level - 1) else bits[place]
            if rows > 16:
                rows = rows // 2
                row = row + bit * rows
            else:
                cols = cols // 2
                col = col + bit * cols
        return row, rows, col, cols

    def spot(level, flip=False, base=0):
        row, rows, col, cols = region(level, flip)
        return aligned(base + row, rows), aligned(col, cols)

    last_low = ranges[-1][0]
    dq_low = o_v
    set_of = [(0, number) for number in range(widths[0][0] // TILE)] + [(1, 0), (2, 0)]
    set_first = [number * ranges[0][2] for number in range(widths[0][0] // TILE)]
    set_first += [ranges[1][0], ranges[2][0]]
    left_of, right_of = (g_hbm, f_hbm, o_hbm), (dz_hbm, du_hbm, datt_hbm)

    def set_copies(number):
        place, group = set_of[number]
        stride = left_of[place].shape[1] // 4
        return [
            pltpu.make_async_copy(
                left_of[place].at[:, pl.ds(owner * stride + group * TILE, TILE)],
                lhs.at[number % 2, owner],
                sem_lhs.at[number % 2, owner],
            )
            for owner in range(4)
        ]

    def step_fetch(index):
        near = lax.rem(index, 4)

        def act(place, span):
            if place < 3:
                pltpu.make_async_copy(
                    right_of[place].at[:, span[1]], rhs.at[near], sem_rhs.at[near]
                ).start()

        by_range(index, act)

    def step_make(index, kinds):
        slot = lax.rem(index, depth)
        near = lax.rem(index, 4)

        def low_piece():
            local_wait(rhs.at[near], sem_rhs.at[near])
            parity = jnp.int32(0)
            for number, low in enumerate(set_first):
                parity = jnp.where(index >= low, number % 2, parity)

                @pl.when(index == low)
                def _(number=number):
                    for copy in set_copies(number):
                        copy.wait()
                    if number + 1 < len(set_first):
                        for copy in set_copies(number + 1):
                            copy.start()

            right_side = rhs[near]
            for owner in range(4):
                made[near, owner // 2, owner % 2] = dot_dims(
                    lhs[parity, owner], right_side, 0, 0
                ).astype(jnp.bfloat16)

        def high_piece():
            number = index - last_low
            if not shallow:
                made[near] = term[:, :, :, aligned(number * TILE, TILE)]
                return

            @pl.when(number < D // TILE)
            def _():
                right_side = dq_low[:, aligned(number * TILE, TILE)]
                for owner in range(4):
                    made[near, owner // 2, owner % 2] = dot_dims(
                        a_b[slots, :, pl.ds(owner * TILE, TILE)], right_side, 0, 0
                    ).astype(jnp.bfloat16)

            @pl.when(number >= D // TILE)
            def _():
                cols = aligned((number - D // TILE) * TILE, TILE)
                for owner in range(4):
                    total = functools.reduce(
                        jnp.add,
                        [
                            dot_dims(a_b[block, :, pl.ds(owner * TILE, TILE)], turned[block, cols, :], 0, 1)
                            for block in range(slots + 1)
                        ],
                    )
                    made[near, owner // 2, owner % 2] = total.astype(jnp.bfloat16)

        if kinds == "low":
            low_piece()
        elif kinds == "high":
            high_piece()
        else:
            pl.when(index < last_low)(low_piece)
            pl.when(index >= last_low)(high_piece)
        remote(
            made.at[near, :, 1 - core], r1.at[slot], send1.at[slot], recv1.at[slot], core_peer
        ).start()

    def finished(move):
        move.wait_send()
        move.wait_recv()

    def step_core(index):
        slot, near = lax.rem(index, depth), lax.rem(index, 4)
        finished(remote(r1.at[slot], r1.at[slot], send1.at[slot], recv1.at[slot], core_peer))
        r1[slot] = r1[slot] + made[near, :, core]
        remote(r1.at[slot, 1 - side], r2.at[slot], send2.at[slot], recv2.at[slot], side_peer).start()

    keep_half = aligned(grp * half, half)
    give_half = aligned((1 - grp) * half, half)

    def step_side(index):
        slot = lax.rem(index, depth)
        finished(remote(r1.at[slot, 1 - side], r2.at[slot], send2.at[slot], recv2.at[slot], side_peer))
        r2[slot] = r2[slot] + r1[slot, side]
        remote(r2.at[slot, give_half], r3.at[slot], send3.at[slot], recv3.at[slot], grp_peer).start()

    fold = n_ctx == 4
    if fold:
        outer = bits[0] == bits[1]
        inner = bits[0] != bits[1]
        mate, middle = level_peers[0], (grp, 3 - ctx, wsh)
        quarter = half // 2
        mine, other = aligned(bits[1] * quarter, quarter), aligned((1 - bits[1]) * quarter, quarter)
        fin_mine = aligned(grp * half + bits[1] * quarter, quarter)
        fin_other = aligned(grp * half + (1 - bits[1]) * quarter, quarter)

        def up_copy(slot):
            return remote(r3.at[slot], zbufs[0].at[slot], rs_send[0].at[slot], rs_recv[0].at[slot], mate)

        def cross_copy(slot):
            return remote(
                r3.at[slot, other], zbufs[1].at[slot], rs_send[1].at[slot], rs_recv[1].at[slot], middle
            )

        def share_copy(slot, rows):
            here = fin.at[slot, rows]
            return remote(here, here, ag_send[1].at[slot], ag_recv[1].at[slot], middle)

        def down_copy(slot):
            here = fin.at[slot, keep_half]
            return remote(here, here, ag_send[0].at[slot], ag_recv[0].at[slot], mate)

        def step_up(index):
            slot = lax.rem(index, depth)

            @pl.when(outer)
            def _():
                up_copy(slot).wait_send()

            @pl.when(inner)
            def _():
                up_copy(slot).wait_recv()
                r3[slot] = r3[slot] + zbufs[0][slot]
                cross_copy(slot).start()

        def step_cross(index):
            slot = lax.rem(index, depth)

            @pl.when(inner)
            def _():
                finished(cross_copy(slot))
                fin[slot, fin_mine] = r3[slot, mine] + zbufs[1][slot]
                share_copy(slot, fin_mine).start()

        def step_share(index):
            slot = lax.rem(index, depth)

            @pl.when(inner)
            def _():
                finished(share_copy(slot, fin_other))
                down_copy(slot).start()

        def step_down(index):
            slot = lax.rem(index, depth)

            @pl.when(inner)
            def _():
                down_copy(slot).wait_send()

            @pl.when(outer)
            def _():
                down_copy(slot).wait_recv()

            back_copy(slot, keep_half).start()

    def rs_copy(level, slot):
        rows, cols = spot(level + 1, True)
        return remote(
            r3.at[slot, rows, cols], zbufs[level].at[slot], rs_send[level].at[slot], rs_recv[level].at[slot], level_peers[level]
        )

    def ag_copy(level, slot, flip=False):
        rows, cols = spot(level + 1, flip, grp * half)
        here = fin.at[slot, rows, cols]
        return remote(here, here, ag_send[level].at[slot], ag_recv[level].at[slot], level_peers[level])

    def back_copy(slot, rows):
        here = fin.at[slot, rows]
        return remote(here, here, send6.at[slot], recv6.at[slot], grp_peer)

    def step_grp(index):
        slot = lax.rem(index, depth)
        finished(remote(r2.at[slot, give_half], r3.at[slot], send3.at[slot], recv3.at[slot], grp_peer))
        r3[slot] = r3[slot] + r2[slot, keep_half]
        if fold:

            @pl.when(outer)
            def _():
                up_copy(slot).start()
        else:
            rs_copy(0, slot).start()

    def step_scatter(level):
        def act(index):
            slot = lax.rem(index, depth)
            finished(rs_copy(level, slot))
            rows, cols = spot(level + 1)
            total = r3[slot, rows, cols] + zbufs[level][slot]
            if level + 1 < levels:
                r3[slot, rows, cols] = total
                rs_copy(level + 1, slot).start()
            else:
                rows, cols = spot(level + 1, False, grp * half)
                fin[slot, rows, cols] = total
                ag_copy(level, slot).start()

        return act

    def step_gather(level):
        def act(index):
            slot = lax.rem(index, depth)
            finished(ag_copy(level, slot, True))
            if level:
                ag_copy(level - 1, slot).start()
            else:
                back_copy(slot, keep_half).start()

        return act

    def out_wait(index):
        slot = lax.rem(index, depth)
        local_wait(fin.at[slot], sem_out.at[slot])

    def step_out(index):
        slot = lax.rem(index, depth)
        finished(back_copy(slot, give_half))

        def act(place, span):
            pltpu.make_async_copy(fin.at[slot], outs[place].at[span[0], span[1]], sem_out.at[slot]).start()

        by_range(index, act)

    z_lag = 2 if fold else 1
    order = [(YLAG, step_side), (XLAG, step_grp)]
    if fold:
        order += [(z_lag, act) for act in (step_up, step_cross, step_share, step_down)]
    else:
        order += [(z_lag, step_scatter(level)) for level in range(levels)]
        order += [(z_lag, step_gather(level)) for level in reversed(range(levels))]
    order += [(BLAG, step_out), (2, out_wait)]
    stages = [(0, step_core)]
    for lag, act in order:
        stages.append((stages[-1][0] + lag, act))
    all_ticks = chunks + stages[-1][0]

    per_slot = BLK // CHAIN
    chain_chunks = slots * per_slot

    def chain_step(stream, send, recv, number, is_first, is_last, target):
        slot = number // per_slot
        rows = aligned((number % per_slot) * CHAIN, CHAIN)
        here = stream.at[slot, rows]

        @pl.when(is_first)
        def _():
            stream[slot, rows, :] = own_part[slot, rows, :]

        @pl.when(jnp.logical_not(is_first))
        def _():
            remote(here, here, send.at[number], recv.at[number], target).wait_recv()
            stream[slot, rows, :] = stream[slot, rows, :] + own_part[slot, rows, :]

        @pl.when(jnp.logical_not(is_last))
        def _():
            remote(here, here, send.at[number], recv.at[number], target).start()

    def chain_tick(step):
        number = step - ctx

        @pl.when((number >= 0) & (number < chain_chunks))
        def _():
            chain_step(left, left_s, left_r, number, ctx == 0, ctx == n_ctx - 1, next_ctx)

        back = step - (n_ctx - 1 - ctx)

        @pl.when((back >= 0) & (back < chain_chunks))
        def _():
            chain_step(right, right_s, right_r, back, ctx == n_ctx - 1, ctx == 0, last_ctx)

    groups = PAIRS // PAIRED
    group_ticks = groups if shallow else 0
    block_ticks = group_ticks + 2
    chain_first = FF_TICKS + block_ticks
    paced = max(0, -(-(chunks - chain_first) // PACE))
    late_first = max(chunks, chain_first)
    late_beats = max(0, chain_chunks + n_ctx - 1 - paced)
    chain_ticks = late_first + TAIL_PACE * max(0, late_beats - 1) + 1

    def tick(step, kinds):
        kinds = kinds if shallow or kinds == "none" else "both"
        if kinds in ("low", "both"):

            @pl.when(step + 3 < chunks)
            def _():
                step_fetch(step + 3)

        if kinds != "none":

            @pl.when(step + 2 < chunks)
            def _():
                step_make(step + 2, kinds)

        for lag, act in stages:
            index = step - lag

            @pl.when((index >= 0) & (index < chunks))
            def _(act=act, index=index):
                act(index)

        beat = step - chain_first

        @pl.when((beat >= 0) & (step < chunks) & (beat % PACE == 0))
        def _():
            chain_tick(beat // PACE)

        late = step - late_first

        @pl.when((late >= 0) & (late % TAIL_PACE == 0))
        def _():
            chain_tick(paced + late // TAIL_PACE)


    for index in range(3):
        step_fetch(jnp.int32(index))
    for copy in set_copies(0):
        copy.start()

    hidden_tiles = u_hbm.shape[1] // SPAN
    datt_v, dz_v, dy_v, hat1_v, hat2_v = own_part.at[0], do_v, left.at[1], right.at[0], right.at[1]

    def tile_copies(tile, parity):
        cols = aligned(tile * SPAN, SPAN)
        return (
            pltpu.make_async_copy(w_down.at[cols, :], own_part.at[parity], sem_ff.at[0, parity]),
            pltpu.make_async_copy(
                w_up.at[:, cols], turned.at[0, aligned(parity * D, D), :], sem_ff.at[1, parity]
            ),
            pltpu.make_async_copy(
                u_hbm.at[:, cols], left.at[0, :, aligned(parity * SPAN, SPAN)], sem_ff.at[2, parity]
            ),
        )

    def du_store(tile, parity):
        return pltpu.make_async_copy(
            kv_b.at[0, :, aligned(parity * SPAN, SPAN)],
            du_hbm.at[:, aligned(tile * SPAN, SPAN)],
            sem_ff.at[3, parity],
        )

    dz_load = pltpu.make_async_copy(dz_hbm, dz_v, sem_in.at[0])
    dz_load.start()
    for copy in tile_copies(0, 0):
        copy.start()
    wide_loads = [
        pltpu.make_async_copy(source, dest, sem_in.at[place + 1])
        for place, (source, dest) in enumerate(
            (
                (dy_hbm, dy_v),
                (hat1_hbm, hat1_v),
                (hat2_hbm, hat2_v),
                (rstd_hbm, lse_v.at[pl.ds(0, 2)]),
                (q_hbm, q_v),
                (o_hbm, o_v),
                (w_hbm, weight),
            )
        )
    ]
    out_loads = [
        pltpu.make_async_copy(
            w_out.at[pl.ds(place * TILE, TILE), :],
            term.at[place // 2, place % 2, :, pl.ds(0, D)],
            sem_in.at[8 + place],
        )
        for place in range(4)
    ]
    lax.fori_loop(0, 2, lambda index, carry: (step_make(index, "low"), carry)[1], 0)
    dz_load.wait()

    def ff_tile(tile, carry):
        start = tile + (tile + 1) // 2
        extra = jnp.where((tile % 2 == 0) | (tile + 1 == hidden_tiles), 1, 0)
        lax.fori_loop(start, start + 1 + extra, lambda index, inner: (tick(index, "low"), inner)[1], 0)

        parity = tile % 2
        for copy in tile_copies(tile, parity):
            copy.wait()

        @pl.when(tile + 1 < hidden_tiles)
        def _():
            for copy in tile_copies(tile + 1, 1 - parity):
                copy.start()

        @pl.when(tile == 0)
        def _():
            for copy in wide_loads + out_loads:
                copy.start()

        @pl.when(tile >= 2)
        def _():
            du_store(tile - 2, parity).wait()

        u_cols = aligned(parity * SPAN, SPAN)
        u_tile = left[0, :, u_cols].astype(jnp.float32)
        square = u_tile * u_tile
        bend = jnp.tanh(GELU_C * u_tile * (1.0 + GELU_A * square))
        slope = 0.5 * (1.0 + bend) + (0.5 * GELU_C) * u_tile * (1.0 - bend * bend) * (
            1.0 + 3.0 * GELU_A * square
        )
        du_tile = (contract_last(dz_v[...], own_part[parity]) * slope).astype(jnp.bfloat16)
        kv_b[0, :, u_cols] = du_tile
        du_store(tile, parity).start()
        fresh = contract_last(du_tile, turned[0, aligned(parity * D, D), :])

        @pl.when(tile == 0)
        def _():
            dq_acc[...] = fresh

        @pl.when(tile > 0)
        def _():
            dq_acc[...] = dq_acc[...] + fresh

        return carry

    lax.fori_loop(0, hidden_tiles, ff_tile, 0)
    for tile in range(hidden_tiles - 2, hidden_tiles):
        du_store(tile, tile % 2).wait()
    for copy in wide_loads:
        copy.wait()
    for copy in block_copies(1):
        copy.start()

    def hidden_back(step, carry):
        gain1, gain2, bias1, bias2 = carry
        rows = aligned(step * CHAIN, CHAIN)
        upstream = dq_acc[rows, :]
        hat = hat2_v[rows, :].astype(jnp.float32)
        grad_h = dy_v[rows, :].astype(jnp.float32) + row_back(
            upstream, hat, lse_v[1, rows, 0:1], gain_ref[2:3, :]
        )
        gain2, bias2 = gain2 + column_sum(upstream * hat), bias2 + column_sum(upstream)
        dq_acc[rows, :] = grad_h
        if shallow:
            gkv[rows, :] = grad_h
        hat = hat1_v[rows, :].astype(jnp.float32)
        datt_v[rows, :] = row_back(grad_h, hat, lse_v[0, rows, 0:1], gain_ref[1:2, :]).astype(
            jnp.bfloat16
        )
        return gain1 + column_sum(grad_h * hat), gain2, bias1 + column_sum(grad_h), bias2

    zero = jnp.zeros((1, D), jnp.float32)
    sums = lax.fori_loop(0, BLK // CHAIN, hidden_back, (zero,) * 4)
    row = lax.broadcasted_iota(jnp.int32, (8, D), 0)
    norm_v[...] = norm_ref[...]
    for place, value in zip((1, 2, 5, 6), sums):
        norm_v[...] = norm_v[...] + jnp.where(row == place, value, 0.0)
    stores = [
        pltpu.make_async_copy(dq_acc, dh_hbm, sem_res.at[0]),
        pltpu.make_async_copy(datt_v, datt_hbm, sem_res.at[1]),
    ]
    lse_load = pltpu.make_async_copy(lse_hbm, lse_v, sem_in.at[0])
    for copy in stores + [lse_load]:
        copy.start()
    for place in range(4):
        out_loads[place].wait()
        do_v[:, pl.ds(place * TILE, TILE)] = contract_last(
            datt_v[...], term[place // 2, place % 2, :, pl.ds(0, D)]
        ).astype(jnp.bfloat16)
    for copy in stores + [lse_load]:
        copy.wait()
    dq_acc[...] = jnp.zeros_like(dq_acc)

    def attend(kv_ref, turned_ref, own, visible, begin):
        def body(group, carry):
            if shallow:
                tick(begin + group, "low")
            for member in range(PAIRED):
                grad_block(
                    q_v, do_v, o_v, lse_v, kv_ref, dq_acc, turned_ref, group * PAIRED + member, own, visible
                )
            return carry

        lax.fori_loop(0, groups, body, 0)

    def first_sums(piece, normed, cols):
        gain_sum[:, cols] = gain_sum[:, cols] + column_sum(piece * normed.astype(jnp.float32))
        bias_sum[:, cols] = bias_sum[:, cols] + column_sum(piece)

    gain_sum[...] = jnp.zeros_like(gain_sum)
    bias_sum[...] = jnp.zeros_like(bias_sum)

    def each_slot(slot, carry):
        visible = slot < own_slot
        index = slot + 1
        place = lax.rem(index, kv_b.shape[0])
        for copy in block_copies(index):
            copy.wait()
        if kv_b.shape[0] > 1:
            for copy in block_copies(index + 1):
                copy.start()
        begin = FF_TICKS + slot * block_ticks
        a_place = slot if shallow else 0
        attend(kv_b.at[place], turned.at[a_place], False, visible, begin)

        def weight_terms(step, inner):
            tick(begin + group_ticks + step, "low")
            rows = aligned(step * 512, 512)
            for part in range(0 if shallow else 2):
                cols = pl.ds(part * D, D)
                product = dot_dims(a_b[a_place, :, rows], turned[a_place, cols, :], 0, 1)
                for down in range(2):
                    target = term.at[step, down, :, pl.ds((part + 1) * D, D)]
                    piece = product[down * TILE : (down + 1) * TILE]

                    @pl.when(slot == 0)
                    def _(target=target, piece=piece):
                        target[...] = piece.astype(target.dtype)

                    @pl.when(slot > 0)
                    def _(target=target, piece=piece):
                        target[...] = (target[...] + piece).astype(target.dtype)

            piece = dot_dims(turned[a_place], weight[rows, pl.ds(D, 2 * D)], 0, 1)
            own_part[slot, :, rows] = piece.astype(jnp.bfloat16)
            first_sums(piece, a_b[a_place, :, rows], rows)
            return inner

        lax.fori_loop(0, 2, weight_terms, 0)
        if kv_b.shape[0] == 1:
            for copy in block_copies(index + 1):
                copy.start()
        return carry

    lax.fori_loop(0, slots, each_slot, 0)
    begin = FF_TICKS + slots * block_ticks
    own_place = (slots + 1) % kv_b.shape[0]
    for copy in block_copies(slots + 1):
        copy.wait()
    own_a = slots if shallow else 0
    attend(kv_b.at[own_place], turned.at[own_a], True, None, begin)
    dq_low[...] = (dq_acc[...] * ALPHA).astype(jnp.bfloat16) * jnp.bfloat16(QSCALE)
    x_load = pltpu.make_async_copy(x_hbm, do_v, sem_in.at[0])
    x_load.start()
    ready = begin + group_ticks

    def last_terms(step, carry):
        tick(begin + group_ticks + step, "both")
        rows = aligned(step * TILE, TILE)
        a_rows = a_b[0, :, rows]
        up, down = step // 2, step % 2
        term[up, down, :, pl.ds(0, D)] = dot_dims(a_rows, dq_low[...], 0, 0).astype(jnp.bfloat16)
        for part in range(2):
            cols = pl.ds(part * D, D)
            target = term.at[up, down, :, pl.ds((part + 1) * D, D)]
            target[...] = (target[...] + dot_dims(a_rows, turned[0, cols, :], 0, 1)).astype(jnp.bfloat16)
        return carry

    if not shallow:
        lax.fori_loop(0, 4, last_terms, 0)
        ready = ready + 4
    assert ready <= last_low - 2
    da_acc = dq_acc

    spare = max(0, last_low - 2 - ready - 4) if shallow else 0

    def own_grad(step, carry):
        if shallow:
            begins = ready + step + jnp.where(step > 0, spare, 0)
            ends = ready + step + 1 + spare
            lax.fori_loop(begins, ends, lambda index, inner: (tick(index, "low"), inner)[1], 0)
        else:
            tick(ready + step, "low")
        rows = aligned(step * TILE, TILE)
        piece = dot_dims(dq_low[...], weight[rows, pl.ds(0, D)], 1, 1) + dot_dims(
            turned[own_a], weight[rows, pl.ds(D, 2 * D)], 0, 1
        )
        da_acc[:, rows] = piece
        first_sums(piece, a_b[own_a, :, rows], rows)
        return carry

    lax.fori_loop(0, 4, own_grad, 0)
    ready = ready + 4 + spare

    first_gain = (gain_sum[...] - bias_ref[0:1, :] * bias_sum[...]) / gain_ref[0:1, :]
    norm_v[...] = (
        norm_v[...] + jnp.where(row == 0, first_gain, 0.0) + jnp.where(row == 4, bias_sum[...], 0.0)
    )

    def run_ticks(first, last, kinds):
        if last > first:
            lax.fori_loop(first, last, lambda index, carry: (tick(index, kinds), carry)[1], 0)
        return max(first, last)

    assert ready == last_low - 2 or not shallow
    norm_peers = [core_peer, side_peer, grp_peer] + level_peers
    norm_base = ready
    norm_result = pltpu.make_async_copy(norm_v, norm_out, sem_res.at[1])

    def norm_move(place):
        return remote(norm_v, norm_in.at[place], norm_s.at[place], norm_r.at[place], norm_peers[place])

    def norm_ticks(step, carry):
        for place in range(len(norm_peers) + 1):

            @pl.when(step == norm_base + 3 * place)
            def _(place=place):
                if place:
                    finished(norm_move(place - 1))
                    norm_v[...] = norm_v[...] + norm_in[place - 1]
                if place < len(norm_peers):
                    norm_move(place).start()
                else:
                    norm_result.start()

        tick(step, "high")
        return carry

    last_tick = max(ready + 3 * len(norm_peers) + 1, chain_ticks)
    lax.fori_loop(ready, last_tick, norm_ticks, 0)
    ready = last_tick
    x_load.wait()
    gain = gain_ref[0:1, :]

    def norm_grad(step, carry):
        @pl.when(step % 2 == 0)
        def _():
            tick(ready + step // 2, "none")

        rows = aligned(step * CHAIN, CHAIN)
        upstream = da_acc[rows, :]
        for slot in range(slots):
            joined = left[slot, rows, :].astype(jnp.float32) + right[slot, rows, :].astype(jnp.float32)
            upstream = upstream + jnp.where(own_slot == slot, joined, 0.0)
        values = do_v[rows, :].astype(jnp.float32)
        centre = values - jnp.mean(values, axis=-1, keepdims=True)
        scale = lax.rsqrt(jnp.mean(centre * centre, axis=-1, keepdims=True) + EPS)
        centre = centre * scale
        grad = row_back(upstream, centre, scale, gain)
        da_acc[rows, :] = grad + gkv[rows, :] if shallow else grad
        return carry

    lax.fori_loop(0, BLK // CHAIN, norm_grad, 0)
    ready = ready + BLK // CHAIN // 2
    result = pltpu.make_async_copy(da_acc, grad_out, sem_res.at[0])
    result.start()
    run_ticks(ready, all_ticks, "none")

    def drain_chain(index, carry):
        here = left.at[0, pl.ds(0, CHAIN)]

        @pl.when(ctx < n_ctx - 1)
        def _():
            remote(here, here, left_s.at[index], left_r.at[index], next_ctx).wait_send()

        @pl.when(ctx > 0)
        def _():
            remote(here, here, right_s.at[index], right_r.at[index], last_ctx).wait_send()

        return carry

    lax.fori_loop(0, chain_chunks, drain_chain, 0)
    result.wait()
    norm_result.wait()


def backward_part(n_ctx, slot_vec, gains, biases, norms, saved, weights, ffn):
    slots = n_ctx // 2
    levels = n_ctx.bit_length() - 1
    depth = 16 if n_ctx == 4 else 10
    hidden = weights[1].shape[1]
    widths = [(hidden // 4, D), (D // 4, hidden), (D // 4, D), (D // 4, 3 * D)]
    low, full = jnp.bfloat16, jnp.float32
    dma = pltpu.SemaphoreType.DMA
    hbm = pl.BlockSpec(memory_space=pl.ANY)
    vmem = pl.BlockSpec(memory_space=pltpu.VMEM)
    shape = jax.ShapeDtypeStruct
    buffers = 2 if slots <= 2 else 1
    chain = slots * (BLK // CHAIN)
    zshapes, rows, cols = [], TILE // 2, TILE
    if n_ctx == 4:
        zshapes = [pltpu.VMEM((depth, rows, cols), low), pltpu.VMEM((depth, rows // 2, cols), low)]
    for _ in range(0 if zshapes else levels):
        rows, cols = (rows // 2, cols) if rows > 16 else (rows, cols // 2)
        zshapes.append(pltpu.VMEM((depth, rows, cols), low))
    return pl.pallas_call(
        functools.partial(backward_kernel, n_ctx, widths),
        out_shape=[shape(width, low) for width in widths] + [
            shape((BLK, D), full),
            shape((8, D), full),
            shape((BLK, D), full),
            shape((BLK, hidden), low),
            shape((BLK, D), low),
        ],
        in_specs=[pl.BlockSpec(memory_space=pltpu.SMEM), vmem, vmem, vmem]
        + [hbm] * (len(saved) + len(weights) + len(ffn)),
        out_specs=[hbm] * 9,
        scratch_shapes=[
            pltpu.VMEM((BLK, D), low),
            pltpu.VMEM((BLK, D), low),
            pltpu.VMEM((BLK, D), low),
            pltpu.VMEM((PAIRS, BLK, 128), full),
            pltpu.VMEM((D, 3 * D), low),
            pltpu.VMEM((buffers, BLK, 2 * D), low),
            pltpu.VMEM((slots + 1 if slots <= 2 else 1, BLK, D), low),
            pltpu.VMEM((BLK, D), full),
            pltpu.VMEM((slots + 1 if slots <= 2 else 1, 2 * D, BLK), low),
            pltpu.VMEM((BLK, D) if slots <= 2 else (8, 128), full),
            pltpu.VMEM((2, 2, D // 4, D if slots <= 2 else 3 * D), low),
            pltpu.VMEM((slots, BLK, D), low),
            pltpu.VMEM((slots, BLK, D), low),
            pltpu.VMEM((slots, BLK, D), low),
            pltpu.VMEM((8, D), full),
            pltpu.VMEM((3 + levels, 8, D), full),
            pltpu.VMEM((1, D), full),
            pltpu.VMEM((1, D), full),
            pltpu.VMEM((depth, 2, TILE, TILE), low),
            pltpu.VMEM((depth, TILE, TILE), low),
            pltpu.VMEM((depth, TILE // 2, TILE), low),
            pltpu.VMEM((depth, TILE, TILE), low),
            pltpu.VMEM((4, 2, 2, TILE, TILE), low),
        ]
        + [pltpu.VMEM((2, 4, BLK, TILE), low), pltpu.VMEM((4, BLK, TILE), low)]
        + zshapes
        + [dma((12,)), dma((2, buffers)), dma((4,)), dma((2, 4)), dma((4, 2)), dma((depth,)), dma((2,))]
        + [dma((depth,))] * (8 + 4 * levels)
        + [dma((chain,))] * 4
        + [dma((3 + levels,))] * 2,
        compiler_params=pltpu.CompilerParams(
            collective_id=2, has_side_effects=True, vmem_limit_bytes=67043328
        ),
        cost_estimate=pl.CostEstimate(flops=40 << 30, bytes_accessed=64 << 20, transcendentals=1 << 24),
        name="attend_back_reduce",
    )(
        slot_vec,
        gains,
        biases,
        norms,
        *saved,
        *weights,
        *ffn,
    )


def widen_kernel(*refs):
    count = len(refs) // 2
    for source, dest in zip(refs[: count - 1], refs[count:]):
        dest[...] = source[...].astype(dest.dtype)
    refs[-2][...] = refs[count - 1][0:4, :]
    refs[-1][...] = refs[count - 1][4:8, :]


def widen(arrays, types, norms):
    steps = 8
    specs = [pl.BlockSpec((x.shape[0] // steps, x.shape[1]), lambda i: (i, 0)) for x in arrays]
    shape = jax.ShapeDtypeStruct
    pair = [pl.BlockSpec((4, D), lambda i: (0, 0))] * 2
    return pl.pallas_call(
        widen_kernel,
        out_shape=[shape(x.shape, kind) for x, kind in zip(arrays, types)]
        + [shape((4, D), jnp.float32)] * 2,
        grid=(steps,),
        in_specs=specs + [pl.BlockSpec((8, D), lambda i: (0, 0))],
        out_specs=specs + pair,
        compiler_params=pltpu.CompilerParams(vmem_limit_bytes=67043328),
        name="widen",
    )(*arrays, norms)


def per_device(n_ctx, inputs, w_qkv, w_out, w_up, w_down, norm_gains, norm_biases, block_map, out_grad):
    slots = n_ctx // 2
    raw, seed_low = inputs.reshape(BLK, D), out_grad.reshape(BLK, D)
    block_entry = block_map.reshape(2)
    forward = forward_part(
        n_ctx,
        block_entry,
        norm_gains,
        norm_biases,
        raw,
        seed_low,
        w_qkv,
        w_out,
        w_up,
        w_down,
    )
    every_low, queries, keys_values, attn_low, lse, full_qkv, full_out, full_up, full_down = forward[:9]
    result, active_low, down_low, ffn_low, upward, hat1, hat2, rstd, norms = forward[9:]
    backward = backward_part(
        n_ctx,
        block_entry,
        norm_gains,
        norm_biases,
        norms,
        [raw, queries, keys_values, every_low, attn_low, lse, full_qkv],
        [full_out, full_up, full_down],
        [active_low, down_low, ffn_low, upward, hat1, hat2, rstd, seed_low],
    )
    grad_tokens, norm_total, grad_hidden = backward[4:7]
    if slots > 2:
        grad_tokens = grad_tokens + grad_hidden
    full = jnp.float32
    summed_down, summed_up, summed_out, summed_qkv, grad_input, result, gain_total, bias_total = widen(
        list(backward[:4]) + [grad_tokens, result],
        [full] * 5 + [jnp.bfloat16],
        norm_total,
    )
    return (
        result.reshape(1, 1, BLK, D),
        grad_input.reshape(1, 1, BLK, D),
        summed_qkv,
        summed_out,
        summed_up,
        summed_down,
        gain_total,
        bias_total,
    )


def solution(mesh):
    rows = P("wsh", None)
    blocks = P("grp", "wsh", "ctx", None)
    return jax.shard_map(
        functools.partial(per_device, mesh.shape["ctx"]),
        mesh=mesh,
        in_specs=(blocks, rows, rows, rows, rows, P(), P(), blocks, blocks),
        out_specs=(blocks, blocks, rows, rows, rows, rows, P(), P()),
        check_vma=False,
    )
```

```python
import functools
import math

import jax
import jax.numpy as jnp
from jax import lax
from jax.experimental import pallas as pl
from jax.experimental.pallas import tpu as pltpu
from jax.sharding import PartitionSpec as P

D = 1024
HEADS = 16
DH = 64
BLK = 512
PAIRS = HEADS // 2
QT = 256

EPS = 1e-05
ALPHA = 32.0
NEG = -1e30
LOG2E = 1.4426950408889634
C2 = ALPHA * LOG2E
MESH = pl.DeviceIdType.MESH
QSCALE = 1.0 / (ALPHA * math.sqrt(DH))


def layer_norm(values, gain_row, bias_row):
    centre = values - jnp.mean(values, axis=-1, keepdims=True)
    spread = jnp.mean(centre * centre, axis=-1, keepdims=True)
    return centre * lax.rsqrt(spread + EPS) * gain_row + bias_row


def dot_dims(left_side, right_side, left_dim, right_dim):
    return lax.dot_general(
        left_side,
        right_side,
        (((left_dim,), (right_dim,)), ((), ())),
        preferred_element_type=jnp.float32,
    )


def contract_last(left_side, right_side):
    return dot_dims(left_side, right_side, 1, 1)


def contract_rows(left_side, right_side):
    return dot_dims(left_side, right_side, 0, 0)


def standard_rows(values):
    centre = values - jnp.mean(values, axis=-1, keepdims=True)
    scale = lax.rsqrt(jnp.mean(centre * centre, axis=-1, keepdims=True) + EPS)
    return centre * scale, scale


def row_back(upstream, hat, scale, gain):
    scaled = upstream * gain
    return scale * (
        scaled
        - jnp.mean(scaled, axis=-1, keepdims=True)
        - hat * jnp.mean(scaled * hat, axis=-1, keepdims=True)
    )


def column_sum(values):
    return jnp.sum(values, axis=0, keepdims=True)


def head_lanes(head, rows):
    lane = lax.broadcasted_iota(jnp.int32, (rows, 128), 1)
    return (lane >= DH) if head else (lane < DH)


def causal_tile():
    row = lax.broadcasted_iota(jnp.int32, (QT, QT), 0)
    col = lax.broadcasted_iota(jnp.int32, (QT, QT), 1)
    return col <= row


PIECE = 128
SPAN = 512
CHAIN = 64
HOP = 2
YLAG = 3
XLAG = 2
BLAG = 2
FF_TICKS = 13
TAIL_PACE = 3
GELU_A = 0.044715
GELU_C = math.sqrt(2.0 / math.pi)
PACE = 2
LAG = 2
GROUP = 4
AHEAD = 4


def remote(src, dst, send, recv, peer):
    return pltpu.make_async_remote_copy(
        src_ref=src, dst_ref=dst, send_sem=send, recv_sem=recv, device_id=peer, device_id_type=MESH
    )


def local_wait(ref, sem):
    pltpu.make_async_copy(ref, ref, sem).wait()


def aligned(start, size):
    return pl.ds(pl.multiple_of(start, size), size)


def softmax_block(q_ref, kv_ref, acc, top_ref, sum_ref, pair, base, own, visible):
    lanes = aligned(pair * 128, 128)
    value_lanes = aligned(D + pair * 128, 128)
    causal = causal_tile()
    first = head_lanes(0, QT)
    count = BLK // QT
    q_pair = q_ref[:, lanes]
    keys = kv_ref[pl.ds(base, BLK), lanes]
    values = kv_ref[pl.ds(base, BLK), value_lanes]
    if not own:
        old_top, old_sum, old_out = top_ref[pair], sum_ref[pair], acc[:, lanes]
        hide = jnp.where(visible, 0.0, 1e30)
    results = []
    work = [(tile, head) for tile in range(count) for head in range(2)]
    parts_of = {}
    for tile, head in work:
        q_tile = q_pair[tile * QT : (tile + 1) * QT]
        q_head = jnp.where(head_lanes(head, QT), q_tile, jnp.zeros_like(q_tile))
        span = (tile + 1) * QT if own else BLK
        parts_of[tile, head] = contract_last(q_head, keys[:span])
    top_of, expo_of, total_of = {}, {}, {}
    for tile, head in work:
        part = parts_of[tile, head]
        if own:
            diag = jnp.where(causal, part[:, tile * QT :], NEG)
            part = jnp.concatenate([part[:, : tile * QT], diag], axis=1) if tile else diag
        top = jnp.max(part, axis=-1, keepdims=True) * C2
        if own:
            shift = top
        else:
            top = jnp.maximum(
                jnp.where(visible, top, NEG), old_top[tile * QT : (tile + 1) * QT, head * DH : head * DH + 1]
            )
            shift = top + hide
        expo = jnp.exp2(part * C2 - shift)
        top_of[tile, head] = jnp.broadcast_to(top, (QT, 128))
        total_of[tile, head] = jnp.broadcast_to(jnp.sum(expo, axis=-1, keepdims=True), (QT, 128))
        expo_of[tile, head] = expo.astype(jnp.bfloat16)
    out_of = {}
    for tile, head in work:
        span = (tile + 1) * QT if own else BLK
        out_of[tile, head] = dot_dims(expo_of[tile, head], values[:span], 1, 0)
    for tile in range(count):
        rows = pl.ds(tile * QT, QT)
        new_top = jnp.where(first, top_of[tile, 0], top_of[tile, 1])
        new_sum = jnp.where(first, total_of[tile, 0], total_of[tile, 1])
        new_out = jnp.where(first, out_of[tile, 0], out_of[tile, 1])
        if not own:
            here = slice(tile * QT, (tile + 1) * QT)
            keep = jnp.exp2(old_top[here] - new_top)
            new_sum = new_sum + old_sum[here] * keep
            new_out = new_out + old_out[here] * keep
        top_ref[pair, rows, :] = new_top
        sum_ref[pair, rows, :] = new_sum
        acc[rows, lanes] = new_out


def forward_kernel(n_ctx, *refs):
    slots = n_ctx // 2
    (slot_ref, gain_ref, bias_ref, x_hbm, dy_hbm, w_qkv, w_out, w_up, w_down) = refs[:9]
    (a_out, q_out, kv_out, o_out, lse_out, full_qkv, full_out, full_up, full_down) = refs[9:18]
    (y_out, g_out, dz_out, f_out, u_out, hat1_out, hat2_out, rstd_out, norm_out) = refs[18:27]
    (x_own, left, right, a_all, q_all, kv_all, weight, acc, z_acc, norm_v, tops, sums, hop) = refs[27:40]
    (sem_in, sem_load, sem_store, sem_ff, sem_out, sem_a, sem_kv, side_s, side_r, grp_s, grp_r, cs_s, cs_r, cg_s, cg_r, own_s, own_r, left_s, left_r, right_s, right_r) = refs[40:]
    grp, ctx, wsh = lax.axis_index("grp"), lax.axis_index("ctx"), lax.axis_index("wsh")
    side, core = wsh // 2, wsh % 2
    core_peer = (grp, ctx, side * 2 + 1 - core)
    side_peer = (grp, ctx, (1 - side) * 2 + core)
    grp_peer = (1 - grp, ctx, wsh)
    next_ctx = (grp, lax.rem(ctx + 1, n_ctx), wsh)
    last_ctx = (grp, lax.rem(ctx + n_ctx - 1, n_ctx), wsh)

    load = pltpu.make_async_copy(x_hbm, x_own, sem_in.at[0])
    load.start()
    barrier = pltpu.get_barrier_semaphore()
    for peer in (core_peer, side_peer, grp_peer, next_ctx, last_ctx):
        pl.semaphore_signal(barrier, inc=1, device_id=peer, device_id_type=MESH)
    pl.semaphore_wait(barrier, 5)

    shards = (w_qkv, w_out, w_up, w_down)
    fulls = (weight, full_out, full_up, full_down)
    ranges, start = [], 0
    for shard in shards:
        across = shard.shape[1] // SPAN
        ranges.append((start, start + across * (shard.shape[0] // (2 * PIECE)), across))
        start = ranges[-1][1]
    pieces = start

    def by_range(index, act):
        for place, (low, high, across) in enumerate(ranges):

            @pl.when((index >= low) & (index < high))
            def _(place=place, low=low, across=across):
                act(place, (index - low) // across, aligned(((index - low) % across) * SPAN, SPAN))

    def rows_of(place, owner, half, group):
        shard_rows = shards[place].shape[0]
        return aligned(owner * shard_rows + half * (shard_rows // 2) + group * PIECE, PIECE)

    sides_owner = (1 - side) * 2 + core

    def send_piece(index, carry):
        def act(place, group, cols):
            remote(
                shards[place].at[rows_of(place, 0, grp, group), cols],
                fulls[place].at[rows_of(place, wsh, grp, group), cols],
                side_s.at[index],
                side_r.at[index],
                side_peer,
            ).start()

        by_range(index, act)
        return carry

    def own_copies():
        copies = []
        across = shards[0].shape[1] // SPAN
        for place in range(4):
            shard_rows = shards[place].shape[0]
            mine = aligned(wsh * shard_rows, shard_rows)
            steps = range(across) if place == 0 else [None]
            for step in steps:
                cols = slice(None) if step is None else pl.ds(step * SPAN, SPAN)
                number = len(copies)
                copies.append(
                    remote(
                        shards[place].at[:, cols],
                        fulls[place].at[mine, cols],
                        own_s.at[number],
                        own_r.at[number],
                        core_peer,
                    )
                )
        return copies

    for index in range(AHEAD):
        send_piece(index, 0)
    for copy in own_copies():
        copy.start()
    own_rows = aligned(wsh * w_qkv.shape[0], w_qkv.shape[0])
    own_weight = pltpu.make_async_copy(w_qkv, weight.at[own_rows, :], sem_in.at[1])
    own_weight.start()
    load.wait()

    bounces, start = [], 0
    for shard in shards[1:]:
        across = shard.shape[1] // SPAN
        bounces.append((start, start + across * (shard.shape[0] // (2 * PIECE)), across))
        start = bounces[-1][1]
    moves = start

    def bounce(index, loading):
        slot = lax.rem(index, 3)
        for place, (low, high, across) in enumerate(bounces):

            @pl.when((index >= low) & (index < high))
            def _(place=place + 1, low=low, across=across):
                group = (index - low) // across
                cols = aligned(((index - low) % across) * SPAN, SPAN)
                if loading:
                    here = shards[place].at[aligned(group * 2 * PIECE, 2 * PIECE), cols]
                    pltpu.make_async_copy(here, hop.at[slot], sem_load.at[slot]).start()
                else:
                    rows = aligned(wsh * shards[place].shape[0] + group * 2 * PIECE, 2 * PIECE)
                    local_wait(hop.at[slot], sem_load.at[slot])
                    pltpu.make_async_copy(
                        hop.at[slot], fulls[place].at[rows, cols], sem_store.at[slot]
                    ).start()

    own_slot = slot_ref[1] // BLK
    own_tag = jnp.where(slot_ref[0] == 0, own_slot, n_ctx)
    chain_chunks = slots * (BLK // CHAIN)

    def chain_step(stream, send, recv, number, is_first, is_last, target):
        slot = number // (BLK // CHAIN)
        spot = aligned((number % (BLK // CHAIN)) * CHAIN, CHAIN)
        mine = jnp.where(own_tag == slot, x_own[spot, :], jnp.zeros((CHAIN, D), jnp.bfloat16))
        here = stream.at[slot, spot]

        @pl.when(is_first)
        def _():
            stream[slot, spot, :] = mine

        @pl.when(jnp.logical_not(is_first))
        def _():
            remote(here, here, send.at[number], recv.at[number], target).wait_recv()
            stream[slot, spot, :] = stream[slot, spot, :] + mine

        @pl.when(jnp.logical_not(is_last))
        def _():
            remote(here, here, send.at[number], recv.at[number], target).start()

    def tick(step):
        @pl.when((step >= 1) & (step <= moves))
        def _():
            bounce(step - 1, False)

        @pl.when((step >= 3) & (step < moves))
        def _():
            local_wait(hop.at[lax.rem(step, 3)], sem_store.at[lax.rem(step, 3)])

        @pl.when(step < moves)
        def _():
            bounce(step, True)

        @pl.when(step + AHEAD < pieces)
        def _():
            send_piece(step + AHEAD, 0)

        number = step - HOP * ctx

        @pl.when((number >= 0) & (number < chain_chunks))
        def _():
            chain_step(left, left_s, left_r, number, ctx == 0, ctx == n_ctx - 1, next_ctx)

        back = step - HOP * (n_ctx - 1 - ctx)

        @pl.when((back >= 0) & (back < chain_chunks))
        def _():
            chain_step(right, right_s, right_r, back, ctx == n_ctx - 1, ctx == 0, last_ctx)

        @pl.when(step < pieces)
        def _():
            def act(place, group, cols):
                here = fulls[place].at[rows_of(place, sides_owner, grp, group), cols]
                remote(here, here, side_s.at[step], side_r.at[step], side_peer).wait_recv()
                remote(here, here, grp_s.at[step], grp_r.at[step], grp_peer).start()
                remote(here, here, cs_s.at[step], cs_r.at[step], core_peer).start()

            by_range(step, act)

        late = step - LAG

        @pl.when((late >= 0) & (late < pieces))
        def _():
            def act(place, group, cols):
                here = fulls[place].at[rows_of(place, sides_owner, 1 - grp, group), cols]
                remote(here, here, grp_s.at[late], grp_r.at[late], grp_peer).wait_recv()
                remote(here, here, cg_s.at[late], cg_r.at[late], core_peer).start()

            by_range(late, act)

    def ticks(first, last):
        lax.fori_loop(first, last, lambda index, carry: (tick(index), carry)[1], 0)

    def normalise(source, dest):
        gain, bias = gain_ref[0:1, :], bias_ref[0:1, :]

        def body(index, carry):
            rows = aligned(index * 128, 128)
            values = source(rows).astype(jnp.float32)
            a_all[aligned(dest + index * 128, 128), :] = layer_norm(values, gain, bias).astype(
                jnp.bfloat16
            )
            return carry

        lax.fori_loop(0, BLK // 128, body, 0)

    def piece_ready(index):
        here = fulls[0].at[pl.ds(0, PIECE), pl.ds(0, SPAN)]
        remote(here, here, cs_s.at[index], cs_r.at[index], core_peer).wait_recv()
        remote(here, here, cg_s.at[index], cg_r.at[index], core_peer).wait_recv()
        whole = fulls[0].at[pl.ds(0, 2 * PIECE), pl.ds(0, SPAN)]
        remote(whole, whole, own_s.at[index], own_r.at[index], core_peer).wait_recv()

    tick(0)
    normalise(lambda rows: x_own[rows, :], 0)
    ticks(1, LAG + 1)
    own_weight.wait()

    def project_q(index, carry):
        tick(index + LAG + 1)
        piece_ready(index)
        cols = aligned(index * SPAN, SPAN)
        q_all[:, cols] = (
            jnp.dot(a_all[pl.ds(0, BLK), :], weight[:, cols], preferred_element_type=jnp.float32) * QSCALE
        ).astype(jnp.bfloat16)
        return carry

    lax.fori_loop(0, D // SPAN, project_q, 0)
    head_ticks = LAG + 1 + D // SPAN

    def project_kv(index, base):
        cols = aligned(index * SPAN, SPAN)
        rows = aligned(base, BLK)
        kv_all[rows, cols] = jnp.dot(
            a_all[rows, :], weight[:, aligned(D + index * SPAN, SPAN)], preferred_element_type=jnp.float32
        ).astype(jnp.bfloat16)

    def own_kv(index, carry):
        tick(index + head_ticks)
        piece_ready(index + D // SPAN)
        project_kv(index, 0)
        return carry

    lax.fori_loop(0, 2 * D // SPAN, own_kv, 0)
    own_ticks = head_ticks + 2 * D // SPAN

    def send_block(index):
        rows = aligned(index * BLK, BLK)
        pltpu.make_async_copy(a_all.at[rows, :], a_out.at[rows, :], sem_a.at[index]).start()
        pltpu.make_async_copy(kv_all.at[rows, :], kv_out.at[rows, :], sem_kv.at[index]).start()

    outputs = [
        pltpu.make_async_copy(weight, full_qkv, sem_out.at[0]),
        pltpu.make_async_copy(q_all, q_out, sem_out.at[1]),
    ]
    for copy in outputs:
        copy.start()

    send_block(0)

    def own_attention(group, carry):
        ticks(own_ticks + 2 * group, own_ticks + 2 * group + 2)
        for member in range(GROUP):
            softmax_block(q_all, kv_all, acc, tops, sums, group * GROUP + member, 0, True, None)
        return carry

    groups = PAIRS // GROUP
    lax.fori_loop(0, groups, own_attention, 0)
    used = own_ticks + 2 * groups
    per_slot = 2 * D // SPAN + 2 * groups

    need = BLK // CHAIN + HOP * (n_ctx - 1)
    early = max(0, need - used)
    if early:
        lax.fori_loop(0, early, lambda index, carry: (tick(used + index), carry)[1], 0)

    def each_slot(slot, carry):
        base = pl.multiple_of((slot + 1) * BLK, BLK)
        visible = slot < own_slot
        begin = early + used + slot * per_slot

        def total(rows):
            joined = left[slot, rows, :] + right[slot, rows, :]
            return jnp.where(own_tag == slot, x_own[rows, :], joined)

        normalise(total, base)

        def slot_kv(index, inner):
            tick(begin + index)
            project_kv(index, base)
            return inner

        lax.fori_loop(0, 2 * D // SPAN, slot_kv, 0)

        send_block(slot + 1)

        def slot_attention(group, inner):
            start = begin + 2 * D // SPAN + 2 * group
            ticks(start, start + 2)
            for member in range(GROUP):
                softmax_block(
                    q_all, kv_all, acc, tops, sums, group * GROUP + member, base, False, visible
                )
            return inner

        lax.fori_loop(0, groups, slot_attention, 0)
        return carry

    lax.fori_loop(0, slots, each_slot, 0)
    done_ticks = early + used + slots * per_slot

    def finish(pair, carry):
        lanes = aligned(pair * 128, 128)
        x_own[:, lanes] = (acc[:, lanes] / sums[pair]).astype(jnp.bfloat16)
        tops[pair] = tops[pair] + jnp.log2(sums[pair])
        return carry

    lax.fori_loop(0, PAIRS, finish, 0)
    outputs += [
        pltpu.make_async_copy(x_own, o_out, sem_out.at[2]),
        pltpu.make_async_copy(tops, lse_out, sem_out.at[3]),
    ]
    for copy in outputs[2:]:
        copy.start()
    all_ticks = max(pieces + LAG, chain_chunks + HOP * (n_ctx - 1))
    if all_ticks > done_ticks:
        lax.fori_loop(done_ticks, all_ticks, lambda index, carry: (tick(index), carry)[1], 0)

    def drain(index, carry):
        here = fulls[0].at[pl.ds(0, PIECE), pl.ds(0, SPAN)]

        @pl.when(index >= ranges[0][1])
        def _():
            remote(here, here, cs_s.at[index], cs_r.at[index], core_peer).wait_recv()
            remote(here, here, cg_s.at[index], cg_r.at[index], core_peer).wait_recv()

        remote(here, here, side_s.at[index], side_r.at[index], side_peer).wait_send()
        remote(here, here, grp_s.at[index], grp_r.at[index], grp_peer).wait_send()
        remote(here, here, cs_s.at[index], cs_r.at[index], core_peer).wait_send()
        remote(here, here, cg_s.at[index], cg_r.at[index], core_peer).wait_send()
        return carry

    lax.fori_loop(0, pieces, drain, 0)
    copies = own_copies()
    for number, copy in enumerate(copies):
        copy.wait_send()
        if number >= len(copies) - 3:
            copy.wait_recv()
    for index in range(moves - 3, moves):
        local_wait(hop.at[index % 3], sem_store.at[index % 3])

    def drain_chain(index, carry):
        here = left.at[0, pl.ds(0, CHAIN)]

        @pl.when(ctx < n_ctx - 1)
        def _():
            remote(here, here, left_s.at[index], left_r.at[index], next_ctx).wait_send()

        @pl.when(ctx > 0)
        def _():
            remote(here, here, right_s.at[index], right_r.at[index], last_ctx).wait_send()

        return carry

    lax.fori_loop(0, chain_chunks, drain_chain, 0)
    for copy in outputs[:2]:
        copy.wait()
    shallow_tiles = full_up.shape[1] // SPAN

    def down_spot(place):
        return aligned(BLK + (place // 2) * BLK, BLK), aligned((place % 2) * D, D)

    def tile_loads(tile, place):
        cols = aligned(tile * SPAN, SPAN)
        spot = down_spot(place)
        return (
            pltpu.make_async_copy(
                full_up.at[:, cols], weight.at[:, aligned(D + place * SPAN, SPAN)], sem_ff.at[0, place]
            ),
            pltpu.make_async_copy(full_down.at[cols, :], kv_all.at[spot[0], spot[1]], sem_ff.at[1, place]),
        )

    def tile_stores(tile, parity):
        cols = aligned(tile * SPAN, SPAN)
        return [
            pltpu.make_async_copy(
                kv_all.at[pl.ds(0, BLK), aligned(base + parity * SPAN, SPAN)],
                dest.at[:, cols],
                sem_ff.at[2 + place, parity],
            )
            for place, (base, dest) in enumerate(((0, u_out), (D, g_out)))
        ]

    out_load = pltpu.make_async_copy(full_out, weight.at[:, pl.ds(0, D)], sem_in.at[0])
    x_load = pltpu.make_async_copy(x_hbm, right.at[1], sem_in.at[1])
    for copy in (out_load, x_load):
        copy.start()

    def drain_blocks(index, carry):
        rows = aligned(index * BLK, BLK)
        local_wait(a_all.at[rows, :], sem_a.at[index])
        local_wait(kv_all.at[rows, :], sem_kv.at[index])
        return carry

    lax.fori_loop(0, slots + 1, drain_blocks, 0)
    for tile in range(3):
        for copy in tile_loads(tile, tile):
            copy.start()
    out_load.wait()
    for half_cols in range(2):
        cols = pl.ds(half_cols * SPAN, SPAN)
        acc[:, cols] = jnp.dot(x_own[...], weight[:, cols], preferred_element_type=jnp.float32)
    x_load.wait()
    for copy in outputs[2:]:
        copy.wait()
    dy_load = pltpu.make_async_copy(dy_hbm, x_own, sem_in.at[0])
    dy_load.start()

    def inner_rows(step, carry):
        rows = aligned(step * CHAIN, CHAIN)
        hat, scale = standard_rows(acc[rows, :])
        a_all[rows, :] = hat.astype(jnp.bfloat16)
        sums[0, rows, :] = jnp.broadcast_to(scale, (CHAIN, 128))
        hidden = right[1, rows, :].astype(jnp.float32) + hat * gain_ref[1:2, :] + bias_ref[1:2, :]
        acc[rows, :] = hidden
        hat, scale = standard_rows(hidden)
        a_all[aligned(BLK + step * CHAIN, CHAIN), :] = hat.astype(jnp.bfloat16)
        sums[1, rows, :] = jnp.broadcast_to(scale, (CHAIN, 128))
        q_all[rows, :] = (hat * gain_ref[2:3, :] + bias_ref[2:3, :]).astype(jnp.bfloat16)
        return carry

    lax.fori_loop(0, BLK // CHAIN, inner_rows, 0)
    saves = [
        pltpu.make_async_copy(a_all.at[pl.ds(0, BLK), :], hat1_out, sem_out.at[0]),
        pltpu.make_async_copy(a_all.at[pl.ds(BLK, BLK), :], hat2_out, sem_out.at[1]),
        pltpu.make_async_copy(sums.at[pl.ds(0, 2)], rstd_out, sem_out.at[2]),
        pltpu.make_async_copy(q_all, f_out, sem_out.at[3]),
    ]
    for copy in saves:
        copy.start()

    def ff_tile(tile, carry):
        parity, place = tile % 2, tile % 4
        for copy in tile_loads(tile, place):
            copy.wait()

        @pl.when(tile + 3 < shallow_tiles)
        def _():
            for copy in tile_loads(tile + 3, (tile + 3) % 4):
                copy.start()

        @pl.when(tile >= 2)
        def _():
            for copy in tile_stores(tile - 2, parity):
                copy.wait()

        upward = jnp.dot(
            q_all[...], weight[:, aligned(D + place * SPAN, SPAN)], preferred_element_type=jnp.float32
        )
        kv_all[pl.ds(0, BLK), aligned(parity * SPAN, SPAN)] = upward.astype(jnp.bfloat16)
        active = (
            0.5 * upward * (1.0 + jnp.tanh(GELU_C * upward * (1.0 + GELU_A * upward * upward)))
        ).astype(jnp.bfloat16)
        kv_all[pl.ds(0, BLK), aligned(D + parity * SPAN, SPAN)] = active
        for copy in tile_stores(tile, parity):
            copy.start()
        spot = down_spot(place)
        fresh = jnp.dot(active, kv_all[spot[0], spot[1]], preferred_element_type=jnp.float32)

        @pl.when(tile == 0)
        def _():
            z_acc[...] = fresh

        @pl.when(tile > 0)
        def _():
            z_acc[...] = z_acc[...] + fresh

        return carry

    lax.fori_loop(0, shallow_tiles, ff_tile, 0)
    dy_load.wait()

    def outer_rows(step, carry):
        gain_sum, bias_sum = carry
        rows = aligned(step * CHAIN, CHAIN)
        hat, scale = standard_rows(z_acc[rows, :])
        right[0, rows, :] = (acc[rows, :] + hat * gain_ref[3:4, :] + bias_ref[3:4, :]).astype(jnp.bfloat16)
        upstream = x_own[rows, :].astype(jnp.float32)
        a_all[aligned(2 * BLK + step * CHAIN, CHAIN), :] = row_back(
            upstream, hat, scale, gain_ref[3:4, :]
        ).astype(jnp.bfloat16)
        return gain_sum + column_sum(upstream * hat), bias_sum + column_sum(upstream)

    zero = jnp.zeros((1, D), jnp.float32)
    gain_sum, bias_sum = lax.fori_loop(0, BLK // CHAIN, outer_rows, (zero, zero))
    row = lax.broadcasted_iota(jnp.int32, (8, D), 0)
    norm_v[...] = jnp.where(row == 3, gain_sum, 0.0) + jnp.where(row == 7, bias_sum, 0.0)
    ends = [
        pltpu.make_async_copy(right.at[0], y_out, sem_in.at[0]),
        pltpu.make_async_copy(a_all.at[pl.ds(2 * BLK, BLK), :], dz_out, sem_in.at[1]),
        pltpu.make_async_copy(norm_v, norm_out, sem_in.at[2]),
    ]
    for copy in ends:
        copy.start()
    for tile in range(shallow_tiles - 2, shallow_tiles):
        for copy in tile_stores(tile, tile % 2):
            copy.wait()
    for copy in saves + ends:
        copy.wait()


def forward_part(n_ctx, tags, gains, biases, raw, dy, w_qkv, w_out, w_up, w_down):
    slots = n_ctx // 2
    every = (slots + 1) * BLK
    low, full = jnp.bfloat16, jnp.float32
    dma = pltpu.SemaphoreType.DMA
    hbm = pl.BlockSpec(memory_space=pl.ANY)
    vmem = pl.BlockSpec(memory_space=pltpu.VMEM)
    shards = (w_qkv, w_out, w_up, w_down)
    pieces = sum(w.shape[0] * w.shape[1] // (2 * PIECE * SPAN) for w in shards)
    own = w_qkv.shape[1] // SPAN + 3
    chain = slots * (BLK // CHAIN)
    shape = jax.ShapeDtypeStruct
    return pl.pallas_call(
        functools.partial(forward_kernel, n_ctx),
        out_shape=[
            shape((every, D), low),
            shape((BLK, D), low),
            shape((every, 2 * D), low),
            shape((BLK, D), low),
            shape((PAIRS, BLK, 128), full),
        ]
        + [shape((4 * w.shape[0], w.shape[1]), low) for w in shards]
        + [
            shape((BLK, D), low),
            shape((BLK, w_up.shape[1]), low),
            shape((BLK, D), low),
            shape((BLK, D), low),
            shape((BLK, w_up.shape[1]), low),
            shape((BLK, D), low),
            shape((BLK, D), low),
            shape((2, BLK, 128), full),
            shape((8, D), full),
        ],
        in_specs=[pl.BlockSpec(memory_space=pltpu.SMEM), vmem, vmem] + [hbm] * 6,
        out_specs=[hbm] * 18,
        scratch_shapes=[
            pltpu.VMEM((BLK, D), low),
            pltpu.VMEM((slots, BLK, D), low),
            pltpu.VMEM((slots, BLK, D), low),
            pltpu.VMEM((every, D), low),
            pltpu.VMEM((BLK, D), low),
            pltpu.VMEM((every, 2 * D), low),
            pltpu.VMEM((D, 3 * D), low),
            pltpu.VMEM((BLK, D), full),
            pltpu.VMEM((BLK, D), full),
            pltpu.VMEM((8, D), full),
            pltpu.VMEM((PAIRS, BLK, 128), full),
            pltpu.VMEM((PAIRS, BLK, 128), full),
            pltpu.VMEM((3, 2 * PIECE, SPAN), low),
            dma((3,)),
            dma((3,)),
            dma((3,)),
            dma((4, 4)),
            dma((4,)),
            dma((slots + 1,)),
            dma((slots + 1,)),
        ]
        + [dma((pieces,))] * 8
        + [dma((own,))] * 2
        + [dma((chain,))] * 4,
        compiler_params=pltpu.CompilerParams(
            collective_id=1, has_side_effects=True, vmem_limit_bytes=67043328
        ),
        cost_estimate=pl.CostEstimate(flops=20 << 30, bytes_accessed=64 << 20, transcendentals=1 << 24),
        name="gather_attend",
    )(tags, gains, biases, raw, dy, *shards)


TILE = 256
PAIRED = 2


def grad_block(q_ref, do_ref, o_ref, lse_ref, kv_ref, dq_acc, turned, pair, own, visible):
    lanes = aligned(pair * 128, 128)
    value_lanes = aligned(D + pair * 128, 128)
    size = QT if own else BLK
    count = BLK // size
    q_pair, do_pair, lse_pair = q_ref[:, lanes], do_ref[:, lanes], lse_ref[pair]
    prod = do_pair.astype(jnp.float32) * o_ref[:, lanes].astype(jnp.float32)
    keys, values = kv_ref[:, lanes], kv_ref[:, value_lanes]
    q_turned, do_turned = q_pair.T, do_pair.T
    old_dq = dq_acc[:, lanes]
    causal = causal_tile()
    hide = 0.0 if own else jnp.where(visible, 0.0, 1e30)
    lanes_of = [head_lanes(head, size) for head in range(2)]
    work = [(tile, head) for tile in range(count) for head in range(2)]
    score, dprob, dlogit, prob_low = {}, {}, {}, {}
    for tile, head in work:
        rows = slice(tile * size, (tile + 1) * size)
        span = (tile + 1) * size if own else BLK
        zero = jnp.zeros((size, 128), jnp.bfloat16)
        score[tile, head] = contract_last(jnp.where(lanes_of[head], q_pair[rows], zero), keys[:span])
        dprob[tile, head] = contract_last(jnp.where(lanes_of[head], do_pair[rows], zero), values[:span])
    for tile, head in work:
        rows = slice(tile * size, (tile + 1) * size)
        delta = jnp.sum(jnp.where(lanes_of[head], prod[rows], 0.0), axis=-1, keepdims=True)
        shift = lse_pair[rows, head * DH : head * DH + 1] + hide
        prob = jnp.exp2(score[tile, head] * C2 - shift)
        if own:
            diag = jnp.where(causal, prob[:, tile * size :], 0.0)
            prob = jnp.concatenate([prob[:, : tile * size], diag], axis=1) if tile else diag
        dlogit[tile, head] = (prob * (dprob[tile, head] - delta)).astype(jnp.bfloat16)
        prob_low[tile, head] = prob.astype(jnp.bfloat16)
    for tile in range(count):
        rows = slice(tile * size, (tile + 1) * size)
        span = (tile + 1) * size if own else BLK
        parts = [dot_dims(dlogit[tile, head], keys[:span], 1, 0) for head in range(2)]
        dq_acc[pl.ds(tile * size, size), lanes] = old_dq[rows] + jnp.where(lanes_of[0], parts[0], parts[1])
    for head in range(2):
        for offset, left_side, right_side, scale in (
            (0, q_turned, dlogit, ALPHA),
            (D, do_turned, prob_low, 1.0),
        ):
            spot = aligned(offset + pair * 128 + head * DH, DH)
            left_head = left_side[head * DH : (head + 1) * DH]
            terms = [
                dot_dims(left_head[:, tile * size : (tile + 1) * size], right_side[tile, head], 1, 0)
                for tile in range(count)
            ]
            for tile in range(count):
                cols = slice(tile * size, (tile + 1) * size)
                total = functools.reduce(
                    jnp.add, [terms[other][:, cols] for other in range(tile, count)]
                ) if own else terms[0]
                turned[spot, cols if own else slice(None)] = (total * scale).astype(jnp.bfloat16)


def backward_kernel(n_ctx, widths, *refs):
    slots = n_ctx // 2
    levels = n_ctx.bit_length() - 1
    depth = 16 if n_ctx == 4 else 10
    shallow = slots <= 2
    (slot_ref, gain_ref, bias_ref, norm_ref, x_hbm, q_hbm, kv_hbm, a_hbm, o_hbm, lse_hbm, w_hbm) = refs[:11]
    (w_out, w_up, w_down, g_hbm, dz_hbm, f_hbm, u_hbm, hat1_hbm, hat2_hbm, rstd_hbm, dy_hbm) = refs[11:22]
    outs = refs[22:26]
    grad_out, norm_out, dh_hbm, du_hbm, datt_hbm = refs[26:31]
    scratch = list(refs[31:])
    own_slot = slot_ref[1] // BLK

    def take(count):
        taken = scratch[:count]
        del scratch[:count]
        return taken

    q_v, o_v, do_v, lse_v, weight, kv_b, a_b, dq_acc, turned, gkv, term, own_part, left, right, norm_v, norm_in, gain_sum, bias_sum = take(18)
    r1, r2, r3, fin, made = take(5)
    lhs, rhs = take(2)
    zbufs = take(levels)
    sem_in, sem_blk, sem_rhs, sem_lhs, sem_ff, sem_out, sem_res = take(7)
    send1, recv1, send2, recv2, send3, recv3, send6, recv6 = take(8)
    rs_send, rs_recv, ag_send, ag_recv = take(levels), take(levels), take(levels), take(levels)
    left_s, left_r, right_s, right_r, norm_s, norm_r = take(6)
    grp, ctx, wsh = lax.axis_index("grp"), lax.axis_index("ctx"), lax.axis_index("wsh")
    side, core = wsh // 2, wsh % 2
    core_peer = (grp, ctx, side * 2 + 1 - core)
    side_peer = (grp, ctx, (1 - side) * 2 + core)
    grp_peer = (1 - grp, ctx, wsh)
    next_ctx = (grp, lax.rem(ctx + 1, n_ctx), wsh)
    last_ctx = (grp, lax.rem(ctx + n_ctx - 1, n_ctx), wsh)
    bits = [(ctx // (1 << level)) % 2 for level in range(levels)]
    level_peers = [(grp, ctx + (1 - 2 * bits[level]) * (1 << level), wsh) for level in range(levels)]

    def block_copies(index):
        rows = aligned(lax.rem(index, slots + 1) * BLK, BLK)
        slot = lax.rem(index, kv_b.shape[0])
        a_slot = index - 1 if shallow else 0
        return (
            pltpu.make_async_copy(kv_hbm.at[rows, :], kv_b.at[slot], sem_blk.at[0, slot]),
            pltpu.make_async_copy(a_hbm.at[rows, :], a_b.at[a_slot], sem_blk.at[1, slot]),
        )

    barrier = pltpu.get_barrier_semaphore()
    peers = [core_peer, side_peer, grp_peer, next_ctx, last_ctx] + level_peers
    for peer in peers:
        pl.semaphore_signal(barrier, inc=1, device_id=peer, device_id_type=MESH)
    pl.semaphore_wait(barrier, len(peers))

    half = TILE // 2
    ranges, first = [], 0
    for rows, cols in widths:
        across = cols // TILE
        ranges.append((first, first + (rows // TILE) * across, across))
        first = ranges[-1][1]
    chunks = first

    def by_range(index, act):
        for place, (low, high, across) in enumerate(ranges):

            @pl.when((index >= low) & (index < high))
            def _(place=place, low=low, across=across):
                number = index - low
                act(place, (aligned((number // across) * TILE, TILE), aligned((number % across) * TILE, TILE)))

    def region(level, flip):
        row, rows, col, cols = 0, half, 0, TILE
        for place in range(level):
            bit = 1 - bits[place] if (flip and place == level - 1) else bits[place]
            if rows > 16:
                rows = rows // 2
                row = row + bit * rows
            else:
                cols = cols // 2
                col = col + bit * cols
        return row, rows, col, cols

    def spot(level, flip=False, base=0):
        row, rows, col, cols = region(level, flip)
        return aligned(base + row, rows), aligned(col, cols)

    last_low = ranges[-1][0]
    dq_low = o_v
    set_of = [(0, number) for number in range(widths[0][0] // TILE)] + [(1, 0), (2, 0)]
    set_first = [number * ranges[0][2] for number in range(widths[0][0] // TILE)]
    set_first += [ranges[1][0], ranges[2][0]]
    left_of, right_of = (g_hbm, f_hbm, o_hbm), (dz_hbm, du_hbm, datt_hbm)

    def set_copies(number):
        place, group = set_of[number]
        stride = left_of[place].shape[1] // 4
        return [
            pltpu.make_async_copy(
                left_of[place].at[:, pl.ds(owner * stride + group * TILE, TILE)],
                lhs.at[number % 2, owner],
                sem_lhs.at[number % 2, owner],
            )
            for owner in range(4)
        ]

    def step_fetch(index):
        near = lax.rem(index, 4)

        def act(place, span):
            if place < 3:
                pltpu.make_async_copy(
                    right_of[place].at[:, span[1]], rhs.at[near], sem_rhs.at[near]
                ).start()

        by_range(index, act)

    def step_make(index, kinds):
        slot = lax.rem(index, depth)
        near = lax.rem(index, 4)

        def low_piece():
            local_wait(rhs.at[near], sem_rhs.at[near])
            parity = jnp.int32(0)
            for number, low in enumerate(set_first):
                parity = jnp.where(index >= low, number % 2, parity)

                @pl.when(index == low)
                def _(number=number):
                    for copy in set_copies(number):
                        copy.wait()
                    if number + 1 < len(set_first):
                        for copy in set_copies(number + 1):
                            copy.start()

            right_side = rhs[near]

            def owner_pair(upper, carry):
                for core_of in range(2):
                    made[near, upper, core_of] = dot_dims(
                        lhs[parity, upper * 2 + core_of], right_side, 0, 0
                    ).astype(jnp.bfloat16)
                return carry

            lax.fori_loop(0, 2, owner_pair, 0)

        def high_piece():
            number = index - last_low
            if not shallow:
                made[near] = term[:, :, :, aligned(number * TILE, TILE)]
                return

            @pl.when(number < D // TILE)
            def _():
                right_side = dq_low[:, aligned(number * TILE, TILE)]
                for owner in range(4):
                    made[near, owner // 2, owner % 2] = dot_dims(
                        a_b[slots, :, pl.ds(owner * TILE, TILE)], right_side, 0, 0
                    ).astype(jnp.bfloat16)

            @pl.when(number >= D // TILE)
            def _():
                cols = aligned((number - D // TILE) * TILE, TILE)
                for owner in range(4):
                    total = functools.reduce(
                        jnp.add,
                        [
                            dot_dims(a_b[block, :, pl.ds(owner * TILE, TILE)], turned[block, cols, :], 0, 1)
                            for block in range(slots + 1)
                        ],
                    )
                    made[near, owner // 2, owner % 2] = total.astype(jnp.bfloat16)

        if kinds == "low":
            low_piece()
        elif kinds == "high":
            high_piece()
        else:
            pl.when(index < last_low)(low_piece)
            pl.when(index >= last_low)(high_piece)
        remote(
            made.at[near, :, 1 - core], r1.at[slot], send1.at[slot], recv1.at[slot], core_peer
        ).start()

    def finished(move):
        move.wait_send()
        move.wait_recv()

    def step_core(index):
        slot, near = lax.rem(index, depth), lax.rem(index, 4)
        finished(remote(r1.at[slot], r1.at[slot], send1.at[slot], recv1.at[slot], core_peer))
        r1[slot] = r1[slot] + made[near, :, core]
        remote(r1.at[slot, 1 - side], r2.at[slot], send2.at[slot], recv2.at[slot], side_peer).start()

    keep_half = aligned(grp * half, half)
    give_half = aligned((1 - grp) * half, half)

    def step_side(index):
        slot = lax.rem(index, depth)
        finished(remote(r1.at[slot, 1 - side], r2.at[slot], send2.at[slot], recv2.at[slot], side_peer))
        r2[slot] = r2[slot] + r1[slot, side]
        remote(r2.at[slot, give_half], r3.at[slot], send3.at[slot], recv3.at[slot], grp_peer).start()

    fold = n_ctx == 4
    if fold:
        outer = bits[0] == bits[1]
        inner = bits[0] != bits[1]
        mate, middle = level_peers[0], (grp, 3 - ctx, wsh)
        quarter = half // 2
        mine, other = aligned(bits[1] * quarter, quarter), aligned((1 - bits[1]) * quarter, quarter)
        fin_mine = aligned(grp * half + bits[1] * quarter, quarter)
        fin_other = aligned(grp * half + (1 - bits[1]) * quarter, quarter)

        def up_copy(slot):
            return remote(r3.at[slot], zbufs[0].at[slot], rs_send[0].at[slot], rs_recv[0].at[slot], mate)

        def cross_copy(slot):
            return remote(
                r3.at[slot, other], zbufs[1].at[slot], rs_send[1].at[slot], rs_recv[1].at[slot], middle
            )

        def share_copy(slot, rows):
            here = fin.at[slot, rows]
            return remote(here, here, ag_send[1].at[slot], ag_recv[1].at[slot], middle)

        def down_copy(slot):
            here = fin.at[slot, keep_half]
            return remote(here, here, ag_send[0].at[slot], ag_recv[0].at[slot], mate)

        def step_up(index):
            slot = lax.rem(index, depth)

            @pl.when(outer)
            def _():
                up_copy(slot).wait_send()

            @pl.when(inner)
            def _():
                up_copy(slot).wait_recv()
                r3[slot] = r3[slot] + zbufs[0][slot]
                cross_copy(slot).start()

        def step_cross(index):
            slot = lax.rem(index, depth)

            @pl.when(inner)
            def _():
                finished(cross_copy(slot))
                fin[slot, fin_mine] = r3[slot, mine] + zbufs[1][slot]
                share_copy(slot, fin_mine).start()

        def step_share(index):
            slot = lax.rem(index, depth)

            @pl.when(inner)
            def _():
                finished(share_copy(slot, fin_other))
                down_copy(slot).start()

        def step_down(index):
            slot = lax.rem(index, depth)

            @pl.when(inner)
            def _():
                down_copy(slot).wait_send()

            @pl.when(outer)
            def _():
                down_copy(slot).wait_recv()

            back_copy(slot, keep_half).start()

    def rs_copy(level, slot):
        rows, cols = spot(level + 1, True)
        return remote(
            r3.at[slot, rows, cols], zbufs[level].at[slot], rs_send[level].at[slot], rs_recv[level].at[slot], level_peers[level]
        )

    def ag_copy(level, slot, flip=False):
        rows, cols = spot(level + 1, flip, grp * half)
        here = fin.at[slot, rows, cols]
        return remote(here, here, ag_send[level].at[slot], ag_recv[level].at[slot], level_peers[level])

    def back_copy(slot, rows):
        here = fin.at[slot, rows]
        return remote(here, here, send6.at[slot], recv6.at[slot], grp_peer)

    def step_grp(index):
        slot = lax.rem(index, depth)
        finished(remote(r2.at[slot, give_half], r3.at[slot], send3.at[slot], recv3.at[slot], grp_peer))
        r3[slot] = r3[slot] + r2[slot, keep_half]
        if fold:

            @pl.when(outer)
            def _():
                up_copy(slot).start()
        else:
            rs_copy(0, slot).start()

    def step_scatter(level):
        def act(index):
            slot = lax.rem(index, depth)
            finished(rs_copy(level, slot))
            rows, cols = spot(level + 1)
            total = r3[slot, rows, cols] + zbufs[level][slot]
            if level + 1 < levels:
                r3[slot, rows, cols] = total
                rs_copy(level + 1, slot).start()
            else:
                rows, cols = spot(level + 1, False, grp * half)
                fin[slot, rows, cols] = total
                ag_copy(level, slot).start()

        return act

    def step_gather(level):
        def act(index):
            slot = lax.rem(index, depth)
            finished(ag_copy(level, slot, True))
            if level:
                ag_copy(level - 1, slot).start()
            else:
                back_copy(slot, keep_half).start()

        return act

    def out_wait(index):
        slot = lax.rem(index, depth)
        local_wait(fin.at[slot], sem_out.at[slot])

    def step_out(index):
        slot = lax.rem(index, depth)
        finished(back_copy(slot, give_half))

        def act(place, span):
            pltpu.make_async_copy(fin.at[slot], outs[place].at[span[0], span[1]], sem_out.at[slot]).start()

        by_range(index, act)

    z_lag = 2 if fold else 1
    order = [(YLAG, step_side), (XLAG, step_grp)]
    if fold:
        order += [(z_lag, act) for act in (step_up, step_cross, step_share, step_down)]
    else:
        order += [(z_lag, step_scatter(level)) for level in range(levels)]
        order += [(z_lag, step_gather(level)) for level in reversed(range(levels))]
    order += [(BLAG, step_out), (2, out_wait)]
    stages = [(0, step_core)]
    for lag, act in order:
        stages.append((stages[-1][0] + lag, act))
    all_ticks = chunks + stages[-1][0]

    per_slot = BLK // CHAIN
    chain_chunks = slots * per_slot

    def chain_step(stream, send, recv, number, is_first, is_last, target):
        slot = number // per_slot
        rows = aligned((number % per_slot) * CHAIN, CHAIN)
        here = stream.at[slot, rows]

        @pl.when(is_first)
        def _():
            stream[slot, rows, :] = own_part[slot, rows, :]

        @pl.when(jnp.logical_not(is_first))
        def _():
            remote(here, here, send.at[number], recv.at[number], target).wait_recv()
            stream[slot, rows, :] = stream[slot, rows, :] + own_part[slot, rows, :]

        @pl.when(jnp.logical_not(is_last))
        def _():
            remote(here, here, send.at[number], recv.at[number], target).start()

    def chain_tick(step):
        number = step - ctx

        @pl.when((number >= 0) & (number < chain_chunks))
        def _():
            chain_step(left, left_s, left_r, number, ctx == 0, ctx == n_ctx - 1, next_ctx)

        back = step - (n_ctx - 1 - ctx)

        @pl.when((back >= 0) & (back < chain_chunks))
        def _():
            chain_step(right, right_s, right_r, back, ctx == n_ctx - 1, ctx == 0, last_ctx)

    groups = PAIRS // PAIRED
    group_ticks = groups if shallow else 0
    block_ticks = group_ticks + 2
    chain_first = FF_TICKS + block_ticks
    paced = max(0, -(-(chunks - chain_first) // PACE))
    late_first = max(chunks, chain_first)
    late_beats = max(0, chain_chunks + n_ctx - 1 - paced)
    chain_ticks = late_first + TAIL_PACE * max(0, late_beats - 1) + 1

    def tick(step, kinds):
        kinds = kinds if shallow or kinds == "none" else "both"
        if kinds in ("low", "both"):

            @pl.when(step + 3 < chunks)
            def _():
                step_fetch(step + 3)

        if kinds != "none":

            @pl.when(step + 2 < chunks)
            def _():
                step_make(step + 2, kinds)

        for lag, act in stages:
            index = step - lag

            @pl.when((index >= 0) & (index < chunks))
            def _(act=act, index=index):
                act(index)

        beat = step - chain_first

        @pl.when((beat >= 0) & (step < chunks) & (beat % PACE == 0))
        def _():
            chain_tick(beat // PACE)

        late = step - late_first

        @pl.when((late >= 0) & (late % TAIL_PACE == 0))
        def _():
            chain_tick(paced + late // TAIL_PACE)


    for index in range(3):
        step_fetch(jnp.int32(index))
    for copy in set_copies(0):
        copy.start()

    hidden_tiles = u_hbm.shape[1] // SPAN
    datt_v, dz_v, dy_v, hat1_v, hat2_v = own_part.at[0], do_v, left.at[1], right.at[0], right.at[1]

    def tile_copies(tile, parity):
        cols = aligned(tile * SPAN, SPAN)
        return (
            pltpu.make_async_copy(w_down.at[cols, :], own_part.at[parity], sem_ff.at[0, parity]),
            pltpu.make_async_copy(
                w_up.at[:, cols], turned.at[0, aligned(parity * D, D), :], sem_ff.at[1, parity]
            ),
            pltpu.make_async_copy(
                u_hbm.at[:, cols], left.at[0, :, aligned(parity * SPAN, SPAN)], sem_ff.at[2, parity]
            ),
        )

    def du_store(tile, parity):
        return pltpu.make_async_copy(
            kv_b.at[0, :, aligned(parity * SPAN, SPAN)],
            du_hbm.at[:, aligned(tile * SPAN, SPAN)],
            sem_ff.at[3, parity],
        )

    dz_load = pltpu.make_async_copy(dz_hbm, dz_v, sem_in.at[0])
    dz_load.start()
    for copy in tile_copies(0, 0):
        copy.start()
    wide_loads = [
        pltpu.make_async_copy(source, dest, sem_in.at[place + 1])
        for place, (source, dest) in enumerate(
            (
                (dy_hbm, dy_v),
                (hat1_hbm, hat1_v),
                (hat2_hbm, hat2_v),
                (rstd_hbm, lse_v.at[pl.ds(0, 2)]),
                (q_hbm, q_v),
                (o_hbm, o_v),
                (w_hbm, weight),
            )
        )
    ]
    out_loads = [
        pltpu.make_async_copy(
            w_out.at[pl.ds(place * TILE, TILE), :],
            term.at[place // 2, place % 2, :, pl.ds(0, D)],
            sem_in.at[8 + place],
        )
        for place in range(4)
    ]
    lax.fori_loop(0, 2, lambda index, carry: (step_make(index, "low"), carry)[1], 0)
    dz_load.wait()

    def ff_tile(tile, carry):
        start = tile + (tile + 1) // 2
        extra = jnp.where((tile % 2 == 0) | (tile + 1 == hidden_tiles), 1, 0)
        lax.fori_loop(start, start + 1 + extra, lambda index, inner: (tick(index, "low"), inner)[1], 0)

        parity = tile % 2
        for copy in tile_copies(tile, parity):
            copy.wait()

        @pl.when(tile + 1 < hidden_tiles)
        def _():
            for copy in tile_copies(tile + 1, 1 - parity):
                copy.start()

        @pl.when(tile == 0)
        def _():
            for copy in wide_loads + out_loads:
                copy.start()

        @pl.when(tile >= 2)
        def _():
            du_store(tile - 2, parity).wait()

        u_cols = aligned(parity * SPAN, SPAN)
        u_tile = left[0, :, u_cols].astype(jnp.float32)
        square = u_tile * u_tile
        bend = jnp.tanh(GELU_C * u_tile * (1.0 + GELU_A * square))
        slope = 0.5 * (1.0 + bend) + (0.5 * GELU_C) * u_tile * (1.0 - bend * bend) * (
            1.0 + 3.0 * GELU_A * square
        )
        du_tile = (contract_last(dz_v[...], own_part[parity]) * slope).astype(jnp.bfloat16)
        kv_b[0, :, u_cols] = du_tile
        du_store(tile, parity).start()
        fresh = contract_last(du_tile, turned[0, aligned(parity * D, D), :])

        @pl.when(tile == 0)
        def _():
            dq_acc[...] = fresh

        @pl.when(tile > 0)
        def _():
            dq_acc[...] = dq_acc[...] + fresh

        return carry

    lax.fori_loop(0, hidden_tiles, ff_tile, 0)
    for tile in range(hidden_tiles - 2, hidden_tiles):
        du_store(tile, tile % 2).wait()
    for copy in wide_loads:
        copy.wait()
    for copy in block_copies(1):
        copy.start()

    def hidden_back(step, carry):
        gain1, gain2, bias1, bias2 = carry
        rows = aligned(step * CHAIN, CHAIN)
        upstream = dq_acc[rows, :]
        hat = hat2_v[rows, :].astype(jnp.float32)
        grad_h = dy_v[rows, :].astype(jnp.float32) + row_back(
            upstream, hat, lse_v[1, rows, 0:1], gain_ref[2:3, :]
        )
        gain2, bias2 = gain2 + column_sum(upstream * hat), bias2 + column_sum(upstream)
        dq_acc[rows, :] = grad_h
        if shallow:
            gkv[rows, :] = grad_h
        hat = hat1_v[rows, :].astype(jnp.float32)
        datt_v[rows, :] = row_back(grad_h, hat, lse_v[0, rows, 0:1], gain_ref[1:2, :]).astype(
            jnp.bfloat16
        )
        return gain1 + column_sum(grad_h * hat), gain2, bias1 + column_sum(grad_h), bias2

    zero = jnp.zeros((1, D), jnp.float32)
    sums = lax.fori_loop(0, BLK // CHAIN, hidden_back, (zero,) * 4)
    row = lax.broadcasted_iota(jnp.int32, (8, D), 0)
    norm_v[...] = norm_ref[...]
    for place, value in zip((1, 2, 5, 6), sums):
        norm_v[...] = norm_v[...] + jnp.where(row == place, value, 0.0)
    stores = [
        pltpu.make_async_copy(dq_acc, dh_hbm, sem_res.at[0]),
        pltpu.make_async_copy(datt_v, datt_hbm, sem_res.at[1]),
    ]
    lse_load = pltpu.make_async_copy(lse_hbm, lse_v, sem_in.at[0])
    for copy in stores + [lse_load]:
        copy.start()
    for place in range(4):
        out_loads[place].wait()
        do_v[:, pl.ds(place * TILE, TILE)] = contract_last(
            datt_v[...], term[place // 2, place % 2, :, pl.ds(0, D)]
        ).astype(jnp.bfloat16)
    for copy in stores + [lse_load]:
        copy.wait()
    dq_acc[...] = jnp.zeros_like(dq_acc)

    def attend(kv_ref, turned_ref, own, visible, begin):
        def body(group, carry):
            if shallow:
                tick(begin + group, "low")
            for member in range(PAIRED):
                grad_block(
                    q_v, do_v, o_v, lse_v, kv_ref, dq_acc, turned_ref, group * PAIRED + member, own, visible
                )
            return carry

        lax.fori_loop(0, groups, body, 0)

    def first_sums(piece, normed, cols):
        gain_sum[:, cols] = gain_sum[:, cols] + column_sum(piece * normed.astype(jnp.float32))
        bias_sum[:, cols] = bias_sum[:, cols] + column_sum(piece)

    gain_sum[...] = jnp.zeros_like(gain_sum)
    bias_sum[...] = jnp.zeros_like(bias_sum)

    def each_slot(slot, carry):
        visible = slot < own_slot
        index = slot + 1
        place = lax.rem(index, kv_b.shape[0])
        for copy in block_copies(index):
            copy.wait()
        if kv_b.shape[0] > 1:
            for copy in block_copies(index + 1):
                copy.start()
        begin = FF_TICKS + slot * block_ticks
        a_place = slot if shallow else 0
        attend(kv_b.at[place], turned.at[a_place], False, visible, begin)

        def weight_terms(step, inner):
            tick(begin + group_ticks + step, "low")
            rows = aligned(step * 512, 512)
            for part in range(0 if shallow else 2):
                cols = pl.ds(part * D, D)
                product = dot_dims(a_b[a_place, :, rows], turned[a_place, cols, :], 0, 1)
                for down in range(2):
                    target = term.at[step, down, :, pl.ds((part + 1) * D, D)]
                    piece = product[down * TILE : (down + 1) * TILE]

                    @pl.when(slot == 0)
                    def _(target=target, piece=piece):
                        target[...] = piece.astype(target.dtype)

                    @pl.when(slot > 0)
                    def _(target=target, piece=piece):
                        target[...] = (target[...] + piece).astype(target.dtype)

            piece = dot_dims(turned[a_place], weight[rows, pl.ds(D, 2 * D)], 0, 1)
            own_part[slot, :, rows] = piece.astype(jnp.bfloat16)
            first_sums(piece, a_b[a_place, :, rows], rows)
            return inner

        lax.fori_loop(0, 2, weight_terms, 0)
        if kv_b.shape[0] == 1:
            for copy in block_copies(index + 1):
                copy.start()
        return carry

    lax.fori_loop(0, slots, each_slot, 0)
    begin = FF_TICKS + slots * block_ticks
    own_place = (slots + 1) % kv_b.shape[0]
    for copy in block_copies(slots + 1):
        copy.wait()
    own_a = slots if shallow else 0
    attend(kv_b.at[own_place], turned.at[own_a], True, None, begin)
    dq_low[...] = (dq_acc[...] * ALPHA).astype(jnp.bfloat16) * jnp.bfloat16(QSCALE)
    x_load = pltpu.make_async_copy(x_hbm, do_v, sem_in.at[0])
    x_load.start()
    ready = begin + group_ticks

    def last_terms(step, carry):
        tick(begin + group_ticks + step, "both")
        rows = aligned(step * TILE, TILE)
        a_rows = a_b[0, :, rows]
        up, down = step // 2, step % 2
        term[up, down, :, pl.ds(0, D)] = dot_dims(a_rows, dq_low[...], 0, 0).astype(jnp.bfloat16)
        for part in range(2):
            cols = pl.ds(part * D, D)
            target = term.at[up, down, :, pl.ds((part + 1) * D, D)]
            target[...] = (target[...] + dot_dims(a_rows, turned[0, cols, :], 0, 1)).astype(jnp.bfloat16)
        return carry

    if not shallow:
        lax.fori_loop(0, 4, last_terms, 0)
        ready = ready + 4
    assert ready <= last_low - 2
    da_acc = dq_acc

    spare = max(0, last_low - 2 - ready - 4) if shallow else 0

    def own_grad(step, carry):
        if shallow:
            begins = ready + step + jnp.where(step > 0, spare, 0)
            ends = ready + step + 1 + spare
            lax.fori_loop(begins, ends, lambda index, inner: (tick(index, "low"), inner)[1], 0)
        else:
            tick(ready + step, "low")
        rows = aligned(step * TILE, TILE)
        piece = dot_dims(dq_low[...], weight[rows, pl.ds(0, D)], 1, 1) + dot_dims(
            turned[own_a], weight[rows, pl.ds(D, 2 * D)], 0, 1
        )
        da_acc[:, rows] = piece
        first_sums(piece, a_b[own_a, :, rows], rows)
        return carry

    lax.fori_loop(0, 4, own_grad, 0)
    ready = ready + 4 + spare

    first_gain = (gain_sum[...] - bias_ref[0:1, :] * bias_sum[...]) / gain_ref[0:1, :]
    norm_v[...] = (
        norm_v[...] + jnp.where(row == 0, first_gain, 0.0) + jnp.where(row == 4, bias_sum[...], 0.0)
    )

    def run_ticks(first, last, kinds):
        if last > first:
            lax.fori_loop(first, last, lambda index, carry: (tick(index, kinds), carry)[1], 0)
        return max(first, last)

    assert ready == last_low - 2 or not shallow
    norm_peers = [core_peer, side_peer, grp_peer] + level_peers
    norm_base = ready
    norm_result = pltpu.make_async_copy(norm_v, norm_out, sem_res.at[1])

    def norm_move(place):
        return remote(norm_v, norm_in.at[place], norm_s.at[place], norm_r.at[place], norm_peers[place])

    def norm_ticks(step, carry):
        for place in range(len(norm_peers) + 1):

            @pl.when(step == norm_base + 3 * place)
            def _(place=place):
                if place:
                    finished(norm_move(place - 1))
                    norm_v[...] = norm_v[...] + norm_in[place - 1]
                if place < len(norm_peers):
                    norm_move(place).start()
                else:
                    norm_result.start()

        tick(step, "high")
        return carry

    last_tick = max(ready + 3 * len(norm_peers) + 1, chain_ticks)
    lax.fori_loop(ready, last_tick, norm_ticks, 0)
    ready = last_tick
    x_load.wait()
    gain = gain_ref[0:1, :]

    def norm_grad(step, carry):
        @pl.when(step % 2 == 0)
        def _():
            tick(ready + step // 2, "none")

        rows = aligned(step * CHAIN, CHAIN)
        upstream = da_acc[rows, :]
        for slot in range(slots):
            joined = left[slot, rows, :].astype(jnp.float32) + right[slot, rows, :].astype(jnp.float32)
            upstream = upstream + jnp.where(own_slot == slot, joined, 0.0)
        values = do_v[rows, :].astype(jnp.float32)
        centre = values - jnp.mean(values, axis=-1, keepdims=True)
        scale = lax.rsqrt(jnp.mean(centre * centre, axis=-1, keepdims=True) + EPS)
        centre = centre * scale
        grad = row_back(upstream, centre, scale, gain)
        da_acc[rows, :] = grad + gkv[rows, :] if shallow else grad
        return carry

    lax.fori_loop(0, BLK // CHAIN, norm_grad, 0)
    ready = ready + BLK // CHAIN // 2
    result = pltpu.make_async_copy(da_acc, grad_out, sem_res.at[0])
    result.start()
    run_ticks(ready, all_ticks, "none")

    def drain_chain(index, carry):
        here = left.at[0, pl.ds(0, CHAIN)]

        @pl.when(ctx < n_ctx - 1)
        def _():
            remote(here, here, left_s.at[index], left_r.at[index], next_ctx).wait_send()

        @pl.when(ctx > 0)
        def _():
            remote(here, here, right_s.at[index], right_r.at[index], last_ctx).wait_send()

        return carry

    lax.fori_loop(0, chain_chunks, drain_chain, 0)
    result.wait()
    norm_result.wait()


def backward_part(n_ctx, slot_vec, gains, biases, norms, saved, weights, ffn):
    slots = n_ctx // 2
    levels = n_ctx.bit_length() - 1
    depth = 16 if n_ctx == 4 else 10
    hidden = weights[1].shape[1]
    widths = [(hidden // 4, D), (D // 4, hidden), (D // 4, D), (D // 4, 3 * D)]
    low, full = jnp.bfloat16, jnp.float32
    dma = pltpu.SemaphoreType.DMA
    hbm = pl.BlockSpec(memory_space=pl.ANY)
    vmem = pl.BlockSpec(memory_space=pltpu.VMEM)
    shape = jax.ShapeDtypeStruct
    buffers = 2 if slots <= 2 else 1
    chain = slots * (BLK // CHAIN)
    zshapes, rows, cols = [], TILE // 2, TILE
    if n_ctx == 4:
        zshapes = [pltpu.VMEM((depth, rows, cols), low), pltpu.VMEM((depth, rows // 2, cols), low)]
    for _ in range(0 if zshapes else levels):
        rows, cols = (rows // 2, cols) if rows > 16 else (rows, cols // 2)
        zshapes.append(pltpu.VMEM((depth, rows, cols), low))
    return pl.pallas_call(
        functools.partial(backward_kernel, n_ctx, widths),
        out_shape=[shape(width, low) for width in widths] + [
            shape((BLK, D), full),
            shape((8, D), full),
            shape((BLK, D), full),
            shape((BLK, hidden), low),
            shape((BLK, D), low),
        ],
        in_specs=[pl.BlockSpec(memory_space=pltpu.SMEM), vmem, vmem, vmem]
        + [hbm] * (len(saved) + len(weights) + len(ffn)),
        out_specs=[hbm] * 9,
        scratch_shapes=[
            pltpu.VMEM((BLK, D), low),
            pltpu.VMEM((BLK, D), low),
            pltpu.VMEM((BLK, D), low),
            pltpu.VMEM((PAIRS, BLK, 128), full),
            pltpu.VMEM((D, 3 * D), low),
            pltpu.VMEM((buffers, BLK, 2 * D), low),
            pltpu.VMEM((slots + 1 if slots <= 2 else 1, BLK, D), low),
            pltpu.VMEM((BLK, D), full),
            pltpu.VMEM((slots + 1 if slots <= 2 else 1, 2 * D, BLK), low),
            pltpu.VMEM((BLK, D) if slots <= 2 else (8, 128), full),
            pltpu.VMEM((2, 2, D // 4, D if slots <= 2 else 3 * D), low),
            pltpu.VMEM((slots, BLK, D), low),
            pltpu.VMEM((slots, BLK, D), low),
            pltpu.VMEM((slots, BLK, D), low),
            pltpu.VMEM((8, D), full),
            pltpu.VMEM((3 + levels, 8, D), full),
            pltpu.VMEM((1, D), full),
            pltpu.VMEM((1, D), full),
            pltpu.VMEM((depth, 2, TILE, TILE), low),
            pltpu.VMEM((depth, TILE, TILE), low),
            pltpu.VMEM((depth, TILE // 2, TILE), low),
            pltpu.VMEM((depth, TILE, TILE), low),
            pltpu.VMEM((4, 2, 2, TILE, TILE), low),
        ]
        + [pltpu.VMEM((2, 4, BLK, TILE), low), pltpu.VMEM((4, BLK, TILE), low)]
        + zshapes
        + [dma((12,)), dma((2, buffers)), dma((4,)), dma((2, 4)), dma((4, 2)), dma((depth,)), dma((2,))]
        + [dma((depth,))] * (8 + 4 * levels)
        + [dma((chain,))] * 4
        + [dma((3 + levels,))] * 2,
        compiler_params=pltpu.CompilerParams(
            collective_id=2, has_side_effects=True, vmem_limit_bytes=67043328
        ),
        cost_estimate=pl.CostEstimate(flops=40 << 30, bytes_accessed=64 << 20, transcendentals=1 << 24),
        name="attend_back_reduce",
    )(
        slot_vec,
        gains,
        biases,
        norms,
        *saved,
        *weights,
        *ffn,
    )


def widen_kernel(*refs):
    count = len(refs) // 2
    for source, dest in zip(refs[: count - 1], refs[count:]):
        dest[...] = source[...].astype(dest.dtype)
    refs[-2][...] = refs[count - 1][0:4, :]
    refs[-1][...] = refs[count - 1][4:8, :]


def widen(arrays, types, norms):
    steps = 4
    specs = [pl.BlockSpec((x.shape[0] // steps, x.shape[1]), lambda i: (i, 0)) for x in arrays]
    shape = jax.ShapeDtypeStruct
    pair = [pl.BlockSpec((4, D), lambda i: (0, 0))] * 2
    return pl.pallas_call(
        widen_kernel,
        out_shape=[shape(x.shape, kind) for x, kind in zip(arrays, types)]
        + [shape((4, D), jnp.float32)] * 2,
        grid=(steps,),
        in_specs=specs + [pl.BlockSpec((8, D), lambda i: (0, 0))],
        out_specs=specs + pair,
        compiler_params=pltpu.CompilerParams(vmem_limit_bytes=67043328),
        name="widen",
    )(*arrays, norms)


def per_device(n_ctx, inputs, w_qkv, w_out, w_up, w_down, norm_gains, norm_biases, block_map, out_grad):
    slots = n_ctx // 2
    raw, seed_low = inputs.reshape(BLK, D), out_grad.reshape(BLK, D)
    block_entry = block_map.reshape(2)
    forward = forward_part(
        n_ctx,
        block_entry,
        norm_gains,
        norm_biases,
        raw,
        seed_low,
        w_qkv,
        w_out,
        w_up,
        w_down,
    )
    every_low, queries, keys_values, attn_low, lse, full_qkv, full_out, full_up, full_down = forward[:9]
    result, active_low, down_low, ffn_low, upward, hat1, hat2, rstd, norms = forward[9:]
    backward = backward_part(
        n_ctx,
        block_entry,
        norm_gains,
        norm_biases,
        norms,
        [raw, queries, keys_values, every_low, attn_low, lse, full_qkv],
        [full_out, full_up, full_down],
        [active_low, down_low, ffn_low, upward, hat1, hat2, rstd, seed_low],
    )
    grad_tokens, norm_total, grad_hidden = backward[4:7]
    if slots > 2:
        grad_tokens = grad_tokens + grad_hidden
    full = jnp.float32
    summed_down, summed_up, summed_out, summed_qkv, grad_input, result, gain_total, bias_total = widen(
        list(backward[:4]) + [grad_tokens, result],
        [full] * 5 + [jnp.bfloat16],
        norm_total,
    )
    return (
        result.reshape(1, 1, BLK, D),
        grad_input.reshape(1, 1, BLK, D),
        summed_qkv,
        summed_out,
        summed_up,
        summed_down,
        gain_total,
        bias_total,
    )


def solution(mesh):
    rows = P("wsh", None)
    blocks = P("grp", "wsh", "ctx", None)
    return jax.shard_map(
        functools.partial(per_device, mesh.shape["ctx"]),
        mesh=mesh,
        in_specs=(blocks, rows, rows, rows, rows, P(), P(), blocks, blocks),
        out_specs=(blocks, blocks, rows, rows, rows, rows, P(), P()),
        check_vma=False,
    )
```

```python
import functools
import math

import jax
import jax.numpy as jnp
from jax import lax
from jax.experimental import pallas as pl
from jax.experimental.pallas import tpu as pltpu
from jax.sharding import PartitionSpec as P

D = 1024
HEADS = 16
DH = 64
BLK = 512
PAIRS = HEADS // 2
QT = 256

EPS = 1e-05
ALPHA = 32.0
NEG = -1e30
LOG2E = 1.4426950408889634
C2 = ALPHA * LOG2E
MESH = pl.DeviceIdType.MESH
QSCALE = 1.0 / (ALPHA * math.sqrt(DH))


def layer_norm(values, gain_row, bias_row):
    centre = values - jnp.mean(values, axis=-1, keepdims=True)
    spread = jnp.mean(centre * centre, axis=-1, keepdims=True)
    return centre * lax.rsqrt(spread + EPS) * gain_row + bias_row


def dot_dims(left_side, right_side, left_dim, right_dim):
    return lax.dot_general(
        left_side,
        right_side,
        (((left_dim,), (right_dim,)), ((), ())),
        preferred_element_type=jnp.float32,
    )


def contract_last(left_side, right_side):
    return dot_dims(left_side, right_side, 1, 1)


def contract_rows(left_side, right_side):
    return dot_dims(left_side, right_side, 0, 0)


def standard_rows(values):
    centre = values - jnp.mean(values, axis=-1, keepdims=True)
    scale = lax.rsqrt(jnp.mean(centre * centre, axis=-1, keepdims=True) + EPS)
    return centre * scale, scale


def row_back(upstream, hat, scale, gain):
    scaled = upstream * gain
    return scale * (
        scaled
        - jnp.mean(scaled, axis=-1, keepdims=True)
        - hat * jnp.mean(scaled * hat, axis=-1, keepdims=True)
    )


def column_sum(values):
    return jnp.sum(values, axis=0, keepdims=True)


def head_lanes(head, rows):
    lane = lax.broadcasted_iota(jnp.int32, (rows, 128), 1)
    return (lane >= DH) if head else (lane < DH)


def causal_tile():
    row = lax.broadcasted_iota(jnp.int32, (QT, QT), 0)
    col = lax.broadcasted_iota(jnp.int32, (QT, QT), 1)
    return col <= row


PIECE = 128
SPAN = 512
CHAIN = 64
HOP = 2
YLAG = 3
XLAG = 2
BLAG = 2
FF_TICKS = 13
TAIL_PACE = 3
GELU_A = 0.044715
GELU_C = math.sqrt(2.0 / math.pi)
PACE = 2
LAG = 2
GROUP = 4
AHEAD = 4


def remote(src, dst, send, recv, peer):
    return pltpu.make_async_remote_copy(
        src_ref=src, dst_ref=dst, send_sem=send, recv_sem=recv, device_id=peer, device_id_type=MESH
    )


def local_wait(ref, sem):
    pltpu.make_async_copy(ref, ref, sem).wait()


def aligned(start, size):
    return pl.ds(pl.multiple_of(start, size), size)


def softmax_block(q_ref, kv_ref, acc, top_ref, sum_ref, pair, base, own, visible):
    lanes = aligned(pair * 128, 128)
    value_lanes = aligned(D + pair * 128, 128)
    causal = causal_tile()
    first = head_lanes(0, QT)
    count = BLK // QT
    q_pair = q_ref[:, lanes]
    keys = kv_ref[pl.ds(base, BLK), lanes]
    values = kv_ref[pl.ds(base, BLK), value_lanes]
    if not own:
        old_top, old_sum, old_out = top_ref[pair], sum_ref[pair], acc[:, lanes]
        hide = jnp.where(visible, 0.0, 1e30)
    results = []
    work = [(tile, head) for tile in range(count) for head in range(2)]
    parts_of = {}
    for tile, head in work:
        q_tile = q_pair[tile * QT : (tile + 1) * QT]
        q_head = jnp.where(head_lanes(head, QT), q_tile, jnp.zeros_like(q_tile))
        span = (tile + 1) * QT if own else BLK
        parts_of[tile, head] = contract_last(q_head, keys[:span])
    top_of, expo_of, total_of = {}, {}, {}
    for tile, head in work:
        part = parts_of[tile, head]
        if own:
            diag = jnp.where(causal, part[:, tile * QT :], NEG)
            part = jnp.concatenate([part[:, : tile * QT], diag], axis=1) if tile else diag
        top = jnp.max(part, axis=-1, keepdims=True) * C2
        if own:
            shift = top
        else:
            top = jnp.maximum(
                jnp.where(visible, top, NEG), old_top[tile * QT : (tile + 1) * QT, head * DH : head * DH + 1]
            )
            shift = top + hide
        expo = jnp.exp2(part * C2 - shift)
        top_of[tile, head] = jnp.broadcast_to(top, (QT, 128))
        total_of[tile, head] = jnp.broadcast_to(jnp.sum(expo, axis=-1, keepdims=True), (QT, 128))
        expo_of[tile, head] = expo.astype(jnp.bfloat16)
    out_of = {}
    for tile, head in work:
        span = (tile + 1) * QT if own else BLK
        out_of[tile, head] = dot_dims(expo_of[tile, head], values[:span], 1, 0)
    for tile in range(count):
        rows = pl.ds(tile * QT, QT)
        new_top = jnp.where(first, top_of[tile, 0], top_of[tile, 1])
        new_sum = jnp.where(first, total_of[tile, 0], total_of[tile, 1])
        new_out = jnp.where(first, out_of[tile, 0], out_of[tile, 1])
        if not own:
            here = slice(tile * QT, (tile + 1) * QT)
            keep = jnp.exp2(old_top[here] - new_top)
            new_sum = new_sum + old_sum[here] * keep
            new_out = new_out + old_out[here] * keep
        top_ref[pair, rows, :] = new_top
        sum_ref[pair, rows, :] = new_sum
        acc[rows, lanes] = new_out


def forward_kernel(n_ctx, *refs):
    slots = n_ctx // 2
    (slot_ref, gain_ref, bias_ref, x_hbm, dy_hbm, w_qkv, w_out, w_up, w_down) = refs[:9]
    (a_out, q_out, kv_out, o_out, lse_out, full_qkv, full_out, full_up, full_down) = refs[9:18]
    (y_out, g_out, dz_out, f_out, u_out, hat1_out, hat2_out, rstd_out, norm_out) = refs[18:27]
    (x_own, left, right, a_all, q_all, kv_all, weight, acc, z_acc, norm_v, tops, sums, hop) = refs[27:40]
    (sem_in, sem_load, sem_store, sem_ff, sem_out, sem_a, sem_kv, side_s, side_r, grp_s, grp_r, cs_s, cs_r, cg_s, cg_r, own_s, own_r, left_s, left_r, right_s, right_r) = refs[40:]
    grp, ctx, wsh = lax.axis_index("grp"), lax.axis_index("ctx"), lax.axis_index("wsh")
    side, core = wsh // 2, wsh % 2
    core_peer = (grp, ctx, side * 2 + 1 - core)
    side_peer = (grp, ctx, (1 - side) * 2 + core)
    grp_peer = (1 - grp, ctx, wsh)
    next_ctx = (grp, lax.rem(ctx + 1, n_ctx), wsh)
    last_ctx = (grp, lax.rem(ctx + n_ctx - 1, n_ctx), wsh)

    load = pltpu.make_async_copy(x_hbm, x_own, sem_in.at[0])
    load.start()
    barrier = pltpu.get_barrier_semaphore()
    for peer in (core_peer, side_peer, grp_peer, next_ctx, last_ctx):
        pl.semaphore_signal(barrier, inc=1, device_id=peer, device_id_type=MESH)
    pl.semaphore_wait(barrier, 5)

    shards = (w_qkv, w_out, w_up, w_down)
    fulls = (weight, full_out, full_up, full_down)
    ranges, start = [], 0
    for shard in shards:
        across = shard.shape[1] // SPAN
        ranges.append((start, start + across * (shard.shape[0] // (2 * PIECE)), across))
        start = ranges[-1][1]
    pieces = start

    def by_range(index, act):
        for place, (low, high, across) in enumerate(ranges):

            @pl.when((index >= low) & (index < high))
            def _(place=place, low=low, across=across):
                act(place, (index - low) // across, aligned(((index - low) % across) * SPAN, SPAN))

    def rows_of(place, owner, half, group):
        shard_rows = shards[place].shape[0]
        return aligned(owner * shard_rows + half * (shard_rows // 2) + group * PIECE, PIECE)

    sides_owner = (1 - side) * 2 + core

    def send_piece(index, carry):
        def act(place, group, cols):
            remote(
                shards[place].at[rows_of(place, 0, grp, group), cols],
                fulls[place].at[rows_of(place, wsh, grp, group), cols],
                side_s.at[index],
                side_r.at[index],
                side_peer,
            ).start()

        by_range(index, act)
        return carry

    def own_copies():
        copies = []
        across = shards[0].shape[1] // SPAN
        for place in range(4):
            shard_rows = shards[place].shape[0]
            mine = aligned(wsh * shard_rows, shard_rows)
            steps = range(across) if place == 0 else [None]
            for step in steps:
                cols = slice(None) if step is None else pl.ds(step * SPAN, SPAN)
                number = len(copies)
                copies.append(
                    remote(
                        shards[place].at[:, cols],
                        fulls[place].at[mine, cols],
                        own_s.at[number],
                        own_r.at[number],
                        core_peer,
                    )
                )
        return copies

    for index in range(AHEAD):
        send_piece(index, 0)
    for copy in own_copies():
        copy.start()
    own_rows = aligned(wsh * w_qkv.shape[0], w_qkv.shape[0])
    own_weight = pltpu.make_async_copy(w_qkv, weight.at[own_rows, :], sem_in.at[1])
    own_weight.start()
    load.wait()

    bounces, start = [], 0
    for shard in shards[1:]:
        across = shard.shape[1] // SPAN
        bounces.append((start, start + across * (shard.shape[0] // (2 * PIECE)), across))
        start = bounces[-1][1]
    moves = start

    def bounce(index, loading):
        slot = lax.rem(index, 3)
        for place, (low, high, across) in enumerate(bounces):

            @pl.when((index >= low) & (index < high))
            def _(place=place + 1, low=low, across=across):
                group = (index - low) // across
                cols = aligned(((index - low) % across) * SPAN, SPAN)
                if loading:
                    here = shards[place].at[aligned(group * 2 * PIECE, 2 * PIECE), cols]
                    pltpu.make_async_copy(here, hop.at[slot], sem_load.at[slot]).start()
                else:
                    rows = aligned(wsh * shards[place].shape[0] + group * 2 * PIECE, 2 * PIECE)
                    local_wait(hop.at[slot], sem_load.at[slot])
                    pltpu.make_async_copy(
                        hop.at[slot], fulls[place].at[rows, cols], sem_store.at[slot]
                    ).start()

    own_slot = slot_ref[1] // BLK
    own_tag = jnp.where(slot_ref[0] == 0, own_slot, n_ctx)
    chain_chunks = slots * (BLK // CHAIN)

    def chain_step(stream, send, recv, number, is_first, is_last, target):
        slot = number // (BLK // CHAIN)
        spot = aligned((number % (BLK // CHAIN)) * CHAIN, CHAIN)
        mine = jnp.where(own_tag == slot, x_own[spot, :], jnp.zeros((CHAIN, D), jnp.bfloat16))
        here = stream.at[slot, spot]

        @pl.when(is_first)
        def _():
            stream[slot, spot, :] = mine

        @pl.when(jnp.logical_not(is_first))
        def _():
            remote(here, here, send.at[number], recv.at[number], target).wait_recv()
            stream[slot, spot, :] = stream[slot, spot, :] + mine

        @pl.when(jnp.logical_not(is_last))
        def _():
            remote(here, here, send.at[number], recv.at[number], target).start()

    def tick(step):
        @pl.when((step >= 1) & (step <= moves))
        def _():
            bounce(step - 1, False)

        @pl.when((step >= 3) & (step < moves))
        def _():
            local_wait(hop.at[lax.rem(step, 3)], sem_store.at[lax.rem(step, 3)])

        @pl.when(step < moves)
        def _():
            bounce(step, True)

        @pl.when(step + AHEAD < pieces)
        def _():
            send_piece(step + AHEAD, 0)

        number = step - HOP * ctx

        @pl.when((number >= 0) & (number < chain_chunks))
        def _():
            chain_step(left, left_s, left_r, number, ctx == 0, ctx == n_ctx - 1, next_ctx)

        back = step - HOP * (n_ctx - 1 - ctx)

        @pl.when((back >= 0) & (back < chain_chunks))
        def _():
            chain_step(right, right_s, right_r, back, ctx == n_ctx - 1, ctx == 0, last_ctx)

        @pl.when(step < pieces)
        def _():
            def act(place, group, cols):
                here = fulls[place].at[rows_of(place, sides_owner, grp, group), cols]
                remote(here, here, side_s.at[step], side_r.at[step], side_peer).wait_recv()
                remote(here, here, grp_s.at[step], grp_r.at[step], grp_peer).start()
                remote(here, here, cs_s.at[step], cs_r.at[step], core_peer).start()

            by_range(step, act)

        late = step - LAG

        @pl.when((late >= 0) & (late < pieces))
        def _():
            def act(place, group, cols):
                here = fulls[place].at[rows_of(place, sides_owner, 1 - grp, group), cols]
                remote(here, here, grp_s.at[late], grp_r.at[late], grp_peer).wait_recv()
                remote(here, here, cg_s.at[late], cg_r.at[late], core_peer).start()

            by_range(late, act)

    def ticks(first, last):
        lax.fori_loop(first, last, lambda index, carry: (tick(index), carry)[1], 0)

    def normalise(source, dest):
        gain, bias = gain_ref[0:1, :], bias_ref[0:1, :]

        def body(index, carry):
            rows = aligned(index * 128, 128)
            values = source(rows).astype(jnp.float32)
            a_all[aligned(dest + index * 128, 128), :] = layer_norm(values, gain, bias).astype(
                jnp.bfloat16
            )
            return carry

        lax.fori_loop(0, BLK // 128, body, 0)

    def piece_ready(index):
        here = fulls[0].at[pl.ds(0, PIECE), pl.ds(0, SPAN)]
        remote(here, here, cs_s.at[index], cs_r.at[index], core_peer).wait_recv()
        remote(here, here, cg_s.at[index], cg_r.at[index], core_peer).wait_recv()
        whole = fulls[0].at[pl.ds(0, 2 * PIECE), pl.ds(0, SPAN)]
        remote(whole, whole, own_s.at[index], own_r.at[index], core_peer).wait_recv()

    tick(0)
    normalise(lambda rows: x_own[rows, :], 0)
    ticks(1, LAG + 1)
    own_weight.wait()

    def project_q(index, carry):
        tick(index + LAG + 1)
        piece_ready(index)
        cols = aligned(index * SPAN, SPAN)
        q_all[:, cols] = (
            jnp.dot(a_all[pl.ds(0, BLK), :], weight[:, cols], preferred_element_type=jnp.float32) * QSCALE
        ).astype(jnp.bfloat16)
        return carry

    lax.fori_loop(0, D // SPAN, project_q, 0)
    head_ticks = LAG + 1 + D // SPAN

    def project_kv(index, base):
        cols = aligned(index * SPAN, SPAN)
        rows = aligned(base, BLK)
        kv_all[rows, cols] = jnp.dot(
            a_all[rows, :], weight[:, aligned(D + index * SPAN, SPAN)], preferred_element_type=jnp.float32
        ).astype(jnp.bfloat16)

    def own_kv(index, carry):
        tick(index + head_ticks)
        piece_ready(index + D // SPAN)
        project_kv(index, 0)
        return carry

    lax.fori_loop(0, 2 * D // SPAN, own_kv, 0)
    own_ticks = head_ticks + 2 * D // SPAN

    def send_block(index):
        rows = aligned(index * BLK, BLK)
        pltpu.make_async_copy(a_all.at[rows, :], a_out.at[rows, :], sem_a.at[index]).start()
        pltpu.make_async_copy(kv_all.at[rows, :], kv_out.at[rows, :], sem_kv.at[index]).start()

    outputs = [
        pltpu.make_async_copy(weight, full_qkv, sem_out.at[0]),
        pltpu.make_async_copy(q_all, q_out, sem_out.at[1]),
    ]
    for copy in outputs:
        copy.start()

    send_block(0)

    def own_attention(group, carry):
        ticks(own_ticks + 2 * group, own_ticks + 2 * group + 2)
        for member in range(GROUP):
            softmax_block(q_all, kv_all, acc, tops, sums, group * GROUP + member, 0, True, None)
        return carry

    groups = PAIRS // GROUP
    lax.fori_loop(0, groups, own_attention, 0)
    used = own_ticks + 2 * groups
    per_slot = 2 * D // SPAN + 2 * groups

    need = BLK // CHAIN + HOP * (n_ctx - 1)
    early = max(0, need - used)
    if early:
        lax.fori_loop(0, early, lambda index, carry: (tick(used + index), carry)[1], 0)

    def each_slot(slot, carry):
        base = pl.multiple_of((slot + 1) * BLK, BLK)
        visible = slot < own_slot
        begin = early + used + slot * per_slot

        def total(rows):
            joined = left[slot, rows, :] + right[slot, rows, :]
            return jnp.where(own_tag == slot, x_own[rows, :], joined)

        normalise(total, base)

        def slot_kv(index, inner):
            tick(begin + index)
            project_kv(index, base)
            return inner

        lax.fori_loop(0, 2 * D // SPAN, slot_kv, 0)

        send_block(slot + 1)

        def slot_attention(group, inner):
            start = begin + 2 * D // SPAN + 2 * group
            ticks(start, start + 2)
            for member in range(GROUP):
                softmax_block(
                    q_all, kv_all, acc, tops, sums, group * GROUP + member, base, False, visible
                )
            return inner

        lax.fori_loop(0, groups, slot_attention, 0)
        return carry

    lax.fori_loop(0, slots, each_slot, 0)
    done_ticks = early + used + slots * per_slot

    def finish(pair, carry):
        lanes = aligned(pair * 128, 128)
        x_own[:, lanes] = (acc[:, lanes] / sums[pair]).astype(jnp.bfloat16)
        tops[pair] = tops[pair] + jnp.log2(sums[pair])
        return carry

    lax.fori_loop(0, PAIRS, finish, 0)
    outputs += [
        pltpu.make_async_copy(x_own, o_out, sem_out.at[2]),
        pltpu.make_async_copy(tops, lse_out, sem_out.at[3]),
    ]
    for copy in outputs[2:]:
        copy.start()
    all_ticks = max(pieces + LAG, chain_chunks + HOP * (n_ctx - 1))
    if all_ticks > done_ticks:
        lax.fori_loop(done_ticks, all_ticks, lambda index, carry: (tick(index), carry)[1], 0)

    def drain(index, carry):
        here = fulls[0].at[pl.ds(0, PIECE), pl.ds(0, SPAN)]

        @pl.when(index >= ranges[0][1])
        def _():
            remote(here, here, cs_s.at[index], cs_r.at[index], core_peer).wait_recv()
            remote(here, here, cg_s.at[index], cg_r.at[index], core_peer).wait_recv()

        remote(here, here, side_s.at[index], side_r.at[index], side_peer).wait_send()
        remote(here, here, grp_s.at[index], grp_r.at[index], grp_peer).wait_send()
        remote(here, here, cs_s.at[index], cs_r.at[index], core_peer).wait_send()
        remote(here, here, cg_s.at[index], cg_r.at[index], core_peer).wait_send()
        return carry

    lax.fori_loop(0, pieces, drain, 0)
    copies = own_copies()
    for number, copy in enumerate(copies):
        copy.wait_send()
        if number >= len(copies) - 3:
            copy.wait_recv()
    for index in range(moves - 3, moves):
        local_wait(hop.at[index % 3], sem_store.at[index % 3])

    def drain_chain(index, carry):
        here = left.at[0, pl.ds(0, CHAIN)]

        @pl.when(ctx < n_ctx - 1)
        def _():
            remote(here, here, left_s.at[index], left_r.at[index], next_ctx).wait_send()

        @pl.when(ctx > 0)
        def _():
            remote(here, here, right_s.at[index], right_r.at[index], last_ctx).wait_send()

        return carry

    lax.fori_loop(0, chain_chunks, drain_chain, 0)
    for copy in outputs[:2]:
        copy.wait()
    shallow_tiles = full_up.shape[1] // SPAN

    def tile_loads(tile, parity):
        cols = aligned(tile * SPAN, SPAN)
        return (
            pltpu.make_async_copy(
                full_up.at[:, cols], weight.at[:, aligned(D + parity * SPAN, SPAN)], sem_ff.at[0, parity]
            ),
            pltpu.make_async_copy(full_down.at[cols, :], left.at[parity], sem_ff.at[1, parity]),
        )

    def tile_stores(tile, parity):
        cols = aligned(tile * SPAN, SPAN)
        return [
            pltpu.make_async_copy(
                kv_all.at[pl.ds(0, BLK), aligned(base + parity * SPAN, SPAN)],
                dest.at[:, cols],
                sem_ff.at[2 + place, parity],
            )
            for place, (base, dest) in enumerate(((0, u_out), (D, g_out)))
        ]

    out_load = pltpu.make_async_copy(full_out, weight.at[:, pl.ds(0, D)], sem_in.at[0])
    x_load = pltpu.make_async_copy(x_hbm, right.at[1], sem_in.at[1])
    for copy in (out_load, x_load) + tile_loads(0, 0):
        copy.start()

    def drain_blocks(index, carry):
        rows = aligned(index * BLK, BLK)
        local_wait(a_all.at[rows, :], sem_a.at[index])
        local_wait(kv_all.at[rows, :], sem_kv.at[index])
        return carry

    lax.fori_loop(0, slots + 1, drain_blocks, 0)
    out_load.wait()
    for half_cols in range(2):
        cols = pl.ds(half_cols * SPAN, SPAN)
        acc[:, cols] = jnp.dot(x_own[...], weight[:, cols], preferred_element_type=jnp.float32)
    x_load.wait()
    for copy in outputs[2:]:
        copy.wait()
    dy_load = pltpu.make_async_copy(dy_hbm, x_own, sem_in.at[0])
    dy_load.start()

    def inner_rows(step, carry):
        rows = aligned(step * CHAIN, CHAIN)
        hat, scale = standard_rows(acc[rows, :])
        a_all[rows, :] = hat.astype(jnp.bfloat16)
        sums[0, rows, :] = jnp.broadcast_to(scale, (CHAIN, 128))
        hidden = right[1, rows, :].astype(jnp.float32) + hat * gain_ref[1:2, :] + bias_ref[1:2, :]
        acc[rows, :] = hidden
        hat, scale = standard_rows(hidden)
        a_all[aligned(BLK + step * CHAIN, CHAIN), :] = hat.astype(jnp.bfloat16)
        sums[1, rows, :] = jnp.broadcast_to(scale, (CHAIN, 128))
        q_all[rows, :] = (hat * gain_ref[2:3, :] + bias_ref[2:3, :]).astype(jnp.bfloat16)
        return carry

    lax.fori_loop(0, BLK // CHAIN, inner_rows, 0)
    saves = [
        pltpu.make_async_copy(a_all.at[pl.ds(0, BLK), :], hat1_out, sem_out.at[0]),
        pltpu.make_async_copy(a_all.at[pl.ds(BLK, BLK), :], hat2_out, sem_out.at[1]),
        pltpu.make_async_copy(sums.at[pl.ds(0, 2)], rstd_out, sem_out.at[2]),
        pltpu.make_async_copy(q_all, f_out, sem_out.at[3]),
    ]
    for copy in saves:
        copy.start()

    def ff_tile(tile, carry):
        parity = tile % 2
        for copy in tile_loads(tile, parity):
            copy.wait()

        @pl.when(tile + 1 < shallow_tiles)
        def _():
            for copy in tile_loads(tile + 1, 1 - parity):
                copy.start()

        @pl.when(tile >= 2)
        def _():
            for copy in tile_stores(tile - 2, parity):
                copy.wait()

        upward = jnp.dot(
            q_all[...], weight[:, aligned(D + parity * SPAN, SPAN)], preferred_element_type=jnp.float32
        )
        kv_all[pl.ds(0, BLK), aligned(parity * SPAN, SPAN)] = upward.astype(jnp.bfloat16)
        active = (
            0.5 * upward * (1.0 + jnp.tanh(GELU_C * upward * (1.0 + GELU_A * upward * upward)))
        ).astype(jnp.bfloat16)
        kv_all[pl.ds(0, BLK), aligned(D + parity * SPAN, SPAN)] = active
        for copy in tile_stores(tile, parity):
            copy.start()
        fresh = jnp.dot(active, left[parity], preferred_element_type=jnp.float32)

        @pl.when(tile == 0)
        def _():
            z_acc[...] = fresh

        @pl.when(tile > 0)
        def _():
            z_acc[...] = z_acc[...] + fresh

        return carry

    lax.fori_loop(0, shallow_tiles, ff_tile, 0)
    dy_load.wait()

    def outer_rows(step, carry):
        gain_sum, bias_sum = carry
        rows = aligned(step * CHAIN, CHAIN)
        hat, scale = standard_rows(z_acc[rows, :])
        right[0, rows, :] = (acc[rows, :] + hat * gain_ref[3:4, :] + bias_ref[3:4, :]).astype(jnp.bfloat16)
        upstream = x_own[rows, :].astype(jnp.float32)
        a_all[aligned(2 * BLK + step * CHAIN, CHAIN), :] = row_back(
            upstream, hat, scale, gain_ref[3:4, :]
        ).astype(jnp.bfloat16)
        return gain_sum + column_sum(upstream * hat), bias_sum + column_sum(upstream)

    zero = jnp.zeros((1, D), jnp.float32)
    gain_sum, bias_sum = lax.fori_loop(0, BLK // CHAIN, outer_rows, (zero, zero))
    row = lax.broadcasted_iota(jnp.int32, (8, D), 0)
    norm_v[...] = jnp.where(row == 3, gain_sum, 0.0) + jnp.where(row == 7, bias_sum, 0.0)
    ends = [
        pltpu.make_async_copy(right.at[0], y_out, sem_in.at[0]),
        pltpu.make_async_copy(a_all.at[pl.ds(2 * BLK, BLK), :], dz_out, sem_in.at[1]),
        pltpu.make_async_copy(norm_v, norm_out, sem_in.at[2]),
    ]
    for copy in ends:
        copy.start()
    for tile in range(shallow_tiles - 2, shallow_tiles):
        for copy in tile_stores(tile, tile % 2):
            copy.wait()
    for copy in saves + ends:
        copy.wait()


def forward_part(n_ctx, tags, gains, biases, raw, dy, w_qkv, w_out, w_up, w_down):
    slots = n_ctx // 2
    every = (slots + 1) * BLK
    low, full = jnp.bfloat16, jnp.float32
    dma = pltpu.SemaphoreType.DMA
    hbm = pl.BlockSpec(memory_space=pl.ANY)
    vmem = pl.BlockSpec(memory_space=pltpu.VMEM)
    shards = (w_qkv, w_out, w_up, w_down)
    pieces = sum(w.shape[0] * w.shape[1] // (2 * PIECE * SPAN) for w in shards)
    own = w_qkv.shape[1] // SPAN + 3
    chain = slots * (BLK // CHAIN)
    shape = jax.ShapeDtypeStruct
    return pl.pallas_call(
        functools.partial(forward_kernel, n_ctx),
        out_shape=[
            shape((every, D), low),
            shape((BLK, D), low),
            shape((every, 2 * D), low),
            shape((BLK, D), low),
            shape((PAIRS, BLK, 128), full),
        ]
        + [shape((4 * w.shape[0], w.shape[1]), low) for w in shards]
        + [
            shape((BLK, D), low),
            shape((BLK, w_up.shape[1]), low),
            shape((BLK, D), low),
            shape((BLK, D), low),
            shape((BLK, w_up.shape[1]), low),
            shape((BLK, D), low),
            shape((BLK, D), low),
            shape((2, BLK, 128), full),
            shape((8, D), full),
        ],
        in_specs=[pl.BlockSpec(memory_space=pltpu.SMEM), vmem, vmem] + [hbm] * 6,
        out_specs=[hbm] * 18,
        scratch_shapes=[
            pltpu.VMEM((BLK, D), low),
            pltpu.VMEM((slots, BLK, D), low),
            pltpu.VMEM((slots, BLK, D), low),
            pltpu.VMEM((every, D), low),
            pltpu.VMEM((BLK, D), low),
            pltpu.VMEM((every, 2 * D), low),
            pltpu.VMEM((D, 3 * D), low),
            pltpu.VMEM((BLK, D), full),
            pltpu.VMEM((BLK, D), full),
            pltpu.VMEM((8, D), full),
            pltpu.VMEM((PAIRS, BLK, 128), full),
            pltpu.VMEM((PAIRS, BLK, 128), full),
            pltpu.VMEM((3, 2 * PIECE, SPAN), low),
            dma((3,)),
            dma((3,)),
            dma((3,)),
            dma((4, 2)),
            dma((4,)),
            dma((slots + 1,)),
            dma((slots + 1,)),
        ]
        + [dma((pieces,))] * 8
        + [dma((own,))] * 2
        + [dma((chain,))] * 4,
        compiler_params=pltpu.CompilerParams(
            collective_id=1, has_side_effects=True, vmem_limit_bytes=67043328
        ),
        cost_estimate=pl.CostEstimate(flops=20 << 30, bytes_accessed=64 << 20, transcendentals=1 << 24),
        name="gather_attend",
    )(tags, gains, biases, raw, dy, *shards)


TILE = 256
PAIRED = 2


def grad_block(q_ref, do_ref, o_ref, lse_ref, kv_ref, dq_acc, turned, pair, own, visible):
    lanes = aligned(pair * 128, 128)
    value_lanes = aligned(D + pair * 128, 128)
    size = QT if own else BLK
    count = BLK // size
    q_pair, do_pair, lse_pair = q_ref[:, lanes], do_ref[:, lanes], lse_ref[pair]
    prod = do_pair.astype(jnp.float32) * o_ref[:, lanes].astype(jnp.float32)
    keys, values = kv_ref[:, lanes], kv_ref[:, value_lanes]
    q_turned, do_turned = q_pair.T, do_pair.T
    old_dq = dq_acc[:, lanes]
    causal = causal_tile()
    hide = 0.0 if own else jnp.where(visible, 0.0, 1e30)
    lanes_of = [head_lanes(head, size) for head in range(2)]
    work = [(tile, head) for tile in range(count) for head in range(2)]
    score, dprob, dlogit, prob_low = {}, {}, {}, {}
    for tile, head in work:
        rows = slice(tile * size, (tile + 1) * size)
        span = (tile + 1) * size if own else BLK
        zero = jnp.zeros((size, 128), jnp.bfloat16)
        score[tile, head] = contract_last(jnp.where(lanes_of[head], q_pair[rows], zero), keys[:span])
        dprob[tile, head] = contract_last(jnp.where(lanes_of[head], do_pair[rows], zero), values[:span])
    for tile, head in work:
        rows = slice(tile * size, (tile + 1) * size)
        delta = jnp.sum(jnp.where(lanes_of[head], prod[rows], 0.0), axis=-1, keepdims=True)
        shift = lse_pair[rows, head * DH : head * DH + 1] + hide
        prob = jnp.exp2(score[tile, head] * C2 - shift)
        if own:
            diag = jnp.where(causal, prob[:, tile * size :], 0.0)
            prob = jnp.concatenate([prob[:, : tile * size], diag], axis=1) if tile else diag
        dlogit[tile, head] = (prob * (dprob[tile, head] - delta)).astype(jnp.bfloat16)
        prob_low[tile, head] = prob.astype(jnp.bfloat16)
    for tile in range(count):
        rows = slice(tile * size, (tile + 1) * size)
        span = (tile + 1) * size if own else BLK
        parts = [dot_dims(dlogit[tile, head], keys[:span], 1, 0) for head in range(2)]
        dq_acc[pl.ds(tile * size, size), lanes] = old_dq[rows] + jnp.where(lanes_of[0], parts[0], parts[1])
    for head in range(2):
        for offset, left_side, right_side, scale in (
            (0, q_turned, dlogit, ALPHA),
            (D, do_turned, prob_low, 1.0),
        ):
            spot = aligned(offset + pair * 128 + head * DH, DH)
            left_head = left_side[head * DH : (head + 1) * DH]
            terms = [
                dot_dims(left_head[:, tile * size : (tile + 1) * size], right_side[tile, head], 1, 0)
                for tile in range(count)
            ]
            for tile in range(count):
                cols = slice(tile * size, (tile + 1) * size)
                total = functools.reduce(
                    jnp.add, [terms[other][:, cols] for other in range(tile, count)]
                ) if own else terms[0]
                turned[spot, cols if own else slice(None)] = (total * scale).astype(jnp.bfloat16)


def backward_kernel(n_ctx, widths, *refs):
    slots = n_ctx // 2
    levels = n_ctx.bit_length() - 1
    depth = 16 if n_ctx == 4 else 10
    shallow = slots <= 2
    (slot_ref, gain_ref, bias_ref, norm_ref, x_hbm, q_hbm, kv_hbm, a_hbm, o_hbm, lse_hbm, w_hbm) = refs[:11]
    (w_out, w_up, w_down, g_hbm, dz_hbm, f_hbm, u_hbm, hat1_hbm, hat2_hbm, rstd_hbm, dy_hbm) = refs[11:22]
    outs = refs[22:26]
    grad_out, norm_out, dh_hbm, du_hbm, datt_hbm = refs[26:31]
    scratch = list(refs[31:])
    own_slot = slot_ref[1] // BLK

    def take(count):
        taken = scratch[:count]
        del scratch[:count]
        return taken

    q_v, o_v, do_v, lse_v, weight, kv_b, a_b, dq_acc, turned, gkv, term, own_part, left, right, norm_v, norm_in, gain_sum, bias_sum = take(18)
    r1, r2, r3, fin, made = take(5)
    lhs, rhs = take(2)
    zbufs = take(levels)
    sem_in, sem_blk, sem_rhs, sem_lhs, sem_ff, sem_out, sem_res = take(7)
    send1, recv1, send2, recv2, send3, recv3, send6, recv6 = take(8)
    rs_send, rs_recv, ag_send, ag_recv = take(levels), take(levels), take(levels), take(levels)
    left_s, left_r, right_s, right_r, norm_s, norm_r = take(6)
    grp, ctx, wsh = lax.axis_index("grp"), lax.axis_index("ctx"), lax.axis_index("wsh")
    side, core = wsh // 2, wsh % 2
    core_peer = (grp, ctx, side * 2 + 1 - core)
    side_peer = (grp, ctx, (1 - side) * 2 + core)
    grp_peer = (1 - grp, ctx, wsh)
    next_ctx = (grp, lax.rem(ctx + 1, n_ctx), wsh)
    last_ctx = (grp, lax.rem(ctx + n_ctx - 1, n_ctx), wsh)
    bits = [(ctx // (1 << level)) % 2 for level in range(levels)]
    level_peers = [(grp, ctx + (1 - 2 * bits[level]) * (1 << level), wsh) for level in range(levels)]

    def block_copies(index):
        rows = aligned(lax.rem(index, slots + 1) * BLK, BLK)
        slot = lax.rem(index, kv_b.shape[0])
        a_slot = index - 1 if shallow else 0
        return (
            pltpu.make_async_copy(kv_hbm.at[rows, :], kv_b.at[slot], sem_blk.at[0, slot]),
            pltpu.make_async_copy(a_hbm.at[rows, :], a_b.at[a_slot], sem_blk.at[1, slot]),
        )

    barrier = pltpu.get_barrier_semaphore()
    peers = [core_peer, side_peer, grp_peer, next_ctx, last_ctx] + level_peers
    for peer in peers:
        pl.semaphore_signal(barrier, inc=1, device_id=peer, device_id_type=MESH)

    half = TILE // 2
    ranges, first = [], 0
    for rows, cols in widths:
        across = cols // TILE
        ranges.append((first, first + (rows // TILE) * across, across))
        first = ranges[-1][1]
    chunks = first

    def by_range(index, act):
        for place, (low, high, across) in enumerate(ranges):

            @pl.when((index >= low) & (index < high))
            def _(place=place, low=low, across=across):
                number = index - low
                act(place, (aligned((number // across) * TILE, TILE), aligned((number % across) * TILE, TILE)))

    def region(level, flip):
        row, rows, col, cols = 0, half, 0, TILE
        for place in range(level):
            bit = 1 - bits[place] if (flip and place == level - 1) else bits[place]
            if rows > 16:
                rows = rows // 2
                row = row + bit * rows
            else:
                cols = cols // 2
                col = col + bit * cols
        return row, rows, col, cols

    def spot(level, flip=False, base=0):
        row, rows, col, cols = region(level, flip)
        return aligned(base + row, rows), aligned(col, cols)

    last_low = ranges[-1][0]
    dq_low = o_v
    set_of = [(0, number) for number in range(widths[0][0] // TILE)] + [(1, 0), (2, 0)]
    set_first = [number * ranges[0][2] for number in range(widths[0][0] // TILE)]
    set_first += [ranges[1][0], ranges[2][0]]
    left_of, right_of = (g_hbm, f_hbm, o_hbm), (dz_hbm, du_hbm, datt_hbm)

    def set_copies(number):
        place, group = set_of[number]
        stride = left_of[place].shape[1] // 4
        return [
            pltpu.make_async_copy(
                left_of[place].at[:, pl.ds(owner * stride + group * TILE, TILE)],
                lhs.at[number % 2, owner],
                sem_lhs.at[number % 2, owner],
            )
            for owner in range(4)
        ]

    def step_fetch(index):
        near = lax.rem(index, 4)

        def act(place, span):
            if place < 3:
                pltpu.make_async_copy(
                    right_of[place].at[:, span[1]], rhs.at[near], sem_rhs.at[near]
                ).start()

        by_range(index, act)

    def step_make(index, kinds):
        slot = lax.rem(index, depth)
        near = lax.rem(index, 4)

        def low_piece():
            local_wait(rhs.at[near], sem_rhs.at[near])
            parity = jnp.int32(0)
            for number, low in enumerate(set_first):
                parity = jnp.where(index >= low, number % 2, parity)

                @pl.when(index == low)
                def _(number=number):
                    for copy in set_copies(number):
                        copy.wait()
                    if number + 1 < len(set_first):
                        for copy in set_copies(number + 1):
                            copy.start()

            right_side = rhs[near]
            for owner in range(4):
                made[near, owner // 2, owner % 2] = dot_dims(
                    lhs[parity, owner], right_side, 0, 0
                ).astype(jnp.bfloat16)

        def high_piece():
            number = index - last_low
            if not shallow:
                made[near] = term[:, :, :, aligned(number * TILE, TILE)]
                return

            @pl.when(number < D // TILE)
            def _():
                right_side = dq_low[:, aligned(number * TILE, TILE)]
                for owner in range(4):
                    made[near, owner // 2, owner % 2] = dot_dims(
                        a_b[slots, :, pl.ds(owner * TILE, TILE)], right_side, 0, 0
                    ).astype(jnp.bfloat16)

            @pl.when(number >= D // TILE)
            def _():
                cols = aligned((number - D // TILE) * TILE, TILE)
                for owner in range(4):
                    total = functools.reduce(
                        jnp.add,
                        [
                            dot_dims(a_b[block, :, pl.ds(owner * TILE, TILE)], turned[block, cols, :], 0, 1)
                            for block in range(slots + 1)
                        ],
                    )
                    made[near, owner // 2, owner % 2] = total.astype(jnp.bfloat16)

        if kinds == "low":
            low_piece()
        elif kinds == "high":
            high_piece()
        else:
            pl.when(index < last_low)(low_piece)
            pl.when(index >= last_low)(high_piece)
        remote(
            made.at[near, :, 1 - core], r1.at[slot], send1.at[slot], recv1.at[slot], core_peer
        ).start()

    def finished(move):
        move.wait_send()
        move.wait_recv()

    def step_core(index):
        slot, near = lax.rem(index, depth), lax.rem(index, 4)
        finished(remote(r1.at[slot], r1.at[slot], send1.at[slot], recv1.at[slot], core_peer))
        r1[slot] = r1[slot] + made[near, :, core]
        remote(r1.at[slot, 1 - side], r2.at[slot], send2.at[slot], recv2.at[slot], side_peer).start()

    keep_half = aligned(grp * half, half)
    give_half = aligned((1 - grp) * half, half)

    def step_side(index):
        slot = lax.rem(index, depth)
        finished(remote(r1.at[slot, 1 - side], r2.at[slot], send2.at[slot], recv2.at[slot], side_peer))
        r2[slot] = r2[slot] + r1[slot, side]
        remote(r2.at[slot, give_half], r3.at[slot], send3.at[slot], recv3.at[slot], grp_peer).start()

    fold = n_ctx == 4
    if fold:
        outer = bits[0] == bits[1]
        inner = bits[0] != bits[1]
        mate, middle = level_peers[0], (grp, 3 - ctx, wsh)
        quarter = half // 2
        mine, other = aligned(bits[1] * quarter, quarter), aligned((1 - bits[1]) * quarter, quarter)
        fin_mine = aligned(grp * half + bits[1] * quarter, quarter)
        fin_other = aligned(grp * half + (1 - bits[1]) * quarter, quarter)

        def up_copy(slot):
            return remote(r3.at[slot], zbufs[0].at[slot], rs_send[0].at[slot], rs_recv[0].at[slot], mate)

        def cross_copy(slot):
            return remote(
                r3.at[slot, other], zbufs[1].at[slot], rs_send[1].at[slot], rs_recv[1].at[slot], middle
            )

        def share_copy(slot, rows):
            here = fin.at[slot, rows]
            return remote(here, here, ag_send[1].at[slot], ag_recv[1].at[slot], middle)

        def down_copy(slot):
            here = fin.at[slot, keep_half]
            return remote(here, here, ag_send[0].at[slot], ag_recv[0].at[slot], mate)

        def step_up(index):
            slot = lax.rem(index, depth)

            @pl.when(outer)
            def _():
                up_copy(slot).wait_send()

            @pl.when(inner)
            def _():
                up_copy(slot).wait_recv()
                r3[slot] = r3[slot] + zbufs[0][slot]
                cross_copy(slot).start()

        def step_cross(index):
            slot = lax.rem(index, depth)

            @pl.when(inner)
            def _():
                finished(cross_copy(slot))
                fin[slot, fin_mine] = r3[slot, mine] + zbufs[1][slot]
                share_copy(slot, fin_mine).start()

        def step_share(index):
            slot = lax.rem(index, depth)

            @pl.when(inner)
            def _():
                finished(share_copy(slot, fin_other))
                down_copy(slot).start()

        def step_down(index):
            slot = lax.rem(index, depth)

            @pl.when(inner)
            def _():
                down_copy(slot).wait_send()

            @pl.when(outer)
            def _():
                down_copy(slot).wait_recv()

            back_copy(slot, keep_half).start()

    def rs_copy(level, slot):
        rows, cols = spot(level + 1, True)
        return remote(
            r3.at[slot, rows, cols], zbufs[level].at[slot], rs_send[level].at[slot], rs_recv[level].at[slot], level_peers[level]
        )

    def ag_copy(level, slot, flip=False):
        rows, cols = spot(level + 1, flip, grp * half)
        here = fin.at[slot, rows, cols]
        return remote(here, here, ag_send[level].at[slot], ag_recv[level].at[slot], level_peers[level])

    def back_copy(slot, rows):
        here = fin.at[slot, rows]
        return remote(here, here, send6.at[slot], recv6.at[slot], grp_peer)

    def step_grp(index):
        slot = lax.rem(index, depth)
        finished(remote(r2.at[slot, give_half], r3.at[slot], send3.at[slot], recv3.at[slot], grp_peer))
        r3[slot] = r3[slot] + r2[slot, keep_half]
        if fold:

            @pl.when(outer)
            def _():
                up_copy(slot).start()
        else:
            rs_copy(0, slot).start()

    def step_scatter(level):
        def act(index):
            slot = lax.rem(index, depth)
            finished(rs_copy(level, slot))
            rows, cols = spot(level + 1)
            total = r3[slot, rows, cols] + zbufs[level][slot]
            if level + 1 < levels:
                r3[slot, rows, cols] = total
                rs_copy(level + 1, slot).start()
            else:
                rows, cols = spot(level + 1, False, grp * half)
                fin[slot, rows, cols] = total
                ag_copy(level, slot).start()

        return act

    def step_gather(level):
        def act(index):
            slot = lax.rem(index, depth)
            finished(ag_copy(level, slot, True))
            if level:
                ag_copy(level - 1, slot).start()
            else:
                back_copy(slot, keep_half).start()

        return act

    def out_wait(index):
        slot = lax.rem(index, depth)
        local_wait(fin.at[slot], sem_out.at[slot])

    def step_out(index):
        slot = lax.rem(index, depth)
        finished(back_copy(slot, give_half))

        def act(place, span):
            pltpu.make_async_copy(fin.at[slot], outs[place].at[span[0], span[1]], sem_out.at[slot]).start()

        by_range(index, act)

    z_lag = 2 if fold else 1
    order = [(YLAG, step_side), (XLAG, step_grp)]
    if fold:
        order += [(z_lag, act) for act in (step_up, step_cross, step_share, step_down)]
    else:
        order += [(z_lag, step_scatter(level)) for level in range(levels)]
        order += [(z_lag, step_gather(level)) for level in reversed(range(levels))]
    order += [(BLAG, step_out), (2, out_wait)]
    stages = [(0, step_core)]
    for lag, act in order:
        stages.append((stages[-1][0] + lag, act))
    all_ticks = chunks + stages[-1][0]

    per_slot = BLK // CHAIN
    chain_chunks = slots * per_slot

    def chain_step(stream, send, recv, number, is_first, is_last, target):
        slot = number // per_slot
        rows = aligned((number % per_slot) * CHAIN, CHAIN)
        here = stream.at[slot, rows]

        @pl.when(is_first)
        def _():
            stream[slot, rows, :] = own_part[slot, rows, :]

        @pl.when(jnp.logical_not(is_first))
        def _():
            remote(here, here, send.at[number], recv.at[number], target).wait_recv()
            stream[slot, rows, :] = stream[slot, rows, :] + own_part[slot, rows, :]

        @pl.when(jnp.logical_not(is_last))
        def _():
            remote(here, here, send.at[number], recv.at[number], target).start()

    def chain_tick(step):
        number = step - ctx

        @pl.when((number >= 0) & (number < chain_chunks))
        def _():
            chain_step(left, left_s, left_r, number, ctx == 0, ctx == n_ctx - 1, next_ctx)

        back = step - (n_ctx - 1 - ctx)

        @pl.when((back >= 0) & (back < chain_chunks))
        def _():
            chain_step(right, right_s, right_r, back, ctx == n_ctx - 1, ctx == 0, last_ctx)

    groups = PAIRS // PAIRED
    group_ticks = groups if shallow else 0
    block_ticks = group_ticks + 2
    chain_first = FF_TICKS + block_ticks
    paced = max(0, -(-(chunks - chain_first) // PACE))
    late_first = max(chunks, chain_first)
    late_beats = max(0, chain_chunks + n_ctx - 1 - paced)
    chain_ticks = late_first + TAIL_PACE * max(0, late_beats - 1) + 1

    def tick(step, kinds):
        kinds = kinds if shallow or kinds == "none" else "both"
        if kinds in ("low", "both"):

            @pl.when(step + 3 < chunks)
            def _():
                step_fetch(step + 3)

        if kinds != "none":

            @pl.when(step + 2 < chunks)
            def _():
                step_make(step + 2, kinds)

        for lag, act in stages:
            index = step - lag

            @pl.when((index >= 0) & (index < chunks))
            def _(act=act, index=index):
                act(index)

        beat = step - chain_first

        @pl.when((beat >= 0) & (step < chunks) & (beat % PACE == 0))
        def _():
            chain_tick(beat // PACE)

        late = step - late_first

        @pl.when((late >= 0) & (late % TAIL_PACE == 0))
        def _():
            chain_tick(paced + late // TAIL_PACE)


    for index in range(3):
        step_fetch(jnp.int32(index))
    for copy in set_copies(0):
        copy.start()

    hidden_tiles = u_hbm.shape[1] // SPAN
    datt_v, dz_v, dy_v, hat1_v, hat2_v = own_part.at[0], do_v, left.at[1], right.at[0], right.at[1]

    def tile_copies(tile, parity):
        cols = aligned(tile * SPAN, SPAN)
        return (
            pltpu.make_async_copy(w_down.at[cols, :], own_part.at[parity], sem_ff.at[0, parity]),
            pltpu.make_async_copy(
                w_up.at[:, cols], turned.at[0, aligned(parity * D, D), :], sem_ff.at[1, parity]
            ),
            pltpu.make_async_copy(
                u_hbm.at[:, cols], left.at[0, :, aligned(parity * SPAN, SPAN)], sem_ff.at[2, parity]
            ),
        )

    def du_store(tile, parity):
        return pltpu.make_async_copy(
            kv_b.at[0, :, aligned(parity * SPAN, SPAN)],
            du_hbm.at[:, aligned(tile * SPAN, SPAN)],
            sem_ff.at[3, parity],
        )

    dz_load = pltpu.make_async_copy(dz_hbm, dz_v, sem_in.at[0])
    dz_load.start()
    for copy in tile_copies(0, 0):
        copy.start()
    wide_loads = [
        pltpu.make_async_copy(source, dest, sem_in.at[place + 1])
        for place, (source, dest) in enumerate(
            (
                (dy_hbm, dy_v),
                (hat1_hbm, hat1_v),
                (hat2_hbm, hat2_v),
                (rstd_hbm, lse_v.at[pl.ds(0, 2)]),
                (q_hbm, q_v),
                (o_hbm, o_v),
                (w_hbm, weight),
            )
        )
    ]
    out_loads = [
        pltpu.make_async_copy(
            w_out.at[pl.ds(place * TILE, TILE), :],
            term.at[place // 2, place % 2, :, pl.ds(0, D)],
            sem_in.at[8 + place],
        )
        for place in range(4)
    ]
    pl.semaphore_wait(barrier, len(peers))
    lax.fori_loop(0, 2, lambda index, carry: (step_make(index, "low"), carry)[1], 0)
    dz_load.wait()

    def ff_tile(tile, carry):
        start = tile + (tile + 1) // 2
        extra = jnp.where((tile % 2 == 0) | (tile + 1 == hidden_tiles), 1, 0)
        lax.fori_loop(start, start + 1 + extra, lambda index, inner: (tick(index, "low"), inner)[1], 0)

        parity = tile % 2
        for copy in tile_copies(tile, parity):
            copy.wait()

        @pl.when(tile + 1 < hidden_tiles)
        def _():
            for copy in tile_copies(tile + 1, 1 - parity):
                copy.start()

        @pl.when(tile == 0)
        def _():
            for copy in wide_loads + out_loads:
                copy.start()

        @pl.when(tile >= 2)
        def _():
            du_store(tile - 2, parity).wait()

        u_cols = aligned(parity * SPAN, SPAN)
        u_tile = left[0, :, u_cols].astype(jnp.float32)
        square = u_tile * u_tile
        bend = jnp.tanh(GELU_C * u_tile * (1.0 + GELU_A * square))
        slope = 0.5 * (1.0 + bend) + (0.5 * GELU_C) * u_tile * (1.0 - bend * bend) * (
            1.0 + 3.0 * GELU_A * square
        )
        du_tile = (contract_last(dz_v[...], own_part[parity]) * slope).astype(jnp.bfloat16)
        kv_b[0, :, u_cols] = du_tile
        du_store(tile, parity).start()
        fresh = contract_last(du_tile, turned[0, aligned(parity * D, D), :])

        @pl.when(tile == 0)
        def _():
            dq_acc[...] = fresh

        @pl.when(tile > 0)
        def _():
            dq_acc[...] = dq_acc[...] + fresh

        return carry

    lax.fori_loop(0, hidden_tiles, ff_tile, 0)
    for tile in range(hidden_tiles - 2, hidden_tiles):
        du_store(tile, tile % 2).wait()
    for copy in wide_loads:
        copy.wait()
    for copy in block_copies(1):
        copy.start()

    def hidden_back(step, carry):
        gain1, gain2, bias1, bias2 = carry
        rows = aligned(step * CHAIN, CHAIN)
        upstream = dq_acc[rows, :]
        hat = hat2_v[rows, :].astype(jnp.float32)
        grad_h = dy_v[rows, :].astype(jnp.float32) + row_back(
            upstream, hat, lse_v[1, rows, 0:1], gain_ref[2:3, :]
        )
        gain2, bias2 = gain2 + column_sum(upstream * hat), bias2 + column_sum(upstream)
        dq_acc[rows, :] = grad_h
        if shallow:
            gkv[rows, :] = grad_h
        hat = hat1_v[rows, :].astype(jnp.float32)
        datt_v[rows, :] = row_back(grad_h, hat, lse_v[0, rows, 0:1], gain_ref[1:2, :]).astype(
            jnp.bfloat16
        )
        return gain1 + column_sum(grad_h * hat), gain2, bias1 + column_sum(grad_h), bias2

    zero = jnp.zeros((1, D), jnp.float32)
    sums = lax.fori_loop(0, BLK // CHAIN, hidden_back, (zero,) * 4)
    row = lax.broadcasted_iota(jnp.int32, (8, D), 0)
    norm_v[...] = norm_ref[...]
    for place, value in zip((1, 2, 5, 6), sums):
        norm_v[...] = norm_v[...] + jnp.where(row == place, value, 0.0)
    stores = [
        pltpu.make_async_copy(dq_acc, dh_hbm, sem_res.at[0]),
        pltpu.make_async_copy(datt_v, datt_hbm, sem_res.at[1]),
    ]
    lse_load = pltpu.make_async_copy(lse_hbm, lse_v, sem_in.at[0])
    for copy in stores + [lse_load]:
        copy.start()
    for place in range(4):
        out_loads[place].wait()
        do_v[:, pl.ds(place * TILE, TILE)] = contract_last(
            datt_v[...], term[place // 2, place % 2, :, pl.ds(0, D)]
        ).astype(jnp.bfloat16)
    for copy in stores + [lse_load]:
        copy.wait()
    dq_acc[...] = jnp.zeros_like(dq_acc)

    def attend(kv_ref, turned_ref, own, visible, begin):
        def body(group, carry):
            if shallow:
                tick(begin + group, "low")
            for member in range(PAIRED):
                grad_block(
                    q_v, do_v, o_v, lse_v, kv_ref, dq_acc, turned_ref, group * PAIRED + member, own, visible
                )
            return carry

        lax.fori_loop(0, groups, body, 0)

    def first_sums(piece, normed, cols):
        gain_sum[:, cols] = gain_sum[:, cols] + column_sum(piece * normed.astype(jnp.float32))
        bias_sum[:, cols] = bias_sum[:, cols] + column_sum(piece)

    gain_sum[...] = jnp.zeros_like(gain_sum)
    bias_sum[...] = jnp.zeros_like(bias_sum)

    def each_slot(slot, carry):
        visible = slot < own_slot
        index = slot + 1
        place = lax.rem(index, kv_b.shape[0])
        for copy in block_copies(index):
            copy.wait()
        if kv_b.shape[0] > 1:
            for copy in block_copies(index + 1):
                copy.start()
        begin = FF_TICKS + slot * block_ticks
        a_place = slot if shallow else 0
        attend(kv_b.at[place], turned.at[a_place], False, visible, begin)

        def weight_terms(step, inner):
            tick(begin + group_ticks + step, "low")
            rows = aligned(step * 512, 512)
            for part in range(0 if shallow else 2):
                cols = pl.ds(part * D, D)
                product = dot_dims(a_b[a_place, :, rows], turned[a_place, cols, :], 0, 1)
                for down in range(2):
                    target = term.at[step, down, :, pl.ds((part + 1) * D, D)]
                    piece = product[down * TILE : (down + 1) * TILE]

                    @pl.when(slot == 0)
                    def _(target=target, piece=piece):
                        target[...] = piece.astype(target.dtype)

                    @pl.when(slot > 0)
                    def _(target=target, piece=piece):
                        target[...] = (target[...] + piece).astype(target.dtype)

            piece = dot_dims(turned[a_place], weight[rows, pl.ds(D, 2 * D)], 0, 1)
            own_part[slot, :, rows] = piece.astype(jnp.bfloat16)
            first_sums(piece, a_b[a_place, :, rows], rows)
            return inner

        lax.fori_loop(0, 2, weight_terms, 0)
        if kv_b.shape[0] == 1:
            for copy in block_copies(index + 1):
                copy.start()
        return carry

    lax.fori_loop(0, slots, each_slot, 0)
    begin = FF_TICKS + slots * block_ticks
    own_place = (slots + 1) % kv_b.shape[0]
    for copy in block_copies(slots + 1):
        copy.wait()
    own_a = slots if shallow else 0
    attend(kv_b.at[own_place], turned.at[own_a], True, None, begin)
    dq_low[...] = (dq_acc[...] * ALPHA).astype(jnp.bfloat16) * jnp.bfloat16(QSCALE)
    x_load = pltpu.make_async_copy(x_hbm, do_v, sem_in.at[0])
    x_load.start()
    ready = begin + group_ticks

    def last_terms(step, carry):
        tick(begin + group_ticks + step, "both")
        rows = aligned(step * TILE, TILE)
        a_rows = a_b[0, :, rows]
        up, down = step // 2, step % 2
        term[up, down, :, pl.ds(0, D)] = dot_dims(a_rows, dq_low[...], 0, 0).astype(jnp.bfloat16)
        for part in range(2):
            cols = pl.ds(part * D, D)
            target = term.at[up, down, :, pl.ds((part + 1) * D, D)]
            target[...] = (target[...] + dot_dims(a_rows, turned[0, cols, :], 0, 1)).astype(jnp.bfloat16)
        return carry

    if not shallow:
        lax.fori_loop(0, 4, last_terms, 0)
        ready = ready + 4
    assert ready <= last_low - 2
    da_acc = dq_acc

    spare = max(0, last_low - 2 - ready - 4) if shallow else 0

    def own_grad(step, carry):
        if shallow:
            begins = ready + step + jnp.where(step > 0, spare, 0)
            ends = ready + step + 1 + spare
            lax.fori_loop(begins, ends, lambda index, inner: (tick(index, "low"), inner)[1], 0)
        else:
            tick(ready + step, "low")
        rows = aligned(step * TILE, TILE)
        piece = dot_dims(dq_low[...], weight[rows, pl.ds(0, D)], 1, 1) + dot_dims(
            turned[own_a], weight[rows, pl.ds(D, 2 * D)], 0, 1
        )
        da_acc[:, rows] = piece
        first_sums(piece, a_b[own_a, :, rows], rows)
        return carry

    lax.fori_loop(0, 4, own_grad, 0)
    ready = ready + 4 + spare

    first_gain = (gain_sum[...] - bias_ref[0:1, :] * bias_sum[...]) / gain_ref[0:1, :]
    norm_v[...] = (
        norm_v[...] + jnp.where(row == 0, first_gain, 0.0) + jnp.where(row == 4, bias_sum[...], 0.0)
    )

    def run_ticks(first, last, kinds):
        if last > first:
            lax.fori_loop(first, last, lambda index, carry: (tick(index, kinds), carry)[1], 0)
        return max(first, last)

    assert ready == last_low - 2 or not shallow
    norm_peers = [core_peer, side_peer, grp_peer] + level_peers
    norm_base = ready
    norm_result = pltpu.make_async_copy(norm_v, norm_out, sem_res.at[1])

    def norm_move(place):
        return remote(norm_v, norm_in.at[place], norm_s.at[place], norm_r.at[place], norm_peers[place])

    def norm_ticks(step, carry):
        for place in range(len(norm_peers) + 1):

            @pl.when(step == norm_base + 3 * place)
            def _(place=place):
                if place:
                    finished(norm_move(place - 1))
                    norm_v[...] = norm_v[...] + norm_in[place - 1]
                if place < len(norm_peers):
                    norm_move(place).start()
                else:
                    norm_result.start()

        tick(step, "high")
        return carry

    last_tick = max(ready + 3 * len(norm_peers) + 1, chain_ticks)
    lax.fori_loop(ready, last_tick, norm_ticks, 0)
    ready = last_tick
    x_load.wait()
    gain = gain_ref[0:1, :]

    def norm_grad(step, carry):
        @pl.when(step % 2 == 0)
        def _():
            tick(ready + step // 2, "none")

        rows = aligned(step * CHAIN, CHAIN)
        upstream = da_acc[rows, :]
        for slot in range(slots):
            joined = left[slot, rows, :].astype(jnp.float32) + right[slot, rows, :].astype(jnp.float32)
            upstream = upstream + jnp.where(own_slot == slot, joined, 0.0)
        values = do_v[rows, :].astype(jnp.float32)
        centre = values - jnp.mean(values, axis=-1, keepdims=True)
        scale = lax.rsqrt(jnp.mean(centre * centre, axis=-1, keepdims=True) + EPS)
        centre = centre * scale
        grad = row_back(upstream, centre, scale, gain)
        da_acc[rows, :] = grad + gkv[rows, :] if shallow else grad
        return carry

    lax.fori_loop(0, BLK // CHAIN, norm_grad, 0)
    ready = ready + BLK // CHAIN // 2
    result = pltpu.make_async_copy(da_acc, grad_out, sem_res.at[0])
    result.start()
    run_ticks(ready, all_ticks, "none")

    def drain_chain(index, carry):
        here = left.at[0, pl.ds(0, CHAIN)]

        @pl.when(ctx < n_ctx - 1)
        def _():
            remote(here, here, left_s.at[index], left_r.at[index], next_ctx).wait_send()

        @pl.when(ctx > 0)
        def _():
            remote(here, here, right_s.at[index], right_r.at[index], last_ctx).wait_send()

        return carry

    lax.fori_loop(0, chain_chunks, drain_chain, 0)
    result.wait()
    norm_result.wait()


def backward_part(n_ctx, slot_vec, gains, biases, norms, saved, weights, ffn):
    slots = n_ctx // 2
    levels = n_ctx.bit_length() - 1
    depth = 16 if n_ctx == 4 else 10
    hidden = weights[1].shape[1]
    widths = [(hidden // 4, D), (D // 4, hidden), (D // 4, D), (D // 4, 3 * D)]
    low, full = jnp.bfloat16, jnp.float32
    dma = pltpu.SemaphoreType.DMA
    hbm = pl.BlockSpec(memory_space=pl.ANY)
    vmem = pl.BlockSpec(memory_space=pltpu.VMEM)
    shape = jax.ShapeDtypeStruct
    buffers = 2 if slots <= 2 else 1
    chain = slots * (BLK // CHAIN)
    zshapes, rows, cols = [], TILE // 2, TILE
    if n_ctx == 4:
        zshapes = [pltpu.VMEM((depth, rows, cols), low), pltpu.VMEM((depth, rows // 2, cols), low)]
    for _ in range(0 if zshapes else levels):
        rows, cols = (rows // 2, cols) if rows > 16 else (rows, cols // 2)
        zshapes.append(pltpu.VMEM((depth, rows, cols), low))
    return pl.pallas_call(
        functools.partial(backward_kernel, n_ctx, widths),
        out_shape=[shape(width, low) for width in widths] + [
            shape((BLK, D), full),
            shape((8, D), full),
            shape((BLK, D), full),
            shape((BLK, hidden), low),
            shape((BLK, D), low),
        ],
        in_specs=[pl.BlockSpec(memory_space=pltpu.SMEM), vmem, vmem, vmem]
        + [hbm] * (len(saved) + len(weights) + len(ffn)),
        out_specs=[hbm] * 9,
        scratch_shapes=[
            pltpu.VMEM((BLK, D), low),
            pltpu.VMEM((BLK, D), low),
            pltpu.VMEM((BLK, D), low),
            pltpu.VMEM((PAIRS, BLK, 128), full),
            pltpu.VMEM((D, 3 * D), low),
            pltpu.VMEM((buffers, BLK, 2 * D), low),
            pltpu.VMEM((slots + 1 if slots <= 2 else 1, BLK, D), low),
            pltpu.VMEM((BLK, D), full),
            pltpu.VMEM((slots + 1 if slots <= 2 else 1, 2 * D, BLK), low),
            pltpu.VMEM((BLK, D) if slots <= 2 else (8, 128), full),
            pltpu.VMEM((2, 2, D // 4, D if slots <= 2 else 3 * D), low),
            pltpu.VMEM((slots, BLK, D), low),
            pltpu.VMEM((slots, BLK, D), low),
            pltpu.VMEM((slots, BLK, D), low),
            pltpu.VMEM((8, D), full),
            pltpu.VMEM((3 + levels, 8, D), full),
            pltpu.VMEM((1, D), full),
            pltpu.VMEM((1, D), full),
            pltpu.VMEM((depth, 2, TILE, TILE), low),
            pltpu.VMEM((depth, TILE, TILE), low),
            pltpu.VMEM((depth, TILE // 2, TILE), low),
            pltpu.VMEM((depth, TILE, TILE), low),
            pltpu.VMEM((4, 2, 2, TILE, TILE), low),
        ]
        + [pltpu.VMEM((2, 4, BLK, TILE), low), pltpu.VMEM((4, BLK, TILE), low)]
        + zshapes
        + [dma((12,)), dma((2, buffers)), dma((4,)), dma((2, 4)), dma((4, 2)), dma((depth,)), dma((2,))]
        + [dma((depth,))] * (8 + 4 * levels)
        + [dma((chain,))] * 4
        + [dma((3 + levels,))] * 2,
        compiler_params=pltpu.CompilerParams(
            collective_id=2, has_side_effects=True, vmem_limit_bytes=67043328
        ),
        cost_estimate=pl.CostEstimate(flops=40 << 30, bytes_accessed=64 << 20, transcendentals=1 << 24),
        name="attend_back_reduce",
    )(
        slot_vec,
        gains,
        biases,
        norms,
        *saved,
        *weights,
        *ffn,
    )


def widen_kernel(*refs):
    count = len(refs) // 2
    for source, dest in zip(refs[: count - 1], refs[count:]):
        dest[...] = source[...].astype(dest.dtype)
    refs[-2][...] = refs[count - 1][0:4, :]
    refs[-1][...] = refs[count - 1][4:8, :]


def widen(arrays, types, norms):
    steps = 4
    specs = [pl.BlockSpec((x.shape[0] // steps, x.shape[1]), lambda i: (i, 0)) for x in arrays]
    shape = jax.ShapeDtypeStruct
    pair = [pl.BlockSpec((4, D), lambda i: (0, 0))] * 2
    return pl.pallas_call(
        widen_kernel,
        out_shape=[shape(x.shape, kind) for x, kind in zip(arrays, types)]
        + [shape((4, D), jnp.float32)] * 2,
        grid=(steps,),
        in_specs=specs + [pl.BlockSpec((8, D), lambda i: (0, 0))],
        out_specs=specs + pair,
        compiler_params=pltpu.CompilerParams(vmem_limit_bytes=67043328),
        name="widen",
    )(*arrays, norms)


def per_device(n_ctx, inputs, w_qkv, w_out, w_up, w_down, norm_gains, norm_biases, block_map, out_grad):
    slots = n_ctx // 2
    raw, seed_low = inputs.reshape(BLK, D), out_grad.reshape(BLK, D)
    block_entry = block_map.reshape(2)
    forward = forward_part(
        n_ctx,
        block_entry,
        norm_gains,
        norm_biases,
        raw,
        seed_low,
        w_qkv,
        w_out,
        w_up,
        w_down,
    )
    every_low, queries, keys_values, attn_low, lse, full_qkv, full_out, full_up, full_down = forward[:9]
    result, active_low, down_low, ffn_low, upward, hat1, hat2, rstd, norms = forward[9:]
    backward = backward_part(
        n_ctx,
        block_entry,
        norm_gains,
        norm_biases,
        norms,
        [raw, queries, keys_values, every_low, attn_low, lse, full_qkv],
        [full_out, full_up, full_down],
        [active_low, down_low, ffn_low, upward, hat1, hat2, rstd, seed_low],
    )
    grad_tokens, norm_total, grad_hidden = backward[4:7]
    if slots > 2:
        grad_tokens = grad_tokens + grad_hidden
    full = jnp.float32
    summed_down, summed_up, summed_out, summed_qkv, grad_input, result, gain_total, bias_total = widen(
        list(backward[:4]) + [grad_tokens, result],
        [full] * 5 + [jnp.bfloat16],
        norm_total,
    )
    return (
        result.reshape(1, 1, BLK, D),
        grad_input.reshape(1, 1, BLK, D),
        summed_qkv,
        summed_out,
        summed_up,
        summed_down,
        gain_total,
        bias_total,
    )


def solution(mesh):
    rows = P("wsh", None)
    blocks = P("grp", "wsh", "ctx", None)
    return jax.shard_map(
        functools.partial(per_device, mesh.shape["ctx"]),
        mesh=mesh,
        in_specs=(blocks, rows, rows, rows, rows, P(), P(), blocks, blocks),
        out_specs=(blocks, blocks, rows, rows, rows, rows, P(), P()),
        check_vma=False,
    )
```

```python
import functools
import math

import jax
import jax.numpy as jnp
from jax import lax
from jax.experimental import pallas as pl
from jax.experimental.pallas import tpu as pltpu
from jax.sharding import PartitionSpec as P

D = 1024
HEADS = 16
DH = 64
BLK = 512
PAIRS = HEADS // 2
QT = 256

EPS = 1e-05
ALPHA = 32.0
NEG = -1e30
LOG2E = 1.4426950408889634
C2 = ALPHA * LOG2E
MESH = pl.DeviceIdType.MESH
QSCALE = 1.0 / (ALPHA * math.sqrt(DH))


def layer_norm(values, gain_row, bias_row):
    centre = values - jnp.mean(values, axis=-1, keepdims=True)
    spread = jnp.mean(centre * centre, axis=-1, keepdims=True)
    return centre * lax.rsqrt(spread + EPS) * gain_row + bias_row


def dot_dims(left_side, right_side, left_dim, right_dim):
    return lax.dot_general(
        left_side,
        right_side,
        (((left_dim,), (right_dim,)), ((), ())),
        preferred_element_type=jnp.float32,
    )


def contract_last(left_side, right_side):
    return dot_dims(left_side, right_side, 1, 1)


def contract_rows(left_side, right_side):
    return dot_dims(left_side, right_side, 0, 0)


def standard_rows(values):
    centre = values - jnp.mean(values, axis=-1, keepdims=True)
    scale = lax.rsqrt(jnp.mean(centre * centre, axis=-1, keepdims=True) + EPS)
    return centre * scale, scale


def row_back(upstream, hat, scale, gain):
    scaled = upstream * gain
    return scale * (
        scaled
        - jnp.mean(scaled, axis=-1, keepdims=True)
        - hat * jnp.mean(scaled * hat, axis=-1, keepdims=True)
    )


def column_sum(values):
    return jnp.sum(values, axis=0, keepdims=True)


def head_lanes(head, rows):
    lane = lax.broadcasted_iota(jnp.int32, (rows, 128), 1)
    return (lane >= DH) if head else (lane < DH)


def causal_tile():
    row = lax.broadcasted_iota(jnp.int32, (QT, QT), 0)
    col = lax.broadcasted_iota(jnp.int32, (QT, QT), 1)
    return col <= row


PIECE = 128
SPAN = 512
CHAIN = 64
HOP = 2
YLAG = 3
XLAG = 2
BLAG = 2
FF_TICKS = 13
TAIL_PACE = 3
GELU_A = 0.044715
GELU_C = math.sqrt(2.0 / math.pi)
PACE = 2
LAG = 2
GROUP = 4
AHEAD = 4


def remote(src, dst, send, recv, peer):
    return pltpu.make_async_remote_copy(
        src_ref=src, dst_ref=dst, send_sem=send, recv_sem=recv, device_id=peer, device_id_type=MESH
    )


def local_wait(ref, sem):
    pltpu.make_async_copy(ref, ref, sem).wait()


def aligned(start, size):
    return pl.ds(pl.multiple_of(start, size), size)


def softmax_block(q_ref, kv_ref, acc, top_ref, sum_ref, pair, base, own, visible):
    lanes = aligned(pair * 128, 128)
    value_lanes = aligned(D + pair * 128, 128)
    causal = causal_tile()
    first = head_lanes(0, QT)
    count = BLK // QT
    q_pair = q_ref[:, lanes]
    keys = kv_ref[pl.ds(base, BLK), lanes]
    values = kv_ref[pl.ds(base, BLK), value_lanes]
    if not own:
        old_top, old_sum, old_out = top_ref[pair], sum_ref[pair], acc[:, lanes]
        hide = jnp.where(visible, 0.0, 1e30)
    results = []
    work = [(tile, head) for tile in range(count) for head in range(2)]
    parts_of = {}
    for tile, head in work:
        q_tile = q_pair[tile * QT : (tile + 1) * QT]
        q_head = jnp.where(head_lanes(head, QT), q_tile, jnp.zeros_like(q_tile))
        span = (tile + 1) * QT if own else BLK
        parts_of[tile, head] = contract_last(q_head, keys[:span])
    top_of, expo_of, total_of = {}, {}, {}
    for tile, head in work:
        part = parts_of[tile, head]
        if own:
            diag = jnp.where(causal, part[:, tile * QT :], NEG)
            part = jnp.concatenate([part[:, : tile * QT], diag], axis=1) if tile else diag
        top = jnp.max(part, axis=-1, keepdims=True) * C2
        if own:
            shift = top
        else:
            top = jnp.maximum(
                jnp.where(visible, top, NEG), old_top[tile * QT : (tile + 1) * QT, head * DH : head * DH + 1]
            )
            shift = top + hide
        expo = jnp.exp2(part * C2 - shift)
        top_of[tile, head] = jnp.broadcast_to(top, (QT, 128))
        total_of[tile, head] = jnp.broadcast_to(jnp.sum(expo, axis=-1, keepdims=True), (QT, 128))
        expo_of[tile, head] = expo.astype(jnp.bfloat16)
    out_of = {}
    for tile, head in work:
        span = (tile + 1) * QT if own else BLK
        out_of[tile, head] = dot_dims(expo_of[tile, head], values[:span], 1, 0)
    for tile in range(count):
        rows = pl.ds(tile * QT, QT)
        new_top = jnp.where(first, top_of[tile, 0], top_of[tile, 1])
        new_sum = jnp.where(first, total_of[tile, 0], total_of[tile, 1])
        new_out = jnp.where(first, out_of[tile, 0], out_of[tile, 1])
        if not own:
            here = slice(tile * QT, (tile + 1) * QT)
            keep = jnp.exp2(old_top[here] - new_top)
            new_sum = new_sum + old_sum[here] * keep
            new_out = new_out + old_out[here] * keep
        top_ref[pair, rows, :] = new_top
        sum_ref[pair, rows, :] = new_sum
        acc[rows, lanes] = new_out


def forward_kernel(n_ctx, *refs):
    slots = n_ctx // 2
    (slot_ref, gain_ref, bias_ref, x_hbm, dy_hbm, w_qkv, w_out, w_up, w_down) = refs[:9]
    (a_out, q_out, kv_out, o_out, lse_out, full_qkv, full_out, full_up, full_down) = refs[9:18]
    (y_out, g_out, dz_out, f_out, u_out, hat1_out, hat2_out, rstd_out, norm_out) = refs[18:27]
    (x_own, left, right, a_all, q_all, kv_all, weight, acc, z_acc, norm_v, tops, sums, hop) = refs[27:40]
    (sem_in, sem_load, sem_store, sem_ff, sem_out, sem_a, sem_kv, side_s, side_r, grp_s, grp_r, cs_s, cs_r, cg_s, cg_r, own_s, own_r, left_s, left_r, right_s, right_r) = refs[40:]
    grp, ctx, wsh = lax.axis_index("grp"), lax.axis_index("ctx"), lax.axis_index("wsh")
    side, core = wsh // 2, wsh % 2
    core_peer = (grp, ctx, side * 2 + 1 - core)
    side_peer = (grp, ctx, (1 - side) * 2 + core)
    grp_peer = (1 - grp, ctx, wsh)
    next_ctx = (grp, lax.rem(ctx + 1, n_ctx), wsh)
    last_ctx = (grp, lax.rem(ctx + n_ctx - 1, n_ctx), wsh)

    load = pltpu.make_async_copy(x_hbm, x_own, sem_in.at[0])
    load.start()
    barrier = pltpu.get_barrier_semaphore()
    for peer in (core_peer, side_peer, grp_peer, next_ctx, last_ctx):
        pl.semaphore_signal(barrier, inc=1, device_id=peer, device_id_type=MESH)
    pl.semaphore_wait(barrier, 5)

    shards = (w_qkv, w_out, w_up, w_down)
    fulls = (weight, full_out, full_up, full_down)
    ranges, start = [], 0
    for shard in shards:
        across = shard.shape[1] // SPAN
        ranges.append((start, start + across * (shard.shape[0] // (2 * PIECE)), across))
        start = ranges[-1][1]
    pieces = start

    def by_range(index, act):
        for place, (low, high, across) in enumerate(ranges):

            @pl.when((index >= low) & (index < high))
            def _(place=place, low=low, across=across):
                act(place, (index - low) // across, aligned(((index - low) % across) * SPAN, SPAN))

    def rows_of(place, owner, half, group):
        shard_rows = shards[place].shape[0]
        return aligned(owner * shard_rows + half * (shard_rows // 2) + group * PIECE, PIECE)

    sides_owner = (1 - side) * 2 + core

    def send_piece(index, carry):
        def act(place, group, cols):
            remote(
                shards[place].at[rows_of(place, 0, grp, group), cols],
                fulls[place].at[rows_of(place, wsh, grp, group), cols],
                side_s.at[index],
                side_r.at[index],
                side_peer,
            ).start()

        by_range(index, act)
        return carry

    def own_copies():
        copies = []
        across = shards[0].shape[1] // SPAN
        for place in range(4):
            shard_rows = shards[place].shape[0]
            mine = aligned(wsh * shard_rows, shard_rows)
            steps = range(across) if place == 0 else [None]
            for step in steps:
                cols = slice(None) if step is None else pl.ds(step * SPAN, SPAN)
                number = len(copies)
                copies.append(
                    remote(
                        shards[place].at[:, cols],
                        fulls[place].at[mine, cols],
                        own_s.at[number],
                        own_r.at[number],
                        core_peer,
                    )
                )
        return copies

    for index in range(AHEAD):
        send_piece(index, 0)
    for copy in own_copies():
        copy.start()
    own_rows = aligned(wsh * w_qkv.shape[0], w_qkv.shape[0])
    own_weight = pltpu.make_async_copy(w_qkv, weight.at[own_rows, :], sem_in.at[1])
    own_weight.start()
    load.wait()

    bounces, start = [], 0
    for shard in shards[1:]:
        across = shard.shape[1] // SPAN
        bounces.append((start, start + across * (shard.shape[0] // (2 * PIECE)), across))
        start = bounces[-1][1]
    moves = start

    def bounce(index, loading):
        slot = lax.rem(index, 3)
        for place, (low, high, across) in enumerate(bounces):

            @pl.when((index >= low) & (index < high))
            def _(place=place + 1, low=low, across=across):
                group = (index - low) // across
                cols = aligned(((index - low) % across) * SPAN, SPAN)
                if loading:
                    here = shards[place].at[aligned(group * 2 * PIECE, 2 * PIECE), cols]
                    pltpu.make_async_copy(here, hop.at[slot], sem_load.at[slot]).start()
                else:
                    rows = aligned(wsh * shards[place].shape[0] + group * 2 * PIECE, 2 * PIECE)
                    local_wait(hop.at[slot], sem_load.at[slot])
                    pltpu.make_async_copy(
                        hop.at[slot], fulls[place].at[rows, cols], sem_store.at[slot]
                    ).start()

    own_slot = slot_ref[1] // BLK
    own_tag = jnp.where(slot_ref[0] == 0, own_slot, n_ctx)
    chain_chunks = slots * (BLK // CHAIN)

    def chain_step(stream, send, recv, number, is_first, is_last, target):
        slot = number // (BLK // CHAIN)
        spot = aligned((number % (BLK // CHAIN)) * CHAIN, CHAIN)
        mine = jnp.where(own_tag == slot, x_own[spot, :], jnp.zeros((CHAIN, D), jnp.bfloat16))
        here = stream.at[slot, spot]

        @pl.when(is_first)
        def _():
            stream[slot, spot, :] = mine

        @pl.when(jnp.logical_not(is_first))
        def _():
            remote(here, here, send.at[number], recv.at[number], target).wait_recv()
            stream[slot, spot, :] = stream[slot, spot, :] + mine

        @pl.when(jnp.logical_not(is_last))
        def _():
            remote(here, here, send.at[number], recv.at[number], target).start()

    def tick(step):
        @pl.when((step >= 1) & (step <= moves))
        def _():
            bounce(step - 1, False)

        @pl.when((step >= 3) & (step < moves))
        def _():
            local_wait(hop.at[lax.rem(step, 3)], sem_store.at[lax.rem(step, 3)])

        @pl.when(step < moves)
        def _():
            bounce(step, True)

        @pl.when(step + AHEAD < pieces)
        def _():
            send_piece(step + AHEAD, 0)

        number = step - HOP * ctx

        @pl.when((number >= 0) & (number < chain_chunks))
        def _():
            chain_step(left, left_s, left_r, number, ctx == 0, ctx == n_ctx - 1, next_ctx)

        back = step - HOP * (n_ctx - 1 - ctx)

        @pl.when((back >= 0) & (back < chain_chunks))
        def _():
            chain_step(right, right_s, right_r, back, ctx == n_ctx - 1, ctx == 0, last_ctx)

        @pl.when(step < pieces)
        def _():
            def act(place, group, cols):
                here = fulls[place].at[rows_of(place, sides_owner, grp, group), cols]
                remote(here, here, side_s.at[step], side_r.at[step], side_peer).wait_recv()
                remote(here, here, grp_s.at[step], grp_r.at[step], grp_peer).start()
                remote(here, here, cs_s.at[step], cs_r.at[step], core_peer).start()

            by_range(step, act)

        late = step - LAG

        @pl.when((late >= 0) & (late < pieces))
        def _():
            def act(place, group, cols):
                here = fulls[place].at[rows_of(place, sides_owner, 1 - grp, group), cols]
                remote(here, here, grp_s.at[late], grp_r.at[late], grp_peer).wait_recv()
                remote(here, here, cg_s.at[late], cg_r.at[late], core_peer).start()

            by_range(late, act)

    def ticks(first, last):
        lax.fori_loop(first, last, lambda index, carry: (tick(index), carry)[1], 0)

    def normalise(source, dest):
        gain, bias = gain_ref[0:1, :], bias_ref[0:1, :]

        def body(index, carry):
            rows = aligned(index * 128, 128)
            values = source(rows).astype(jnp.float32)
            a_all[aligned(dest + index * 128, 128), :] = layer_norm(values, gain, bias).astype(
                jnp.bfloat16
            )
            return carry

        lax.fori_loop(0, BLK // 128, body, 0)

    def piece_ready(index):
        here = fulls[0].at[pl.ds(0, PIECE), pl.ds(0, SPAN)]
        remote(here, here, cs_s.at[index], cs_r.at[index], core_peer).wait_recv()
        remote(here, here, cg_s.at[index], cg_r.at[index], core_peer).wait_recv()
        whole = fulls[0].at[pl.ds(0, 2 * PIECE), pl.ds(0, SPAN)]
        remote(whole, whole, own_s.at[index], own_r.at[index], core_peer).wait_recv()

    tick(0)
    normalise(lambda rows: x_own[rows, :], 0)
    ticks(1, LAG + 1)
    own_weight.wait()

    def project_q(index, carry):
        tick(index + LAG + 1)
        piece_ready(index)
        cols = aligned(index * SPAN, SPAN)
        q_all[:, cols] = (
            jnp.dot(a_all[pl.ds(0, BLK), :], weight[:, cols], preferred_element_type=jnp.float32) * QSCALE
        ).astype(jnp.bfloat16)
        return carry

    lax.fori_loop(0, D // SPAN, project_q, 0)
    head_ticks = LAG + 1 + D // SPAN

    def project_kv(index, base):
        cols = aligned(index * SPAN, SPAN)
        rows = aligned(base, BLK)
        kv_all[rows, cols] = jnp.dot(
            a_all[rows, :], weight[:, aligned(D + index * SPAN, SPAN)], preferred_element_type=jnp.float32
        ).astype(jnp.bfloat16)

    def own_kv(index, carry):
        tick(index + head_ticks)
        piece_ready(index + D // SPAN)
        project_kv(index, 0)
        return carry

    lax.fori_loop(0, 2 * D // SPAN, own_kv, 0)
    own_ticks = head_ticks + 2 * D // SPAN

    def send_block(index):
        rows = aligned(index * BLK, BLK)
        pltpu.make_async_copy(a_all.at[rows, :], a_out.at[rows, :], sem_a.at[index]).start()
        pltpu.make_async_copy(kv_all.at[rows, :], kv_out.at[rows, :], sem_kv.at[index]).start()

    outputs = [
        pltpu.make_async_copy(weight, full_qkv, sem_out.at[0]),
        pltpu.make_async_copy(q_all, q_out, sem_out.at[1]),
    ]
    for copy in outputs:
        copy.start()

    send_block(0)

    def own_attention(group, carry):
        ticks(own_ticks + 2 * group, own_ticks + 2 * group + 2)
        for member in range(GROUP):
            softmax_block(q_all, kv_all, acc, tops, sums, group * GROUP + member, 0, True, None)
        return carry

    groups = PAIRS // GROUP
    lax.fori_loop(0, groups, own_attention, 0)
    used = own_ticks + 2 * groups
    per_slot = 2 * D // SPAN + 2 * groups

    need = BLK // CHAIN + HOP * (n_ctx - 1)
    early = max(0, need - used)
    if early:
        lax.fori_loop(0, early, lambda index, carry: (tick(used + index), carry)[1], 0)

    def each_slot(slot, carry):
        base = pl.multiple_of((slot + 1) * BLK, BLK)
        visible = slot < own_slot
        begin = early + used + slot * per_slot

        def total(rows):
            joined = left[slot, rows, :] + right[slot, rows, :]
            return jnp.where(own_tag == slot, x_own[rows, :], joined)

        normalise(total, base)

        def slot_kv(index, inner):
            tick(begin + index)
            project_kv(index, base)
            return inner

        lax.fori_loop(0, 2 * D // SPAN, slot_kv, 0)

        send_block(slot + 1)

        def slot_attention(group, inner):
            start = begin + 2 * D // SPAN + 2 * group
            ticks(start, start + 2)
            for member in range(GROUP):
                softmax_block(
                    q_all, kv_all, acc, tops, sums, group * GROUP + member, base, False, visible
                )
            return inner

        lax.fori_loop(0, groups, slot_attention, 0)
        return carry

    lax.fori_loop(0, slots, each_slot, 0)
    done_ticks = early + used + slots * per_slot

    def finish(pair, carry):
        lanes = aligned(pair * 128, 128)
        x_own[:, lanes] = (acc[:, lanes] / sums[pair]).astype(jnp.bfloat16)
        tops[pair] = tops[pair] + jnp.log2(sums[pair])
        return carry

    lax.fori_loop(0, PAIRS, finish, 0)
    outputs += [
        pltpu.make_async_copy(x_own, o_out, sem_out.at[2]),
        pltpu.make_async_copy(tops, lse_out, sem_out.at[3]),
    ]
    for copy in outputs[2:]:
        copy.start()
    all_ticks = max(pieces + LAG, chain_chunks + HOP * (n_ctx - 1))
    if all_ticks > done_ticks:
        lax.fori_loop(done_ticks, all_ticks, lambda index, carry: (tick(index), carry)[1], 0)

    def drain(index, carry):
        here = fulls[0].at[pl.ds(0, PIECE), pl.ds(0, SPAN)]

        @pl.when(index >= ranges[0][1])
        def _():
            remote(here, here, cs_s.at[index], cs_r.at[index], core_peer).wait_recv()
            remote(here, here, cg_s.at[index], cg_r.at[index], core_peer).wait_recv()

        remote(here, here, side_s.at[index], side_r.at[index], side_peer).wait_send()
        remote(here, here, grp_s.at[index], grp_r.at[index], grp_peer).wait_send()
        remote(here, here, cs_s.at[index], cs_r.at[index], core_peer).wait_send()
        remote(here, here, cg_s.at[index], cg_r.at[index], core_peer).wait_send()
        return carry

    lax.fori_loop(0, pieces, drain, 0)
    copies = own_copies()
    for number, copy in enumerate(copies):
        copy.wait_send()
        if number >= len(copies) - 3:
            copy.wait_recv()
    for index in range(moves - 3, moves):
        local_wait(hop.at[index % 3], sem_store.at[index % 3])

    def drain_chain(index, carry):
        here = left.at[0, pl.ds(0, CHAIN)]

        @pl.when(ctx < n_ctx - 1)
        def _():
            remote(here, here, left_s.at[index], left_r.at[index], next_ctx).wait_send()

        @pl.when(ctx > 0)
        def _():
            remote(here, here, right_s.at[index], right_r.at[index], last_ctx).wait_send()

        return carry

    lax.fori_loop(0, chain_chunks, drain_chain, 0)
    for copy in outputs[:2]:
        copy.wait()
    shallow_tiles = full_up.shape[1] // SPAN

    def tile_loads(tile, parity):
        cols = aligned(tile * SPAN, SPAN)
        return (
            pltpu.make_async_copy(
                full_up.at[:, cols], weight.at[:, aligned(D + parity * SPAN, SPAN)], sem_ff.at[0, parity]
            ),
            pltpu.make_async_copy(full_down.at[cols, :], left.at[parity], sem_ff.at[1, parity]),
        )

    def tile_stores(tile, parity):
        cols = aligned(tile * SPAN, SPAN)
        return [
            pltpu.make_async_copy(
                kv_all.at[pl.ds(0, BLK), aligned(base + parity * SPAN, SPAN)],
                dest.at[:, cols],
                sem_ff.at[2 + place, parity],
            )
            for place, (base, dest) in enumerate(((0, u_out), (D, g_out)))
        ]

    out_load = pltpu.make_async_copy(full_out, weight.at[:, pl.ds(0, D)], sem_in.at[0])
    x_load = pltpu.make_async_copy(x_hbm, right.at[1], sem_in.at[1])
    for copy in (out_load, x_load) + tile_loads(0, 0):
        copy.start()

    def drain_blocks(index, carry):
        rows = aligned(index * BLK, BLK)
        local_wait(a_all.at[rows, :], sem_a.at[index])
        local_wait(kv_all.at[rows, :], sem_kv.at[index])
        return carry

    lax.fori_loop(0, slots + 1, drain_blocks, 0)
    out_load.wait()

    def out_half(index, carry):
        cols = aligned(index * SPAN, SPAN)
        acc[:, cols] = jnp.dot(x_own[...], weight[:, cols], preferred_element_type=jnp.float32)
        return carry

    lax.fori_loop(0, D // SPAN, out_half, 0)
    x_load.wait()
    for copy in outputs[2:]:
        copy.wait()
    dy_load = pltpu.make_async_copy(dy_hbm, x_own, sem_in.at[0])
    dy_load.start()

    def inner_rows(step, carry):
        rows = aligned(step * CHAIN, CHAIN)
        hat, scale = standard_rows(acc[rows, :])
        a_all[rows, :] = hat.astype(jnp.bfloat16)
        sums[0, rows, :] = jnp.broadcast_to(scale, (CHAIN, 128))
        hidden = right[1, rows, :].astype(jnp.float32) + hat * gain_ref[1:2, :] + bias_ref[1:2, :]
        acc[rows, :] = hidden
        hat, scale = standard_rows(hidden)
        a_all[aligned(BLK + step * CHAIN, CHAIN), :] = hat.astype(jnp.bfloat16)
        sums[1, rows, :] = jnp.broadcast_to(scale, (CHAIN, 128))
        q_all[rows, :] = (hat * gain_ref[2:3, :] + bias_ref[2:3, :]).astype(jnp.bfloat16)
        return carry

    lax.fori_loop(0, BLK // CHAIN, inner_rows, 0)
    saves = [
        pltpu.make_async_copy(a_all.at[pl.ds(0, BLK), :], hat1_out, sem_out.at[0]),
        pltpu.make_async_copy(a_all.at[pl.ds(BLK, BLK), :], hat2_out, sem_out.at[1]),
        pltpu.make_async_copy(sums.at[pl.ds(0, 2)], rstd_out, sem_out.at[2]),
        pltpu.make_async_copy(q_all, f_out, sem_out.at[3]),
    ]
    for copy in saves:
        copy.start()

    def ff_tile(tile, carry):
        parity = tile % 2
        for copy in tile_loads(tile, parity):
            copy.wait()

        @pl.when(tile + 1 < shallow_tiles)
        def _():
            for copy in tile_loads(tile + 1, 1 - parity):
                copy.start()

        @pl.when(tile >= 2)
        def _():
            for copy in tile_stores(tile - 2, parity):
                copy.wait()

        upward = jnp.dot(
            q_all[...], weight[:, aligned(D + parity * SPAN, SPAN)], preferred_element_type=jnp.float32
        )
        kv_all[pl.ds(0, BLK), aligned(parity * SPAN, SPAN)] = upward.astype(jnp.bfloat16)
        active = (
            0.5 * upward * (1.0 + jnp.tanh(GELU_C * upward * (1.0 + GELU_A * upward * upward)))
        ).astype(jnp.bfloat16)
        kv_all[pl.ds(0, BLK), aligned(D + parity * SPAN, SPAN)] = active
        for copy in tile_stores(tile, parity):
            copy.start()
        fresh = jnp.dot(active, left[parity], preferred_element_type=jnp.float32)

        @pl.when(tile == 0)
        def _():
            z_acc[...] = fresh

        @pl.when(tile > 0)
        def _():
            z_acc[...] = z_acc[...] + fresh

        return carry

    lax.fori_loop(0, shallow_tiles, ff_tile, 0)
    dy_load.wait()

    def outer_rows(step, carry):
        gain_sum, bias_sum = carry
        rows = aligned(step * CHAIN, CHAIN)
        hat, scale = standard_rows(z_acc[rows, :])
        right[0, rows, :] = (acc[rows, :] + hat * gain_ref[3:4, :] + bias_ref[3:4, :]).astype(jnp.bfloat16)
        upstream = x_own[rows, :].astype(jnp.float32)
        a_all[aligned(2 * BLK + step * CHAIN, CHAIN), :] = row_back(
            upstream, hat, scale, gain_ref[3:4, :]
        ).astype(jnp.bfloat16)
        return gain_sum + column_sum(upstream * hat), bias_sum + column_sum(upstream)

    zero = jnp.zeros((1, D), jnp.float32)
    gain_sum, bias_sum = lax.fori_loop(0, BLK // CHAIN, outer_rows, (zero, zero))
    row = lax.broadcasted_iota(jnp.int32, (8, D), 0)
    norm_v[...] = jnp.where(row == 3, gain_sum, 0.0) + jnp.where(row == 7, bias_sum, 0.0)
    ends = [
        pltpu.make_async_copy(right.at[0], y_out, sem_in.at[0]),
        pltpu.make_async_copy(a_all.at[pl.ds(2 * BLK, BLK), :], dz_out, sem_in.at[1]),
        pltpu.make_async_copy(norm_v, norm_out, sem_in.at[2]),
    ]
    for copy in ends:
        copy.start()
    for tile in range(shallow_tiles - 2, shallow_tiles):
        for copy in tile_stores(tile, tile % 2):
            copy.wait()
    for copy in saves + ends:
        copy.wait()


def forward_part(n_ctx, tags, gains, biases, raw, dy, w_qkv, w_out, w_up, w_down):
    slots = n_ctx // 2
    every = (slots + 1) * BLK
    low, full = jnp.bfloat16, jnp.float32
    dma = pltpu.SemaphoreType.DMA
    hbm = pl.BlockSpec(memory_space=pl.ANY)
    vmem = pl.BlockSpec(memory_space=pltpu.VMEM)
    shards = (w_qkv, w_out, w_up, w_down)
    pieces = sum(w.shape[0] * w.shape[1] // (2 * PIECE * SPAN) for w in shards)
    own = w_qkv.shape[1] // SPAN + 3
    chain = slots * (BLK // CHAIN)
    shape = jax.ShapeDtypeStruct
    return pl.pallas_call(
        functools.partial(forward_kernel, n_ctx),
        out_shape=[
            shape((every, D), low),
            shape((BLK, D), low),
            shape((every, 2 * D), low),
            shape((BLK, D), low),
            shape((PAIRS, BLK, 128), full),
        ]
        + [shape((4 * w.shape[0], w.shape[1]), low) for w in shards]
        + [
            shape((BLK, D), low),
            shape((BLK, w_up.shape[1]), low),
            shape((BLK, D), low),
            shape((BLK, D), low),
            shape((BLK, w_up.shape[1]), low),
            shape((BLK, D), low),
            shape((BLK, D), low),
            shape((2, BLK, 128), full),
            shape((8, D), full),
        ],
        in_specs=[pl.BlockSpec(memory_space=pltpu.SMEM), vmem, vmem] + [hbm] * 6,
        out_specs=[hbm] * 18,
        scratch_shapes=[
            pltpu.VMEM((BLK, D), low),
            pltpu.VMEM((slots, BLK, D), low),
            pltpu.VMEM((slots, BLK, D), low),
            pltpu.VMEM((every, D), low),
            pltpu.VMEM((BLK, D), low),
            pltpu.VMEM((every, 2 * D), low),
            pltpu.VMEM((D, 3 * D), low),
            pltpu.VMEM((BLK, D), full),
            pltpu.VMEM((BLK, D), full),
            pltpu.VMEM((8, D), full),
            pltpu.VMEM((PAIRS, BLK, 128), full),
            pltpu.VMEM((PAIRS, BLK, 128), full),
            pltpu.VMEM((3, 2 * PIECE, SPAN), low),
            dma((3,)),
            dma((3,)),
            dma((3,)),
            dma((4, 2)),
            dma((4,)),
            dma((slots + 1,)),
            dma((slots + 1,)),
        ]
        + [dma((pieces,))] * 8
        + [dma((own,))] * 2
        + [dma((chain,))] * 4,
        compiler_params=pltpu.CompilerParams(
            collective_id=1, has_side_effects=True, vmem_limit_bytes=67043328
        ),
        cost_estimate=pl.CostEstimate(flops=20 << 30, bytes_accessed=64 << 20, transcendentals=1 << 24),
        name="gather_attend",
    )(tags, gains, biases, raw, dy, *shards)


TILE = 256
PAIRED = 2


def grad_block(q_ref, do_ref, o_ref, lse_ref, kv_ref, dq_acc, turned, pair, own, visible):
    lanes = aligned(pair * 128, 128)
    value_lanes = aligned(D + pair * 128, 128)
    size = QT if own else BLK
    count = BLK // size
    q_pair, do_pair, lse_pair = q_ref[:, lanes], do_ref[:, lanes], lse_ref[pair]
    prod = do_pair.astype(jnp.float32) * o_ref[:, lanes].astype(jnp.float32)
    keys, values = kv_ref[:, lanes], kv_ref[:, value_lanes]
    q_turned, do_turned = q_pair.T, do_pair.T
    old_dq = dq_acc[:, lanes]
    causal = causal_tile()
    hide = 0.0 if own else jnp.where(visible, 0.0, 1e30)
    lanes_of = [head_lanes(head, size) for head in range(2)]
    work = [(tile, head) for tile in range(count) for head in range(2)]
    score, dprob, dlogit, prob_low = {}, {}, {}, {}
    for tile, head in work:
        rows = slice(tile * size, (tile + 1) * size)
        span = (tile + 1) * size if own else BLK
        zero = jnp.zeros((size, 128), jnp.bfloat16)
        score[tile, head] = contract_last(jnp.where(lanes_of[head], q_pair[rows], zero), keys[:span])
        dprob[tile, head] = contract_last(jnp.where(lanes_of[head], do_pair[rows], zero), values[:span])
    for tile, head in work:
        rows = slice(tile * size, (tile + 1) * size)
        delta = jnp.sum(jnp.where(lanes_of[head], prod[rows], 0.0), axis=-1, keepdims=True)
        shift = lse_pair[rows, head * DH : head * DH + 1] + hide
        prob = jnp.exp2(score[tile, head] * C2 - shift)
        if own:
            diag = jnp.where(causal, prob[:, tile * size :], 0.0)
            prob = jnp.concatenate([prob[:, : tile * size], diag], axis=1) if tile else diag
        dlogit[tile, head] = (prob * (dprob[tile, head] - delta)).astype(jnp.bfloat16)
        prob_low[tile, head] = prob.astype(jnp.bfloat16)
    for tile in range(count):
        rows = slice(tile * size, (tile + 1) * size)
        span = (tile + 1) * size if own else BLK
        parts = [dot_dims(dlogit[tile, head], keys[:span], 1, 0) for head in range(2)]
        dq_acc[pl.ds(tile * size, size), lanes] = old_dq[rows] + jnp.where(lanes_of[0], parts[0], parts[1])
    for head in range(2):
        for offset, left_side, right_side, scale in (
            (0, q_turned, dlogit, ALPHA),
            (D, do_turned, prob_low, 1.0),
        ):
            spot = aligned(offset + pair * 128 + head * DH, DH)
            left_head = left_side[head * DH : (head + 1) * DH]
            terms = [
                dot_dims(left_head[:, tile * size : (tile + 1) * size], right_side[tile, head], 1, 0)
                for tile in range(count)
            ]
            for tile in range(count):
                cols = slice(tile * size, (tile + 1) * size)
                total = functools.reduce(
                    jnp.add, [terms[other][:, cols] for other in range(tile, count)]
                ) if own else terms[0]
                turned[spot, cols if own else slice(None)] = (total * scale).astype(jnp.bfloat16)


def backward_kernel(n_ctx, widths, *refs):
    slots = n_ctx // 2
    levels = n_ctx.bit_length() - 1
    depth = 16 if n_ctx == 4 else 10
    shallow = slots <= 2
    (slot_ref, gain_ref, bias_ref, norm_ref, x_hbm, q_hbm, kv_hbm, a_hbm, o_hbm, lse_hbm, w_hbm) = refs[:11]
    (w_out, w_up, w_down, g_hbm, dz_hbm, f_hbm, u_hbm, hat1_hbm, hat2_hbm, rstd_hbm, dy_hbm) = refs[11:22]
    outs = refs[22:26]
    grad_out, norm_out, dh_hbm, du_hbm, datt_hbm = refs[26:31]
    scratch = list(refs[31:])
    own_slot = slot_ref[1] // BLK

    def take(count):
        taken = scratch[:count]
        del scratch[:count]
        return taken

    q_v, o_v, do_v, lse_v, weight, kv_b, a_b, dq_acc, turned, gkv, term, own_part, left, right, norm_v, norm_in, gain_sum, bias_sum = take(18)
    r1, r2, r3, fin, made = take(5)
    lhs, rhs = take(2)
    zbufs = take(levels)
    sem_in, sem_blk, sem_rhs, sem_lhs, sem_ff, sem_out, sem_res = take(7)
    send1, recv1, send2, recv2, send3, recv3, send6, recv6 = take(8)
    rs_send, rs_recv, ag_send, ag_recv = take(levels), take(levels), take(levels), take(levels)
    left_s, left_r, right_s, right_r, norm_s, norm_r = take(6)
    grp, ctx, wsh = lax.axis_index("grp"), lax.axis_index("ctx"), lax.axis_index("wsh")
    side, core = wsh // 2, wsh % 2
    core_peer = (grp, ctx, side * 2 + 1 - core)
    side_peer = (grp, ctx, (1 - side) * 2 + core)
    grp_peer = (1 - grp, ctx, wsh)
    next_ctx = (grp, lax.rem(ctx + 1, n_ctx), wsh)
    last_ctx = (grp, lax.rem(ctx + n_ctx - 1, n_ctx), wsh)
    bits = [(ctx // (1 << level)) % 2 for level in range(levels)]
    level_peers = [(grp, ctx + (1 - 2 * bits[level]) * (1 << level), wsh) for level in range(levels)]

    def block_copies(index):
        rows = aligned(lax.rem(index, slots + 1) * BLK, BLK)
        slot = lax.rem(index, kv_b.shape[0])
        a_slot = index - 1 if shallow else 0
        return (
            pltpu.make_async_copy(kv_hbm.at[rows, :], kv_b.at[slot], sem_blk.at[0, slot]),
            pltpu.make_async_copy(a_hbm.at[rows, :], a_b.at[a_slot], sem_blk.at[1, slot]),
        )

    barrier = pltpu.get_barrier_semaphore()
    peers = [core_peer, side_peer, grp_peer, next_ctx, last_ctx] + level_peers
    for peer in peers:
        pl.semaphore_signal(barrier, inc=1, device_id=peer, device_id_type=MESH)

    half = TILE // 2
    ranges, first = [], 0
    for rows, cols in widths:
        across = cols // TILE
        ranges.append((first, first + (rows // TILE) * across, across))
        first = ranges[-1][1]
    chunks = first

    def by_range(index, act):
        for place, (low, high, across) in enumerate(ranges):

            @pl.when((index >= low) & (index < high))
            def _(place=place, low=low, across=across):
                number = index - low
                act(place, (aligned((number // across) * TILE, TILE), aligned((number % across) * TILE, TILE)))

    def region(level, flip):
        row, rows, col, cols = 0, half, 0, TILE
        for place in range(level):
            bit = 1 - bits[place] if (flip and place == level - 1) else bits[place]
            if rows > 16:
                rows = rows // 2
                row = row + bit * rows
            else:
                cols = cols // 2
                col = col + bit * cols
        return row, rows, col, cols

    def spot(level, flip=False, base=0):
        row, rows, col, cols = region(level, flip)
        return aligned(base + row, rows), aligned(col, cols)

    last_low = ranges[-1][0]
    dq_low = o_v
    set_of = [(0, number) for number in range(widths[0][0] // TILE)] + [(1, 0), (2, 0)]
    set_first = [number * ranges[0][2] for number in range(widths[0][0] // TILE)]
    set_first += [ranges[1][0], ranges[2][0]]
    left_of, right_of = (g_hbm, f_hbm, o_hbm), (dz_hbm, du_hbm, datt_hbm)

    def set_copies(number):
        place, group = set_of[number]
        stride = left_of[place].shape[1] // 4
        return [
            pltpu.make_async_copy(
                left_of[place].at[:, pl.ds(owner * stride + group * TILE, TILE)],
                lhs.at[number % 2, owner],
                sem_lhs.at[number % 2, owner],
            )
            for owner in range(4)
        ]

    def step_fetch(index):
        near = lax.rem(index, 4)

        def act(place, span):
            if place < 3:
                pltpu.make_async_copy(
                    right_of[place].at[:, span[1]], rhs.at[near], sem_rhs.at[near]
                ).start()

        by_range(index, act)

    def step_make(index, kinds):
        slot = lax.rem(index, depth)
        near = lax.rem(index, 4)

        def low_piece():
            local_wait(rhs.at[near], sem_rhs.at[near])
            parity = jnp.int32(0)
            for number, low in enumerate(set_first):
                parity = jnp.where(index >= low, number % 2, parity)

                @pl.when(index == low)
                def _(number=number):
                    for copy in set_copies(number):
                        copy.wait()
                    if number + 1 < len(set_first):
                        for copy in set_copies(number + 1):
                            copy.start()

            right_side = rhs[near]
            for owner in range(4):
                made[near, owner // 2, owner % 2] = dot_dims(
                    lhs[parity, owner], right_side, 0, 0
                ).astype(jnp.bfloat16)

        def high_piece():
            number = index - last_low
            if not shallow:
                made[near] = term[:, :, :, aligned(number * TILE, TILE)]
                return

            @pl.when(number < D // TILE)
            def _():
                right_side = dq_low[:, aligned(number * TILE, TILE)]
                for owner in range(4):
                    made[near, owner // 2, owner % 2] = dot_dims(
                        a_b[slots, :, pl.ds(owner * TILE, TILE)], right_side, 0, 0
                    ).astype(jnp.bfloat16)

            @pl.when(number >= D // TILE)
            def _():
                cols = aligned((number - D // TILE) * TILE, TILE)
                for owner in range(4):
                    total = functools.reduce(
                        jnp.add,
                        [
                            dot_dims(a_b[block, :, pl.ds(owner * TILE, TILE)], turned[block, cols, :], 0, 1)
                            for block in range(slots + 1)
                        ],
                    )
                    made[near, owner // 2, owner % 2] = total.astype(jnp.bfloat16)

        if kinds == "low":
            low_piece()
        elif kinds == "high":
            high_piece()
        else:
            pl.when(index < last_low)(low_piece)
            pl.when(index >= last_low)(high_piece)
        remote(
            made.at[near, :, 1 - core], r1.at[slot], send1.at[slot], recv1.at[slot], core_peer
        ).start()

    def finished(move):
        move.wait_send()
        move.wait_recv()

    def step_core(index):
        slot, near = lax.rem(index, depth), lax.rem(index, 4)
        finished(remote(r1.at[slot], r1.at[slot], send1.at[slot], recv1.at[slot], core_peer))
        r1[slot] = r1[slot] + made[near, :, core]
        remote(r1.at[slot, 1 - side], r2.at[slot], send2.at[slot], recv2.at[slot], side_peer).start()

    keep_half = aligned(grp * half, half)
    give_half = aligned((1 - grp) * half, half)

    def step_side(index):
        slot = lax.rem(index, depth)
        finished(remote(r1.at[slot, 1 - side], r2.at[slot], send2.at[slot], recv2.at[slot], side_peer))
        r2[slot] = r2[slot] + r1[slot, side]
        remote(r2.at[slot, give_half], r3.at[slot], send3.at[slot], recv3.at[slot], grp_peer).start()

    fold = n_ctx == 4
    if fold:
        outer = bits[0] == bits[1]
        inner = bits[0] != bits[1]
        mate, middle = level_peers[0], (grp, 3 - ctx, wsh)
        quarter = half // 2
        mine, other = aligned(bits[1] * quarter, quarter), aligned((1 - bits[1]) * quarter, quarter)
        fin_mine = aligned(grp * half + bits[1] * quarter, quarter)
        fin_other = aligned(grp * half + (1 - bits[1]) * quarter, quarter)

        def up_copy(slot):
            return remote(r3.at[slot], zbufs[0].at[slot], rs_send[0].at[slot], rs_recv[0].at[slot], mate)

        def cross_copy(slot):
            return remote(
                r3.at[slot, other], zbufs[1].at[slot], rs_send[1].at[slot], rs_recv[1].at[slot], middle
            )

        def share_copy(slot, rows):
            here = fin.at[slot, rows]
            return remote(here, here, ag_send[1].at[slot], ag_recv[1].at[slot], middle)

        def down_copy(slot):
            here = fin.at[slot, keep_half]
            return remote(here, here, ag_send[0].at[slot], ag_recv[0].at[slot], mate)

        def step_up(index):
            slot = lax.rem(index, depth)

            @pl.when(outer)
            def _():
                up_copy(slot).wait_send()

            @pl.when(inner)
            def _():
                up_copy(slot).wait_recv()
                r3[slot] = r3[slot] + zbufs[0][slot]
                cross_copy(slot).start()

        def step_cross(index):
            slot = lax.rem(index, depth)

            @pl.when(inner)
            def _():
                finished(cross_copy(slot))
                fin[slot, fin_mine] = r3[slot, mine] + zbufs[1][slot]
                share_copy(slot, fin_mine).start()

        def step_share(index):
            slot = lax.rem(index, depth)

            @pl.when(inner)
            def _():
                finished(share_copy(slot, fin_other))
                down_copy(slot).start()

        def step_down(index):
            slot = lax.rem(index, depth)

            @pl.when(inner)
            def _():
                down_copy(slot).wait_send()

            @pl.when(outer)
            def _():
                down_copy(slot).wait_recv()

            back_copy(slot, keep_half).start()

    def rs_copy(level, slot):
        rows, cols = spot(level + 1, True)
        return remote(
            r3.at[slot, rows, cols], zbufs[level].at[slot], rs_send[level].at[slot], rs_recv[level].at[slot], level_peers[level]
        )

    def ag_copy(level, slot, flip=False):
        rows, cols = spot(level + 1, flip, grp * half)
        here = fin.at[slot, rows, cols]
        return remote(here, here, ag_send[level].at[slot], ag_recv[level].at[slot], level_peers[level])

    def back_copy(slot, rows):
        here = fin.at[slot, rows]
        return remote(here, here, send6.at[slot], recv6.at[slot], grp_peer)

    def step_grp(index):
        slot = lax.rem(index, depth)
        finished(remote(r2.at[slot, give_half], r3.at[slot], send3.at[slot], recv3.at[slot], grp_peer))
        r3[slot] = r3[slot] + r2[slot, keep_half]
        if fold:

            @pl.when(outer)
            def _():
                up_copy(slot).start()
        else:
            rs_copy(0, slot).start()

    def step_scatter(level):
        def act(index):
            slot = lax.rem(index, depth)
            finished(rs_copy(level, slot))
            rows, cols = spot(level + 1)
            total = r3[slot, rows, cols] + zbufs[level][slot]
            if level + 1 < levels:
                r3[slot, rows, cols] = total
                rs_copy(level + 1, slot).start()
            else:
                rows, cols = spot(level + 1, False, grp * half)
                fin[slot, rows, cols] = total
                ag_copy(level, slot).start()

        return act

    def step_gather(level):
        def act(index):
            slot = lax.rem(index, depth)
            finished(ag_copy(level, slot, True))
            if level:
                ag_copy(level - 1, slot).start()
            else:
                back_copy(slot, keep_half).start()

        return act

    def out_wait(index):
        slot = lax.rem(index, depth)
        local_wait(fin.at[slot], sem_out.at[slot])

    def step_out(index):
        slot = lax.rem(index, depth)
        finished(back_copy(slot, give_half))

        def act(place, span):
            pltpu.make_async_copy(fin.at[slot], outs[place].at[span[0], span[1]], sem_out.at[slot]).start()

        by_range(index, act)

    z_lag = 2 if fold else 1
    order = [(YLAG, step_side), (XLAG, step_grp)]
    if fold:
        order += [(z_lag, act) for act in (step_up, step_cross, step_share, step_down)]
    else:
        order += [(z_lag, step_scatter(level)) for level in range(levels)]
        order += [(z_lag, step_gather(level)) for level in reversed(range(levels))]
    order += [(BLAG, step_out), (2, out_wait)]
    stages = [(0, step_core)]
    for lag, act in order:
        stages.append((stages[-1][0] + lag, act))
    all_ticks = chunks + stages[-1][0]

    per_slot = BLK // CHAIN
    chain_chunks = slots * per_slot

    def chain_step(stream, send, recv, number, is_first, is_last, target):
        slot = number // per_slot
        rows = aligned((number % per_slot) * CHAIN, CHAIN)
        here = stream.at[slot, rows]

        @pl.when(is_first)
        def _():
            stream[slot, rows, :] = own_part[slot, rows, :]

        @pl.when(jnp.logical_not(is_first))
        def _():
            remote(here, here, send.at[number], recv.at[number], target).wait_recv()
            stream[slot, rows, :] = stream[slot, rows, :] + own_part[slot, rows, :]

        @pl.when(jnp.logical_not(is_last))
        def _():
            remote(here, here, send.at[number], recv.at[number], target).start()

    def chain_tick(step):
        number = step - ctx

        @pl.when((number >= 0) & (number < chain_chunks))
        def _():
            chain_step(left, left_s, left_r, number, ctx == 0, ctx == n_ctx - 1, next_ctx)

        back = step - (n_ctx - 1 - ctx)

        @pl.when((back >= 0) & (back < chain_chunks))
        def _():
            chain_step(right, right_s, right_r, back, ctx == n_ctx - 1, ctx == 0, last_ctx)

    groups = PAIRS // PAIRED
    group_ticks = groups if shallow else 0
    block_ticks = group_ticks + 2
    chain_first = FF_TICKS + block_ticks
    paced = max(0, -(-(chunks - chain_first) // PACE))
    late_first = max(chunks, chain_first)
    late_beats = max(0, chain_chunks + n_ctx - 1 - paced)
    chain_ticks = late_first + TAIL_PACE * max(0, late_beats - 1) + 1

    def tick(step, kinds):
        kinds = kinds if shallow or kinds == "none" else "both"
        if kinds in ("low", "both"):

            @pl.when(step + 3 < chunks)
            def _():
                step_fetch(step + 3)

        if kinds != "none":

            @pl.when(step + 2 < chunks)
            def _():
                step_make(step + 2, kinds)

        for lag, act in stages:
            index = step - lag

            @pl.when((index >= 0) & (index < chunks))
            def _(act=act, index=index):
                act(index)

        beat = step - chain_first

        @pl.when((beat >= 0) & (step < chunks) & (beat % PACE == 0))
        def _():
            chain_tick(beat // PACE)

        late = step - late_first

        @pl.when((late >= 0) & (late % TAIL_PACE == 0))
        def _():
            chain_tick(paced + late // TAIL_PACE)


    for index in range(3):
        step_fetch(jnp.int32(index))
    for copy in set_copies(0):
        copy.start()

    hidden_tiles = u_hbm.shape[1] // SPAN
    datt_v, dz_v, dy_v, hat1_v, hat2_v = own_part.at[0], do_v, left.at[1], right.at[0], right.at[1]

    def tile_copies(tile, parity):
        cols = aligned(tile * SPAN, SPAN)
        return (
            pltpu.make_async_copy(w_down.at[cols, :], own_part.at[parity], sem_ff.at[0, parity]),
            pltpu.make_async_copy(
                w_up.at[:, cols], turned.at[0, aligned(parity * D, D), :], sem_ff.at[1, parity]
            ),
            pltpu.make_async_copy(
                u_hbm.at[:, cols], left.at[0, :, aligned(parity * SPAN, SPAN)], sem_ff.at[2, parity]
            ),
        )

    def du_store(tile, parity):
        return pltpu.make_async_copy(
            kv_b.at[0, :, aligned(parity * SPAN, SPAN)],
            du_hbm.at[:, aligned(tile * SPAN, SPAN)],
            sem_ff.at[3, parity],
        )

    dz_load = pltpu.make_async_copy(dz_hbm, dz_v, sem_in.at[0])
    dz_load.start()
    for copy in tile_copies(0, 0):
        copy.start()
    wide_loads = [
        pltpu.make_async_copy(source, dest, sem_in.at[place + 1])
        for place, (source, dest) in enumerate(
            (
                (dy_hbm, dy_v),
                (hat1_hbm, hat1_v),
                (hat2_hbm, hat2_v),
                (rstd_hbm, lse_v.at[pl.ds(0, 2)]),
                (q_hbm, q_v),
                (o_hbm, o_v),
                (w_hbm, weight),
            )
        )
    ]
    out_loads = [
        pltpu.make_async_copy(
            w_out.at[pl.ds(place * TILE, TILE), :],
            term.at[place // 2, place % 2, :, pl.ds(0, D)],
            sem_in.at[8 + place],
        )
        for place in range(4)
    ]
    pl.semaphore_wait(barrier, len(peers))
    lax.fori_loop(0, 2, lambda index, carry: (step_make(index, "low"), carry)[1], 0)
    dz_load.wait()

    def ff_tile(tile, carry):
        start = tile + (tile + 1) // 2
        extra = jnp.where((tile % 2 == 0) | (tile + 1 == hidden_tiles), 1, 0)
        lax.fori_loop(start, start + 1 + extra, lambda index, inner: (tick(index, "low"), inner)[1], 0)

        parity = tile % 2
        for copy in tile_copies(tile, parity):
            copy.wait()

        @pl.when(tile + 1 < hidden_tiles)
        def _():
            for copy in tile_copies(tile + 1, 1 - parity):
                copy.start()

        @pl.when(tile == 0)
        def _():
            for copy in wide_loads + out_loads:
                copy.start()

        @pl.when(tile >= 2)
        def _():
            du_store(tile - 2, parity).wait()

        u_cols = aligned(parity * SPAN, SPAN)
        u_tile = left[0, :, u_cols].astype(jnp.float32)
        square = u_tile * u_tile
        bend = jnp.tanh(GELU_C * u_tile * (1.0 + GELU_A * square))
        slope = 0.5 * (1.0 + bend) + (0.5 * GELU_C) * u_tile * (1.0 - bend * bend) * (
            1.0 + 3.0 * GELU_A * square
        )
        du_tile = (contract_last(dz_v[...], own_part[parity]) * slope).astype(jnp.bfloat16)
        kv_b[0, :, u_cols] = du_tile
        du_store(tile, parity).start()
        fresh = contract_last(du_tile, turned[0, aligned(parity * D, D), :])

        @pl.when(tile == 0)
        def _():
            dq_acc[...] = fresh

        @pl.when(tile > 0)
        def _():
            dq_acc[...] = dq_acc[...] + fresh

        return carry

    lax.fori_loop(0, hidden_tiles, ff_tile, 0)
    for tile in range(hidden_tiles - 2, hidden_tiles):
        du_store(tile, tile % 2).wait()
    for copy in wide_loads:
        copy.wait()
    for copy in block_copies(1):
        copy.start()

    def hidden_back(step, carry):
        gain1, gain2, bias1, bias2 = carry
        rows = aligned(step * CHAIN, CHAIN)
        upstream = dq_acc[rows, :]
        hat = hat2_v[rows, :].astype(jnp.float32)
        grad_h = dy_v[rows, :].astype(jnp.float32) + row_back(
            upstream, hat, lse_v[1, rows, 0:1], gain_ref[2:3, :]
        )
        gain2, bias2 = gain2 + column_sum(upstream * hat), bias2 + column_sum(upstream)
        dq_acc[rows, :] = grad_h
        if shallow:
            gkv[rows, :] = grad_h
        hat = hat1_v[rows, :].astype(jnp.float32)
        datt_v[rows, :] = row_back(grad_h, hat, lse_v[0, rows, 0:1], gain_ref[1:2, :]).astype(
            jnp.bfloat16
        )
        return gain1 + column_sum(grad_h * hat), gain2, bias1 + column_sum(grad_h), bias2

    zero = jnp.zeros((1, D), jnp.float32)
    sums = lax.fori_loop(0, BLK // CHAIN, hidden_back, (zero,) * 4)
    row = lax.broadcasted_iota(jnp.int32, (8, D), 0)
    norm_v[...] = norm_ref[...]
    for place, value in zip((1, 2, 5, 6), sums):
        norm_v[...] = norm_v[...] + jnp.where(row == place, value, 0.0)
    stores = [
        pltpu.make_async_copy(dq_acc, dh_hbm, sem_res.at[0]),
        pltpu.make_async_copy(datt_v, datt_hbm, sem_res.at[1]),
    ]
    lse_load = pltpu.make_async_copy(lse_hbm, lse_v, sem_in.at[0])
    for copy in stores + [lse_load]:
        copy.start()
    for load in out_loads:
        load.wait()

    def out_back(place, carry):
        do_v[:, aligned(place * TILE, TILE)] = contract_last(
            datt_v[...], term[place // 2, place % 2, :, pl.ds(0, D)]
        ).astype(jnp.bfloat16)
        return carry

    lax.fori_loop(0, 4, out_back, 0)
    for copy in stores + [lse_load]:
        copy.wait()
    dq_acc[...] = jnp.zeros_like(dq_acc)

    def attend(kv_ref, turned_ref, own, visible, begin):
        def body(group, carry):
            if shallow:
                tick(begin + group, "low")
            for member in range(PAIRED):
                grad_block(
                    q_v, do_v, o_v, lse_v, kv_ref, dq_acc, turned_ref, group * PAIRED + member, own, visible
                )
            return carry

        lax.fori_loop(0, groups, body, 0)

    def first_sums(piece, normed, cols):
        gain_sum[:, cols] = gain_sum[:, cols] + column_sum(piece * normed.astype(jnp.float32))
        bias_sum[:, cols] = bias_sum[:, cols] + column_sum(piece)

    gain_sum[...] = jnp.zeros_like(gain_sum)
    bias_sum[...] = jnp.zeros_like(bias_sum)

    def each_slot(slot, carry):
        visible = slot < own_slot
        index = slot + 1
        place = lax.rem(index, kv_b.shape[0])
        for copy in block_copies(index):
            copy.wait()
        if kv_b.shape[0] > 1:
            for copy in block_copies(index + 1):
                copy.start()
        begin = FF_TICKS + slot * block_ticks
        a_place = slot if shallow else 0
        attend(kv_b.at[place], turned.at[a_place], False, visible, begin)

        def weight_terms(step, inner):
            tick(begin + group_ticks + step, "low")
            rows = aligned(step * 512, 512)
            for part in range(0 if shallow else 2):
                cols = pl.ds(part * D, D)
                product = dot_dims(a_b[a_place, :, rows], turned[a_place, cols, :], 0, 1)
                for down in range(2):
                    target = term.at[step, down, :, pl.ds((part + 1) * D, D)]
                    piece = product[down * TILE : (down + 1) * TILE]

                    @pl.when(slot == 0)
                    def _(target=target, piece=piece):
                        target[...] = piece.astype(target.dtype)

                    @pl.when(slot > 0)
                    def _(target=target, piece=piece):
                        target[...] = (target[...] + piece).astype(target.dtype)

            piece = dot_dims(turned[a_place], weight[rows, pl.ds(D, 2 * D)], 0, 1)
            own_part[slot, :, rows] = piece.astype(jnp.bfloat16)
            first_sums(piece, a_b[a_place, :, rows], rows)
            return inner

        lax.fori_loop(0, 2, weight_terms, 0)
        if kv_b.shape[0] == 1:
            for copy in block_copies(index + 1):
                copy.start()
        return carry

    lax.fori_loop(0, slots, each_slot, 0)
    begin = FF_TICKS + slots * block_ticks
    own_place = (slots + 1) % kv_b.shape[0]
    for copy in block_copies(slots + 1):
        copy.wait()
    own_a = slots if shallow else 0
    attend(kv_b.at[own_place], turned.at[own_a], True, None, begin)
    dq_low[...] = (dq_acc[...] * ALPHA).astype(jnp.bfloat16) * jnp.bfloat16(QSCALE)
    x_load = pltpu.make_async_copy(x_hbm, do_v, sem_in.at[0])
    x_load.start()
    ready = begin + group_ticks

    def last_terms(step, carry):
        tick(begin + group_ticks + step, "both")
        rows = aligned(step * TILE, TILE)
        a_rows = a_b[0, :, rows]
        up, down = step // 2, step % 2
        term[up, down, :, pl.ds(0, D)] = dot_dims(a_rows, dq_low[...], 0, 0).astype(jnp.bfloat16)
        for part in range(2):
            cols = pl.ds(part * D, D)
            target = term.at[up, down, :, pl.ds((part + 1) * D, D)]
            target[...] = (target[...] + dot_dims(a_rows, turned[0, cols, :], 0, 1)).astype(jnp.bfloat16)
        return carry

    if not shallow:
        lax.fori_loop(0, 4, last_terms, 0)
        ready = ready + 4
    assert ready <= last_low - 2
    da_acc = dq_acc

    spare = max(0, last_low - 2 - ready - 4) if shallow else 0

    def own_grad(step, carry):
        if shallow:
            begins = ready + step + jnp.where(step > 0, spare, 0)
            ends = ready + step + 1 + spare
            lax.fori_loop(begins, ends, lambda index, inner: (tick(index, "low"), inner)[1], 0)
        else:
            tick(ready + step, "low")
        rows = aligned(step * TILE, TILE)
        piece = dot_dims(dq_low[...], weight[rows, pl.ds(0, D)], 1, 1) + dot_dims(
            turned[own_a], weight[rows, pl.ds(D, 2 * D)], 0, 1
        )
        da_acc[:, rows] = piece
        first_sums(piece, a_b[own_a, :, rows], rows)
        return carry

    lax.fori_loop(0, 4, own_grad, 0)
    ready = ready + 4 + spare

    first_gain = (gain_sum[...] - bias_ref[0:1, :] * bias_sum[...]) / gain_ref[0:1, :]
    norm_v[...] = (
        norm_v[...] + jnp.where(row == 0, first_gain, 0.0) + jnp.where(row == 4, bias_sum[...], 0.0)
    )

    def run_ticks(first, last, kinds):
        if last > first:
            lax.fori_loop(first, last, lambda index, carry: (tick(index, kinds), carry)[1], 0)
        return max(first, last)

    assert ready == last_low - 2 or not shallow
    norm_peers = [core_peer, side_peer, grp_peer] + level_peers
    norm_base = ready
    norm_result = pltpu.make_async_copy(norm_v, norm_out, sem_res.at[1])

    def norm_move(place):
        return remote(norm_v, norm_in.at[place], norm_s.at[place], norm_r.at[place], norm_peers[place])

    def norm_ticks(step, carry):
        for place in range(len(norm_peers) + 1):

            @pl.when(step == norm_base + 3 * place)
            def _(place=place):
                if place:
                    finished(norm_move(place - 1))
                    norm_v[...] = norm_v[...] + norm_in[place - 1]
                if place < len(norm_peers):
                    norm_move(place).start()
                else:
                    norm_result.start()

        tick(step, "high")
        return carry

    last_tick = max(ready + 3 * len(norm_peers) + 1, chain_ticks)
    lax.fori_loop(ready, last_tick, norm_ticks, 0)
    ready = last_tick
    x_load.wait()
    gain = gain_ref[0:1, :]

    def norm_grad(step, carry):
        @pl.when(step % 2 == 0)
        def _():
            tick(ready + step // 2, "none")

        rows = aligned(step * CHAIN, CHAIN)
        upstream = da_acc[rows, :]
        for slot in range(slots):
            joined = left[slot, rows, :].astype(jnp.float32) + right[slot, rows, :].astype(jnp.float32)
            upstream = upstream + jnp.where(own_slot == slot, joined, 0.0)
        values = do_v[rows, :].astype(jnp.float32)
        centre = values - jnp.mean(values, axis=-1, keepdims=True)
        scale = lax.rsqrt(jnp.mean(centre * centre, axis=-1, keepdims=True) + EPS)
        centre = centre * scale
        grad = row_back(upstream, centre, scale, gain)
        da_acc[rows, :] = grad + gkv[rows, :] if shallow else grad
        return carry

    lax.fori_loop(0, BLK // CHAIN, norm_grad, 0)
    ready = ready + BLK // CHAIN // 2
    result = pltpu.make_async_copy(da_acc, grad_out, sem_res.at[0])
    result.start()
    run_ticks(ready, all_ticks, "none")

    def drain_chain(index, carry):
        here = left.at[0, pl.ds(0, CHAIN)]

        @pl.when(ctx < n_ctx - 1)
        def _():
            remote(here, here, left_s.at[index], left_r.at[index], next_ctx).wait_send()

        @pl.when(ctx > 0)
        def _():
            remote(here, here, right_s.at[index], right_r.at[index], last_ctx).wait_send()

        return carry

    lax.fori_loop(0, chain_chunks, drain_chain, 0)
    result.wait()
    norm_result.wait()


def backward_part(n_ctx, slot_vec, gains, biases, norms, saved, weights, ffn):
    slots = n_ctx // 2
    levels = n_ctx.bit_length() - 1
    depth = 16 if n_ctx == 4 else 10
    hidden = weights[1].shape[1]
    widths = [(hidden // 4, D), (D // 4, hidden), (D // 4, D), (D // 4, 3 * D)]
    low, full = jnp.bfloat16, jnp.float32
    dma = pltpu.SemaphoreType.DMA
    hbm = pl.BlockSpec(memory_space=pl.ANY)
    vmem = pl.BlockSpec(memory_space=pltpu.VMEM)
    shape = jax.ShapeDtypeStruct
    buffers = 2 if slots <= 2 else 1
    chain = slots * (BLK // CHAIN)
    zshapes, rows, cols = [], TILE // 2, TILE
    if n_ctx == 4:
        zshapes = [pltpu.VMEM((depth, rows, cols), low), pltpu.VMEM((depth, rows // 2, cols), low)]
    for _ in range(0 if zshapes else levels):
        rows, cols = (rows // 2, cols) if rows > 16 else (rows, cols // 2)
        zshapes.append(pltpu.VMEM((depth, rows, cols), low))
    return pl.pallas_call(
        functools.partial(backward_kernel, n_ctx, widths),
        out_shape=[shape(width, low) for width in widths] + [
            shape((BLK, D), full),
            shape((8, D), full),
            shape((BLK, D), full),
            shape((BLK, hidden), low),
            shape((BLK, D), low),
        ],
        in_specs=[pl.BlockSpec(memory_space=pltpu.SMEM), vmem, vmem, vmem]
        + [hbm] * (len(saved) + len(weights) + len(ffn)),
        out_specs=[hbm] * 9,
        scratch_shapes=[
            pltpu.VMEM((BLK, D), low),
            pltpu.VMEM((BLK, D), low),
            pltpu.VMEM((BLK, D), low),
            pltpu.VMEM((PAIRS, BLK, 128), full),
            pltpu.VMEM((D, 3 * D), low),
            pltpu.VMEM((buffers, BLK, 2 * D), low),
            pltpu.VMEM((slots + 1 if slots <= 2 else 1, BLK, D), low),
            pltpu.VMEM((BLK, D), full),
            pltpu.VMEM((slots + 1 if slots <= 2 else 1, 2 * D, BLK), low),
            pltpu.VMEM((BLK, D) if slots <= 2 else (8, 128), full),
            pltpu.VMEM((2, 2, D // 4, D if slots <= 2 else 3 * D), low),
            pltpu.VMEM((slots, BLK, D), low),
            pltpu.VMEM((slots, BLK, D), low),
            pltpu.VMEM((slots, BLK, D), low),
            pltpu.VMEM((8, D), full),
            pltpu.VMEM((3 + levels, 8, D), full),
            pltpu.VMEM((1, D), full),
            pltpu.VMEM((1, D), full),
            pltpu.VMEM((depth, 2, TILE, TILE), low),
            pltpu.VMEM((depth, TILE, TILE), low),
            pltpu.VMEM((depth, TILE // 2, TILE), low),
            pltpu.VMEM((depth, TILE, TILE), low),
            pltpu.VMEM((4, 2, 2, TILE, TILE), low),
        ]
        + [pltpu.VMEM((2, 4, BLK, TILE), low), pltpu.VMEM((4, BLK, TILE), low)]
        + zshapes
        + [dma((12,)), dma((2, buffers)), dma((4,)), dma((2, 4)), dma((4, 2)), dma((depth,)), dma((2,))]
        + [dma((depth,))] * (8 + 4 * levels)
        + [dma((chain,))] * 4
        + [dma((3 + levels,))] * 2,
        compiler_params=pltpu.CompilerParams(
            collective_id=2, has_side_effects=True, vmem_limit_bytes=67043328
        ),
        cost_estimate=pl.CostEstimate(flops=40 << 30, bytes_accessed=64 << 20, transcendentals=1 << 24),
        name="attend_back_reduce",
    )(
        slot_vec,
        gains,
        biases,
        norms,
        *saved,
        *weights,
        *ffn,
    )


def widen_kernel(*refs):
    count = len(refs) // 2
    for source, dest in zip(refs[: count - 1], refs[count:]):
        dest[...] = source[...].astype(dest.dtype)
    refs[-2][...] = refs[count - 1][0:4, :]
    refs[-1][...] = refs[count - 1][4:8, :]


def widen(arrays, types, norms):
    steps = 4
    specs = [pl.BlockSpec((x.shape[0] // steps, x.shape[1]), lambda i: (i, 0)) for x in arrays]
    shape = jax.ShapeDtypeStruct
    pair = [pl.BlockSpec((4, D), lambda i: (0, 0))] * 2
    return pl.pallas_call(
        widen_kernel,
        out_shape=[shape(x.shape, kind) for x, kind in zip(arrays, types)]
        + [shape((4, D), jnp.float32)] * 2,
        grid=(steps,),
        in_specs=specs + [pl.BlockSpec((8, D), lambda i: (0, 0))],
        out_specs=specs + pair,
        compiler_params=pltpu.CompilerParams(vmem_limit_bytes=67043328),
        name="widen",
    )(*arrays, norms)


def per_device(n_ctx, inputs, w_qkv, w_out, w_up, w_down, norm_gains, norm_biases, block_map, out_grad):
    slots = n_ctx // 2
    raw, seed_low = inputs.reshape(BLK, D), out_grad.reshape(BLK, D)
    block_entry = block_map.reshape(2)
    forward = forward_part(
        n_ctx,
        block_entry,
        norm_gains,
        norm_biases,
        raw,
        seed_low,
        w_qkv,
        w_out,
        w_up,
        w_down,
    )
    every_low, queries, keys_values, attn_low, lse, full_qkv, full_out, full_up, full_down = forward[:9]
    result, active_low, down_low, ffn_low, upward, hat1, hat2, rstd, norms = forward[9:]
    backward = backward_part(
        n_ctx,
        block_entry,
        norm_gains,
        norm_biases,
        norms,
        [raw, queries, keys_values, every_low, attn_low, lse, full_qkv],
        [full_out, full_up, full_down],
        [active_low, down_low, ffn_low, upward, hat1, hat2, rstd, seed_low],
    )
    grad_tokens, norm_total, grad_hidden = backward[4:7]
    if slots > 2:
        grad_tokens = grad_tokens + grad_hidden
    full = jnp.float32
    summed_down, summed_up, summed_out, summed_qkv, grad_input, result, gain_total, bias_total = widen(
        list(backward[:4]) + [grad_tokens, result],
        [full] * 5 + [jnp.bfloat16],
        norm_total,
    )
    return (
        result.reshape(1, 1, BLK, D),
        grad_input.reshape(1, 1, BLK, D),
        summed_qkv,
        summed_out,
        summed_up,
        summed_down,
        gain_total,
        bias_total,
    )


def solution(mesh):
    rows = P("wsh", None)
    blocks = P("grp", "wsh", "ctx", None)
    return jax.shard_map(
        functools.partial(per_device, mesh.shape["ctx"]),
        mesh=mesh,
        in_specs=(blocks, rows, rows, rows, rows, P(), P(), blocks, blocks),
        out_specs=(blocks, blocks, rows, rows, rows, rows, P(), P()),
        check_vma=False,
    )
```

```python
import functools
import math

import jax
import jax.numpy as jnp
from jax import lax
from jax.experimental import pallas as pl
from jax.experimental.pallas import tpu as pltpu
from jax.sharding import PartitionSpec as P

D = 1024
HEADS = 16
DH = 64
BLK = 512
PAIRS = HEADS // 2
QT = 256

EPS = 1e-05
ALPHA = 32.0
NEG = -1e30
LOG2E = 1.4426950408889634
C2 = ALPHA * LOG2E
MESH = pl.DeviceIdType.MESH
QSCALE = 1.0 / (ALPHA * math.sqrt(DH))


def layer_norm(values, gain_row, bias_row):
    centre = values - jnp.mean(values, axis=-1, keepdims=True)
    spread = jnp.mean(centre * centre, axis=-1, keepdims=True)
    return centre * lax.rsqrt(spread + EPS) * gain_row + bias_row


def dot_dims(left_side, right_side, left_dim, right_dim):
    return lax.dot_general(
        left_side,
        right_side,
        (((left_dim,), (right_dim,)), ((), ())),
        preferred_element_type=jnp.float32,
    )


def contract_last(left_side, right_side):
    return dot_dims(left_side, right_side, 1, 1)


def contract_rows(left_side, right_side):
    return dot_dims(left_side, right_side, 0, 0)


def standard_rows(values):
    centre = values - jnp.mean(values, axis=-1, keepdims=True)
    scale = lax.rsqrt(jnp.mean(centre * centre, axis=-1, keepdims=True) + EPS)
    return centre * scale, scale


def row_back(upstream, hat, scale, gain):
    scaled = upstream * gain
    return scale * (
        scaled
        - jnp.mean(scaled, axis=-1, keepdims=True)
        - hat * jnp.mean(scaled * hat, axis=-1, keepdims=True)
    )


def column_sum(values):
    return jnp.sum(values, axis=0, keepdims=True)


def head_lanes(head, rows):
    lane = lax.broadcasted_iota(jnp.int32, (rows, 128), 1)
    return (lane >= DH) if head else (lane < DH)


def causal_tile():
    row = lax.broadcasted_iota(jnp.int32, (QT, QT), 0)
    col = lax.broadcasted_iota(jnp.int32, (QT, QT), 1)
    return col <= row


PIECE = 128
SPAN = 512
CHAIN = 64
HOP = 2
YLAG = 3
XLAG = 2
BLAG = 2
FF_TICKS = 13
TAIL_PACE = 3
GELU_A = 0.044715
GELU_C = math.sqrt(2.0 / math.pi)
PACE = 2
LAG = 2
GROUP = 4
AHEAD = 4


def remote(src, dst, send, recv, peer):
    return pltpu.make_async_remote_copy(
        src_ref=src, dst_ref=dst, send_sem=send, recv_sem=recv, device_id=peer, device_id_type=MESH
    )


def local_wait(ref, sem):
    pltpu.make_async_copy(ref, ref, sem).wait()


def aligned(start, size):
    return pl.ds(pl.multiple_of(start, size), size)


def softmax_block(q_ref, kv_ref, acc, top_ref, sum_ref, pair, base, own, visible):
    lanes = aligned(pair * 128, 128)
    value_lanes = aligned(D + pair * 128, 128)
    causal = causal_tile()
    first = head_lanes(0, QT)
    count = BLK // QT
    q_pair = q_ref[:, lanes]
    keys = kv_ref[pl.ds(base, BLK), lanes]
    values = kv_ref[pl.ds(base, BLK), value_lanes]
    if not own:
        old_top, old_sum, old_out = top_ref[pair], sum_ref[pair], acc[:, lanes]
        hide = jnp.where(visible, 0.0, 1e30)
    results = []
    work = [(tile, head) for tile in range(count) for head in range(2)]
    parts_of = {}
    for tile, head in work:
        q_tile = q_pair[tile * QT : (tile + 1) * QT]
        q_head = jnp.where(head_lanes(head, QT), q_tile, jnp.zeros_like(q_tile))
        span = (tile + 1) * QT if own else BLK
        parts_of[tile, head] = contract_last(q_head, keys[:span])
    top_of, expo_of, total_of = {}, {}, {}
    for tile, head in work:
        part = parts_of[tile, head]
        if own:
            diag = jnp.where(causal, part[:, tile * QT :], NEG)
            part = jnp.concatenate([part[:, : tile * QT], diag], axis=1) if tile else diag
        top = jnp.max(part, axis=-1, keepdims=True) * C2
        if own:
            shift = top
        else:
            top = jnp.maximum(
                jnp.where(visible, top, NEG), old_top[tile * QT : (tile + 1) * QT, head * DH : head * DH + 1]
            )
            shift = top + hide
        expo = jnp.exp2(part * C2 - shift)
        top_of[tile, head] = jnp.broadcast_to(top, (QT, 128))
        total_of[tile, head] = jnp.broadcast_to(jnp.sum(expo, axis=-1, keepdims=True), (QT, 128))
        expo_of[tile, head] = expo.astype(jnp.bfloat16)
    out_of = {}
    for tile, head in work:
        span = (tile + 1) * QT if own else BLK
        out_of[tile, head] = dot_dims(expo_of[tile, head], values[:span], 1, 0)
    for tile in range(count):
        rows = pl.ds(tile * QT, QT)
        new_top = jnp.where(first, top_of[tile, 0], top_of[tile, 1])
        new_sum = jnp.where(first, total_of[tile, 0], total_of[tile, 1])
        new_out = jnp.where(first, out_of[tile, 0], out_of[tile, 1])
        if not own:
            here = slice(tile * QT, (tile + 1) * QT)
            keep = jnp.exp2(old_top[here] - new_top)
            new_sum = new_sum + old_sum[here] * keep
            new_out = new_out + old_out[here] * keep
        top_ref[pair, rows, :] = new_top
        sum_ref[pair, rows, :] = new_sum
        acc[rows, lanes] = new_out


def forward_kernel(n_ctx, *refs):
    slots = n_ctx // 2
    (slot_ref, gain_ref, bias_ref, x_hbm, dy_hbm, w_qkv, w_out, w_up, w_down) = refs[:9]
    (a_out, q_out, kv_out, o_out, lse_out, full_qkv, full_out, full_up, full_down) = refs[9:18]
    (y_out, g_out, dz_out, f_out, u_out, hat1_out, hat2_out, rstd_out, norm_out) = refs[18:27]
    (x_own, left, right, a_all, q_all, kv_all, weight, acc, z_acc, norm_v, tops, sums, hop) = refs[27:40]
    (sem_in, sem_load, sem_store, sem_ff, sem_out, sem_a, sem_kv, side_s, side_r, grp_s, grp_r, cs_s, cs_r, cg_s, cg_r, own_s, own_r, left_s, left_r, right_s, right_r) = refs[40:]
    grp, ctx, wsh = lax.axis_index("grp"), lax.axis_index("ctx"), lax.axis_index("wsh")
    side, core = wsh // 2, wsh % 2
    core_peer = (grp, ctx, side * 2 + 1 - core)
    side_peer = (grp, ctx, (1 - side) * 2 + core)
    grp_peer = (1 - grp, ctx, wsh)
    next_ctx = (grp, lax.rem(ctx + 1, n_ctx), wsh)
    last_ctx = (grp, lax.rem(ctx + n_ctx - 1, n_ctx), wsh)

    load = pltpu.make_async_copy(x_hbm, x_own, sem_in.at[0])
    load.start()
    barrier = pltpu.get_barrier_semaphore()
    for peer in (core_peer, side_peer, grp_peer, next_ctx, last_ctx):
        pl.semaphore_signal(barrier, inc=1, device_id=peer, device_id_type=MESH)
    pl.semaphore_wait(barrier, 5)

    shards = (w_qkv, w_out, w_up, w_down)
    fulls = (weight, full_out, full_up, full_down)
    ranges, start = [], 0
    for shard in shards:
        across = shard.shape[1] // SPAN
        ranges.append((start, start + across * (shard.shape[0] // (2 * PIECE)), across))
        start = ranges[-1][1]
    pieces = start

    def by_range(index, act):
        for place, (low, high, across) in enumerate(ranges):

            @pl.when((index >= low) & (index < high))
            def _(place=place, low=low, across=across):
                act(place, (index - low) // across, aligned(((index - low) % across) * SPAN, SPAN))

    def rows_of(place, owner, half, group):
        shard_rows = shards[place].shape[0]
        return aligned(owner * shard_rows + half * (shard_rows // 2) + group * PIECE, PIECE)

    sides_owner = (1 - side) * 2 + core

    def send_piece(index, carry):
        def act(place, group, cols):
            remote(
                shards[place].at[rows_of(place, 0, grp, group), cols],
                fulls[place].at[rows_of(place, wsh, grp, group), cols],
                side_s.at[index],
                side_r.at[index],
                side_peer,
            ).start()

        by_range(index, act)
        return carry

    def own_copies():
        copies = []
        across = shards[0].shape[1] // SPAN
        for place in range(4):
            shard_rows = shards[place].shape[0]
            mine = aligned(wsh * shard_rows, shard_rows)
            steps = range(across) if place == 0 else [None]
            for step in steps:
                cols = slice(None) if step is None else pl.ds(step * SPAN, SPAN)
                number = len(copies)
                copies.append(
                    remote(
                        shards[place].at[:, cols],
                        fulls[place].at[mine, cols],
                        own_s.at[number],
                        own_r.at[number],
                        core_peer,
                    )
                )
        return copies

    for index in range(AHEAD):
        send_piece(index, 0)
    for copy in own_copies():
        copy.start()
    own_rows = aligned(wsh * w_qkv.shape[0], w_qkv.shape[0])
    own_weight = pltpu.make_async_copy(w_qkv, weight.at[own_rows, :], sem_in.at[1])
    own_weight.start()
    load.wait()

    bounces, start = [], 0
    for shard in shards[1:]:
        across = shard.shape[1] // SPAN
        bounces.append((start, start + across * (shard.shape[0] // (2 * PIECE)), across))
        start = bounces[-1][1]
    moves = start

    def bounce(index, loading):
        slot = lax.rem(index, 3)
        for place, (low, high, across) in enumerate(bounces):

            @pl.when((index >= low) & (index < high))
            def _(place=place + 1, low=low, across=across):
                group = (index - low) // across
                cols = aligned(((index - low) % across) * SPAN, SPAN)
                if loading:
                    here = shards[place].at[aligned(group * 2 * PIECE, 2 * PIECE), cols]
                    pltpu.make_async_copy(here, hop.at[slot], sem_load.at[slot]).start()
                else:
                    rows = aligned(wsh * shards[place].shape[0] + group * 2 * PIECE, 2 * PIECE)
                    local_wait(hop.at[slot], sem_load.at[slot])
                    pltpu.make_async_copy(
                        hop.at[slot], fulls[place].at[rows, cols], sem_store.at[slot]
                    ).start()

    own_slot = slot_ref[1] // BLK
    own_tag = jnp.where(slot_ref[0] == 0, own_slot, n_ctx)
    chain_chunks = slots * (BLK // CHAIN)

    def chain_step(stream, send, recv, number, is_first, is_last, target):
        slot = number // (BLK // CHAIN)
        spot = aligned((number % (BLK // CHAIN)) * CHAIN, CHAIN)
        mine = jnp.where(own_tag == slot, x_own[spot, :], jnp.zeros((CHAIN, D), jnp.bfloat16))
        here = stream.at[slot, spot]

        @pl.when(is_first)
        def _():
            stream[slot, spot, :] = mine

        @pl.when(jnp.logical_not(is_first))
        def _():
            remote(here, here, send.at[number], recv.at[number], target).wait_recv()
            stream[slot, spot, :] = stream[slot, spot, :] + mine

        @pl.when(jnp.logical_not(is_last))
        def _():
            remote(here, here, send.at[number], recv.at[number], target).start()

    def tick(step):
        @pl.when((step >= 1) & (step <= moves))
        def _():
            bounce(step - 1, False)

        @pl.when((step >= 3) & (step < moves))
        def _():
            local_wait(hop.at[lax.rem(step, 3)], sem_store.at[lax.rem(step, 3)])

        @pl.when(step < moves)
        def _():
            bounce(step, True)

        @pl.when(step + AHEAD < pieces)
        def _():
            send_piece(step + AHEAD, 0)

        number = step - HOP * ctx

        @pl.when((number >= 0) & (number < chain_chunks))
        def _():
            chain_step(left, left_s, left_r, number, ctx == 0, ctx == n_ctx - 1, next_ctx)

        back = step - HOP * (n_ctx - 1 - ctx)

        @pl.when((back >= 0) & (back < chain_chunks))
        def _():
            chain_step(right, right_s, right_r, back, ctx == n_ctx - 1, ctx == 0, last_ctx)

        @pl.when(step < pieces)
        def _():
            def act(place, group, cols):
                here = fulls[place].at[rows_of(place, sides_owner, grp, group), cols]
                remote(here, here, side_s.at[step], side_r.at[step], side_peer).wait_recv()
                remote(here, here, grp_s.at[step], grp_r.at[step], grp_peer).start()
                remote(here, here, cs_s.at[step], cs_r.at[step], core_peer).start()

            by_range(step, act)

        late = step - LAG

        @pl.when((late >= 0) & (late < pieces))
        def _():
            def act(place, group, cols):
                here = fulls[place].at[rows_of(place, sides_owner, 1 - grp, group), cols]
                remote(here, here, grp_s.at[late], grp_r.at[late], grp_peer).wait_recv()
                remote(here, here, cg_s.at[late], cg_r.at[late], core_peer).start()

            by_range(late, act)

    def ticks(first, last):
        lax.fori_loop(first, last, lambda index, carry: (tick(index), carry)[1], 0)

    def normalise(source, dest):
        gain, bias = gain_ref[0:1, :], bias_ref[0:1, :]

        def body(index, carry):
            rows = aligned(index * 128, 128)
            values = source(rows).astype(jnp.float32)
            a_all[aligned(dest + index * 128, 128), :] = layer_norm(values, gain, bias).astype(
                jnp.bfloat16
            )
            return carry

        lax.fori_loop(0, BLK // 128, body, 0)

    def piece_ready(index):
        here = fulls[0].at[pl.ds(0, PIECE), pl.ds(0, SPAN)]
        remote(here, here, cs_s.at[index], cs_r.at[index], core_peer).wait_recv()
        remote(here, here, cg_s.at[index], cg_r.at[index], core_peer).wait_recv()
        whole = fulls[0].at[pl.ds(0, 2 * PIECE), pl.ds(0, SPAN)]
        remote(whole, whole, own_s.at[index], own_r.at[index], core_peer).wait_recv()

    tick(0)
    normalise(lambda rows: x_own[rows, :], 0)
    ticks(1, LAG + 1)
    own_weight.wait()

    def project_q(index, carry):
        tick(index + LAG + 1)
        piece_ready(index)
        cols = aligned(index * SPAN, SPAN)
        q_all[:, cols] = (
            jnp.dot(a_all[pl.ds(0, BLK), :], weight[:, cols], preferred_element_type=jnp.float32) * QSCALE
        ).astype(jnp.bfloat16)
        return carry

    lax.fori_loop(0, D // SPAN, project_q, 0)
    head_ticks = LAG + 1 + D // SPAN

    def project_kv(index, base):
        cols = aligned(index * SPAN, SPAN)
        rows = aligned(base, BLK)
        kv_all[rows, cols] = jnp.dot(
            a_all[rows, :], weight[:, aligned(D + index * SPAN, SPAN)], preferred_element_type=jnp.float32
        ).astype(jnp.bfloat16)

    def own_kv(index, carry):
        tick(index + head_ticks)
        piece_ready(index + D // SPAN)
        project_kv(index, 0)
        return carry

    lax.fori_loop(0, 2 * D // SPAN, own_kv, 0)
    own_ticks = head_ticks + 2 * D // SPAN

    def send_block(index):
        rows = aligned(index * BLK, BLK)
        pltpu.make_async_copy(a_all.at[rows, :], a_out.at[rows, :], sem_a.at[index]).start()
        pltpu.make_async_copy(kv_all.at[rows, :], kv_out.at[rows, :], sem_kv.at[index]).start()

    outputs = [
        pltpu.make_async_copy(weight, full_qkv, sem_out.at[0]),
        pltpu.make_async_copy(q_all, q_out, sem_out.at[1]),
    ]
    for copy in outputs:
        copy.start()

    send_block(0)

    def own_attention(group, carry):
        ticks(own_ticks + 2 * group, own_ticks + 2 * group + 2)
        for member in range(GROUP):
            softmax_block(q_all, kv_all, acc, tops, sums, group * GROUP + member, 0, True, None)
        return carry

    groups = PAIRS // GROUP
    lax.fori_loop(0, groups, own_attention, 0)
    used = own_ticks + 2 * groups
    per_slot = 2 * D // SPAN + 2 * groups

    need = BLK // CHAIN + HOP * (n_ctx - 1)
    early = max(0, need - used)
    if early:
        lax.fori_loop(0, early, lambda index, carry: (tick(used + index), carry)[1], 0)

    def each_slot(slot, carry):
        base = pl.multiple_of((slot + 1) * BLK, BLK)
        visible = slot < own_slot
        begin = early + used + slot * per_slot

        def total(rows):
            joined = left[slot, rows, :] + right[slot, rows, :]
            return jnp.where(own_tag == slot, x_own[rows, :], joined)

        normalise(total, base)

        def slot_kv(index, inner):
            tick(begin + index)
            project_kv(index, base)
            return inner

        lax.fori_loop(0, 2 * D // SPAN, slot_kv, 0)

        send_block(slot + 1)

        def slot_attention(group, inner):
            start = begin + 2 * D // SPAN + 2 * group
            ticks(start, start + 2)
            for member in range(GROUP):
                softmax_block(
                    q_all, kv_all, acc, tops, sums, group * GROUP + member, base, False, visible
                )
            return inner

        lax.fori_loop(0, groups, slot_attention, 0)
        return carry

    lax.fori_loop(0, slots, each_slot, 0)
    done_ticks = early + used + slots * per_slot

    def finish(pair, carry):
        lanes = aligned(pair * 128, 128)
        x_own[:, lanes] = (acc[:, lanes] / sums[pair]).astype(jnp.bfloat16)
        tops[pair] = tops[pair] + jnp.log2(sums[pair])
        return carry

    lax.fori_loop(0, PAIRS, finish, 0)
    outputs += [
        pltpu.make_async_copy(x_own, o_out, sem_out.at[2]),
        pltpu.make_async_copy(tops, lse_out, sem_out.at[3]),
    ]
    for copy in outputs[2:]:
        copy.start()
    all_ticks = max(pieces + LAG, chain_chunks + HOP * (n_ctx - 1))
    if all_ticks > done_ticks:
        lax.fori_loop(done_ticks, all_ticks, lambda index, carry: (tick(index), carry)[1], 0)

    def drain(index, carry):
        here = fulls[0].at[pl.ds(0, PIECE), pl.ds(0, SPAN)]

        @pl.when(index >= ranges[0][1])
        def _():
            remote(here, here, cs_s.at[index], cs_r.at[index], core_peer).wait_recv()
            remote(here, here, cg_s.at[index], cg_r.at[index], core_peer).wait_recv()

        remote(here, here, side_s.at[index], side_r.at[index], side_peer).wait_send()
        remote(here, here, grp_s.at[index], grp_r.at[index], grp_peer).wait_send()
        remote(here, here, cs_s.at[index], cs_r.at[index], core_peer).wait_send()
        remote(here, here, cg_s.at[index], cg_r.at[index], core_peer).wait_send()
        return carry

    lax.fori_loop(0, pieces, drain, 0)
    copies = own_copies()
    for number, copy in enumerate(copies):
        copy.wait_send()
        if number >= len(copies) - 3:
            copy.wait_recv()
    for index in range(moves - 3, moves):
        local_wait(hop.at[index % 3], sem_store.at[index % 3])

    def drain_chain(index, carry):
        here = left.at[0, pl.ds(0, CHAIN)]

        @pl.when(ctx < n_ctx - 1)
        def _():
            remote(here, here, left_s.at[index], left_r.at[index], next_ctx).wait_send()

        @pl.when(ctx > 0)
        def _():
            remote(here, here, right_s.at[index], right_r.at[index], last_ctx).wait_send()

        return carry

    lax.fori_loop(0, chain_chunks, drain_chain, 0)
    for copy in outputs[:2]:
        copy.wait()
    shallow_tiles = full_up.shape[1] // SPAN

    def tile_loads(tile, parity):
        cols = aligned(tile * SPAN, SPAN)
        return (
            pltpu.make_async_copy(
                full_up.at[:, cols], weight.at[:, aligned(D + parity * SPAN, SPAN)], sem_ff.at[0, parity]
            ),
            pltpu.make_async_copy(full_down.at[cols, :], left.at[parity], sem_ff.at[1, parity]),
        )

    def tile_stores(tile, parity):
        cols = aligned(tile * SPAN, SPAN)
        return [
            pltpu.make_async_copy(
                kv_all.at[pl.ds(0, BLK), aligned(base + parity * SPAN, SPAN)],
                dest.at[:, cols],
                sem_ff.at[2 + place, parity],
            )
            for place, (base, dest) in enumerate(((0, u_out), (D, g_out)))
        ]

    out_load = pltpu.make_async_copy(full_out, weight.at[:, pl.ds(0, D)], sem_in.at[0])
    x_load = pltpu.make_async_copy(x_hbm, right.at[1], sem_in.at[1])
    for copy in (out_load, x_load) + tile_loads(0, 0):
        copy.start()

    def drain_blocks(index, carry):
        rows = aligned(index * BLK, BLK)
        local_wait(a_all.at[rows, :], sem_a.at[index])
        local_wait(kv_all.at[rows, :], sem_kv.at[index])
        return carry

    lax.fori_loop(0, slots + 1, drain_blocks, 0)
    out_load.wait()

    def out_half(index, carry):
        cols = aligned(index * SPAN, SPAN)
        acc[:, cols] = jnp.dot(x_own[...], weight[:, cols], preferred_element_type=jnp.float32)
        return carry

    lax.fori_loop(0, D // SPAN, out_half, 0)
    x_load.wait()
    for copy in outputs[2:]:
        copy.wait()
    dy_load = pltpu.make_async_copy(dy_hbm, x_own, sem_in.at[0])
    dy_load.start()

    def inner_rows(step, carry):
        rows = aligned(step * CHAIN, CHAIN)
        hat, scale = standard_rows(acc[rows, :])
        a_all[rows, :] = hat.astype(jnp.bfloat16)
        sums[0, rows, :] = jnp.broadcast_to(scale, (CHAIN, 128))
        hidden = right[1, rows, :].astype(jnp.float32) + hat * gain_ref[1:2, :] + bias_ref[1:2, :]
        acc[rows, :] = hidden
        hat, scale = standard_rows(hidden)
        a_all[aligned(BLK + step * CHAIN, CHAIN), :] = hat.astype(jnp.bfloat16)
        sums[1, rows, :] = jnp.broadcast_to(scale, (CHAIN, 128))
        q_all[rows, :] = (hat * gain_ref[2:3, :] + bias_ref[2:3, :]).astype(jnp.bfloat16)
        return carry

    lax.fori_loop(0, BLK // CHAIN, inner_rows, 0)
    saves = [
        pltpu.make_async_copy(a_all.at[pl.ds(0, BLK), :], hat1_out, sem_out.at[0]),
        pltpu.make_async_copy(a_all.at[pl.ds(BLK, BLK), :], hat2_out, sem_out.at[1]),
        pltpu.make_async_copy(sums.at[pl.ds(0, 2)], rstd_out, sem_out.at[2]),
        pltpu.make_async_copy(q_all, f_out, sem_out.at[3]),
    ]
    for copy in saves:
        copy.start()

    def ff_tile(tile, carry):
        parity = tile % 2
        for copy in tile_loads(tile, parity):
            copy.wait()

        @pl.when(tile + 1 < shallow_tiles)
        def _():
            for copy in tile_loads(tile + 1, 1 - parity):
                copy.start()

        @pl.when(tile >= 2)
        def _():
            for copy in tile_stores(tile - 2, parity):
                copy.wait()

        upward = jnp.dot(
            q_all[...], weight[:, aligned(D + parity * SPAN, SPAN)], preferred_element_type=jnp.float32
        )
        kv_all[pl.ds(0, BLK), aligned(parity * SPAN, SPAN)] = upward.astype(jnp.bfloat16)
        active = (
            0.5 * upward * (1.0 + jnp.tanh(GELU_C * upward * (1.0 + GELU_A * upward * upward)))
        ).astype(jnp.bfloat16)
        kv_all[pl.ds(0, BLK), aligned(D + parity * SPAN, SPAN)] = active
        for copy in tile_stores(tile, parity):
            copy.start()
        fresh = jnp.dot(active, left[parity], preferred_element_type=jnp.float32)

        @pl.when(tile == 0)
        def _():
            z_acc[...] = fresh

        @pl.when(tile > 0)
        def _():
            z_acc[...] = z_acc[...] + fresh

        return carry

    lax.fori_loop(0, shallow_tiles, ff_tile, 0)
    dy_load.wait()

    def outer_rows(step, carry):
        gain_sum, bias_sum = carry
        rows = aligned(step * CHAIN, CHAIN)
        hat, scale = standard_rows(z_acc[rows, :])
        right[0, rows, :] = (acc[rows, :] + hat * gain_ref[3:4, :] + bias_ref[3:4, :]).astype(jnp.bfloat16)
        upstream = x_own[rows, :].astype(jnp.float32)
        a_all[aligned(2 * BLK + step * CHAIN, CHAIN), :] = row_back(
            upstream, hat, scale, gain_ref[3:4, :]
        ).astype(jnp.bfloat16)
        return gain_sum + column_sum(upstream * hat), bias_sum + column_sum(upstream)

    zero = jnp.zeros((1, D), jnp.float32)
    gain_sum, bias_sum = lax.fori_loop(0, BLK // CHAIN, outer_rows, (zero, zero))
    row = lax.broadcasted_iota(jnp.int32, (8, D), 0)
    norm_v[...] = jnp.where(row == 3, gain_sum, 0.0) + jnp.where(row == 7, bias_sum, 0.0)
    ends = [
        pltpu.make_async_copy(right.at[0], y_out, sem_in.at[0]),
        pltpu.make_async_copy(a_all.at[pl.ds(2 * BLK, BLK), :], dz_out, sem_in.at[1]),
        pltpu.make_async_copy(norm_v, norm_out, sem_in.at[2]),
    ]
    for copy in ends:
        copy.start()
    for tile in range(shallow_tiles - 2, shallow_tiles):
        for copy in tile_stores(tile, tile % 2):
            copy.wait()
    for copy in saves + ends:
        copy.wait()


def forward_part(n_ctx, tags, gains, biases, raw, dy, w_qkv, w_out, w_up, w_down):
    slots = n_ctx // 2
    every = (slots + 1) * BLK
    low, full = jnp.bfloat16, jnp.float32
    dma = pltpu.SemaphoreType.DMA
    hbm = pl.BlockSpec(memory_space=pl.ANY)
    vmem = pl.BlockSpec(memory_space=pltpu.VMEM)
    shards = (w_qkv, w_out, w_up, w_down)
    pieces = sum(w.shape[0] * w.shape[1] // (2 * PIECE * SPAN) for w in shards)
    own = w_qkv.shape[1] // SPAN + 3
    chain = slots * (BLK // CHAIN)
    shape = jax.ShapeDtypeStruct
    return pl.pallas_call(
        functools.partial(forward_kernel, n_ctx),
        out_shape=[
            shape((every, D), low),
            shape((BLK, D), low),
            shape((every, 2 * D), low),
            shape((BLK, D), low),
            shape((PAIRS, BLK, 128), full),
        ]
        + [shape((4 * w.shape[0], w.shape[1]), low) for w in shards]
        + [
            shape((BLK, D), low),
            shape((BLK, w_up.shape[1]), low),
            shape((BLK, D), low),
            shape((BLK, D), low),
            shape((BLK, w_up.shape[1]), low),
            shape((BLK, D), low),
            shape((BLK, D), low),
            shape((2, BLK, 128), full),
            shape((8, D), full),
        ],
        in_specs=[pl.BlockSpec(memory_space=pltpu.SMEM), vmem, vmem] + [hbm] * 6,
        out_specs=[hbm] * 18,
        scratch_shapes=[
            pltpu.VMEM((BLK, D), low),
            pltpu.VMEM((slots, BLK, D), low),
            pltpu.VMEM((slots, BLK, D), low),
            pltpu.VMEM((every, D), low),
            pltpu.VMEM((BLK, D), low),
            pltpu.VMEM((every, 2 * D), low),
            pltpu.VMEM((D, 3 * D), low),
            pltpu.VMEM((BLK, D), full),
            pltpu.VMEM((BLK, D), full),
            pltpu.VMEM((8, D), full),
            pltpu.VMEM((PAIRS, BLK, 128), full),
            pltpu.VMEM((PAIRS, BLK, 128), full),
            pltpu.VMEM((3, 2 * PIECE, SPAN), low),
            dma((3,)),
            dma((3,)),
            dma((3,)),
            dma((4, 2)),
            dma((4,)),
            dma((slots + 1,)),
            dma((slots + 1,)),
        ]
        + [dma((pieces,))] * 8
        + [dma((own,))] * 2
        + [dma((chain,))] * 4,
        compiler_params=pltpu.CompilerParams(
            collective_id=1, has_side_effects=True, vmem_limit_bytes=67043328
        ),
        cost_estimate=pl.CostEstimate(flops=20 << 30, bytes_accessed=64 << 20, transcendentals=1 << 24),
        name="gather_attend",
    )(tags, gains, biases, raw, dy, *shards)


TILE = 256
PAIRED = 2


def grad_block(q_ref, do_ref, o_ref, lse_ref, kv_ref, dq_acc, turned, pair, own, visible):
    lanes = aligned(pair * 128, 128)
    value_lanes = aligned(D + pair * 128, 128)
    size = QT if own else BLK
    count = BLK // size
    q_pair, do_pair, lse_pair = q_ref[:, lanes], do_ref[:, lanes], lse_ref[pair]
    prod = do_pair.astype(jnp.float32) * o_ref[:, lanes].astype(jnp.float32)
    keys, values = kv_ref[:, lanes], kv_ref[:, value_lanes]
    q_turned, do_turned = q_pair.T, do_pair.T
    old_dq = dq_acc[:, lanes]
    causal = causal_tile()
    hide = 0.0 if own else jnp.where(visible, 0.0, 1e30)
    lanes_of = [head_lanes(head, size) for head in range(2)]
    work = [(tile, head) for tile in range(count) for head in range(2)]
    score, dprob, dlogit, prob_low = {}, {}, {}, {}
    for tile, head in work:
        rows = slice(tile * size, (tile + 1) * size)
        span = (tile + 1) * size if own else BLK
        zero = jnp.zeros((size, 128), jnp.bfloat16)
        score[tile, head] = contract_last(jnp.where(lanes_of[head], q_pair[rows], zero), keys[:span])
        dprob[tile, head] = contract_last(jnp.where(lanes_of[head], do_pair[rows], zero), values[:span])
    for tile, head in work:
        rows = slice(tile * size, (tile + 1) * size)
        delta = jnp.sum(jnp.where(lanes_of[head], prod[rows], 0.0), axis=-1, keepdims=True)
        shift = lse_pair[rows, head * DH : head * DH + 1] + hide
        prob = jnp.exp2(score[tile, head] * C2 - shift)
        if own:
            diag = jnp.where(causal, prob[:, tile * size :], 0.0)
            prob = jnp.concatenate([prob[:, : tile * size], diag], axis=1) if tile else diag
        dlogit[tile, head] = (prob * (dprob[tile, head] - delta)).astype(jnp.bfloat16)
        prob_low[tile, head] = prob.astype(jnp.bfloat16)
    for tile in range(count):
        rows = slice(tile * size, (tile + 1) * size)
        span = (tile + 1) * size if own else BLK
        parts = [dot_dims(dlogit[tile, head], keys[:span], 1, 0) for head in range(2)]
        dq_acc[pl.ds(tile * size, size), lanes] = old_dq[rows] + jnp.where(lanes_of[0], parts[0], parts[1])
    for head in range(2):
        for offset, left_side, right_side, scale in (
            (0, q_turned, dlogit, ALPHA),
            (D, do_turned, prob_low, 1.0),
        ):
            spot = aligned(offset + pair * 128 + head * DH, DH)
            left_head = left_side[head * DH : (head + 1) * DH]
            terms = [
                dot_dims(left_head[:, tile * size : (tile + 1) * size], right_side[tile, head], 1, 0)
                for tile in range(count)
            ]
            for tile in range(count):
                cols = slice(tile * size, (tile + 1) * size)
                total = functools.reduce(
                    jnp.add, [terms[other][:, cols] for other in range(tile, count)]
                ) if own else terms[0]
                turned[spot, cols if own else slice(None)] = (total * scale).astype(jnp.bfloat16)


def backward_kernel(n_ctx, widths, *refs):
    slots = n_ctx // 2
    levels = n_ctx.bit_length() - 1
    depth = 16 if n_ctx == 4 else 10
    shallow = slots <= 2
    (slot_ref, gain_ref, bias_ref, norm_ref, x_hbm, q_hbm, kv_hbm, a_hbm, o_hbm, lse_hbm, w_hbm) = refs[:11]
    (w_out, w_up, w_down, g_hbm, dz_hbm, f_hbm, u_hbm, hat1_hbm, hat2_hbm, rstd_hbm, dy_hbm) = refs[11:22]
    outs = refs[22:26]
    grad_out, norm_out, dh_hbm, du_hbm, datt_hbm = refs[26:31]
    scratch = list(refs[31:])
    own_slot = slot_ref[1] // BLK

    def take(count):
        taken = scratch[:count]
        del scratch[:count]
        return taken

    q_v, o_v, do_v, lse_v, weight, kv_b, a_b, dq_acc, turned, gkv, term, own_part, left, right, norm_v, norm_in, gain_sum, bias_sum = take(18)
    r1, r2, r3, fin, made = take(5)
    lhs, rhs = take(2)
    zbufs = take(levels)
    sem_in, sem_blk, sem_rhs, sem_lhs, sem_ff, sem_out, sem_res = take(7)
    send1, recv1, send2, recv2, send3, recv3, send6, recv6 = take(8)
    rs_send, rs_recv, ag_send, ag_recv = take(levels), take(levels), take(levels), take(levels)
    left_s, left_r, right_s, right_r, norm_s, norm_r = take(6)
    grp, ctx, wsh = lax.axis_index("grp"), lax.axis_index("ctx"), lax.axis_index("wsh")
    side, core = wsh // 2, wsh % 2
    core_peer = (grp, ctx, side * 2 + 1 - core)
    side_peer = (grp, ctx, (1 - side) * 2 + core)
    grp_peer = (1 - grp, ctx, wsh)
    next_ctx = (grp, lax.rem(ctx + 1, n_ctx), wsh)
    last_ctx = (grp, lax.rem(ctx + n_ctx - 1, n_ctx), wsh)
    bits = [(ctx // (1 << level)) % 2 for level in range(levels)]
    level_peers = [(grp, ctx + (1 - 2 * bits[level]) * (1 << level), wsh) for level in range(levels)]

    def block_copies(index):
        rows = aligned(lax.rem(index, slots + 1) * BLK, BLK)
        slot = lax.rem(index, kv_b.shape[0])
        a_slot = index - 1 if shallow else 0
        return (
            pltpu.make_async_copy(kv_hbm.at[rows, :], kv_b.at[slot], sem_blk.at[0, slot]),
            pltpu.make_async_copy(a_hbm.at[rows, :], a_b.at[a_slot], sem_blk.at[1, slot]),
        )

    barrier = pltpu.get_barrier_semaphore()
    peers = [core_peer, side_peer, grp_peer, next_ctx, last_ctx] + level_peers
    for peer in peers:
        pl.semaphore_signal(barrier, inc=1, device_id=peer, device_id_type=MESH)

    half = TILE // 2
    ranges, first = [], 0
    for rows, cols in widths:
        across = cols // TILE
        ranges.append((first, first + (rows // TILE) * across, across))
        first = ranges[-1][1]
    chunks = first

    def by_range(index, act):
        for place, (low, high, across) in enumerate(ranges):

            @pl.when((index >= low) & (index < high))
            def _(place=place, low=low, across=across):
                number = index - low
                act(place, (aligned((number // across) * TILE, TILE), aligned((number % across) * TILE, TILE)))

    def region(level, flip):
        row, rows, col, cols = 0, half, 0, TILE
        for place in range(level):
            bit = 1 - bits[place] if (flip and place == level - 1) else bits[place]
            if rows > 16:
                rows = rows // 2
                row = row + bit * rows
            else:
                cols = cols // 2
                col = col + bit * cols
        return row, rows, col, cols

    def spot(level, flip=False, base=0):
        row, rows, col, cols = region(level, flip)
        return aligned(base + row, rows), aligned(col, cols)

    last_low = ranges[-1][0]
    dq_low = o_v
    set_of = [(0, number) for number in range(widths[0][0] // TILE)] + [(1, 0), (2, 0)]
    set_first = [number * ranges[0][2] for number in range(widths[0][0] // TILE)]
    set_first += [ranges[1][0], ranges[2][0]]
    left_of, right_of = (g_hbm, f_hbm, o_hbm), (dz_hbm, du_hbm, datt_hbm)

    def set_copies(number):
        place, group = set_of[number]
        stride = left_of[place].shape[1] // 4
        return [
            pltpu.make_async_copy(
                left_of[place].at[:, pl.ds(owner * stride + group * TILE, TILE)],
                lhs.at[number % 2, owner],
                sem_lhs.at[number % 2, owner],
            )
            for owner in range(4)
        ]

    def step_fetch(index):
        near = lax.rem(index, 4)

        def act(place, span):
            if place < 3:
                pltpu.make_async_copy(
                    right_of[place].at[:, span[1]], rhs.at[near], sem_rhs.at[near]
                ).start()

        by_range(index, act)

    def step_make(index, kinds):
        slot = lax.rem(index, depth)
        near = lax.rem(index, 4)

        def low_piece():
            local_wait(rhs.at[near], sem_rhs.at[near])
            parity = jnp.int32(0)
            for number, low in enumerate(set_first):
                parity = jnp.where(index >= low, number % 2, parity)

                @pl.when(index == low)
                def _(number=number):
                    for copy in set_copies(number):
                        copy.wait()
                    if number + 1 < len(set_first):
                        for copy in set_copies(number + 1):
                            copy.start()

            right_side = rhs[near]
            for owner in range(4):
                made[near, owner // 2, owner % 2] = dot_dims(
                    lhs[parity, owner], right_side, 0, 0
                ).astype(jnp.bfloat16)

        def high_piece():
            number = index - last_low
            if not shallow:
                made[near] = term[:, :, :, aligned(number * TILE, TILE)]
                return

            @pl.when(number < D // TILE)
            def _():
                right_side = dq_low[:, aligned(number * TILE, TILE)]
                for owner in range(4):
                    made[near, owner // 2, owner % 2] = dot_dims(
                        a_b[slots, :, pl.ds(owner * TILE, TILE)], right_side, 0, 0
                    ).astype(jnp.bfloat16)

            @pl.when(number >= D // TILE)
            def _():
                cols = aligned((number - D // TILE) * TILE, TILE)
                for owner in range(4):
                    total = functools.reduce(
                        jnp.add,
                        [
                            dot_dims(a_b[block, :, pl.ds(owner * TILE, TILE)], turned[block, cols, :], 0, 1)
                            for block in range(slots + 1)
                        ],
                    )
                    made[near, owner // 2, owner % 2] = total.astype(jnp.bfloat16)

        if kinds == "low":
            low_piece()
        elif kinds == "high":
            high_piece()
        else:
            pl.when(index < last_low)(low_piece)
            pl.when(index >= last_low)(high_piece)
        remote(
            made.at[near, :, 1 - core], r1.at[slot], send1.at[slot], recv1.at[slot], core_peer
        ).start()

    def finished(move):
        move.wait_send()
        move.wait_recv()

    def step_core(index):
        slot, near = lax.rem(index, depth), lax.rem(index, 4)
        finished(remote(r1.at[slot], r1.at[slot], send1.at[slot], recv1.at[slot], core_peer))
        r1[slot] = r1[slot] + made[near, :, core]
        remote(r1.at[slot, 1 - side], r2.at[slot], send2.at[slot], recv2.at[slot], side_peer).start()

    keep_half = aligned(grp * half, half)
    give_half = aligned((1 - grp) * half, half)

    def step_side(index):
        slot = lax.rem(index, depth)
        finished(remote(r1.at[slot, 1 - side], r2.at[slot], send2.at[slot], recv2.at[slot], side_peer))
        r2[slot] = r2[slot] + r1[slot, side]
        remote(r2.at[slot, give_half], r3.at[slot], send3.at[slot], recv3.at[slot], grp_peer).start()

    fold = n_ctx == 4
    if fold:
        outer = bits[0] == bits[1]
        inner = bits[0] != bits[1]
        mate, middle = level_peers[0], (grp, 3 - ctx, wsh)
        quarter = half // 2
        mine, other = aligned(bits[1] * quarter, quarter), aligned((1 - bits[1]) * quarter, quarter)
        fin_mine = aligned(grp * half + bits[1] * quarter, quarter)
        fin_other = aligned(grp * half + (1 - bits[1]) * quarter, quarter)

        def up_copy(slot):
            return remote(r3.at[slot], zbufs[0].at[slot], rs_send[0].at[slot], rs_recv[0].at[slot], mate)

        def cross_copy(slot):
            return remote(
                r3.at[slot, other], zbufs[1].at[slot], rs_send[1].at[slot], rs_recv[1].at[slot], middle
            )

        def share_copy(slot, rows):
            here = fin.at[slot, rows]
            return remote(here, here, ag_send[1].at[slot], ag_recv[1].at[slot], middle)

        def down_copy(slot):
            here = fin.at[slot, keep_half]
            return remote(here, here, ag_send[0].at[slot], ag_recv[0].at[slot], mate)

        def step_up(index):
            slot = lax.rem(index, depth)

            @pl.when(outer)
            def _():
                up_copy(slot).wait_send()

            @pl.when(inner)
            def _():
                up_copy(slot).wait_recv()
                r3[slot] = r3[slot] + zbufs[0][slot]
                cross_copy(slot).start()

        def step_cross(index):
            slot = lax.rem(index, depth)

            @pl.when(inner)
            def _():
                finished(cross_copy(slot))
                fin[slot, fin_mine] = r3[slot, mine] + zbufs[1][slot]
                share_copy(slot, fin_mine).start()

        def step_share(index):
            slot = lax.rem(index, depth)

            @pl.when(inner)
            def _():
                finished(share_copy(slot, fin_other))
                down_copy(slot).start()

        def step_down(index):
            slot = lax.rem(index, depth)

            @pl.when(inner)
            def _():
                down_copy(slot).wait_send()

            @pl.when(outer)
            def _():
                down_copy(slot).wait_recv()

            back_copy(slot, keep_half).start()

    def rs_copy(level, slot):
        rows, cols = spot(level + 1, True)
        return remote(
            r3.at[slot, rows, cols], zbufs[level].at[slot], rs_send[level].at[slot], rs_recv[level].at[slot], level_peers[level]
        )

    def ag_copy(level, slot, flip=False):
        rows, cols = spot(level + 1, flip, grp * half)
        here = fin.at[slot, rows, cols]
        return remote(here, here, ag_send[level].at[slot], ag_recv[level].at[slot], level_peers[level])

    def back_copy(slot, rows):
        here = fin.at[slot, rows]
        return remote(here, here, send6.at[slot], recv6.at[slot], grp_peer)

    def step_grp(index):
        slot = lax.rem(index, depth)
        finished(remote(r2.at[slot, give_half], r3.at[slot], send3.at[slot], recv3.at[slot], grp_peer))
        r3[slot] = r3[slot] + r2[slot, keep_half]
        if fold:

            @pl.when(outer)
            def _():
                up_copy(slot).start()
        else:
            rs_copy(0, slot).start()

    def step_scatter(level):
        def act(index):
            slot = lax.rem(index, depth)
            finished(rs_copy(level, slot))
            rows, cols = spot(level + 1)
            total = r3[slot, rows, cols] + zbufs[level][slot]
            if level + 1 < levels:
                r3[slot, rows, cols] = total
                rs_copy(level + 1, slot).start()
            else:
                rows, cols = spot(level + 1, False, grp * half)
                fin[slot, rows, cols] = total
                ag_copy(level, slot).start()

        return act

    def step_gather(level):
        def act(index):
            slot = lax.rem(index, depth)
            finished(ag_copy(level, slot, True))
            if level:
                ag_copy(level - 1, slot).start()
            else:
                back_copy(slot, keep_half).start()

        return act

    def out_wait(index):
        slot = lax.rem(index, depth)
        local_wait(fin.at[slot], sem_out.at[slot])

    def step_out(index):
        slot = lax.rem(index, depth)
        finished(back_copy(slot, give_half))

        def act(place, span):
            pltpu.make_async_copy(fin.at[slot], outs[place].at[span[0], span[1]], sem_out.at[slot]).start()

        by_range(index, act)

    z_lag = 2 if fold else 1
    order = [(YLAG, step_side), (XLAG, step_grp)]
    if fold:
        order += [(z_lag, act) for act in (step_up, step_cross, step_share, step_down)]
    else:
        order += [(z_lag, step_scatter(level)) for level in range(levels)]
        order += [(z_lag, step_gather(level)) for level in reversed(range(levels))]
    order += [(BLAG, step_out), (2, out_wait)]
    stages = [(0, step_core)]
    for lag, act in order:
        stages.append((stages[-1][0] + lag, act))
    all_ticks = chunks + stages[-1][0]

    per_slot = BLK // CHAIN
    chain_chunks = slots * per_slot

    def chain_step(stream, send, recv, number, is_first, is_last, target):
        slot = number // per_slot
        rows = aligned((number % per_slot) * CHAIN, CHAIN)
        here = stream.at[slot, rows]

        @pl.when(is_first)
        def _():
            stream[slot, rows, :] = own_part[slot, rows, :]

        @pl.when(jnp.logical_not(is_first))
        def _():
            remote(here, here, send.at[number], recv.at[number], target).wait_recv()
            stream[slot, rows, :] = stream[slot, rows, :] + own_part[slot, rows, :]

        @pl.when(jnp.logical_not(is_last))
        def _():
            remote(here, here, send.at[number], recv.at[number], target).start()

    def chain_tick(step):
        number = step - ctx

        @pl.when((number >= 0) & (number < chain_chunks))
        def _():
            chain_step(left, left_s, left_r, number, ctx == 0, ctx == n_ctx - 1, next_ctx)

        back = step - (n_ctx - 1 - ctx)

        @pl.when((back >= 0) & (back < chain_chunks))
        def _():
            chain_step(right, right_s, right_r, back, ctx == n_ctx - 1, ctx == 0, last_ctx)

    groups = PAIRS // PAIRED
    group_ticks = groups if shallow else 0
    block_ticks = group_ticks + 2
    chain_first = FF_TICKS + block_ticks
    paced = max(0, -(-(chunks - chain_first) // PACE))
    late_first = max(chunks, chain_first)
    late_beats = max(0, chain_chunks + n_ctx - 1 - paced)
    chain_ticks = late_first + TAIL_PACE * max(0, late_beats - 1) + 1

    def tick(step, kinds):
        kinds = kinds if shallow or kinds == "none" else "both"
        if kinds in ("low", "both"):

            @pl.when(step + 3 < chunks)
            def _():
                step_fetch(step + 3)

        if kinds != "none":

            @pl.when(step + 2 < chunks)
            def _():
                step_make(step + 2, kinds)

        for lag, act in stages:
            index = step - lag

            @pl.when((index >= 0) & (index < chunks))
            def _(act=act, index=index):
                act(index)

        beat = step - chain_first

        @pl.when((beat >= 0) & (step < chunks) & (beat % PACE == 0))
        def _():
            chain_tick(beat // PACE)

        late = step - late_first

        @pl.when((late >= 0) & (late % TAIL_PACE == 0))
        def _():
            chain_tick(paced + late // TAIL_PACE)


    for index in range(3):
        step_fetch(jnp.int32(index))
    for copy in set_copies(0):
        copy.start()

    hidden_tiles = u_hbm.shape[1] // SPAN
    datt_v, dz_v, dy_v, hat1_v, hat2_v = own_part.at[0], do_v, left.at[1], right.at[0], right.at[1]

    def tile_copies(tile, parity):
        cols = aligned(tile * SPAN, SPAN)
        return (
            pltpu.make_async_copy(w_down.at[cols, :], own_part.at[parity], sem_ff.at[0, parity]),
            pltpu.make_async_copy(
                w_up.at[:, cols], turned.at[0, aligned(parity * D, D), :], sem_ff.at[1, parity]
            ),
            pltpu.make_async_copy(
                u_hbm.at[:, cols], left.at[0, :, aligned(parity * SPAN, SPAN)], sem_ff.at[2, parity]
            ),
        )

    def du_store(tile, parity):
        return pltpu.make_async_copy(
            kv_b.at[0, :, aligned(parity * SPAN, SPAN)],
            du_hbm.at[:, aligned(tile * SPAN, SPAN)],
            sem_ff.at[3, parity],
        )

    dz_load = pltpu.make_async_copy(dz_hbm, dz_v, sem_in.at[0])
    dz_load.start()
    for copy in tile_copies(0, 0):
        copy.start()
    wide_loads = [
        pltpu.make_async_copy(source, dest, sem_in.at[place + 1])
        for place, (source, dest) in enumerate(
            (
                (dy_hbm, dy_v),
                (hat1_hbm, hat1_v),
                (hat2_hbm, hat2_v),
                (rstd_hbm, lse_v.at[pl.ds(0, 2)]),
                (q_hbm, q_v),
                (o_hbm, o_v),
                (w_hbm, weight),
            )
        )
    ]
    out_loads = [
        pltpu.make_async_copy(
            w_out.at[pl.ds(place * TILE, TILE), :],
            term.at[place // 2, place % 2, :, pl.ds(0, D)],
            sem_in.at[8 + place],
        )
        for place in range(4)
    ]
    pl.semaphore_wait(barrier, len(peers))
    lax.fori_loop(0, 2, lambda index, carry: (step_make(index, "low"), carry)[1], 0)
    dz_load.wait()

    def ff_tile(tile, carry):
        start = tile + (tile + 1) // 2
        extra = jnp.where((tile % 2 == 0) | (tile + 1 == hidden_tiles), 1, 0)
        lax.fori_loop(start, start + 1 + extra, lambda index, inner: (tick(index, "low"), inner)[1], 0)

        parity = tile % 2
        for copy in tile_copies(tile, parity):
            copy.wait()

        @pl.when(tile + 1 < hidden_tiles)
        def _():
            for copy in tile_copies(tile + 1, 1 - parity):
                copy.start()

        @pl.when(tile == 2)
        def _():
            for copy in wide_loads + out_loads:
                copy.start()

        @pl.when(tile >= 2)
        def _():
            du_store(tile - 2, parity).wait()

        u_cols = aligned(parity * SPAN, SPAN)
        u_tile = left[0, :, u_cols].astype(jnp.float32)
        square = u_tile * u_tile
        bend = jnp.tanh(GELU_C * u_tile * (1.0 + GELU_A * square))
        slope = 0.5 * (1.0 + bend) + (0.5 * GELU_C) * u_tile * (1.0 - bend * bend) * (
            1.0 + 3.0 * GELU_A * square
        )
        du_tile = (contract_last(dz_v[...], own_part[parity]) * slope).astype(jnp.bfloat16)
        kv_b[0, :, u_cols] = du_tile
        du_store(tile, parity).start()
        fresh = contract_last(du_tile, turned[0, aligned(parity * D, D), :])

        @pl.when(tile == 0)
        def _():
            dq_acc[...] = fresh

        @pl.when(tile > 0)
        def _():
            dq_acc[...] = dq_acc[...] + fresh

        return carry

    lax.fori_loop(0, hidden_tiles, ff_tile, 0)
    for tile in range(hidden_tiles - 2, hidden_tiles):
        du_store(tile, tile % 2).wait()
    for copy in wide_loads:
        copy.wait()
    for copy in block_copies(1):
        copy.start()

    def hidden_back(step, carry):
        gain1, gain2, bias1, bias2 = carry
        rows = aligned(step * CHAIN, CHAIN)
        upstream = dq_acc[rows, :]
        hat = hat2_v[rows, :].astype(jnp.float32)
        grad_h = dy_v[rows, :].astype(jnp.float32) + row_back(
            upstream, hat, lse_v[1, rows, 0:1], gain_ref[2:3, :]
        )
        gain2, bias2 = gain2 + column_sum(upstream * hat), bias2 + column_sum(upstream)
        dq_acc[rows, :] = grad_h
        if shallow:
            gkv[rows, :] = grad_h
        hat = hat1_v[rows, :].astype(jnp.float32)
        datt_v[rows, :] = row_back(grad_h, hat, lse_v[0, rows, 0:1], gain_ref[1:2, :]).astype(
            jnp.bfloat16
        )
        return gain1 + column_sum(grad_h * hat), gain2, bias1 + column_sum(grad_h), bias2

    zero = jnp.zeros((1, D), jnp.float32)
    sums = lax.fori_loop(0, BLK // CHAIN, hidden_back, (zero,) * 4)
    row = lax.broadcasted_iota(jnp.int32, (8, D), 0)
    norm_v[...] = norm_ref[...]
    for place, value in zip((1, 2, 5, 6), sums):
        norm_v[...] = norm_v[...] + jnp.where(row == place, value, 0.0)
    stores = [
        pltpu.make_async_copy(dq_acc, dh_hbm, sem_res.at[0]),
        pltpu.make_async_copy(datt_v, datt_hbm, sem_res.at[1]),
    ]
    lse_load = pltpu.make_async_copy(lse_hbm, lse_v, sem_in.at[0])
    for copy in stores + [lse_load]:
        copy.start()
    for load in out_loads:
        load.wait()

    def out_back(place, carry):
        do_v[:, aligned(place * TILE, TILE)] = contract_last(
            datt_v[...], term[place // 2, place % 2, :, pl.ds(0, D)]
        ).astype(jnp.bfloat16)
        return carry

    lax.fori_loop(0, 4, out_back, 0)
    for copy in stores + [lse_load]:
        copy.wait()
    dq_acc[...] = jnp.zeros_like(dq_acc)

    def attend(kv_ref, turned_ref, own, visible, begin):
        def body(group, carry):
            if shallow:
                tick(begin + group, "low")
            for member in range(PAIRED):
                grad_block(
                    q_v, do_v, o_v, lse_v, kv_ref, dq_acc, turned_ref, group * PAIRED + member, own, visible
                )
            return carry

        lax.fori_loop(0, groups, body, 0)

    def first_sums(piece, normed, cols):
        gain_sum[:, cols] = gain_sum[:, cols] + column_sum(piece * normed.astype(jnp.float32))
        bias_sum[:, cols] = bias_sum[:, cols] + column_sum(piece)

    gain_sum[...] = jnp.zeros_like(gain_sum)
    bias_sum[...] = jnp.zeros_like(bias_sum)

    def each_slot(slot, carry):
        visible = slot < own_slot
        index = slot + 1
        place = lax.rem(index, kv_b.shape[0])
        for copy in block_copies(index):
            copy.wait()
        if kv_b.shape[0] > 1:
            for copy in block_copies(index + 1):
                copy.start()
        begin = FF_TICKS + slot * block_ticks
        a_place = slot if shallow else 0
        attend(kv_b.at[place], turned.at[a_place], False, visible, begin)

        def weight_terms(step, inner):
            tick(begin + group_ticks + step, "low")
            rows = aligned(step * 512, 512)
            for part in range(0 if shallow else 2):
                cols = pl.ds(part * D, D)
                product = dot_dims(a_b[a_place, :, rows], turned[a_place, cols, :], 0, 1)
                for down in range(2):
                    target = term.at[step, down, :, pl.ds((part + 1) * D, D)]
                    piece = product[down * TILE : (down + 1) * TILE]

                    @pl.when(slot == 0)
                    def _(target=target, piece=piece):
                        target[...] = piece.astype(target.dtype)

                    @pl.when(slot > 0)
                    def _(target=target, piece=piece):
                        target[...] = (target[...] + piece).astype(target.dtype)

            piece = dot_dims(turned[a_place], weight[rows, pl.ds(D, 2 * D)], 0, 1)
            own_part[slot, :, rows] = piece.astype(jnp.bfloat16)
            first_sums(piece, a_b[a_place, :, rows], rows)
            return inner

        lax.fori_loop(0, 2, weight_terms, 0)
        if kv_b.shape[0] == 1:
            for copy in block_copies(index + 1):
                copy.start()
        return carry

    lax.fori_loop(0, slots, each_slot, 0)
    begin = FF_TICKS + slots * block_ticks
    own_place = (slots + 1) % kv_b.shape[0]
    for copy in block_copies(slots + 1):
        copy.wait()
    own_a = slots if shallow else 0
    attend(kv_b.at[own_place], turned.at[own_a], True, None, begin)
    dq_low[...] = (dq_acc[...] * ALPHA).astype(jnp.bfloat16) * jnp.bfloat16(QSCALE)
    x_load = pltpu.make_async_copy(x_hbm, do_v, sem_in.at[0])
    x_load.start()
    ready = begin + group_ticks

    def last_terms(step, carry):
        tick(begin + group_ticks + step, "both")
        rows = aligned(step * TILE, TILE)
        a_rows = a_b[0, :, rows]
        up, down = step // 2, step % 2
        term[up, down, :, pl.ds(0, D)] = dot_dims(a_rows, dq_low[...], 0, 0).astype(jnp.bfloat16)
        for part in range(2):
            cols = pl.ds(part * D, D)
            target = term.at[up, down, :, pl.ds((part + 1) * D, D)]
            target[...] = (target[...] + dot_dims(a_rows, turned[0, cols, :], 0, 1)).astype(jnp.bfloat16)
        return carry

    if not shallow:
        lax.fori_loop(0, 4, last_terms, 0)
        ready = ready + 4
    assert ready <= last_low - 2
    da_acc = dq_acc

    spare = max(0, last_low - 2 - ready - 4) if shallow else 0

    def own_grad(step, carry):
        if shallow:
            begins = ready + step + jnp.where(step > 0, spare, 0)
            ends = ready + step + 1 + spare
            lax.fori_loop(begins, ends, lambda index, inner: (tick(index, "low"), inner)[1], 0)
        else:
            tick(ready + step, "low")
        rows = aligned(step * TILE, TILE)
        piece = dot_dims(dq_low[...], weight[rows, pl.ds(0, D)], 1, 1) + dot_dims(
            turned[own_a], weight[rows, pl.ds(D, 2 * D)], 0, 1
        )
        da_acc[:, rows] = piece
        first_sums(piece, a_b[own_a, :, rows], rows)
        return carry

    lax.fori_loop(0, 4, own_grad, 0)
    ready = ready + 4 + spare

    first_gain = (gain_sum[...] - bias_ref[0:1, :] * bias_sum[...]) / gain_ref[0:1, :]
    norm_v[...] = (
        norm_v[...] + jnp.where(row == 0, first_gain, 0.0) + jnp.where(row == 4, bias_sum[...], 0.0)
    )

    def run_ticks(first, last, kinds):
        if last > first:
            lax.fori_loop(first, last, lambda index, carry: (tick(index, kinds), carry)[1], 0)
        return max(first, last)

    assert ready == last_low - 2 or not shallow
    norm_peers = [core_peer, side_peer, grp_peer] + level_peers
    norm_base = ready
    norm_result = pltpu.make_async_copy(norm_v, norm_out, sem_res.at[1])

    def norm_move(place):
        return remote(norm_v, norm_in.at[place], norm_s.at[place], norm_r.at[place], norm_peers[place])

    def norm_ticks(step, carry):
        for place in range(len(norm_peers) + 1):

            @pl.when(step == norm_base + 3 * place)
            def _(place=place):
                if place:
                    finished(norm_move(place - 1))
                    norm_v[...] = norm_v[...] + norm_in[place - 1]
                if place < len(norm_peers):
                    norm_move(place).start()
                else:
                    norm_result.start()

        tick(step, "high")
        return carry

    last_tick = max(ready + 3 * len(norm_peers) + 1, chain_ticks)
    lax.fori_loop(ready, last_tick, norm_ticks, 0)
    ready = last_tick
    x_load.wait()
    gain = gain_ref[0:1, :]

    def norm_grad(step, carry):
        @pl.when(step % 2 == 0)
        def _():
            tick(ready + step // 2, "none")

        rows = aligned(step * CHAIN, CHAIN)
        upstream = da_acc[rows, :]
        for slot in range(slots):
            joined = left[slot, rows, :].astype(jnp.float32) + right[slot, rows, :].astype(jnp.float32)
            upstream = upstream + jnp.where(own_slot == slot, joined, 0.0)
        values = do_v[rows, :].astype(jnp.float32)
        centre = values - jnp.mean(values, axis=-1, keepdims=True)
        scale = lax.rsqrt(jnp.mean(centre * centre, axis=-1, keepdims=True) + EPS)
        centre = centre * scale
        grad = row_back(upstream, centre, scale, gain)
        da_acc[rows, :] = grad + gkv[rows, :] if shallow else grad
        return carry

    lax.fori_loop(0, BLK // CHAIN, norm_grad, 0)
    ready = ready + BLK // CHAIN // 2
    result = pltpu.make_async_copy(da_acc, grad_out, sem_res.at[0])
    result.start()
    run_ticks(ready, all_ticks, "none")

    def drain_chain(index, carry):
        here = left.at[0, pl.ds(0, CHAIN)]

        @pl.when(ctx < n_ctx - 1)
        def _():
            remote(here, here, left_s.at[index], left_r.at[index], next_ctx).wait_send()

        @pl.when(ctx > 0)
        def _():
            remote(here, here, right_s.at[index], right_r.at[index], last_ctx).wait_send()

        return carry

    lax.fori_loop(0, chain_chunks, drain_chain, 0)
    result.wait()
    norm_result.wait()


def backward_part(n_ctx, slot_vec, gains, biases, norms, saved, weights, ffn):
    slots = n_ctx // 2
    levels = n_ctx.bit_length() - 1
    depth = 16 if n_ctx == 4 else 10
    hidden = weights[1].shape[1]
    widths = [(hidden // 4, D), (D // 4, hidden), (D // 4, D), (D // 4, 3 * D)]
    low, full = jnp.bfloat16, jnp.float32
    dma = pltpu.SemaphoreType.DMA
    hbm = pl.BlockSpec(memory_space=pl.ANY)
    vmem = pl.BlockSpec(memory_space=pltpu.VMEM)
    shape = jax.ShapeDtypeStruct
    buffers = 2 if slots <= 2 else 1
    chain = slots * (BLK // CHAIN)
    zshapes, rows, cols = [], TILE // 2, TILE
    if n_ctx == 4:
        zshapes = [pltpu.VMEM((depth, rows, cols), low), pltpu.VMEM((depth, rows // 2, cols), low)]
    for _ in range(0 if zshapes else levels):
        rows, cols = (rows // 2, cols) if rows > 16 else (rows, cols // 2)
        zshapes.append(pltpu.VMEM((depth, rows, cols), low))
    return pl.pallas_call(
        functools.partial(backward_kernel, n_ctx, widths),
        out_shape=[shape(width, low) for width in widths] + [
            shape((BLK, D), full),
            shape((8, D), full),
            shape((BLK, D), full),
            shape((BLK, hidden), low),
            shape((BLK, D), low),
        ],
        in_specs=[pl.BlockSpec(memory_space=pltpu.SMEM), vmem, vmem, vmem]
        + [hbm] * (len(saved) + len(weights) + len(ffn)),
        out_specs=[hbm] * 9,
        scratch_shapes=[
            pltpu.VMEM((BLK, D), low),
            pltpu.VMEM((BLK, D), low),
            pltpu.VMEM((BLK, D), low),
            pltpu.VMEM((PAIRS, BLK, 128), full),
            pltpu.VMEM((D, 3 * D), low),
            pltpu.VMEM((buffers, BLK, 2 * D), low),
            pltpu.VMEM((slots + 1 if slots <= 2 else 1, BLK, D), low),
            pltpu.VMEM((BLK, D), full),
            pltpu.VMEM((slots + 1 if slots <= 2 else 1, 2 * D, BLK), low),
            pltpu.VMEM((BLK, D) if slots <= 2 else (8, 128), full),
            pltpu.VMEM((2, 2, D // 4, D if slots <= 2 else 3 * D), low),
            pltpu.VMEM((slots, BLK, D), low),
            pltpu.VMEM((slots, BLK, D), low),
            pltpu.VMEM((slots, BLK, D), low),
            pltpu.VMEM((8, D), full),
            pltpu.VMEM((3 + levels, 8, D), full),
            pltpu.VMEM((1, D), full),
            pltpu.VMEM((1, D), full),
            pltpu.VMEM((depth, 2, TILE, TILE), low),
            pltpu.VMEM((depth, TILE, TILE), low),
            pltpu.VMEM((depth, TILE // 2, TILE), low),
            pltpu.VMEM((depth, TILE, TILE), low),
            pltpu.VMEM((4, 2, 2, TILE, TILE), low),
        ]
        + [pltpu.VMEM((2, 4, BLK, TILE), low), pltpu.VMEM((4, BLK, TILE), low)]
        + zshapes
        + [dma((12,)), dma((2, buffers)), dma((4,)), dma((2, 4)), dma((4, 2)), dma((depth,)), dma((2,))]
        + [dma((depth,))] * (8 + 4 * levels)
        + [dma((chain,))] * 4
        + [dma((3 + levels,))] * 2,
        compiler_params=pltpu.CompilerParams(
            collective_id=2, has_side_effects=True, vmem_limit_bytes=67043328
        ),
        cost_estimate=pl.CostEstimate(flops=40 << 30, bytes_accessed=64 << 20, transcendentals=1 << 24),
        name="attend_back_reduce",
    )(
        slot_vec,
        gains,
        biases,
        norms,
        *saved,
        *weights,
        *ffn,
    )


def widen_kernel(*refs):
    count = len(refs) // 2
    for source, dest in zip(refs[: count - 1], refs[count:]):
        dest[...] = source[...].astype(dest.dtype)
    refs[-2][...] = refs[count - 1][0:4, :]
    refs[-1][...] = refs[count - 1][4:8, :]


def widen(arrays, types, norms):
    steps = 4
    specs = [pl.BlockSpec((x.shape[0] // steps, x.shape[1]), lambda i: (i, 0)) for x in arrays]
    shape = jax.ShapeDtypeStruct
    pair = [pl.BlockSpec((4, D), lambda i: (0, 0))] * 2
    return pl.pallas_call(
        widen_kernel,
        out_shape=[shape(x.shape, kind) for x, kind in zip(arrays, types)]
        + [shape((4, D), jnp.float32)] * 2,
        grid=(steps,),
        in_specs=specs + [pl.BlockSpec((8, D), lambda i: (0, 0))],
        out_specs=specs + pair,
        compiler_params=pltpu.CompilerParams(vmem_limit_bytes=67043328),
        name="widen",
    )(*arrays, norms)


def per_device(n_ctx, inputs, w_qkv, w_out, w_up, w_down, norm_gains, norm_biases, block_map, out_grad):
    slots = n_ctx // 2
    raw, seed_low = inputs.reshape(BLK, D), out_grad.reshape(BLK, D)
    block_entry = block_map.reshape(2)
    forward = forward_part(
        n_ctx,
        block_entry,
        norm_gains,
        norm_biases,
        raw,
        seed_low,
        w_qkv,
        w_out,
        w_up,
        w_down,
    )
    every_low, queries, keys_values, attn_low, lse, full_qkv, full_out, full_up, full_down = forward[:9]
    result, active_low, down_low, ffn_low, upward, hat1, hat2, rstd, norms = forward[9:]
    backward = backward_part(
        n_ctx,
        block_entry,
        norm_gains,
        norm_biases,
        norms,
        [raw, queries, keys_values, every_low, attn_low, lse, full_qkv],
        [full_out, full_up, full_down],
        [active_low, down_low, ffn_low, upward, hat1, hat2, rstd, seed_low],
    )
    grad_tokens, norm_total, grad_hidden = backward[4:7]
    if slots > 2:
        grad_tokens = grad_tokens + grad_hidden
    full = jnp.float32
    summed_down, summed_up, summed_out, summed_qkv, grad_input, result, gain_total, bias_total = widen(
        list(backward[:4]) + [grad_tokens, result],
        [full] * 5 + [jnp.bfloat16],
        norm_total,
    )
    return (
        result.reshape(1, 1, BLK, D),
        grad_input.reshape(1, 1, BLK, D),
        summed_qkv,
        summed_out,
        summed_up,
        summed_down,
        gain_total,
        bias_total,
    )


def solution(mesh):
    rows = P("wsh", None)
    blocks = P("grp", "wsh", "ctx", None)
    return jax.shard_map(
        functools.partial(per_device, mesh.shape["ctx"]),
        mesh=mesh,
        in_specs=(blocks, rows, rows, rows, rows, P(), P(), blocks, blocks),
        out_specs=(blocks, blocks, rows, rows, rows, rows, P(), P()),
        check_vma=False,
    )
```
